32 devices in a mesh: shard: 4 (over x, core), ctx: 4 (over z), tp: 2 (over y).
Axes of the slice: x: 2, y: 2, z: 4, core: 2. Of those that a mesh axis runs over, the one named last changes fastest.
Arguments:
- block_input: float32 [8, 1024, 2048], P('shard', 'ctx'), may hold values from -6 to 6
- segment_ids: int32 [8, 1024], P('shard', 'ctx'), may hold values from 0 to 3, never falling along the last dimension, each value on 1 to 800 neighbouring positions
- norm_gain: float32 [2048], replicated, may hold values from 0.25 to 1.75
- lower: float32 [2048], P('tp'), may hold values from 0.5 to 0.9999
- w_input: float32 [2048, 2048], P(('shard', 'ctx'), 'tp'), may hold values from -0.125 to 0.125
- w_forget: float32 [2048, 2048], P(('shard', 'ctx'), 'tp'), may hold values from -0.125 to 0.125
- w_gate: float32 [2048, 2048], P(('shard', 'ctx'), 'tp'), may hold values from -0.125 to 0.125
- hidden_gain: float32 [2048], P('tp'), may hold values from 0.25 to 1.75
- w_out: float32 [2048, 2048], P(('shard', 'ctx'), 'tp'), may hold values from -0.125 to 0.125
- mlp_gain: float32 [2048], replicated, may hold values from 0.25 to 1.75
- w_mlp_gate: float32 [2048, 5632], P(('shard', 'ctx'), 'tp'), may hold values from -0.125 to 0.125
- w_mlp_up: float32 [2048, 5632], P(('shard', 'ctx'), 'tp'), may hold values from -0.125 to 0.125
- w_down: float32 [2048, 5632], P(('shard', 'ctx'), 'tp'), may hold values from -0.078125 to 0.078125
- cotangent: float32 [8, 1024, 2048], P('shard', 'ctx'), may hold values from -6 to 6
Outputs:
- block_output: float32 [8, 1024, 2048], P('shard', 'ctx')
- input_grad: float32 [8, 1024, 2048], P('shard', 'ctx')
- norm_gain_grad: float32 [2048], replicated
- lower_grad: float32 [2048], P('tp')
- w_input_grad: float32 [2048, 2048], P(('shard', 'ctx'), 'tp')
- w_forget_grad: float32 [2048, 2048], P(('shard', 'ctx'), 'tp')
- w_gate_grad: float32 [2048, 2048], P(('shard', 'ctx'), 'tp')
- hidden_gain_grad: float32 [2048], P('tp')
- w_out_grad: float32 [2048, 2048], P(('shard', 'ctx'), 'tp')
- mlp_gain_grad: float32 [2048], replicated
- w_mlp_gate_grad: float32 [2048, 5632], P(('shard', 'ctx'), 'tp')
- w_mlp_up_grad: float32 [2048, 5632], P(('shard', 'ctx'), 'tp')
- w_down_grad: float32 [2048, 5632], P(('shard', 'ctx'), 'tp')
The draws below stay inside these ranges and needn't reach their ends.
Inputs may be any that keep to these rules, and one draw needn't show every extreme that they name: `segment_ids`: document ids of each sequence; they never fall along a sequence, and one document holds at most 800 tokens.
All inputs are finite; a program needn't handle non-finite values.
Results may differ from the reference program's by a relative error of at most 0.018.
Values may be sent and summed in bfloat16 or wider, within the bound.
A program may use at most 256 MiB of HBM per device.

```python
import math
import jax
import jax.numpy as jnp
import numpy as np
from jax import lax

D = 2048
FF = 5632
SEQS = 2
LEN = 1024
SEG_COUNT = 4
SEG_MOST = 800
BATCH = 8


def draw_lower(key, part):
    uniform_part = jax.random.uniform(key, (D,), jnp.float32)
    log_floor = math.log(0.0001)
    log_ceiling = math.log(0.5)
    return 1.0 - jnp.exp(log_floor + uniform_part * (log_ceiling - log_floor))


def block_scale(own_key, extent, split, least, largest):
    def one(position, parts):
        steps = jax.random.uniform(jax.random.fold_in(jax.random.fold_in(own_key, 6), position), (parts,), jnp.float32, least / len(split), largest / len(split))
        return jnp.repeat(jnp.exp(steps), extent[position] // parts).reshape((-1,) + (1,) * (len(extent) - position - 1))

    factor_of = one(*split[0])
    for cut in split[1:]:
        factor_of = factor_of * one(*cut)
    return factor_of


def profile(number_of, total, limit, slope):
    portions = [(1 << 20) // math.isqrt(rank ** slope) + 1 for rank in range(2, number_of + 1)]
    rest, given = total - limit - (number_of - 1), [1] * (number_of - 1)
    while rest > 0:
        free = [i for i in range(number_of - 1) if given[i] < limit]
        mass, left = sum([portions[i] for i in free]), rest
        for i in free:
            addition = min(limit - given[i], max(1, left * portions[i] // mass), rest)
            given[i] = given[i] + addition
            rest = rest - addition
    return np.array([limit] + given)


def uneven(rng, amount, total, most, slope):
    if amount == 2:
        one = jax.random.randint(rng, (), max(1, total - most), min(most, total - 1) + 1)
        return jnp.stack([one, total - one])
    sizes = jnp.asarray(profile(amount, total, most, slope), jnp.int32)
    couples = (amount - 1) // 2
    giver, sink = sizes[1:1 + 2 * couples:2], sizes[2:2 + 2 * couples:2]
    margin = jnp.minimum(giver - 1, most - sink)
    shifted = jax.random.randint(jax.random.fold_in(rng, 1), (couples,), 0, 1 << 20) % (margin + 1)
    sizes = sizes.at[1:1 + 2 * couples:2].set(giver - shifted).at[2:2 + 2 * couples:2].set(sink + shifted)
    return sizes[jax.random.permutation(jax.random.fold_in(rng, 2), amount)]


def normal_values(rng, shape, scale, most, cuts=(), dtype=jnp.bfloat16):
    values = jax.random.normal(rng, shape, jnp.float32) * scale
    if len(cuts) > 0:
        values = block_scale(rng, shape, cuts, -0.22, 0.18) * values
    return jnp.clip(values, min=-most, max=most).astype(dtype)


def setup_inputs(seed: int = 0) -> dict:
    seeds = jax.random.split(jax.random.key(seed), 15)
    block_input = normal_values(seeds[0], (BATCH, LEN, D), 1.0, 6.0, ((0, 4), (1, 4)), jnp.float32)
    segment_ids = jax.vmap(lambda own: jnp.searchsorted(jnp.cumsum(uneven(own, SEG_COUNT, LEN, SEG_MOST, 0)), jnp.arange(LEN), side="right"))(jax.random.split(seeds[1], BATCH)).reshape((BATCH, LEN)).astype(jnp.int32)
    norm_gain = jnp.clip(1.0 + 0.15 * jax.random.normal(seeds[2], (D,), jnp.float32), 0.25, 1.75)
    lower = draw_lower(jax.random.fold_in(seeds[14], 71), 0)
    w_input = normal_values(seeds[4], (D, D), D ** -0.5, 0.125, ((0, 16), (1, 2)), jnp.float32)
    w_forget = normal_values(seeds[5], (D, D), D ** -0.5, 0.125, ((0, 16), (1, 2)), jnp.float32)
    w_gate = normal_values(seeds[6], (D, D), D ** -0.5, 0.125, ((0, 16), (1, 2)), jnp.float32)
    hidden_gain = jnp.clip(1.0 + 0.15 * jax.random.normal(seeds[7], (D,), jnp.float32), 0.25, 1.75)
    w_out = normal_values(seeds[8], (D, D), D ** -0.5, 0.125, ((0, 16), (1, 2)), jnp.float32)
    mlp_gain = jnp.clip(1.0 + 0.15 * jax.random.normal(seeds[9], (D,), jnp.float32), 0.25, 1.75)
    w_mlp_gate = normal_values(seeds[10], (D, FF), D ** -0.5, 0.125, ((0, 16), (1, 2)), jnp.float32)
    w_mlp_up = normal_values(seeds[11], (D, FF), D ** -0.5, 0.125, ((0, 16), (1, 2)), jnp.float32)
    w_down = normal_values(seeds[12], (D, FF), FF ** -0.5, 0.078125, ((0, 16), (1, 2)), jnp.float32)
    cotangent = normal_values(seeds[13], (BATCH, LEN, D), 1.0, 6.0, ((0, 4), (1, 4)), jnp.float32)
    return {"block_input": block_input, "segment_ids": segment_ids, "norm_gain": norm_gain, "lower": lower, "w_input": w_input, "w_forget": w_forget, "w_gate": w_gate, "hidden_gain": hidden_gain, "w_out": w_out, "mlp_gain": mlp_gain, "w_mlp_gate": w_mlp_gate, "w_mlp_up": w_mlp_up, "w_down": w_down, "cotangent": cotangent}


@jax.custom_vjp
def low(v):
    return lax.optimization_barrier(v.astype(jnp.bfloat16)).astype(jnp.float32)

@jax.custom_vjp
def low_back(v):
    return v

def low_keep(v):
    return (low(v), None)

def low_pass(kept, grad):
    return (grad,)

def back_keep(v):
    return (v, None)

def back_low(kept, grad):
    return (low(grad),)
low.defvjp(low_keep, low_pass)
low_back.defvjp(back_keep, back_low)

def inverse_rms(inputs):
    return lax.rsqrt(lax.optimization_barrier(jnp.mean(inputs * inputs, axis=-1, keepdims=True)) + 1e-06)

def product(left_mat, right_mat):
    return jnp.dot(left_mat, right_mat, precision=lax.Precision.HIGHEST, preferred_element_type=jnp.float32)

def linear_step(first_part, second_part):
    return (first_part[0] * second_part[0], second_part[0] * first_part[1] + second_part[1])

def residual_block(tokens_in, segments, params):
    norm_gain, lower, w_input, w_forget, w_gate, hidden_gain, w_out, mlp_gain, w_mlp_gate, w_mlp_up, w_down = params
    same_doc = jnp.where(segments[:, 1:] == segments[:, :-1], 1.0, 0.0).astype(jnp.float32)
    linked = jnp.concatenate([jnp.zeros((segments.shape[0], 1), jnp.float32), same_doc], axis=1)
    normed_one = low(tokens_in * inverse_rms(tokens_in) * norm_gain)
    proj_input = low_back(product(normed_one, low(w_input)))
    proj_forget = low_back(product(normed_one, low(w_forget)))
    proj_gate = low_back(product(normed_one, low(w_gate)))
    sigmoid_f = jax.nn.sigmoid(proj_forget)
    forget = lower + (1.0 - lower) * sigmoid_f
    candidate = jax.nn.silu(proj_input) * (1.0 - forget)
    decay_all, states = lax.associative_scan(linear_step, (forget * linked[:, :, None], candidate), axis=1)
    mixed_in = low(states * inverse_rms(states) * hidden_gain * jax.nn.silu(proj_gate))
    middle = tokens_in + low_back(product(mixed_in, low(w_out).T))
    normed_two = low(middle * inverse_rms(middle) * mlp_gain)
    gate_pre = low_back(product(normed_two, low(w_mlp_gate)))
    up_pre = low_back(product(normed_two, low(w_mlp_up)))
    activated = low(jax.nn.silu(gate_pre) * up_pre)
    return middle + low_back(product(activated, low(w_down).T))

def reference(block_input, segment_ids, norm_gain, lower, w_input, w_forget, w_gate, hidden_gain, w_out, mlp_gain, w_mlp_gate, w_mlp_up, w_down, cotangent):
    params = (norm_gain, lower, w_input, w_forget, w_gate, hidden_gain, w_out, mlp_gain, w_mlp_gate, w_mlp_up, w_down)
    groups = block_input.shape[0] // SEQS
    inputs_grouped = block_input.reshape(groups, SEQS, LEN, D)
    segments_grouped = segment_ids.reshape(groups, SEQS, LEN)
    upstream_grouped = cotangent.reshape(groups, SEQS, LEN, D)

    def one_group(totals, group_item):
        tokens_in, segments, upstream = group_item
        result, pullback = jax.vjp(lambda inside, weights: residual_block(inside, segments, weights), tokens_in, params)
        grad_in, grad_params = pullback(upstream)
        summed = jax.tree.map(lambda before_sum, fresh: before_sum + fresh, totals, grad_params)
        return (summed, (result, grad_in))
    zeros_init = jax.tree.map(jnp.zeros_like, params)
    totals, (outputs, grads_in) = lax.scan(one_group, zeros_init, (inputs_grouped, segments_grouped, upstream_grouped))
    return (outputs.reshape(block_input.shape), grads_in.reshape(block_input.shape), totals[0], totals[1], totals[2], totals[3], totals[4], totals[5], totals[6], totals[7], totals[8], totals[9], totals[10])
```

```python
import functools
import jax
import jax.numpy as jnp
from jax import lax
from jax.experimental import pallas as pl
from jax.experimental.pallas import tpu as pltpu
from jax.sharding import PartitionSpec as P

epsilon = 1e-06
MESH = pl.DeviceIdType.MESH


def remote(src, dst, send_sem, recv_sem, device):
    return pltpu.make_async_remote_copy(
        src_ref=src, dst_ref=dst, send_sem=send_sem, recv_sem=recv_sem,
        device_id=device, device_id_type=MESH)


def gather_body(nw, Z, ahead, relay, *refs):
    own, out = refs[:nw], refs[nw:2 * nw]
    (s_up, r_up, s_dn, r_dn, s_x, r_x, s_c, r_c, s_h, r_h, l_sem) = refs[2 * nw:]
    s, z = lax.axis_index("shard"), lax.axis_index("ctx")
    q, c = s // 2, lax.rem(s, 2)
    sx, sc = (1 - q) * 2 + c, q * 2 + (1 - c)
    sxc = (1 - q) * 2 + (1 - c)
    even = lax.rem(z, 2) == 0
    zp = jnp.where(even, z + 1, z - 1)
    rows = [r.shape[0] for r in own]

    def block(w, s_, z_, part=0):
        R = rows[w]
        start = pl.multiple_of((s_ * Z + z_) * R, R)
        if part == 0:
            return out[w].at[pl.ds(start, R), :]
        H = R // 2
        return out[w].at[pl.ds(pl.multiple_of(start + (part - 1) * H, H), H), :]

    UP, DN, XX, CC, ZP = {"ctx": z + 1}, {"ctx": z - 1}, {"shard": sx}, {"shard": sc}, {"ctx": zp}

    def up(w, k, src=None):
        b = block(w, s, z - k)
        return remote(b if src is None else src, b, s_up.at[w, k], r_up.at[w, k], UP)

    def dn(w, k, src=None):
        b = block(w, s, z + k)
        return remote(b if src is None else src, b, s_dn.at[w, k], r_dn.at[w, k], DN)

    def origin(j):
        return z if j == 0 else (z - j if j < Z else z + j - Z + 1)

    def valid(j):
        return (z >= j) if j < Z else (z + j - Z + 1 <= Z - 1)

    def xx(w, j, part, src=None):
        b = block(w, s, origin(j), part)
        return remote(b if src is None else src, b, s_x.at[w, j], r_x.at[w, j], XX)

    def xx_in(w, j, part):
        b = block(w, sx, origin(j), part)
        return remote(b, b, s_x.at[w, j], r_x.at[w, j], XX)

    def cc(w, j, src=None):
        b = block(w, s if j < 2 * Z - 1 else sx, origin(j % (2 * Z - 1)))
        return remote(b if src is None else src, b, s_c.at[w, j], r_c.at[w, j], CC)

    def cc_in(w, j):
        b = block(w, sc if j < 2 * Z - 1 else sxc, origin(j % (2 * Z - 1)))
        return remote(b, b, s_c.at[w, j], r_c.at[w, j], CC)

    def half(w):
        b = block(w, sx, z, 1)
        return remote(b, b, s_h.at[w], r_h.at[w], ZP)

    def half_in(w):
        b = block(w, sx, zp, 1)
        return remote(b, b, s_h.at[w], r_h.at[w], ZP)

    barrier = pltpu.get_barrier_semaphore()
    for d in (XX, CC):
        pl.semaphore_signal(barrier, inc=1, device_id=d, device_id_type=MESH)

    @pl.when(z < Z - 1)
    def _():
        pl.semaphore_signal(barrier, inc=1, device_id=UP, device_id_type=MESH)

    @pl.when(z > 0)
    def _():
        pl.semaphore_signal(barrier, inc=1, device_id=DN, device_id_type=MESH)

    pl.semaphore_wait(barrier, 2 + (z < Z - 1).astype(jnp.int32) + (z > 0).astype(jnp.int32))

    local = []
    for w in range(nw):
        cp = pltpu.make_async_copy(own[w], block(w, s, z), l_sem.at[w])
        cp.start()
        local.append(cp)

    def begin(w):
        @pl.when(z < Z - 1)
        def _():
            up(w, 0, own[w]).start()

        @pl.when(z > 0)
        def _():
            dn(w, 0, own[w]).start()

        xx(w, 0, 0, own[w]).start()
        cc(w, 0, own[w]).start()

    def is_pair(j):
        if j == 1:
            return jnp.logical_not(even)
        if j == Z:
            return even
        return None

    def for_part(w, j, fn):
        pair = is_pair(j) if relay else None
        if pair is None:
            fn(0)
        else:
            @pl.when(pair)
            def _():
                fn(2)

            @pl.when(jnp.logical_not(pair))
            def _():
                fn(0)

    def step(w, k):
        @pl.when(z >= k)
        def _():
            remote(block(w, s, z - k), block(w, s, z - k), s_up.at[w, k - 1], r_up.at[w, k - 1], UP).wait_recv()
            if k < Z - 1:
                @pl.when(z < Z - 1)
                def _():
                    up(w, k).start()
            for_part(w, k, lambda p: xx(w, k, p).start())
            cc(w, k).start()

        @pl.when(z + k <= Z - 1)
        def _():
            remote(block(w, s, z + k), block(w, s, z + k), s_dn.at[w, k - 1], r_dn.at[w, k - 1], DN).wait_recv()
            if k < Z - 1:
                @pl.when(z > 0)
                def _():
                    dn(w, k).start()
            for_part(w, Z - 1 + k, lambda p: xx(w, Z - 1 + k, p).start())
            cc(w, Z - 1 + k).start()

    def xstep(w, j):
        @pl.when(valid(j))
        def _():
            for_part(w, j, lambda p: xx_in(w, j, p).wait_recv())
            if j == 0:
                if relay:
                    half(w).start()
                cc(w, 2 * Z - 1).start()
            else:
                if relay and is_pair(j) is not None:
                    @pl.when(is_pair(j))
                    def _():
                        half_in(w).wait_recv()
                cc(w, 2 * Z - 1 + j).start()

    def finish(w):
        for j in range(4 * Z - 2):
            @pl.when(valid(j % (2 * Z - 1)))
            def _():
                cc_in(w, j).wait_recv()
                cc(w, j).wait_send()
        for j in range(2 * Z - 1):
            @pl.when(valid(j))
            def _():
                for_part(w, j, lambda p: xx(w, j, p).wait_send())
        for k in range(Z - 1):
            @pl.when((z >= k) & (z < Z - 1))
            def _():
                up(w, k).wait_send()

            @pl.when((z + k <= Z - 1) & (z > 0))
            def _():
                dn(w, k).wait_send()
        if relay:
            half(w).wait_send()
        local[w].wait()

    for w in range(min(ahead, nw)):
        begin(w)
    for w in range(nw):
        for k in range(1, Z):
            step(w, k)
            if k == 1:
                xstep(w, 0)
                if w + ahead < nw:
                    begin(w + ahead)
            else:
                xstep(w, k - 1)
                xstep(w, Z - 1 + k - 1)
            if w > 0 and k == 1:
                xstep(w - 1, Z - 1)
                xstep(w - 1, 2 * Z - 2)
    xstep(nw - 1, Z - 1)
    xstep(nw - 1, 2 * Z - 2)
    for w in range(nw):
        finish(w)


def gather_all(shards, S, Z, collective_id=0, ahead=2, relay=True):
    nw = len(shards)
    dma = pltpu.SemaphoreType.DMA
    return pl.pallas_call(
        functools.partial(gather_body, nw, Z, ahead, relay),
        out_shape=[jax.ShapeDtypeStruct((a.shape[0] * S * Z, a.shape[1]), a.dtype) for a in shards],
        in_specs=[pl.BlockSpec(memory_space=pltpu.VMEM)] * nw,
        out_specs=[pl.BlockSpec(memory_space=pl.ANY)] * nw,
        scratch_shapes=[
            dma((nw, Z - 1)), dma((nw, Z - 1)), dma((nw, Z - 1)), dma((nw, Z - 1)),
            dma((nw, 2 * Z - 1)), dma((nw, 2 * Z - 1)),
            dma((nw, 4 * Z - 2)), dma((nw, 4 * Z - 2)), dma((nw,)), dma((nw,)), dma((nw,)),
        ],
        compiler_params=pltpu.CompilerParams(collective_id=collective_id, has_side_effects=True),
        name="weights_in",
    )(*shards)


def carried_in(x, axis, combine, identity, reverse):
    size, position = (lax.axis_size(axis), lax.axis_index(axis))
    everything = jax.tree.map(lambda part: lax.all_gather(part, axis), x)
    start = jax.tree.map(
        lambda part, zero: jnp.broadcast_to(jnp.asarray(zero, part.dtype), part.shape), x, identity
    )

    def turn(k, before):
        at = size - 1 - k if reverse else k
        reached = at > position if reverse else at < position
        new = combine(before, jax.tree.map(lambda part: part[at], everything))
        return jax.tree.map(lambda a, b: jnp.where(reached, a, b), new, before)

    return lax.fori_loop(0, size, turn, start)


def inverse_rms(inputs):
    return lax.rsqrt(jnp.mean(inputs * inputs, axis=-1, keepdims=True) + epsilon)


def rms_backward(inputs, row_scale, gain_vec, upstream):
    weighted = upstream * gain_vec
    inner_sum = jnp.mean(weighted * inputs, axis=-1, keepdims=True)
    return weighted * row_scale - inputs * (row_scale * row_scale * row_scale) * inner_sum


def silu_slope(inputs):
    sig_part = jax.nn.sigmoid(inputs)
    return sig_part * (1.0 + inputs * (1.0 - sig_part))


def times_back(left_mat, right_mat):
    return lax.dot_general(
        left_mat, right_mat, (((1,), (1,)), ((), ())), preferred_element_type=jnp.float32
    )


def outer_sum(left_mat, right_mat):
    return lax.dot_general(
        left_mat, right_mat, (((0,), (0,)), ((), ())), preferred_element_type=jnp.float32
    )


def linear_step(first_part, second_part):
    return (first_part[0] * second_part[0], second_part[0] * first_part[1] + second_part[1])


def joined(last_ids, first_ids):
    return jnp.where((last_ids == first_ids) | (last_ids < 0.0) | (first_ids < 0.0), 1.0, 0.0)


def forward_join(first_part, second_part):
    linked = joined(first_part[3], second_part[2])[:, None]
    return (
        first_part[0] * second_part[0] * linked,
        second_part[0] * linked * first_part[1] + second_part[1],
        jnp.where(first_part[2] < 0.0, second_part[2], first_part[2]),
        jnp.where(second_part[3] < 0.0, first_part[3], second_part[3]),
    )


def backward_join(first_part, second_part):
    linked = joined(second_part[3], first_part[2])[:, None]
    return (
        second_part[0] * linked * first_part[0],
        second_part[0] * linked * first_part[1] + second_part[1],
        jnp.where(second_part[2] < 0.0, first_part[2], second_part[2]),
        jnp.where(first_part[3] < 0.0, second_part[3], first_part[3]),
    )


def on_device(
    block_input,
    segment_ids,
    norm_gain,
    lower,
    w_input,
    w_forget,
    w_gate,
    hidden_gain,
    w_out,
    mlp_gain,
    w_mlp_gate,
    w_mlp_up,
    w_down,
    cotangent,
):
    bfloat = jnp.bfloat16
    seq_count, span_len, model_width = block_input.shape
    rows_all = seq_count * span_len
    shards = [
        w.astype(bfloat) for w in (w_input, w_forget, w_gate, w_out, w_mlp_gate, w_mlp_up, w_down)
    ]
    if lax.axis_size("shard") == 4:
        wide = gather_all(shards, 4, lax.axis_size("ctx"))
    else:
        wide = [lax.all_gather(w, ("shard", "ctx"), axis=0, tiled=True) for w in shards]
    wide_input, wide_forget, wide_gate, wide_out, wide_mgate, wide_mup, wide_down = wide
    residual_in = block_input.reshape(rows_all, model_width)
    scale_one = inverse_rms(residual_in)
    normed_one = (residual_in * scale_one * norm_gain).astype(bfloat)
    proj_input = jnp.dot(normed_one, wide_input, preferred_element_type=jnp.float32)
    proj_forget = jnp.dot(normed_one, wide_forget, preferred_element_type=jnp.float32)
    proj_gate = jnp.dot(normed_one, wide_gate, preferred_element_type=jnp.float32)
    channels = proj_input.shape[1]
    sigmoid_f = jax.nn.sigmoid(proj_forget)
    forget = lower + (1.0 - lower) * sigmoid_f
    silu_in = jax.nn.silu(proj_input)
    candidate = silu_in * (1.0 - forget)
    seg_float = segment_ids.astype(jnp.float32)
    inner_link = jnp.concatenate(
        [
            jnp.ones((seq_count, 1), jnp.float32),
            jnp.where(seg_float[:, 1:] == seg_float[:, :-1], 1.0, 0.0),
        ],
        axis=1,
    )
    forget_seq = forget.reshape(seq_count, span_len, channels)
    decay_rate = forget_seq * inner_link[:, :, None]
    decay_prod, local_state = lax.associative_scan(
        linear_step, (decay_rate, candidate.reshape(seq_count, span_len, channels)), axis=1
    )
    first_ids = seg_float[:, 0]
    last_ids = seg_float[:, -1]
    ones_state = jnp.ones((seq_count, channels), jnp.float32)
    zero_state = jnp.zeros((seq_count, channels), jnp.float32)
    minus_ids = -jnp.ones((seq_count,), jnp.float32)
    prefix = carried_in(
        (decay_prod[:, -1], local_state[:, -1], first_ids, last_ids),
        "ctx",
        forward_join,
        (ones_state, zero_state, minus_ids, minus_ids),
        False,
    )
    start_state = joined(prefix[3], first_ids)[:, None] * prefix[1]
    state_seq = local_state + decay_prod * start_state[:, None, :]
    hidden_state = state_seq.reshape(rows_all, channels)
    squares = lax.psum(jnp.sum(hidden_state * hidden_state, axis=1), "tp")
    scale_mid = lax.rsqrt(squares / model_width + epsilon)[:, None]
    silu_gate = jax.nn.silu(proj_gate)
    mixed_in = (hidden_state * scale_mid * hidden_gain * silu_gate).astype(bfloat)
    mixer_out = lax.psum(times_back(mixed_in, wide_out).astype(jnp.bfloat16), "tp").astype(
        jnp.float32
    )
    middle = residual_in + mixer_out
    scale_two = inverse_rms(middle)
    normed_two = (middle * scale_two * mlp_gain).astype(bfloat)
    gate_pre = jnp.dot(normed_two, wide_mgate, preferred_element_type=jnp.float32)
    up_pre = jnp.dot(normed_two, wide_mup, preferred_element_type=jnp.float32)
    silu_mlp = jax.nn.silu(gate_pre)
    activated = (silu_mlp * up_pre).astype(bfloat)
    mlp_out = lax.psum(times_back(activated, wide_down).astype(jnp.bfloat16), "tp").astype(
        jnp.float32
    )
    output = middle + mlp_out
    upstream = cotangent.reshape(rows_all, model_width)
    upstream_low = upstream.astype(bfloat)
    grad_activ = jnp.dot(upstream_low, wide_down, preferred_element_type=jnp.float32)
    grad_down = outer_sum(upstream_low, activated)
    grad_gate_pre = (grad_activ * up_pre * silu_slope(gate_pre)).astype(bfloat)
    grad_up_pre = (grad_activ * silu_mlp).astype(bfloat)
    grad_mgate = outer_sum(normed_two, grad_gate_pre)
    grad_mup = outer_sum(normed_two, grad_up_pre)
    grad_normed_two = lax.psum(
        (times_back(grad_gate_pre, wide_mgate) + times_back(grad_up_pre, wide_mup)).astype(
            jnp.bfloat16
        ),
        "tp",
    ).astype(jnp.float32)
    grad_mlp_gain = jnp.sum(grad_normed_two * middle * scale_two, axis=0)
    grad_middle = upstream + rms_backward(middle, scale_two, mlp_gain, grad_normed_two)
    middle_low = grad_middle.astype(bfloat)
    grad_mixed_in = jnp.dot(middle_low, wide_out, preferred_element_type=jnp.float32)
    grad_out = outer_sum(middle_low, mixed_in)
    weighted = grad_mixed_in * hidden_gain * silu_gate
    inner_sum = lax.psum(jnp.sum(weighted * hidden_state, axis=1), "tp")
    grad_state = (
        weighted * scale_mid
        - hidden_state * (scale_mid * scale_mid * scale_mid) * (inner_sum / model_width)[:, None]
    )
    grad_hidden_gain = jnp.sum(grad_mixed_in * hidden_state * scale_mid * silu_gate, axis=0)
    grad_gate_proj = (
        grad_mixed_in * hidden_state * scale_mid * hidden_gain * silu_slope(proj_gate)
    ).astype(bfloat)
    next_decay = jnp.concatenate(
        [decay_rate[:, 1:], jnp.ones((seq_count, 1, channels), jnp.float32)], axis=1
    )
    tail_prod, local_grad = lax.associative_scan(
        linear_step,
        (next_decay, grad_state.reshape(seq_count, span_len, channels)),
        reverse=True,
        axis=1,
    )
    suffix = carried_in(
        (decay_prod[:, -1], forget_seq[:, 0] * local_grad[:, 0], first_ids, last_ids),
        "ctx",
        backward_join,
        (ones_state, zero_state, minus_ids, minus_ids),
        True,
    )
    end_grad = joined(last_ids, suffix[2])[:, None] * suffix[1]
    total_grad = (local_grad + tail_prod * end_grad[:, None, :]).reshape(rows_all, channels)
    previous = jnp.concatenate(
        [start_state[:, None, :], inner_link[:, 1:, None] * state_seq[:, :-1]], axis=1
    ).reshape(rows_all, channels)
    grad_forget = total_grad * (previous - silu_in)
    grad_input_proj = (total_grad * (1.0 - forget) * silu_slope(proj_input)).astype(bfloat)
    grad_forget_proj = (grad_forget * (1.0 - lower) * sigmoid_f * (1.0 - sigmoid_f)).astype(bfloat)
    grad_lower = jnp.sum(grad_forget * (1.0 - sigmoid_f), axis=0)
    grad_w_input = outer_sum(normed_one, grad_input_proj)
    grad_w_forget = outer_sum(normed_one, grad_forget_proj)
    grad_w_gate = outer_sum(normed_one, grad_gate_proj)
    grad_normed_one = lax.psum(
        (
            times_back(grad_input_proj, wide_input)
            + times_back(grad_forget_proj, wide_forget)
            + times_back(grad_gate_proj, wide_gate)
        ).astype(jnp.bfloat16),
        "tp",
    ).astype(jnp.float32)
    grad_norm_gain = jnp.sum(grad_normed_one * residual_in * scale_one, axis=0)
    grad_resid = grad_middle + rms_backward(residual_in, scale_one, norm_gain, grad_normed_one)
    mlp_grads = (
        lax.psum_scatter(grad_mgate.astype(bfloat), ("shard", "ctx"), scatter_dimension=0, tiled=True).astype(jnp.float32),
        lax.psum_scatter(grad_mup.astype(bfloat), ("shard", "ctx"), scatter_dimension=0, tiled=True).astype(jnp.float32),
        lax.psum_scatter(grad_down.astype(bfloat), ("shard", "ctx"), scatter_dimension=0, tiled=True).astype(jnp.float32),
    )
    mixer_grads = (
        lax.psum_scatter(grad_w_input.astype(bfloat), ("shard", "ctx"), scatter_dimension=0, tiled=True).astype(jnp.float32),
        lax.psum_scatter(grad_w_forget.astype(bfloat), ("shard", "ctx"), scatter_dimension=0, tiled=True).astype(jnp.float32),
        lax.psum_scatter(grad_w_gate.astype(bfloat), ("shard", "ctx"), scatter_dimension=0, tiled=True).astype(jnp.float32),
        lax.psum_scatter(grad_out.astype(bfloat), ("shard", "ctx"), scatter_dimension=0, tiled=True).astype(jnp.float32),
    )
    gain_grads = lax.psum(
        (grad_norm_gain, grad_lower, grad_hidden_gain, grad_mlp_gain), ("shard", "ctx")
    )
    return (
        output.reshape(block_input.shape),
        grad_resid.reshape(block_input.shape),
        gain_grads[0],
        gain_grads[1],
        mixer_grads[0],
        mixer_grads[1],
        mixer_grads[2],
        gain_grads[2],
        mixer_grads[3],
        gain_grads[3],
        mlp_grads[0],
        mlp_grads[1],
        mlp_grads[2],
    )


def solution(mesh):
    return jax.shard_map(
        on_device,
        mesh=mesh,
        in_specs=(
            P("shard", "ctx", None),
            P("shard", "ctx"),
            P(),
            P("tp"),
            P(("shard", "ctx"), "tp"),
            P(("shard", "ctx"), "tp"),
            P(("shard", "ctx"), "tp"),
            P("tp"),
            P(("shard", "ctx"), "tp"),
            P(),
            P(("shard", "ctx"), "tp"),
            P(("shard", "ctx"), "tp"),
            P(("shard", "ctx"), "tp"),
            P("shard", "ctx", None),
        ),
        out_specs=(
            P("shard", "ctx", None),
            P("shard", "ctx", None),
            P(),
            P("tp"),
            P(("shard", "ctx"), "tp"),
            P(("shard", "ctx"), "tp"),
            P(("shard", "ctx"), "tp"),
            P("tp"),
            P(("shard", "ctx"), "tp"),
            P(),
            P(("shard", "ctx"), "tp"),
            P(("shard", "ctx"), "tp"),
            P(("shard", "ctx"), "tp"),
        ),
        check_vma=False,
    )
```

```python
import functools
import jax
import jax.numpy as jnp
from jax import lax
from jax.experimental import pallas as pl
from jax.experimental.pallas import tpu as pltpu
from jax.sharding import PartitionSpec as P

epsilon = 1e-06
MESH = pl.DeviceIdType.MESH


def remote(src, dst, send_sem, recv_sem, device):
    return pltpu.make_async_remote_copy(
        src_ref=src, dst_ref=dst, send_sem=send_sem, recv_sem=recv_sem,
        device_id=device, device_id_type=MESH)


def gather_body(nw, Z, ahead, relay, *refs):
    own, out = refs[:nw], refs[nw:2 * nw]
    (s_up, r_up, s_dn, r_dn, s_x, r_x, s_c, r_c, s_h, r_h, l_sem) = refs[2 * nw:]
    s, z = lax.axis_index("shard"), lax.axis_index("ctx")
    q, c = s // 2, lax.rem(s, 2)
    sx, sc = (1 - q) * 2 + c, q * 2 + (1 - c)
    sxc = (1 - q) * 2 + (1 - c)
    even = lax.rem(z, 2) == 0
    zp = jnp.where(even, z + 1, z - 1)
    rows = [r.shape[0] for r in own]

    def block(w, s_, z_, part=0):
        R = rows[w]
        start = pl.multiple_of((s_ * Z + z_) * R, R)
        if part == 0:
            return out[w].at[pl.ds(start, R), :]
        H = R // 2
        return out[w].at[pl.ds(pl.multiple_of(start + (part - 1) * H, H), H), :]

    UP, DN, XX, CC, ZP = {"ctx": z + 1}, {"ctx": z - 1}, {"shard": sx}, {"shard": sc}, {"ctx": zp}

    def up(w, k, src=None):
        b = block(w, s, z - k)
        return remote(b if src is None else src, b, s_up.at[w, k], r_up.at[w, k], UP)

    def dn(w, k, src=None):
        b = block(w, s, z + k)
        return remote(b if src is None else src, b, s_dn.at[w, k], r_dn.at[w, k], DN)

    def origin(j):
        return z if j == 0 else (z - j if j < Z else z + j - Z + 1)

    def valid(j):
        return (z >= j) if j < Z else (z + j - Z + 1 <= Z - 1)

    def xx(w, j, part, src=None):
        b = block(w, s, origin(j), part)
        return remote(b if src is None else src, b, s_x.at[w, j], r_x.at[w, j], XX)

    def xx_in(w, j, part):
        b = block(w, sx, origin(j), part)
        return remote(b, b, s_x.at[w, j], r_x.at[w, j], XX)

    def cc(w, j, src=None):
        b = block(w, s if j < 2 * Z - 1 else sx, origin(j % (2 * Z - 1)))
        return remote(b if src is None else src, b, s_c.at[w, j], r_c.at[w, j], CC)

    def cc_in(w, j):
        b = block(w, sc if j < 2 * Z - 1 else sxc, origin(j % (2 * Z - 1)))
        return remote(b, b, s_c.at[w, j], r_c.at[w, j], CC)

    def half(w):
        b = block(w, sx, z, 1)
        return remote(b, b, s_h.at[w], r_h.at[w], ZP)

    def half_in(w):
        b = block(w, sx, zp, 1)
        return remote(b, b, s_h.at[w], r_h.at[w], ZP)

    barrier = pltpu.get_barrier_semaphore()
    for d in (XX, CC):
        pl.semaphore_signal(barrier, inc=1, device_id=d, device_id_type=MESH)

    @pl.when(z < Z - 1)
    def _():
        pl.semaphore_signal(barrier, inc=1, device_id=UP, device_id_type=MESH)

    @pl.when(z > 0)
    def _():
        pl.semaphore_signal(barrier, inc=1, device_id=DN, device_id_type=MESH)

    pl.semaphore_wait(barrier, 2 + (z < Z - 1).astype(jnp.int32) + (z > 0).astype(jnp.int32))

    local = []
    for w in range(nw):
        cp = pltpu.make_async_copy(own[w], block(w, s, z), l_sem.at[w])
        cp.start()
        local.append(cp)

    def begin(w):
        @pl.when(z < Z - 1)
        def _():
            up(w, 0, own[w]).start()

        @pl.when(z > 0)
        def _():
            dn(w, 0, own[w]).start()

        xx(w, 0, 0, own[w]).start()
        cc(w, 0, own[w]).start()

    def is_pair(j):
        if j == 1:
            return jnp.logical_not(even)
        if j == Z:
            return even
        return None

    def for_part(w, j, fn):
        pair = is_pair(j) if relay else None
        if pair is None:
            fn(0)
        else:
            @pl.when(pair)
            def _():
                fn(2)

            @pl.when(jnp.logical_not(pair))
            def _():
                fn(0)

    def step(w, k):
        @pl.when(z >= k)
        def _():
            remote(block(w, s, z - k), block(w, s, z - k), s_up.at[w, k - 1], r_up.at[w, k - 1], UP).wait_recv()
            if k < Z - 1:
                @pl.when(z < Z - 1)
                def _():
                    up(w, k).start()
            for_part(w, k, lambda p: xx(w, k, p).start())
            cc(w, k).start()

        @pl.when(z + k <= Z - 1)
        def _():
            remote(block(w, s, z + k), block(w, s, z + k), s_dn.at[w, k - 1], r_dn.at[w, k - 1], DN).wait_recv()
            if k < Z - 1:
                @pl.when(z > 0)
                def _():
                    dn(w, k).start()
            for_part(w, Z - 1 + k, lambda p: xx(w, Z - 1 + k, p).start())
            cc(w, Z - 1 + k).start()

    def xstep(w, j):
        @pl.when(valid(j))
        def _():
            for_part(w, j, lambda p: xx_in(w, j, p).wait_recv())
            if j == 0:
                if relay:
                    half(w).start()
                cc(w, 2 * Z - 1).start()
            else:
                if relay and is_pair(j) is not None:
                    @pl.when(is_pair(j))
                    def _():
                        half_in(w).wait_recv()
                cc(w, 2 * Z - 1 + j).start()

    def finish(w):
        for j in range(4 * Z - 2):
            @pl.when(valid(j % (2 * Z - 1)))
            def _():
                cc_in(w, j).wait_recv()
                cc(w, j).wait_send()
        for j in range(2 * Z - 1):
            @pl.when(valid(j))
            def _():
                for_part(w, j, lambda p: xx(w, j, p).wait_send())
        for k in range(Z - 1):
            @pl.when((z >= k) & (z < Z - 1))
            def _():
                up(w, k).wait_send()

            @pl.when((z + k <= Z - 1) & (z > 0))
            def _():
                dn(w, k).wait_send()
        if relay:
            half(w).wait_send()
        local[w].wait()

    for w in range(min(ahead, nw)):
        begin(w)
    for w in range(nw):
        for k in range(1, Z):
            step(w, k)
            if k == 1:
                xstep(w, 0)
                if w + ahead < nw:
                    begin(w + ahead)
            else:
                xstep(w, k - 1)
                xstep(w, Z - 1 + k - 1)
            if w > 0 and k == 1:
                xstep(w - 1, Z - 1)
                xstep(w - 1, 2 * Z - 2)
    xstep(nw - 1, Z - 1)
    xstep(nw - 1, 2 * Z - 2)
    for w in range(nw):
        finish(w)


def gather_all(shards, S, Z, collective_id=0, ahead=2, relay=True):
    nw = len(shards)
    dma = pltpu.SemaphoreType.DMA
    return pl.pallas_call(
        functools.partial(gather_body, nw, Z, ahead, relay),
        out_shape=[jax.ShapeDtypeStruct((a.shape[0] * S * Z, a.shape[1]), a.dtype) for a in shards],
        in_specs=[pl.BlockSpec(memory_space=pltpu.VMEM)] * nw,
        out_specs=[pl.BlockSpec(memory_space=pl.ANY)] * nw,
        scratch_shapes=[
            dma((nw, Z - 1)), dma((nw, Z - 1)), dma((nw, Z - 1)), dma((nw, Z - 1)),
            dma((nw, 2 * Z - 1)), dma((nw, 2 * Z - 1)),
            dma((nw, 4 * Z - 2)), dma((nw, 4 * Z - 2)), dma((nw,)), dma((nw,)), dma((nw,)),
        ],
        compiler_params=pltpu.CompilerParams(collective_id=collective_id, has_side_effects=True),
        name="weights_in",
    )(*shards)


def pick(z, values):
    out = jnp.int32(values[-1])
    for k in range(len(values) - 2, -1, -1):
        out = jnp.where(z == k, values[k], out)
    return out


def far_first(Z):
    table = []
    for z in range(Z):
        ups, dns, mine, turn = list(range(Z - 1, z, -1)), list(range(0, z)), [], z < Z // 2
        while ups or dns:
            if (turn and ups) or not dns:
                mine.append(ups.pop(0))
            else:
                mine.append(dns.pop(0))
            turn = not turn
        table.append(mine + [z])
    return table


def cross_order(Z):
    table = []
    for z in range(Z):
        zp = z ^ 1
        table.append([zp] + [k for k in range(Z) if k not in (z, zp)] + [z])
    return table


class Scatter:
    def __init__(self, Z, parts, rc, xr, zu, zd, hr, outs, xs, zs, stage, fin, sems):
        self.Z, self.parts, self.rc, self.xr, self.zu, self.zd, self.hr, self.outs = Z, parts, rc, xr, zu, zd, hr, outs
        self.xs, self.zs, self.stage, self.fin = xs, zs, stage, fin
        (self.c_s, self.c_r, self.x_s, self.x_r, self.z_s, self.u_r, self.d_r, self.h_s, self.h_r, self.l_s, self.f_s) = sems
        s, z = lax.axis_index("shard"), lax.axis_index("ctx")
        q, c = s // 2, lax.rem(s, 2)
        self.z, self.q, self.c = z, q, c
        self.even = lax.rem(z, 2) == 0
        self.zp = jnp.where(self.even, z + 1, z - 1)
        self.X = {"shard": (1 - q) * 2 + c}
        self.C = {"shard": q * 2 + (1 - c)}
        self.UP, self.DN, self.ZP = {"ctx": z + 1}, {"ctx": z - 1}, {"ctx": self.zp}
        self.R = [p.shape[0] // (4 * Z) for p in parts]
        self.N = [p.shape[1] for p in parts]
        self.ffirst = far_first(Z)
        self.xorder = cross_order(Z)

    def part(self, w, q, c, z, n=1):
        R = self.R[w]
        return self.parts[w].at[pl.ds(pl.multiple_of(((2 * q + c) * self.Z + z) * R, R), n * R), :]

    def rows(self, ref, i, w):
        R = self.R[w]
        return ref.at[pl.ds(pl.multiple_of(i * R, R), R), :]

    def hrows(self, ref, i, w, h):
        H = self.R[w] // 2
        return ref.at[pl.ds(pl.multiple_of(i * 2 * H + h * H, H), H), :]

    def c_copy(self, w, k):
        Z, R = self.Z, self.R[w]
        q = self.q if k == 1 else 1 - self.q
        return remote(self.part(w, q, 1 - self.c, 0, Z), self.rc[w].at[pl.ds(k * Z * R, Z * R), :],
                      self.c_s.at[w, k], self.c_r.at[w, k], self.C)

    def c_send(self, w):
        for k in (0, 1):
            self.c_copy(w, k).start()

    def load(self, w, srcs, slot):
        cps = []
        for i, src in enumerate(srcs):
            if src is None:
                continue
            n = src.shape[0]
            cp = pltpu.make_async_copy(src, self.stage.at[slot, i, pl.ds(0, n), pl.ds(0, self.N[w])], self.l_s.at[slot, i])
            cp.start()
            cps.append(cp)
        return cps

    def add(self, w, slot, idx, store, lo=0, hi=None, off=None):
        N = self.N[w]
        hi = self.R[w] if hi is None else hi
        G = 16

        def go(i, _):
            r = pl.multiple_of(lo + i * G, G)
            tot = None
            for k in idx:
                rk = r
                if off is not None and k in off:
                    rk = pl.multiple_of(r + off[k], G)
                v = self.stage[slot, k, pl.ds(rk, G), pl.ds(0, N)].astype(jnp.float32)
                tot = v if tot is None else tot + v
            store(r, tot)
            return 0

        lax.fori_loop(0, (hi - lo) // G, go, 0)

    def x_slot(self, w, n):
        return self.xs.at[w % 2, n, :, pl.ds(0, self.N[w])]

    def x_copy(self, w, n, half=None):
        zt = pick(self.z, [t[n] for t in self.xorder])
        src = self.x_slot(w, n)
        H = self.R[w] // 2
        if half is None:
            return remote(src, self.rows(self.xr[w], zt, w), self.x_s.at[w, n], self.x_r.at[w, n], self.X)
        return remote(src.at[pl.ds(half * H, H), :], self.hrows(self.xr[w], zt, w, half), self.x_s.at[w, n], self.x_r.at[w, n], self.X)

    def h_copy(self, w):
        H = self.R[w] // 2
        return remote(self.x_slot(w, 0).at[pl.ds(0, H), :], self.hr[w], self.h_s.at[w], self.h_r.at[w], self.ZP)

    def x_phase(self, w, n):
        Z, H = self.Z, self.R[w] // 2
        if n == 0:
            self.c_copy(w, 0).wait_recv()
        zt = pick(self.z, [t[n] for t in self.xorder])
        last = n == Z - 1
        cps = self.load(w, [self.part(w, 1 - self.q, self.c, zt), self.rows(self.rc[w], zt, w)], 0)
        if last:
            self.h_copy(w).wait_recv()
            cps += self.load(w, [None, None, self.hr[w]], 0)
        if w >= 2:
            self.x_wait_send(w - 2, n)
        for cp in cps:
            cp.wait()
        dst = self.x_slot(w, n)

        def store(r, v):
            dst[pl.ds(r, 16), :] = v.astype(jnp.bfloat16)

        if last:
            self.add(w, 0, (0, 1, 2), store, 0, H)
            self.add(w, 0, (0, 1), store, H, 2 * H)
        else:
            self.add(w, 0, (0, 1), store)
        if n == 0:
            self.h_copy(w).start()
            self.x_copy(w, 0, 1).start()
        else:
            self.x_copy(w, n).start()

    def x_wait_send(self, w, n):
        if n == 0:
            self.h_copy(w).wait_send()
            self.x_copy(w, 0, 1).wait_send()
        else:
            self.x_copy(w, n).wait_send()

    def z_copy(self, w, n, dest, up):
        src = self.zs.at[w % 2, n, :, pl.ds(0, self.N[w])]
        if up:
            return remote(src, self.rows(self.zu[w], dest, w), self.z_s.at[w, n], self.u_r.at[w, dest], self.UP)
        return remote(src, self.rows(self.zd[w], dest, w), self.z_s.at[w, n], self.d_r.at[w, dest], self.DN)

    def x_wait(self, w, zt):
        for n in range(self.Z):
            @pl.when(zt == pick(self.z, [t[n] for t in self.xorder]))
            def _():
                self.x_copy(w, n, 1 if n == 0 else None).wait_recv()

    def z_phase(self, w, n):
        Z, H = self.Z, self.R[w] // 2
        z = self.z
        last = n == Z - 1
        dest = z if last else pick(z, [t[n] for t in self.ffirst])
        if n == 0:
            self.c_copy(w, 1).wait_recv()
        self.x_wait(w, dest)
        cps = self.load(w, [self.part(w, self.q, self.c, dest), self.rows(self.rc[w], dest + Z, w),
                            self.rows(self.xr[w], dest, w)], 1)
        if not last:
            up = dest > z
            down = dest < z
            has_in = (up & (z > 0)) | (down & (z < Z - 1))

            @pl.when(up & (z > 0))
            def _():
                self.z_copy(w, n, dest, True).wait_recv()
                cp = self.load(w, [None] * 3 + [self.rows(self.zu[w], dest, w)], 1)
                cp[0].wait()

            @pl.when(down & (z < Z - 1))
            def _():
                self.z_copy(w, n, dest, False).wait_recv()
                cp = self.load(w, [None] * 3 + [self.rows(self.zd[w], dest, w)], 1)
                cp[0].wait()

            if w >= 2:
                self.z_wait_send(w - 2, n)
            for cp in cps:
                cp.wait()
            dst = self.zs.at[w % 2, n, :, pl.ds(0, self.N[w])]

            def store(r, v):
                dst[pl.ds(r, 16), :] = v.astype(jnp.bfloat16)

            paired = dest == self.zp
            self.sum_parts(w, paired, has_in, (3,), store)

            @pl.when(up)
            def _():
                self.z_copy(w, n, dest, True).start()

            @pl.when(down)
            def _():
                self.z_copy(w, n, dest, False).start()
        else:
            @pl.when(z > 0)
            def _():
                self.z_copy(w, 0, dest, True).wait_recv()
                cp = self.load(w, [None] * 3 + [self.rows(self.zu[w], dest, w)], 1)
                cp[0].wait()

            @pl.when(z < Z - 1)
            def _():
                self.z_copy(w, 0, dest, False).wait_recv()
                cp = self.load(w, [None] * 4 + [self.rows(self.zd[w], dest, w)], 1)
                cp[0].wait()

            for cp in cps:
                cp.wait()
            if w >= 1:
                self.f_copy(w - 1).wait()
            dst = self.fin.at[:, pl.ds(0, self.N[w])]

            def store(r, v):
                dst[pl.ds(r, 16), :] = v

            @pl.when((z > 0) & (z < Z - 1))
            def _():
                self.add(w, 1, (0, 1, 2, 3, 4), store)

            @pl.when(z == 0)
            def _():
                self.add(w, 1, (0, 1, 2, 4), store)

            @pl.when(z == Z - 1)
            def _():
                self.add(w, 1, (0, 1, 2, 3), store)

            self.f_copy(w).start()

    def sum_parts(self, w, paired, has_in, extra, store):
        H = self.R[w] // 2
        for p in (False, True):
            for e in (False, True):
                cond = (paired if p else jnp.logical_not(paired)) & (has_in if e else jnp.logical_not(has_in))

                @pl.when(cond)
                def _(p=p, e=e):
                    ex = extra if e else ()
                    if p:
                        self.add(w, 1, (0, 1) + ex, store, 0, H)
                        self.add(w, 1, (0, 1, 2) + ex, store, H, 2 * H)
                    else:
                        self.add(w, 1, (0, 1, 2) + ex, store)

    def z_wait_send(self, w, n):
        z = self.z
        dest = pick(z, [t[n] for t in self.ffirst])
        self.z_copy_any(w, n).wait_send()

    def z_copy_any(self, w, n):
        src = self.zs.at[w % 2, n, :, pl.ds(0, self.N[w])]
        return remote(src, self.rows(self.zu[w], 0, w), self.z_s.at[w, n], self.u_r.at[w, 0],
                      {"ctx": jnp.where(pick(self.z, [t[n] for t in self.ffirst]) > self.z, self.z + 1, self.z - 1)})

    def f_copy(self, w):
        return pltpu.make_async_copy(self.fin.at[:, pl.ds(0, self.N[w])], self.outs[w], self.f_s.at[w])

    def drain(self, w, nw):
        for k in (0, 1):
            self.c_copy(w, k).wait_send()
        if w >= nw - 2:
            for n in range(self.Z):
                self.x_wait_send(w, n)
            for n in range(self.Z - 1):
                self.z_wait_send(w, n)
        if w == nw - 1:
            self.f_copy(w).wait()


def scatter_body(nw, Z, *refs):
    parts = refs[:nw]
    vec, vec_out = refs[nw], refs[nw + 1]
    outs = refs[nw + 2:2 * nw + 2]
    rc, xr, zu, zd, hr = (refs[2 + (2 + k) * nw:2 + (3 + k) * nw] for k in range(5))
    xs, zs, stage, fin, vsum, vgot, vbox = refs[7 * nw + 2:7 * nw + 9]
    v_s, v_r, vz_s, vz_r = refs[7 * nw + 9:7 * nw + 13]
    sems = refs[7 * nw + 13:]
    sc = Scatter(Z, parts, rc, xr, zu, zd, hr, outs, xs, zs, stage, fin, sems)
    far = [{"ctx": lax.rem(sc.z + o, Z)} for o in range(1, Z)]
    barrier = pltpu.get_barrier_semaphore()
    for d in [sc.X, sc.C] + far:
        pl.semaphore_signal(barrier, inc=1, device_id=d, device_id_type=MESH)
    pl.semaphore_wait(barrier, 1 + Z)
    first = remote(vec, vgot.at[0], v_s.at[0], v_r.at[0], sc.C)
    first.start()
    for w in range(nw):
        sc.c_send(w)
    first.wait()
    vsum[...] = vec[...] + vgot[0]
    for n in range(Z):
        sc.x_phase(0, n)
    second = remote(vsum, vgot.at[1], v_s.at[1], v_r.at[1], sc.X)
    second.start()
    for n in range(Z):
        sc.x_phase(1, n)
    second.wait()
    vsum[...] = vsum[...] + vgot[1]
    for n in range(Z):
        sc.z_phase(0, n)
    cps = spread(Z, sc.z, vsum, vbox, vz_s, vz_r)
    for w in range(1, nw):
        if w + 1 < nw:
            for n in range(Z):
                sc.x_phase(w + 1, n)
        for n in range(Z):
            sc.z_phase(w, n)
    spread_wait(Z, sc.z, vsum, vbox, vz_s, vz_r, cps)
    total = vbox[0]
    for k in range(1, Z):
        total = total + vbox[k]
    vec_out[...] = total
    for w in range(nw):
        sc.drain(w, nw)


def scatter_all(parts, vec, Z, collective_id=1):
    nw = len(parts)
    dma = pltpu.SemaphoreType.DMA
    bf = jnp.bfloat16
    R = [p.shape[0] // (4 * Z) for p in parts]
    N = [p.shape[1] for p in parts]
    Rm, Nm = max(R), max(N)
    sh = jax.ShapeDtypeStruct
    vmem = pl.BlockSpec(memory_space=pltpu.VMEM)
    anyw = pl.BlockSpec(memory_space=pl.ANY)
    out_shape = ([sh(vec.shape, jnp.float32)] + [sh((r, n), jnp.float32) for r, n in zip(R, N)]
                 + [sh((2 * Z * r, n), bf) for r, n in zip(R, N)]
                 + [sh((Z * r, n), bf) for r, n in zip(R, N)]
                 + [sh((Z * r, n), bf) for r, n in zip(R, N)]
                 + [sh((Z * r, n), bf) for r, n in zip(R, N)]
                 + [sh((r // 2, n), bf) for r, n in zip(R, N)])
    res = pl.pallas_call(
        functools.partial(scatter_body, nw, Z),
        out_shape=out_shape,
        in_specs=[anyw] * nw + [vmem],
        out_specs=[vmem] + [anyw] * (len(out_shape) - 1),
        scratch_shapes=[
            pltpu.VMEM((2, Z, Rm, Nm), bf), pltpu.VMEM((2, Z - 1, Rm, Nm), bf), pltpu.VMEM((2, 5, Rm, Nm), bf),
            pltpu.VMEM((Rm, Nm), jnp.float32),
            pltpu.VMEM(vec.shape, jnp.float32), pltpu.VMEM((2,) + vec.shape, jnp.float32), pltpu.VMEM((Z,) + vec.shape, jnp.float32),
            dma((2,)), dma((2,)), dma((Z - 1,)), dma((Z,)),
            dma((nw, 2)), dma((nw, 2)), dma((nw, Z)), dma((nw, Z)), dma((nw, Z - 1)), dma((nw, Z)), dma((nw, Z)),
            dma((nw,)), dma((nw,)), dma((2, 5)), dma((nw,)),
        ],
        compiler_params=pltpu.CompilerParams(collective_id=collective_id, has_side_effects=True),
        name="grads_out",
    )(*parts, vec)
    return res[0], res[1:nw + 1]


T8 = 8


def spread(Z, z, pay, box, s_sem, r_sem):
    cps = []
    for o in range(1, Z):
        to = lax.rem(z + o, Z)
        cp = remote(pay, box.at[z], s_sem.at[o - 1], r_sem.at[z], {"ctx": to})
        cp.start()
        cps.append(cp)
    box[z] = pay[...]
    return cps


def spread_wait(Z, z, pay, box, s_sem, r_sem, cps):
    for o in range(1, Z):
        frm = lax.rem(z + o, Z)
        remote(pay, box.at[frm], s_sem.at[o - 1], r_sem.at[frm], {"ctx": frm}).wait_recv()
    for cp in cps:
        cp.wait_send()


def joined(box, k):
    last, first = box[k, 6:8, :], box[k + 1, 4:6, :]
    return jnp.where(last == first, 1.0, 0.0)


def prefix_state(Z, z, box):
    state = jnp.zeros(box.shape[2:][:0] + (2, box.shape[2]), jnp.float32)
    mine = state
    for k in range(Z - 1):
        state = joined(box, k) * (box[k, 2:4, :] + box[k, 0:2, :] * state)
        mine = jnp.where(z == k + 1, state, mine)
    return mine


def suffix_state(Z, z, box):
    state = jnp.zeros((2, box.shape[2]), jnp.float32)
    mine = state
    for k in range(Z - 2, -1, -1):
        state = joined(box, k) * (box[k + 1, 2:4, :] + box[k + 1, 0:2, :] * state)
        mine = jnp.where(z == k, state, mine)
    return mine


def diagonal():
    return lax.broadcasted_iota(jnp.int32, (128, 128), 0) == lax.broadcasted_iota(jnp.int32, (128, 128), 1)


def column_to_rows(col_ref, row_ref, n):
    eye = diagonal()
    for k in range(n // 128):
        col = col_ref[pl.ds(k * 128, 128), :]
        row_ref[k:k + 1, :] = jnp.sum(jnp.where(eye, jnp.broadcast_to(col, (128, 128)), 0.0), axis=0, keepdims=True)


def rows_to_column(row, k):
    return jnp.sum(jnp.where(diagonal(), jnp.broadcast_to(row, (128, 128)), 0.0), axis=1, keepdims=True)


def sigmoid(v):
    return jax.nn.sigmoid(v)


def row_at(ref, t):
    return pl.ds(pl.multiple_of(t, T8), T8)


def forward_scan(seqs, length, pi, pf, lower, link, h, cum):
    C = pi.shape[1]
    low = lower[...]
    iota = lax.broadcasted_iota(jnp.int32, (T8, C), 0)
    ends = []
    for sq in range(seqs):
        def tile(i, carry):
            hl, pr = carry
            r = row_at(pi, sq * length + i * T8)
            s = sigmoid(pf[r, :])
            forget = low + (1.0 - low) * s
            x = pi[r, :]
            b = x * sigmoid(x) * (1.0 - forget)
            a = forget * link[r, :]
            for sh in (1, 2, 4):
                keep = iota >= sh
                b = b + jnp.where(keep, a * pltpu.roll(b, sh, 0), 0.0)
                a = jnp.where(keep, a * pltpu.roll(a, sh, 0), a)
            b = b + a * hl
            a = a * pr
            h[r, :] = b
            cum[r, :] = a
            return b[T8 - 1:T8, :], a[T8 - 1:T8, :]

        ends.append(lax.fori_loop(0, length // T8, tile, (jnp.zeros((1, C), jnp.float32), jnp.ones((1, C), jnp.float32)), unroll=2))
    return ends


def forward_finish(seqs, length, h, cum, start, col):
    def tile(i, _, sq):
        r = row_at(h, sq * length + i * T8)
        v = h[r, :] + cum[r, :] * start[sq:sq + 1, :]
        h[r, :] = v
        col[r, :] = jnp.sum(v * v, axis=1, keepdims=True)
        return 0

    for sq in range(seqs):
        lax.fori_loop(0, length // T8, functools.partial(tile, sq=sq), 0, unroll=2)


def swap_columns(col, row, got, s_sem, r_sem, other, n):
    column_to_rows(col, row, n)
    cp = remote(row, got, s_sem, r_sem, {"tp": other})
    cp.start()
    cp.wait()


def scale_columns(row, got, col, n, width, fn):
    for k in range(n // 128):
        col[pl.ds(k * 128, 128), :] = fn(rows_to_column(row[k:k + 1, :] + got[k:k + 1, :], k))


def mixed(h, rh, gain, pg, m, step=16):
    g = gain[...]

    def tile(i, _):
        r = pl.ds(pl.multiple_of(i * step, step), step)
        p = pg[r, :]
        m[r, :] = (h[r, :] * rh[r, :] * g * (p * sigmoid(p))).astype(m.dtype)
        return 0

    lax.fori_loop(0, h.shape[0] // step, tile, 0)


def mixer_forward_body(Z, seqs, length, width, pi, pf, pg, lower, gain, link, ids, h, m, rh, start,
                       cum, pay, box, row, got, s_c, r_c, s_t, r_t):
    z, t = lax.axis_index("ctx"), lax.axis_index("tp")
    n = seqs * length
    barrier_all(Z, z, t)
    ends = forward_scan(seqs, length, pi, pf, lower, link, h, cum)
    pay[4:8, :] = ids[...]
    for sq in range(seqs):
        pay[sq:sq + 1, :] = ends[sq][1]
        pay[2 + sq:3 + sq, :] = ends[sq][0]
    cps = spread(Z, z, pay, box, s_c, r_c)
    spread_wait(Z, z, pay, box, s_c, r_c, cps)
    start[...] = prefix_state(Z, z, box)
    forward_finish(seqs, length, h, cum, start, rh)
    swap_columns(rh, row, got, s_t.at[0], r_t.at[0], 1 - t, n)
    scale_columns(row, got, rh, n, width, lambda v: lax.rsqrt(v / width + epsilon))
    mixed(h, rh, gain, pg, m)


def barrier_all(Z, z, t):
    barrier = pltpu.get_barrier_semaphore()
    for o in range(1, Z):
        pl.semaphore_signal(barrier, inc=1, device_id={"ctx": lax.rem(z + o, Z)}, device_id_type=MESH)
    pl.semaphore_signal(barrier, inc=1, device_id={"tp": 1 - t}, device_id_type=MESH)
    pl.semaphore_wait(barrier, Z)


def slope(v):
    s = sigmoid(v)
    return s * (1.0 + v * (1.0 - s))


def backward_first(n, dm, h, pg, gain, rh, dpg, col, gsum, step=16):
    g = gain[...]

    def tile(i, acc):
        r = pl.ds(pl.multiple_of(i * step, step), step)
        d, hv, p, rv = dm[r, :], h[r, :], pg[r, :], rh[r, :]
        s = sigmoid(p)
        sl = p * s
        q = d * g * sl
        col[r, :] = jnp.sum(q * hv, axis=1, keepdims=True)
        hr = d * hv * rv
        dpg[r, :] = (hr * g * (s * (1.0 + p * (1.0 - s)))).astype(dpg.dtype)
        return acc + jnp.sum(hr * sl, axis=0, keepdims=True)

    gsum[...] = lax.fori_loop(0, n // step, tile, jnp.zeros(gsum.shape, jnp.float32))


def backward_scan(seqs, length, dm, h, pf, pg, lower, gain, link, rh, inner, gl, tail):
    C = dm.shape[1]
    low, g = lower[...], gain[...]
    iota = lax.broadcasted_iota(jnp.int32, (T8, C), 0)
    ends = []
    nt = length // T8
    for sq in range(seqs):
        def tile(k, carry):
            vl, pr = carry
            r = row_at(dm, sq * length + (nt - 1 - k) * T8)
            rv = rh[r, :]
            p = pg[r, :]
            q = dm[r, :] * g * (p * sigmoid(p))
            dh = q * rv - h[r, :] * (rv * rv * rv) * inner[r, :]
            a = (low + (1.0 - low) * sigmoid(pf[r, :])) * link[r, :]
            b = a * dh
            for sh in (1, 2, 4):
                keep = iota < T8 - sh
                b = b + jnp.where(keep, a * pltpu.roll(b, T8 - sh, 0), 0.0)
                a = jnp.where(keep, a * pltpu.roll(a, T8 - sh, 0), a)
            v = b + a * vl
            pa = a * pr
            last = iota == T8 - 1
            gl[r, :] = dh + jnp.where(last, vl, pltpu.roll(v, T8 - 1, 0))
            tail[r, :] = jnp.where(last, pr, pltpu.roll(pa, T8 - 1, 0))
            return v[0:1, :], pa[0:1, :]

        ends.append(lax.fori_loop(0, nt, tile, (jnp.zeros((1, C), jnp.float32), jnp.ones((1, C), jnp.float32)), unroll=2))
    return ends


def backward_last(seqs, length, gl, tail, end, h, start, pi, pf, lower, link, dpi, dpf, lsum):
    C = gl.shape[1]
    low = lower[...]
    iota = lax.broadcasted_iota(jnp.int32, (T8, C), 0)
    total = jnp.zeros((1, C), jnp.float32)
    for sq in range(seqs):
        def tile(i, carry):
            acc, hp = carry
            halves = []
            for half in (0, 1):
                r = row_at(gl, sq * length + i * 16 + half * T8)
                gv = gl[r, :] + tail[r, :] * end[sq:sq + 1, :]
                hv = h[r, :]
                prev = jnp.where(iota == 0, hp, pltpu.roll(hv, 1, 0) * link[r, :])
                if half == 1:
                    prev = jnp.where(iota == 0, prev * link[r, :], prev)
                else:
                    prev = jnp.where((iota == 0) & (i > 0), prev * link[r, :], prev)
                s = sigmoid(pf[r, :])
                forget = low + (1.0 - low) * s
                x = pi[r, :]
                sx = sigmoid(x)
                df = gv * (prev - x * sx)
                halves.append((gv * (1.0 - forget) * (sx * (1.0 + x * (1.0 - sx))), df * (1.0 - low) * s * (1.0 - s)))
                acc = acc + jnp.sum(df * (1.0 - s), axis=0, keepdims=True)
                hp = hv[T8 - 1:T8, :]
            r = pl.ds(pl.multiple_of(sq * length + i * 16, 16), 16)
            dpi[r, :] = jnp.concatenate([halves[0][0], halves[1][0]], axis=0).astype(dpi.dtype)
            dpf[r, :] = jnp.concatenate([halves[0][1], halves[1][1]], axis=0).astype(dpf.dtype)
            return acc, hp

        total, _ = lax.fori_loop(0, length // 16, tile, (total, start[sq:sq + 1, :]))
    lsum[...] = total


def mixer_backward_body(Z, seqs, length, width, dm, h, pi, pf, pg, lower, gain, link, ids, rh, start,
                        dpi, dpf, dpg, gsum, lsum,
                        gl, tail, col, end, pay, box, row, got, s_c, r_c, s_t, r_t):
    z, t = lax.axis_index("ctx"), lax.axis_index("tp")
    n = seqs * length
    barrier_all(Z, z, t)
    backward_first(n, dm, h, pg, gain, rh, dpg, col, gsum)
    swap_columns(col, row, got, s_t.at[0], r_t.at[0], 1 - t, n)
    scale_columns(row, got, col, n, width, lambda v: v / width)
    ends = backward_scan(seqs, length, dm, h, pf, pg, lower, gain, link, rh, col, gl, tail)
    pay[4:8, :] = ids[...]
    for sq in range(seqs):
        pay[sq:sq + 1, :] = ends[sq][1]
        pay[2 + sq:3 + sq, :] = ends[sq][0]
    cps = spread(Z, z, pay, box, s_c, r_c)
    spread_wait(Z, z, pay, box, s_c, r_c, cps)
    end[...] = suffix_state(Z, z, box)
    backward_last(seqs, length, gl, tail, end, h, start, pi, pf, lower, link, dpi, dpf, lsum)


def mixer_scratch(Z, n, C):
    dma = pltpu.SemaphoreType.DMA
    f = jnp.float32
    return [pltpu.VMEM((8, C), f), pltpu.VMEM((Z, 8, C), f), pltpu.VMEM((n // 128, 128), f), pltpu.VMEM((n // 128, 128), f),
            dma((Z - 1,)), dma((Z,)), dma((1,)), dma((1,))]


def mixer_forward(Z, seqs, length, width, pi, pf, pg, lower, gain, link, ids, cid=2):
    n, C = pi.shape
    f = jnp.float32
    sh = jax.ShapeDtypeStruct
    vm = pl.BlockSpec(memory_space=pltpu.VMEM)
    return pl.pallas_call(
        functools.partial(mixer_forward_body, Z, seqs, length, width),
        out_shape=[sh((n, C), f), sh((n, C), jnp.bfloat16), sh((n, 1), f), sh((seqs, C), f)],
        in_specs=[vm] * 7, out_specs=[vm] * 4,
        scratch_shapes=[pltpu.VMEM((n, C), f)] + mixer_scratch(Z, n, C),
        compiler_params=pltpu.CompilerParams(collective_id=cid, has_side_effects=True),
        name="mixer_forward",
    )(pi, pf, pg, lower, gain, link, ids)


def mixer_backward(Z, seqs, length, width, dm, h, pi, pf, pg, lower, gain, link, ids, rh, start, cid=3):
    n, C = pi.shape
    f, bf = jnp.float32, jnp.bfloat16
    sh = jax.ShapeDtypeStruct
    vm = pl.BlockSpec(memory_space=pltpu.VMEM)
    return pl.pallas_call(
        functools.partial(mixer_backward_body, Z, seqs, length, width),
        out_shape=[sh((n, C), bf), sh((n, C), bf), sh((n, C), bf), sh((1, C), f), sh((1, C), f)],
        in_specs=[vm] * 11, out_specs=[vm] * 5,
        scratch_shapes=[pltpu.VMEM((n, C), f), pltpu.VMEM((n, C), f), pltpu.VMEM((n, 1), f), pltpu.VMEM((seqs, C), f)] + mixer_scratch(Z, n, C),
        compiler_params=pltpu.CompilerParams(collective_id=cid, has_side_effects=True),
        name="mixer_backward",
    )(dm, h, pi, pf, pg, lower, gain, link, ids, rh, start)


def carried_in(x, axis, combine, identity, reverse):
    size, position = (lax.axis_size(axis), lax.axis_index(axis))
    everything = jax.tree.map(lambda part: lax.all_gather(part, axis), x)
    start = jax.tree.map(
        lambda part, zero: jnp.broadcast_to(jnp.asarray(zero, part.dtype), part.shape), x, identity
    )

    def turn(k, before):
        at = size - 1 - k if reverse else k
        reached = at > position if reverse else at < position
        new = combine(before, jax.tree.map(lambda part: part[at], everything))
        return jax.tree.map(lambda a, b: jnp.where(reached, a, b), new, before)

    return lax.fori_loop(0, size, turn, start)


def inverse_rms(inputs):
    return lax.rsqrt(jnp.mean(inputs * inputs, axis=-1, keepdims=True) + epsilon)


def rms_backward(inputs, row_scale, gain_vec, upstream):
    weighted = upstream * gain_vec
    inner_sum = jnp.mean(weighted * inputs, axis=-1, keepdims=True)
    return weighted * row_scale - inputs * (row_scale * row_scale * row_scale) * inner_sum


def silu_slope(inputs):
    sig_part = jax.nn.sigmoid(inputs)
    return sig_part * (1.0 + inputs * (1.0 - sig_part))


def times_back(left_mat, right_mat):
    return lax.dot_general(
        left_mat, right_mat, (((1,), (1,)), ((), ())), preferred_element_type=jnp.float32
    )


def outer_sum(left_mat, right_mat):
    return lax.dot_general(
        left_mat, right_mat, (((0,), (0,)), ((), ())), preferred_element_type=jnp.float32
    )


def linear_step(first_part, second_part):
    return (first_part[0] * second_part[0], second_part[0] * first_part[1] + second_part[1])


def joined_ids(last_ids, first_ids):
    return jnp.where((last_ids == first_ids) | (last_ids < 0.0) | (first_ids < 0.0), 1.0, 0.0)


def forward_join(first_part, second_part):
    linked = joined_ids(first_part[3], second_part[2])[:, None]
    return (
        first_part[0] * second_part[0] * linked,
        second_part[0] * linked * first_part[1] + second_part[1],
        jnp.where(first_part[2] < 0.0, second_part[2], first_part[2]),
        jnp.where(second_part[3] < 0.0, first_part[3], second_part[3]),
    )


def backward_join(first_part, second_part):
    linked = joined_ids(second_part[3], first_part[2])[:, None]
    return (
        second_part[0] * linked * first_part[0],
        second_part[0] * linked * first_part[1] + second_part[1],
        jnp.where(second_part[2] < 0.0, first_part[2], second_part[2]),
        jnp.where(first_part[3] < 0.0, second_part[3], first_part[3]),
    )


def mixer_forward_plain(seqs, length, width, pi, pf, pg, lower, gain, segs):
    channels = pi.shape[1]
    forget = lower + (1.0 - lower) * jax.nn.sigmoid(pf)
    candidate = jax.nn.silu(pi) * (1.0 - forget)
    inner_link = jnp.concatenate(
        [jnp.ones((seqs, 1), jnp.float32), jnp.where(segs[:, 1:] == segs[:, :-1], 1.0, 0.0)], axis=1
    )
    decay = forget.reshape(seqs, length, channels) * inner_link[:, :, None]
    prod, local = lax.associative_scan(
        linear_step, (decay, candidate.reshape(seqs, length, channels)), axis=1
    )
    first, last = segs[:, 0], segs[:, -1]
    ones, zero = jnp.ones((seqs, channels), jnp.float32), jnp.zeros((seqs, channels), jnp.float32)
    minus = -jnp.ones((seqs,), jnp.float32)
    prefix = carried_in(
        (prod[:, -1], local[:, -1], first, last), "ctx", forward_join, (ones, zero, minus, minus), False
    )
    start = joined_ids(prefix[3], first)[:, None] * prefix[1]
    h = (local + prod * start[:, None, :]).reshape(seqs * length, channels)
    squares = lax.psum(jnp.sum(h * h, axis=1), "tp")
    rh = lax.rsqrt(squares / width + epsilon)[:, None]
    m = (h * rh * gain * jax.nn.silu(pg)).astype(jnp.bfloat16)
    return h, m, rh, start


def mixer_backward_plain(seqs, length, width, dm, h, pi, pf, pg, lower, gain, segs, rh, start):
    channels = pi.shape[1]
    s = jax.nn.sigmoid(pf)
    forget = lower + (1.0 - lower) * s
    inner_link = jnp.concatenate(
        [jnp.ones((seqs, 1), jnp.float32), jnp.where(segs[:, 1:] == segs[:, :-1], 1.0, 0.0)], axis=1
    )
    forget_seq = forget.reshape(seqs, length, channels)
    decay = forget_seq * inner_link[:, :, None]
    silu_gate = jax.nn.silu(pg)
    weighted = dm * gain * silu_gate
    inner = lax.psum(jnp.sum(weighted * h, axis=1), "tp")
    dh = weighted * rh - h * (rh * rh * rh) * (inner / width)[:, None]
    gain_grad = jnp.sum(dm * h * rh * silu_gate, axis=0)
    dpg = (dm * h * rh * gain * silu_slope(pg)).astype(jnp.bfloat16)
    ones_row = jnp.ones((seqs, 1, channels), jnp.float32)
    following = jnp.concatenate([decay[:, 1:], ones_row], axis=1)
    tail, local = lax.associative_scan(
        linear_step, (following, dh.reshape(seqs, length, channels)), reverse=True, axis=1
    )
    first, last = segs[:, 0], segs[:, -1]
    ones, zero = jnp.ones((seqs, channels), jnp.float32), jnp.zeros((seqs, channels), jnp.float32)
    minus = -jnp.ones((seqs,), jnp.float32)
    suffix = carried_in(
        (decay[:, 0] * tail[:, 0], forget_seq[:, 0] * local[:, 0], first, last),
        "ctx", backward_join, (ones, zero, minus, minus), True,
    )
    end = joined_ids(last, suffix[2])[:, None] * suffix[1]
    g = (local + tail * end[:, None, :]).reshape(seqs * length, channels)
    states = h.reshape(seqs, length, channels)
    previous = jnp.concatenate(
        [start[:, None, :], inner_link[:, 1:, None] * states[:, :-1]], axis=1
    ).reshape(seqs * length, channels)
    dforget = g * (previous - jax.nn.silu(pi))
    dpi = (g * (1.0 - forget) * silu_slope(pi)).astype(jnp.bfloat16)
    dpf = (dforget * (1.0 - lower) * s * (1.0 - s)).astype(jnp.bfloat16)
    return dpi, dpf, dpg, gain_grad, jnp.sum(dforget * (1.0 - s), axis=0)


def on_device(
    block_input,
    segment_ids,
    norm_gain,
    lower,
    w_input,
    w_forget,
    w_gate,
    hidden_gain,
    w_out,
    mlp_gain,
    w_mlp_gate,
    w_mlp_up,
    w_down,
    cotangent,
):
    bfloat, f32 = jnp.bfloat16, jnp.float32
    seqs, length, width = block_input.shape
    rows_all = seqs * length
    small = lax.axis_size("shard") == 4
    Z = lax.axis_size("ctx")
    shards = [
        w.astype(bfloat) for w in (w_input, w_forget, w_gate, w_out, w_mlp_gate, w_mlp_up, w_down)
    ]
    if small:
        wide = gather_all(shards, 4, Z)
    else:
        wide = [lax.all_gather(w, ("shard", "ctx"), axis=0, tiled=True) for w in shards]
    wide_input, wide_forget, wide_gate, wide_out, wide_mgate, wide_mup, wide_down = wide
    segs = segment_ids.astype(f32)
    link = jnp.concatenate(
        [jnp.ones((seqs, 1), f32), jnp.where(segs[:, 1:] == segs[:, :-1], 1.0, 0.0)], axis=1
    ).reshape(rows_all, 1)
    residual_in = block_input.reshape(rows_all, width)
    scale_one = inverse_rms(residual_in)
    normed_one = (residual_in * scale_one * norm_gain).astype(bfloat)
    pi = jnp.dot(normed_one, wide_input, preferred_element_type=f32)
    pf = jnp.dot(normed_one, wide_forget, preferred_element_type=f32)
    pg = jnp.dot(normed_one, wide_gate, preferred_element_type=f32)
    channels = pi.shape[1]
    ids = jnp.broadcast_to(
        jnp.concatenate([segs[:, 0], segs[:, -1]])[:, None], (2 * seqs, channels)
    )
    low_row, gain_row = lower[None, :], hidden_gain[None, :]
    if small:
        h, mixed_in, rh, start = mixer_forward(
            Z, seqs, length, width, pi, pf, pg, low_row, gain_row, link, ids
        )
    else:
        h, mixed_in, rh, start = mixer_forward_plain(
            seqs, length, width, pi, pf, pg, lower, hidden_gain, segs
        )
    mixer_out = lax.psum(times_back(mixed_in, wide_out).astype(bfloat), "tp").astype(f32)
    middle = residual_in + mixer_out
    scale_two = inverse_rms(middle)
    normed_two = (middle * scale_two * mlp_gain).astype(bfloat)
    gate_pre = jnp.dot(normed_two, wide_mgate, preferred_element_type=f32)
    up_pre = jnp.dot(normed_two, wide_mup, preferred_element_type=f32)
    silu_mlp = jax.nn.silu(gate_pre)
    activated = (silu_mlp * up_pre).astype(bfloat)
    mlp_out = lax.psum(times_back(activated, wide_down).astype(bfloat), "tp").astype(f32)
    output = middle + mlp_out
    upstream = cotangent.reshape(rows_all, width)
    upstream_low = upstream.astype(bfloat)
    grad_activ = jnp.dot(upstream_low, wide_down, preferred_element_type=f32)
    grad_down = outer_sum(upstream_low, activated).astype(bfloat)
    grad_gate_pre = (grad_activ * up_pre * silu_slope(gate_pre)).astype(bfloat)
    grad_up_pre = (grad_activ * silu_mlp).astype(bfloat)
    grad_mgate = outer_sum(normed_two, grad_gate_pre).astype(bfloat)
    grad_mup = outer_sum(normed_two, grad_up_pre).astype(bfloat)
    grad_normed_two = lax.psum(
        (times_back(grad_gate_pre, wide_mgate) + times_back(grad_up_pre, wide_mup)).astype(bfloat),
        "tp",
    ).astype(f32)
    grad_mlp_gain = jnp.sum(grad_normed_two * middle * scale_two, axis=0)
    grad_middle = upstream + rms_backward(middle, scale_two, mlp_gain, grad_normed_two)
    middle_low = grad_middle.astype(bfloat)
    dm = jnp.dot(middle_low, wide_out, preferred_element_type=f32)
    grad_out = outer_sum(middle_low, mixed_in).astype(bfloat)
    if small:
        dpi, dpf, dpg, grad_hidden_gain, grad_lower = mixer_backward(
            Z, seqs, length, width, dm, h, pi, pf, pg, low_row, gain_row, link, ids, rh, start
        )
        grad_hidden_gain, grad_lower = grad_hidden_gain[0], grad_lower[0]
    else:
        dpi, dpf, dpg, grad_hidden_gain, grad_lower = mixer_backward_plain(
            seqs, length, width, dm, h, pi, pf, pg, lower, hidden_gain, segs, rh, start
        )
    grad_w_input = outer_sum(normed_one, dpi).astype(bfloat)
    grad_w_forget = outer_sum(normed_one, dpf).astype(bfloat)
    grad_w_gate = outer_sum(normed_one, dpg).astype(bfloat)
    grad_normed_one = lax.psum(
        (
            times_back(dpi, wide_input) + times_back(dpf, wide_forget) + times_back(dpg, wide_gate)
        ).astype(bfloat),
        "tp",
    ).astype(f32)
    grad_norm_gain = jnp.sum(grad_normed_one * residual_in * scale_one, axis=0)
    grad_resid = grad_middle + rms_backward(residual_in, scale_one, norm_gain, grad_normed_one)
    parts = (grad_down, grad_mgate, grad_mup, grad_out, grad_w_input, grad_w_forget, grad_w_gate)
    vectors = jnp.concatenate([grad_norm_gain, grad_mlp_gain, grad_lower, grad_hidden_gain])
    if small:
        vectors, sums = scatter_all(parts, vectors.reshape(-1, 128), Z)
        vectors = vectors.reshape(-1)
    else:
        vectors = lax.psum(vectors, ("shard", "ctx"))
        sums = [
            lax.psum_scatter(p, ("shard", "ctx"), scatter_dimension=0, tiled=True).astype(f32)
            for p in parts
        ]
    return (
        output.reshape(block_input.shape),
        grad_resid.reshape(block_input.shape),
        vectors[:width],
        vectors[2 * width : 2 * width + channels],
        sums[4],
        sums[5],
        sums[6],
        vectors[2 * width + channels :],
        sums[3],
        vectors[width : 2 * width],
        sums[1],
        sums[2],
        sums[0],
    )


def solution(mesh):
    return jax.shard_map(
        on_device,
        mesh=mesh,
        in_specs=(
            P("shard", "ctx", None),
            P("shard", "ctx"),
            P(),
            P("tp"),
            P(("shard", "ctx"), "tp"),
            P(("shard", "ctx"), "tp"),
            P(("shard", "ctx"), "tp"),
            P("tp"),
            P(("shard", "ctx"), "tp"),
            P(),
            P(("shard", "ctx"), "tp"),
            P(("shard", "ctx"), "tp"),
            P(("shard", "ctx"), "tp"),
            P("shard", "ctx", None),
        ),
        out_specs=(
            P("shard", "ctx", None),
            P("shard", "ctx", None),
            P(),
            P("tp"),
            P(("shard", "ctx"), "tp"),
            P(("shard", "ctx"), "tp"),
            P(("shard", "ctx"), "tp"),
            P("tp"),
            P(("shard", "ctx"), "tp"),
            P(),
            P(("shard", "ctx"), "tp"),
            P(("shard", "ctx"), "tp"),
            P(("shard", "ctx"), "tp"),
        ),
        check_vma=False,
    )
```

```python
import functools
import jax
import jax.numpy as jnp
from jax import lax
from jax.experimental import pallas as pl
from jax.experimental.pallas import tpu as pltpu
from jax.sharding import PartitionSpec as P

epsilon = 1e-06
MESH = pl.DeviceIdType.MESH


def remote(src, dst, send_sem, recv_sem, device):
    return pltpu.make_async_remote_copy(
        src_ref=src, dst_ref=dst, send_sem=send_sem, recv_sem=recv_sem,
        device_id=device, device_id_type=MESH)


def gather_body(nw, Z, ahead, relay, *refs):
    own, out = refs[:nw], refs[nw:2 * nw]
    (s_up, r_up, s_dn, r_dn, s_x, r_x, s_c, r_c, s_h, r_h, l_sem) = refs[2 * nw:]
    s, z = lax.axis_index("shard"), lax.axis_index("ctx")
    q, c = s // 2, lax.rem(s, 2)
    sx, sc = (1 - q) * 2 + c, q * 2 + (1 - c)
    sxc = (1 - q) * 2 + (1 - c)
    even = lax.rem(z, 2) == 0
    zp = jnp.where(even, z + 1, z - 1)
    rows = [r.shape[0] for r in own]

    def block(w, s_, z_, part=0):
        R = rows[w]
        start = pl.multiple_of((s_ * Z + z_) * R, R)
        if part == 0:
            return out[w].at[pl.ds(start, R), :]
        H = R // 2
        return out[w].at[pl.ds(pl.multiple_of(start + (part - 1) * H, H), H), :]

    UP, DN, XX, CC, ZP = {"ctx": z + 1}, {"ctx": z - 1}, {"shard": sx}, {"shard": sc}, {"ctx": zp}

    def up(w, k, src=None):
        b = block(w, s, z - k)
        return remote(b if src is None else src, b, s_up.at[w, k], r_up.at[w, k], UP)

    def dn(w, k, src=None):
        b = block(w, s, z + k)
        return remote(b if src is None else src, b, s_dn.at[w, k], r_dn.at[w, k], DN)

    def origin(j):
        return z if j == 0 else (z - j if j < Z else z + j - Z + 1)

    def valid(j):
        return (z >= j) if j < Z else (z + j - Z + 1 <= Z - 1)

    def xx(w, j, part, src=None):
        b = block(w, s, origin(j), part)
        return remote(b if src is None else src, b, s_x.at[w, j], r_x.at[w, j], XX)

    def xx_in(w, j, part):
        b = block(w, sx, origin(j), part)
        return remote(b, b, s_x.at[w, j], r_x.at[w, j], XX)

    def cc(w, j, src=None):
        b = block(w, s if j < 2 * Z - 1 else sx, origin(j % (2 * Z - 1)))
        return remote(b if src is None else src, b, s_c.at[w, j], r_c.at[w, j], CC)

    def cc_in(w, j):
        b = block(w, sc if j < 2 * Z - 1 else sxc, origin(j % (2 * Z - 1)))
        return remote(b, b, s_c.at[w, j], r_c.at[w, j], CC)

    def half(w):
        b = block(w, sx, z, 1)
        return remote(b, b, s_h.at[w], r_h.at[w], ZP)

    def half_in(w):
        b = block(w, sx, zp, 1)
        return remote(b, b, s_h.at[w], r_h.at[w], ZP)

    barrier = pltpu.get_barrier_semaphore()
    for d in (XX, CC):
        pl.semaphore_signal(barrier, inc=1, device_id=d, device_id_type=MESH)

    @pl.when(z < Z - 1)
    def _():
        pl.semaphore_signal(barrier, inc=1, device_id=UP, device_id_type=MESH)

    @pl.when(z > 0)
    def _():
        pl.semaphore_signal(barrier, inc=1, device_id=DN, device_id_type=MESH)

    pl.semaphore_wait(barrier, 2 + (z < Z - 1).astype(jnp.int32) + (z > 0).astype(jnp.int32))

    local = []
    for w in range(nw):
        cp = pltpu.make_async_copy(own[w], block(w, s, z), l_sem.at[w])
        cp.start()
        local.append(cp)

    def begin(w):
        @pl.when(z < Z - 1)
        def _():
            up(w, 0, own[w]).start()

        @pl.when(z > 0)
        def _():
            dn(w, 0, own[w]).start()

        xx(w, 0, 0, own[w]).start()
        cc(w, 0, own[w]).start()

    def is_pair(j):
        if j == 1:
            return jnp.logical_not(even)
        if j == Z:
            return even
        return None

    def for_part(w, j, fn):
        pair = is_pair(j) if relay else None
        if pair is None:
            fn(0)
        else:
            @pl.when(pair)
            def _():
                fn(2)

            @pl.when(jnp.logical_not(pair))
            def _():
                fn(0)

    def step(w, k):
        @pl.when(z >= k)
        def _():
            remote(block(w, s, z - k), block(w, s, z - k), s_up.at[w, k - 1], r_up.at[w, k - 1], UP).wait_recv()
            if k < Z - 1:
                @pl.when(z < Z - 1)
                def _():
                    up(w, k).start()
            for_part(w, k, lambda p: xx(w, k, p).start())
            cc(w, k).start()

        @pl.when(z + k <= Z - 1)
        def _():
            remote(block(w, s, z + k), block(w, s, z + k), s_dn.at[w, k - 1], r_dn.at[w, k - 1], DN).wait_recv()
            if k < Z - 1:
                @pl.when(z > 0)
                def _():
                    dn(w, k).start()
            for_part(w, Z - 1 + k, lambda p: xx(w, Z - 1 + k, p).start())
            cc(w, Z - 1 + k).start()

    def xstep(w, j):
        @pl.when(valid(j))
        def _():
            for_part(w, j, lambda p: xx_in(w, j, p).wait_recv())
            if j == 0:
                if relay:
                    half(w).start()
                cc(w, 2 * Z - 1).start()
            else:
                if relay and is_pair(j) is not None:
                    @pl.when(is_pair(j))
                    def _():
                        half_in(w).wait_recv()
                cc(w, 2 * Z - 1 + j).start()

    def finish(w):
        for j in range(4 * Z - 2):
            @pl.when(valid(j % (2 * Z - 1)))
            def _():
                cc_in(w, j).wait_recv()
                cc(w, j).wait_send()
        for j in range(2 * Z - 1):
            @pl.when(valid(j))
            def _():
                for_part(w, j, lambda p: xx(w, j, p).wait_send())
        for k in range(Z - 1):
            @pl.when((z >= k) & (z < Z - 1))
            def _():
                up(w, k).wait_send()

            @pl.when((z + k <= Z - 1) & (z > 0))
            def _():
                dn(w, k).wait_send()
        if relay:
            half(w).wait_send()
        local[w].wait()

    for w in range(min(ahead, nw)):
        begin(w)
    for w in range(nw):
        for k in range(1, Z):
            step(w, k)
            if k == 1:
                xstep(w, 0)
                if w + ahead < nw:
                    begin(w + ahead)
            else:
                xstep(w, k - 1)
                xstep(w, Z - 1 + k - 1)
            if w > 0 and k == 1:
                xstep(w - 1, Z - 1)
                xstep(w - 1, 2 * Z - 2)
    xstep(nw - 1, Z - 1)
    xstep(nw - 1, 2 * Z - 2)
    for w in range(nw):
        finish(w)


def gather_all(shards, S, Z, collective_id=0, ahead=2, relay=True):
    nw = len(shards)
    dma = pltpu.SemaphoreType.DMA
    return pl.pallas_call(
        functools.partial(gather_body, nw, Z, ahead, relay),
        out_shape=[jax.ShapeDtypeStruct((a.shape[0] * S * Z, a.shape[1]), a.dtype) for a in shards],
        in_specs=[pl.BlockSpec(memory_space=pltpu.VMEM)] * nw,
        out_specs=[pl.BlockSpec(memory_space=pl.ANY)] * nw,
        scratch_shapes=[
            dma((nw, Z - 1)), dma((nw, Z - 1)), dma((nw, Z - 1)), dma((nw, Z - 1)),
            dma((nw, 2 * Z - 1)), dma((nw, 2 * Z - 1)),
            dma((nw, 4 * Z - 2)), dma((nw, 4 * Z - 2)), dma((nw,)), dma((nw,)), dma((nw,)),
        ],
        compiler_params=pltpu.CompilerParams(collective_id=collective_id, has_side_effects=True),
        name="weights_in",
    )(*shards)


def pick(z, values):
    out = jnp.int32(values[-1])
    for k in range(len(values) - 2, -1, -1):
        out = jnp.where(z == k, values[k], out)
    return out


def far_first(Z):
    table = []
    for z in range(Z):
        ups, dns, mine, turn = list(range(Z - 1, z, -1)), list(range(0, z)), [], z < Z // 2
        while ups or dns:
            if (turn and ups) or not dns:
                mine.append(ups.pop(0))
            else:
                mine.append(dns.pop(0))
            turn = not turn
        table.append(mine + [z])
    return table


class Scatter:
    def __init__(self, Z, parts, rc, xr, zu, zd, hr, outs, xs, zs, stage, fin, sems):
        self.Z, self.parts, self.rc, self.xr, self.zu, self.zd, self.hr, self.outs = Z, parts, rc, xr, zu, zd, hr, outs
        self.xs, self.zs, self.stage, self.fin = xs, zs, stage, fin
        (self.c_s, self.c_r, self.x_s, self.x_r, self.z_s, self.u_r, self.d_r, self.h_s, self.h_r, self.l_s, self.f_s) = sems
        s, z = lax.axis_index("shard"), lax.axis_index("ctx")
        q, c = s // 2, lax.rem(s, 2)
        self.z, self.q, self.c = z, q, c
        self.even = lax.rem(z, 2) == 0
        self.zp = jnp.where(self.even, z + 1, z - 1)
        self.X = {"shard": (1 - q) * 2 + c}
        self.C = {"shard": q * 2 + (1 - c)}
        self.UP, self.DN, self.ZP = {"ctx": z + 1}, {"ctx": z - 1}, {"ctx": self.zp}
        self.R = [p.shape[0] // (4 * Z) for p in parts]
        self.N = [p.shape[1] for p in parts]
        self.ffirst = far_first(Z)

    def part(self, w, q, c, z, n=1):
        R = self.R[w]
        return self.parts[w].at[pl.ds(pl.multiple_of(((2 * q + c) * self.Z + z) * R, R), n * R), :]

    def rows(self, ref, i, w):
        R = self.R[w]
        return ref.at[pl.ds(pl.multiple_of(i * R, R), R), :]

    def hrows(self, ref, i, w, h):
        H = self.R[w] // 2
        return ref.at[pl.ds(pl.multiple_of(i * 2 * H + h * H, H), H), :]

    def c_copy(self, w, k):
        Z, R = self.Z, self.R[w]
        q = self.q if k == 1 else 1 - self.q
        return remote(self.part(w, q, 1 - self.c, 0, Z), self.rc[w].at[pl.ds(k * Z * R, Z * R), :],
                      self.c_s.at[w, k], self.c_r.at[w, k], self.C)

    def c_send(self, w):
        for k in (0, 1):
            self.c_copy(w, k).start()

    def stage_of(self, slot):
        return self.stage[0].at[slot] if slot < 2 else self.stage[1]

    def load_waits(self, w, srcs, slot):
        cps = []
        for i, src in enumerate(srcs):
            if src is not None:
                n = src.shape[0]
                cps.append(pltpu.make_async_copy(
                    src, self.stage_of(slot).at[i, pl.ds(0, n), pl.ds(0, self.N[w])], self.l_s.at[slot, i]))
        return cps

    def load(self, w, srcs, slot):
        cps = self.load_waits(w, srcs, slot)
        for cp in cps:
            cp.start()
        return cps

    def add(self, w, slot, idx, store, lo=0, hi=None, off=None):
        N = self.N[w]
        hi = self.R[w] if hi is None else hi
        G = 16

        def go(i, _):
            r = pl.multiple_of(lo + i * G, G)
            tot = None
            for k in idx:
                rk = r
                if off is not None and k in off:
                    rk = pl.multiple_of(r + off[k], G)
                v = self.stage_of(slot)[k, pl.ds(rk, G), pl.ds(0, N)].astype(jnp.float32)
                tot = v if tot is None else tot + v
            store(r, tot)
            return 0

        lax.fori_loop(0, (hi - lo) // G, go, 0)

    def x_slot(self, w, n):
        return self.xs.at[w % 2, n, :, pl.ds(0, self.N[w])]

    def order(self, n):
        return pick(self.z, [t[n] for t in self.ffirst])

    def x_copy(self, w, n, half=None):
        zt = self.order(n)
        src = self.x_slot(w, n)
        H = self.R[w] // 2
        if half is None:
            return remote(src, self.rows(self.xr[w], zt, w), self.x_s.at[w, n], self.x_r.at[w, n], self.X)
        return remote(src.at[pl.ds(half * H, H), :], self.hrows(self.xr[w], zt, w, half), self.x_s.at[w, n], self.x_r.at[w, n], self.X)

    def h_copy(self, w, n=0):
        H = self.R[w] // 2
        return remote(self.x_slot(w, n).at[pl.ds(0, H), :], self.hr[w], self.h_s.at[w], self.h_r.at[w], self.ZP)

    def on_pair(self, n, yes, no):
        if n == self.Z - 1:
            no()
            return
        paired = self.order(n) == self.zp

        @pl.when(paired)
        def _():
            yes()

        @pl.when(jnp.logical_not(paired))
        def _():
            no()

    def x_load(self, w, n):
        zt = self.order(n)
        return self.load(w, [self.part(w, 1 - self.q, self.c, zt), self.rows(self.rc[w], zt, w)], n % 2)

    def x_phase(self, w, n):
        Z, H = self.Z, self.R[w] // 2
        last = n == Z - 1
        if n == 0:
            self.c_copy(w, 0).wait_recv()
            self.x_load(w, 0)
        if not last:
            self.x_load(w, n + 1)
        if last:
            self.h_copy(w).wait_recv()
            for cp in self.load(w, [None, None, self.hr[w]], n % 2):
                cp.wait()
        if w >= 2:
            self.x_wait_send(w - 2, n)
        zt = self.order(n)
        for cp in self.load_waits(w, [self.part(w, 1 - self.q, self.c, zt), self.rows(self.rc[w], zt, w)], n % 2):
            cp.wait()
        dst = self.x_slot(w, n)

        def store(r, v):
            dst[pl.ds(r, 16), :] = v.astype(jnp.bfloat16)

        if last:
            self.add(w, n % 2, (0, 1, 2), store, 0, H)
            self.add(w, n % 2, (0, 1), store, H, 2 * H)
            self.x_copy(w, n).start()
        else:
            self.add(w, n % 2, (0, 1), store)

            def yes():
                self.h_copy(w, n).start()
                self.x_copy(w, n, 1).start()

            self.on_pair(n, yes, lambda: self.x_copy(w, n).start())

    def x_wait_send(self, w, n):
        def yes():
            self.h_copy(w, n).wait_send()
            self.x_copy(w, n, 1).wait_send()

        self.on_pair(n, yes, lambda: self.x_copy(w, n).wait_send())

    def z_copy(self, w, n, dest, up):
        src = self.zs.at[w % 2, n, :, pl.ds(0, self.N[w])]
        if up:
            return remote(src, self.rows(self.zu[w], dest, w), self.z_s.at[w, n], self.u_r.at[w, dest], self.UP)
        return remote(src, self.rows(self.zd[w], dest, w), self.z_s.at[w, n], self.d_r.at[w, dest], self.DN)

    def x_wait(self, w, n):
        self.on_pair(n, lambda: self.x_copy(w, n, 1).wait_recv(), lambda: self.x_copy(w, n).wait_recv())

    def z_phase(self, w, n):
        Z, H = self.Z, self.R[w] // 2
        z = self.z
        last = n == Z - 1
        dest = z if last else pick(z, [t[n] for t in self.ffirst])
        if n == 0:
            self.c_copy(w, 1).wait_recv()
        self.x_wait(w, n)
        cps = self.load(w, [self.part(w, self.q, self.c, dest), self.rows(self.rc[w], dest + Z, w),
                            self.rows(self.xr[w], dest, w)], 2)
        if not last:
            up = dest > z
            down = dest < z
            has_in = (up & (z > 0)) | (down & (z < Z - 1))

            @pl.when(up & (z > 0))
            def _():
                self.z_copy(w, n, dest, True).wait_recv()
                cp = self.load(w, [None] * 3 + [self.rows(self.zu[w], dest, w)], 2)
                cp[0].wait()

            @pl.when(down & (z < Z - 1))
            def _():
                self.z_copy(w, n, dest, False).wait_recv()
                cp = self.load(w, [None] * 3 + [self.rows(self.zd[w], dest, w)], 2)
                cp[0].wait()

            if w >= 2:
                self.z_wait_send(w - 2, n)
            for cp in cps:
                cp.wait()
            dst = self.zs.at[w % 2, n, :, pl.ds(0, self.N[w])]

            def store(r, v):
                dst[pl.ds(r, 16), :] = v.astype(jnp.bfloat16)

            paired = dest == self.zp
            self.sum_parts(w, paired, has_in, (3,), store)

            @pl.when(up)
            def _():
                self.z_copy(w, n, dest, True).start()

            @pl.when(down)
            def _():
                self.z_copy(w, n, dest, False).start()
        else:
            @pl.when(z > 0)
            def _():
                self.z_copy(w, 0, dest, True).wait_recv()
                cp = self.load(w, [None] * 3 + [self.rows(self.zu[w], dest, w)], 2)
                cp[0].wait()

            @pl.when(z < Z - 1)
            def _():
                self.z_copy(w, 0, dest, False).wait_recv()
                cp = self.load(w, [None] * 4 + [self.rows(self.zd[w], dest, w)], 2)
                cp[0].wait()

            for cp in cps:
                cp.wait()
            if w >= 1:
                self.f_copy(w - 1).wait()
            dst = self.fin.at[:, pl.ds(0, self.N[w])]

            def store(r, v):
                dst[pl.ds(r, 16), :] = v

            @pl.when((z > 0) & (z < Z - 1))
            def _():
                self.add(w, 2, (0, 1, 2, 3, 4), store)

            @pl.when(z == 0)
            def _():
                self.add(w, 2, (0, 1, 2, 4), store)

            @pl.when(z == Z - 1)
            def _():
                self.add(w, 2, (0, 1, 2, 3), store)

            self.f_copy(w).start()

    def sum_parts(self, w, paired, has_in, extra, store):
        H = self.R[w] // 2
        for p in (False, True):
            for e in (False, True):
                cond = (paired if p else jnp.logical_not(paired)) & (has_in if e else jnp.logical_not(has_in))

                @pl.when(cond)
                def _(p=p, e=e):
                    ex = extra if e else ()
                    if p:
                        self.add(w, 2, (0, 1) + ex, store, 0, H)
                        self.add(w, 2, (0, 1, 2) + ex, store, H, 2 * H)
                    else:
                        self.add(w, 2, (0, 1, 2) + ex, store)

    def z_wait_send(self, w, n):
        z = self.z
        dest = pick(z, [t[n] for t in self.ffirst])
        self.z_copy_any(w, n).wait_send()

    def z_copy_any(self, w, n):
        src = self.zs.at[w % 2, n, :, pl.ds(0, self.N[w])]
        return remote(src, self.rows(self.zu[w], 0, w), self.z_s.at[w, n], self.u_r.at[w, 0],
                      {"ctx": jnp.where(pick(self.z, [t[n] for t in self.ffirst]) > self.z, self.z + 1, self.z - 1)})

    def f_copy(self, w):
        return pltpu.make_async_copy(self.fin.at[:, pl.ds(0, self.N[w])], self.outs[w], self.f_s.at[w])

    def drain(self, w, nw):
        for k in (0, 1):
            self.c_copy(w, k).wait_send()
        if w >= nw - 2:
            for n in range(self.Z):
                self.x_wait_send(w, n)
            for n in range(self.Z - 1):
                self.z_wait_send(w, n)
        if w == nw - 1:
            self.f_copy(w).wait()


T8 = 8


def spread(Z, z, pay, box, s_sem, r_sem):
    cps = []
    for o in range(1, Z):
        to = lax.rem(z + o, Z)
        cp = remote(pay, box.at[z], s_sem.at[o - 1], r_sem.at[z], {"ctx": to})
        cp.start()
        cps.append(cp)
    box[z] = pay[...]
    return cps


def spread_wait(Z, z, pay, box, s_sem, r_sem, cps):
    for o in range(1, Z):
        frm = lax.rem(z + o, Z)
        remote(pay, box.at[frm], s_sem.at[o - 1], r_sem.at[frm], {"ctx": frm}).wait_recv()
    for cp in cps:
        cp.wait_send()


def joined(box, k):
    last, first = box[k, 6:8, :], box[k + 1, 4:6, :]
    return jnp.where(last == first, 1.0, 0.0)


def prefix_state(Z, z, box):
    state = jnp.zeros(box.shape[2:][:0] + (2, box.shape[2]), jnp.float32)
    mine = state
    for k in range(Z - 1):
        state = joined(box, k) * (box[k, 2:4, :] + box[k, 0:2, :] * state)
        mine = jnp.where(z == k + 1, state, mine)
    return mine


def suffix_state(Z, z, box):
    state = jnp.zeros((2, box.shape[2]), jnp.float32)
    mine = state
    for k in range(Z - 2, -1, -1):
        state = joined(box, k) * (box[k + 1, 2:4, :] + box[k + 1, 0:2, :] * state)
        mine = jnp.where(z == k, state, mine)
    return mine


def diagonal():
    return lax.broadcasted_iota(jnp.int32, (128, 128), 0) == lax.broadcasted_iota(jnp.int32, (128, 128), 1)


def column_to_rows(col_ref, row_ref, n):
    eye = diagonal()
    for k in range(n // 128):
        col = col_ref[pl.ds(k * 128, 128), :]
        row_ref[k:k + 1, :] = jnp.sum(jnp.where(eye, jnp.broadcast_to(col, (128, 128)), 0.0), axis=0, keepdims=True)


def rows_to_column(row, k):
    return jnp.sum(jnp.where(diagonal(), jnp.broadcast_to(row, (128, 128)), 0.0), axis=1, keepdims=True)


def sigmoid(v):
    return jax.nn.sigmoid(v)


def row_at(ref, t):
    return pl.ds(pl.multiple_of(t, T8), T8)


def forward_scan(seqs, length, pi, pf, lower, link, h, cum):
    C = pi.shape[1]
    low = lower[...]
    iota = lax.broadcasted_iota(jnp.int32, (T8, C), 0)
    ends = []
    for sq in range(seqs):
        def tile(i, carry):
            hl, pr = carry
            r = row_at(pi, sq * length + i * T8)
            s = sigmoid(pf[r, :])
            forget = low + (1.0 - low) * s
            x = pi[r, :]
            b = x * sigmoid(x) * (1.0 - forget)
            a = forget * link[r, :]
            for sh in (1, 2, 4):
                keep = iota >= sh
                b = b + jnp.where(keep, a * pltpu.roll(b, sh, 0), 0.0)
                a = jnp.where(keep, a * pltpu.roll(a, sh, 0), a)
            b = b + a * hl
            a = a * pr
            h[r, :] = b
            cum[r, :] = a
            return b[T8 - 1:T8, :], a[T8 - 1:T8, :]

        ends.append(lax.fori_loop(0, length // T8, tile, (jnp.zeros((1, C), jnp.float32), jnp.ones((1, C), jnp.float32)), unroll=2))
    return ends


def forward_finish(seqs, length, h, cum, start, col):
    def tile(i, _, sq):
        r = row_at(h, sq * length + i * T8)
        v = h[r, :] + cum[r, :] * start[sq:sq + 1, :]
        h[r, :] = v
        col[r, :] = jnp.sum(v * v, axis=1, keepdims=True)
        return 0

    for sq in range(seqs):
        lax.fori_loop(0, length // T8, functools.partial(tile, sq=sq), 0, unroll=2)


def swap_columns(col, row, got, s_sem, r_sem, other, n):
    column_to_rows(col, row, n)
    cp = remote(row, got, s_sem, r_sem, {"tp": other})
    cp.start()
    cp.wait()


def scale_columns(row, got, col, n, width, fn):
    for k in range(n // 128):
        col[pl.ds(k * 128, 128), :] = fn(rows_to_column(row[k:k + 1, :] + got[k:k + 1, :], k))


def mixed(h, rh, gain, pg, m, step=16):
    g = gain[...]

    def tile(i, _):
        r = pl.ds(pl.multiple_of(i * step, step), step)
        p = pg[r, :]
        m[r, :] = (h[r, :] * rh[r, :] * g * (p * sigmoid(p))).astype(m.dtype)
        return 0

    lax.fori_loop(0, h.shape[0] // step, tile, 0)


def mixer_forward_body(Z, seqs, length, width, pi, pf, pg, lower, gain, link, ids, h, m, rh, start,
                       cum, pay, box, row, got, s_c, r_c, s_t, r_t):
    z, t = lax.axis_index("ctx"), lax.axis_index("tp")
    n = seqs * length
    barrier_all(Z, z, t)
    ends = forward_scan(seqs, length, pi, pf, lower, link, h, cum)
    pay[4:8, :] = ids[...]
    for sq in range(seqs):
        pay[sq:sq + 1, :] = ends[sq][1]
        pay[2 + sq:3 + sq, :] = ends[sq][0]
    cps = spread(Z, z, pay, box, s_c, r_c)
    spread_wait(Z, z, pay, box, s_c, r_c, cps)
    start[...] = prefix_state(Z, z, box)
    forward_finish(seqs, length, h, cum, start, rh)
    swap_columns(rh, row, got, s_t.at[0], r_t.at[0], 1 - t, n)
    scale_columns(row, got, rh, n, width, lambda v: lax.rsqrt(v / width + epsilon))
    mixed(h, rh, gain, pg, m)


def barrier_all(Z, z, t):
    barrier = pltpu.get_barrier_semaphore()
    for o in range(1, Z):
        pl.semaphore_signal(barrier, inc=1, device_id={"ctx": lax.rem(z + o, Z)}, device_id_type=MESH)
    pl.semaphore_signal(barrier, inc=1, device_id={"tp": 1 - t}, device_id_type=MESH)
    pl.semaphore_wait(barrier, Z)


def slope(v):
    s = sigmoid(v)
    return s * (1.0 + v * (1.0 - s))


def backward_first(n, dm, h, pg, gain, rh, dpg, col, gsum, step=16):
    g = gain[...]

    def tile(i, acc):
        r = pl.ds(pl.multiple_of(i * step, step), step)
        d, hv, p, rv = dm[r, :], h[r, :], pg[r, :], rh[r, :]
        s = sigmoid(p)
        sl = p * s
        q = d * g * sl
        col[r, :] = jnp.sum(q * hv, axis=1, keepdims=True)
        hr = d * hv * rv
        dpg[r, :] = (hr * g * (s * (1.0 + p * (1.0 - s)))).astype(dpg.dtype)
        return acc + jnp.sum(hr * sl, axis=0, keepdims=True)

    gsum[...] = lax.fori_loop(0, n // step, tile, jnp.zeros(gsum.shape, jnp.float32))


def backward_scan(seqs, length, *a):
    return [backward_scan_one(sq, length, *a) for sq in range(seqs)]


def backward_scan_one(sq, length, dm, h, pf, pg, lower, gain, link, rh, inner, gl, tail):
    C = dm.shape[1]
    low, g = lower[...], gain[...]
    iota = lax.broadcasted_iota(jnp.int32, (T8, C), 0)
    nt = length // T8
    def tile(k, carry):
        vl, pr = carry
        r = row_at(dm, sq * length + (nt - 1 - k) * T8)
        rv = rh[r, :]
        p = pg[r, :]
        q = dm[r, :] * g * (p * sigmoid(p))
        dh = q * rv - h[r, :] * (rv * rv * rv) * inner[r, :]
        a = (low + (1.0 - low) * sigmoid(pf[r, :])) * link[r, :]
        b = a * dh
        for sh in (1, 2, 4):
            keep = iota < T8 - sh
            b = b + jnp.where(keep, a * pltpu.roll(b, T8 - sh, 0), 0.0)
            a = jnp.where(keep, a * pltpu.roll(a, T8 - sh, 0), a)
        v = b + a * vl
        pa = a * pr
        last = iota == T8 - 1
        gl[r, :] = dh + jnp.where(last, vl, pltpu.roll(v, T8 - 1, 0))
        tail[r, :] = jnp.where(last, pr, pltpu.roll(pa, T8 - 1, 0))
        return v[0:1, :], pa[0:1, :]

    return lax.fori_loop(0, nt, tile, (jnp.zeros((1, C), jnp.float32), jnp.ones((1, C), jnp.float32)), unroll=2)


def backward_last(seqs, length, gl, tail, end, h, start, pi, pf, lower, link, dpi, dpf, lsum):
    C = gl.shape[1]
    low = lower[...]
    iota = lax.broadcasted_iota(jnp.int32, (T8, C), 0)
    total = jnp.zeros((1, C), jnp.float32)
    for sq in range(seqs):
        def tile(i, carry):
            acc, hp = carry
            halves = []
            for half in (0, 1):
                r = row_at(gl, sq * length + i * 16 + half * T8)
                gv = gl[r, :] + tail[r, :] * end[sq:sq + 1, :]
                hv = h[r, :]
                prev = jnp.where(iota == 0, hp, pltpu.roll(hv, 1, 0) * link[r, :])
                if half == 1:
                    prev = jnp.where(iota == 0, prev * link[r, :], prev)
                else:
                    prev = jnp.where((iota == 0) & (i > 0), prev * link[r, :], prev)
                s = sigmoid(pf[r, :])
                forget = low + (1.0 - low) * s
                x = pi[r, :]
                sx = sigmoid(x)
                df = gv * (prev - x * sx)
                halves.append((gv * (1.0 - forget) * (sx * (1.0 + x * (1.0 - sx))), df * (1.0 - low) * s * (1.0 - s)))
                acc = acc + jnp.sum(df * (1.0 - s), axis=0, keepdims=True)
                hp = hv[T8 - 1:T8, :]
            r = pl.ds(pl.multiple_of(sq * length + i * 16, 16), 16)
            dpi[r, :] = jnp.concatenate([halves[0][0], halves[1][0]], axis=0).astype(dpi.dtype)
            dpf[r, :] = jnp.concatenate([halves[0][1], halves[1][1]], axis=0).astype(dpf.dtype)
            return acc, hp

        total, _ = lax.fori_loop(0, length // 16, tile, (total, start[sq:sq + 1, :]))
    lsum[...] = total


def mixer_scratch(Z, n, C):
    dma = pltpu.SemaphoreType.DMA
    f = jnp.float32
    return [pltpu.VMEM((8, C), f), pltpu.VMEM((Z, 8, C), f), pltpu.VMEM((n // 128, 128), f), pltpu.VMEM((n // 128, 128), f),
            dma((Z - 1,)), dma((Z,)), dma((1,)), dma((1,))]


def mixer_forward(Z, seqs, length, width, pi, pf, pg, lower, gain, link, ids, cid=2):
    n, C = pi.shape
    f = jnp.float32
    sh = jax.ShapeDtypeStruct
    vm = pl.BlockSpec(memory_space=pltpu.VMEM)
    return pl.pallas_call(
        functools.partial(mixer_forward_body, Z, seqs, length, width),
        out_shape=[sh((n, C), f), sh((n, C), jnp.bfloat16), sh((n, 1), f), sh((seqs, C), f)],
        in_specs=[vm] * 7, out_specs=[vm] * 4,
        scratch_shapes=[pltpu.VMEM((n, C), f)] + mixer_scratch(Z, n, C),
        compiler_params=pltpu.CompilerParams(collective_id=cid, has_side_effects=True),
        name="mixer_forward",
    )(pi, pf, pg, lower, gain, link, ids)


TR = 64
TC = 256


def dot_t(a, b):
    return lax.dot_general(a, b, (((1,), (1,)), ((), ())), preferred_element_type=jnp.float32)


def dot_o(a, b):
    return lax.dot_general(a, b, (((0,), (0,)), ((), ())), preferred_element_type=jnp.float32)


def back_body(Z, seqs, length, *refs):
    (gd, gg, gu, pn, po, x, mid, cot, n1, m, w_out, w_in, w_f, w_g, pi_h, pf_h, pg_h, h_h,
     rh, start, ids, link, gain1, gain2, low, hgain) = refs[:26]
    out, dx, vec_out = refs[26:29]
    grads = refs[29:36]
    mparts = refs[36:40]
    rn, ro = refs[40:42]
    k0 = 42
    rc, xr, zu, zd, hr = (refs[k0 + 7 * i:k0 + 7 * (i + 1)] for i in range(5))
    k0 += 35
    (xs, zs, stage, stage_z, fin, dmid, gm, dm, h, pi, pf, pg, gl, tail, dpi, dpf, dpg, n1v, mv, wbuf, wbuf3, stg, sn, rn1,
     e_f, e_b, vec, vgot, vbox, col, end, pay, box, row, got, acc) = refs[k0:k0 + 36]
    k0 += 36
    (l_h, l_n, w_s, g_s, n_s, n_r, o_s, o_r, t_s, t_r, e_s, eo_s, v_s, v_r, vz_s, vz_r, s_c, r_c, s_t, r_t) = refs[k0:k0 + 20]
    sems = refs[k0 + 20:]
    n, width = x.shape
    C = dm.shape[1]
    parts = (gd, gg, gu) + tuple(mparts)
    sc = Scatter(Z, parts, rc, xr, zu, zd, hr, grads, xs, zs, (stage, stage_z), fin, sems)
    z = sc.z
    t = lax.axis_index("tp")
    OTHER = {"tp": 1 - t}

    barrier = pltpu.get_barrier_semaphore()
    for d in [sc.X, sc.C, OTHER] + [{"ctx": lax.rem(z + o, Z)} for o in range(1, Z)]:
        pl.semaphore_signal(barrier, inc=1, device_id=d, device_id_type=MESH)
    pl.semaphore_wait(barrier, 2 + Z)

    for w in range(3):
        sc.c_send(w)

    NP = n // TR
    NC = width // TC

    def rows_of(k):
        return pl.ds(k * TR, TR)

    def pn_copy(k):
        return remote(pn.at[rows_of(k), :], rn.at[rows_of(k), :], n_s.at[k], n_r.at[k], OTHER)

    def po_copy(k):
        return remote(po.at[rows_of(k), :], ro.at[rows_of(k), :], o_s.at[k], o_r.at[k], OTHER)

    for k in range(NP):
        pn_copy(k).start()
    for k in range(NP):
        po_copy(k).start()
    early = [pltpu.make_async_copy(a, b, l_h.at[i]) for i, (a, b) in enumerate(
        ((pi_h, pi), (pf_h, pf), (pg_h, pg), (h_h, h), (n1, n1v), (m, mv)))]
    for cp in early:
        cp.start()
    vec[...] = jnp.zeros_like(vec)

    steps = []

    def X(w):
        return [functools.partial(sc.x_phase, w, k) for k in range(Z)]

    def Zs(w):
        return [functools.partial(sc.z_phase, w, k) for k in range(Z)]

    def tick(*todo):
        for s in todo:
            s()

    def piece(k, s, f_src, b_src):
        r = rows_of(k)
        return ([pltpu.make_async_copy(a.at[r, :], e_f.at[s, i], e_s.at[s, i]) for i, a in enumerate(f_src)]
                + [pltpu.make_async_copy(a.at[r, :], e_b.at[s, i], e_s.at[s, 2 + i]) for i, a in enumerate(b_src)])

    def p1_load(k):
        pn_copy(k).wait_recv()
        for cp in piece(k, k % 2, (mid, cot), (pn, rn)):
            cp.start()

    def p1(k):
        s = k % 2
        for cp in piece(k, s, (mid, cot), (pn, rn)):
            cp.wait()
        g = gain2[...]

        def go(i, a):
            r = pl.ds(pl.multiple_of(i * 16, 16), 16)
            v, ct = e_f[s, 0, r, :], e_f[s, 1, r, :]
            d = e_b[s, 0, r, :].astype(jnp.float32) + e_b[s, 1, r, :].astype(jnp.float32)
            r2 = lax.rsqrt(jnp.mean(v * v, axis=1, keepdims=True) + epsilon)
            gdn = d * g
            inner = jnp.mean(gdn * v, axis=1, keepdims=True)
            o = ct + gdn * r2 - v * (r2 * r2 * r2 * inner)
            rr = pl.ds(pl.multiple_of(k * TR + i * 16, 16), 16)
            dmid[rr, :] = o
            gm[rr, :] = o.astype(jnp.bfloat16)
            return a + jnp.sum(d * v * r2, axis=0, keepdims=True)

        vec[1:2, :] = vec[1:2, :] + lax.fori_loop(0, TR // 16, go, jnp.zeros((1, width), jnp.float32))

    def po_load(k):
        po_copy(k).wait_recv()
        for cp in piece(k, k % 2, (mid,), (po, ro)):
            if cp is not None:
                cp.start()

    def o_store(k):
        return pltpu.make_async_copy(e_f.at[k % 2, 1], out.at[rows_of(k), :], eo_s.at[k % 2])

    def p_out(k):
        s = k % 2
        for cp in piece(k, s, (mid,), (po, ro)):
            cp.wait()
        if k >= 2:
            o_store(k - 2).wait()

        def go(i, _):
            r = pl.ds(pl.multiple_of(i * 16, 16), 16)
            e_f[s, 1, r, :] = e_f[s, 0, r, :] + (e_b[s, 0, r, :].astype(jnp.float32) + e_b[s, 1, r, :].astype(jnp.float32))
            return 0

        lax.fori_loop(0, TR // 16, go, 0)
        o_store(k).start()

    NW = C // TC

    def w_load(j, s):
        return pltpu.make_async_copy(w_out.at[:, pl.ds(pl.multiple_of(j * TC, TC), TC)], wbuf.at[s], w_s.at[s, 0])

    def p2():
        w_load(0, 0).start()

        def go(j, _):
            s = lax.rem(j, 2)

            @pl.when(j + 1 < NW)
            def _():
                w_load(j + 1, 1 - s).start()

            w_load(j, s).wait()
            dm[:, pl.ds(pl.multiple_of(j * TC, TC), TC)] = jnp.dot(gm[...], wbuf[s], preferred_element_type=jnp.float32)
            return 0

        lax.fori_loop(0, NW, go, 0)

    def g_copy(dst, j, s):
        return pltpu.make_async_copy(stg.at[s], dst.at[pl.ds(pl.multiple_of(j * TC, TC), TC), :], g_s.at[s])

    def p4(w, lhs, rhs):
        dst = mparts[w - 3]

        def go(j, _):
            s = lax.rem(j, 2)

            @pl.when(j >= 2)
            def _():
                g_copy(dst, j - 2, s).wait()

            stg[s] = dot_o(lhs[:, pl.ds(pl.multiple_of(j * TC, TC), TC)], rhs[...]).astype(jnp.bfloat16)
            g_copy(dst, j, s).start()
            return 0

        lax.fori_loop(0, NC, go, 0)
        g_copy(dst, NC - 2, NC % 2).wait()
        g_copy(dst, NC - 1, (NC - 1) % 2).wait()
        sc.c_send(w)

    def w3_start(j, s):
        for i, a in enumerate((w_in, w_f, w_g)):
            pltpu.make_async_copy(a.at[pl.ds(pl.multiple_of(j * TC, TC), TC), :], wbuf3.at[s, i], w_s.at[2 + s, i]).start()

    def w3_wait(j, s):
        for i, a in enumerate((w_in, w_f, w_g)):
            pltpu.make_async_copy(a.at[pl.ds(pl.multiple_of(j * TC, TC), TC), :], wbuf3.at[s, i], w_s.at[2 + s, i]).wait()

    def n_copy(j):
        return remote(sn.at[j], rn1.at[j], t_s.at[j], t_r.at[j], OTHER)

    def p5(j0, j1):
        def go(j, _):
            s = lax.rem(j, 2)

            @pl.when(j + 1 < NC)
            def _():
                w3_start(j + 1, 1 - s)

            w3_wait(j, s)
            o = dot_t(dpi[...], wbuf3[s, 0]) + dot_t(dpf[...], wbuf3[s, 1]) + dot_t(dpg[...], wbuf3[s, 2])
            sn[j] = o.astype(jnp.bfloat16)
            n_copy(j).start()
            return 0

        lax.fori_loop(j0, j1, go, 0)

    def x_load(j, s):
        return pltpu.make_async_copy(x.at[:, pl.ds(j * TC, TC)], tail.at[:, pl.ds(s * TC, TC)], e_s.at[s, 0])

    def p6a(j):
        s = j % 2
        if j == 0:
            x_load(0, 0).start()
        if j + 1 < NC:
            x_load(j + 1, 1 - s).start()
        x_load(j, s).wait()
        n_copy(j).wait_recv()
        g = gain1[:, j * TC:(j + 1) * TC]

        def go(i, _):
            r = pl.ds(pl.multiple_of(i * 16, 16), 16)
            v = tail[r, s * TC:(s + 1) * TC]
            d = sn[j, r, :].astype(jnp.float32) + rn1[j, r, :].astype(jnp.float32)
            a, b = v * v, d * g * v
            a, b = a[:, :128] + a[:, 128:], b[:, :128] + b[:, 128:]
            if j == 0:
                acc[0, r, :] = a
                acc[1, r, :] = b
            else:
                acc[0, r, :] = acc[0, r, :] + a
                acc[1, r, :] = acc[1, r, :] + b
            return 0

        lax.fori_loop(0, n // 16, go, 0, unroll=2)

    def p6b():
        def go(i, _):
            r = pl.ds(pl.multiple_of(i * 16, 16), 16)
            r1 = lax.rsqrt(jnp.sum(acc[0, r, :], axis=1, keepdims=True) / width + epsilon)
            inner = jnp.sum(acc[1, r, :], axis=1, keepdims=True) / width
            acc[0, r, :] = jnp.broadcast_to(r1, (16, 128))
            acc[1, r, :] = jnp.broadcast_to(r1 * r1 * r1 * inner, (16, 128))
            return 0

        lax.fori_loop(0, n // 16, go, 0, unroll=2)

    def dx_copy(j):
        s = j % 2
        return pltpu.make_async_copy(gl.at[:, pl.ds(s * TC, TC)], dx.at[:, pl.ds(j * TC, TC)], eo_s.at[s])

    def p6c(j):
        s = j % 2
        if j == 0:
            x_load(0, 0).start()
        if j + 1 < NC:
            x_load(j + 1, 1 - s).start()
        x_load(j, s).wait()
        if j >= 2:
            dx_copy(j - 2).wait()
        g = gain1[:, j * TC:(j + 1) * TC]

        def go(i, total):
            r = pl.ds(pl.multiple_of(i * 16, 16), 16)
            v = tail[r, s * TC:(s + 1) * TC]
            d = sn[j, r, :].astype(jnp.float32) + rn1[j, r, :].astype(jnp.float32)
            r1 = jnp.concatenate([acc[0, r, :], acc[0, r, :]], axis=1)
            ri = jnp.concatenate([acc[1, r, :], acc[1, r, :]], axis=1)
            gl[r, s * TC:(s + 1) * TC] = dmid[r, j * TC:(j + 1) * TC] + d * g * r1 - v * ri
            return total + jnp.sum(d * v * r1, axis=0, keepdims=True)

        vec[0:1, j * TC:(j + 1) * TC] = lax.fori_loop(0, n // 16, go, jnp.zeros((1, TC), jnp.float32), unroll=2)
        dx_copy(j).start()

    x0, x1, x2, z0, z1, z2 = X(0), X(1), X(2), Zs(0), Zs(1), Zs(2)
    x3, x4, x5, x6 = X(3), X(4), X(5), X(6)
    z3, z4, z5, z6 = Zs(3), Zs(4), Zs(5), Zs(6)
    tick(*x0, x1[0])
    p1_load(0)
    tick(x1[1])
    between = [[z0[0], x1[2]], [x1[3]], [z0[1]], [], [z0[2], x2[0]], [], [z0[3], x2[1]], [x2[2]]]
    for k in range(NP):
        if k + 1 < NP:
            p1_load(k + 1)
        p1(k)
        tick(*(between[k] if k < len(between) else []))
    p2()
    tick(x2[3], z1[0])
    for cp in early:
        cp.wait()
    p4(3, gm, mv)
    tick(z1[1])
    backward_first(n, dm, h, pg, hgain, rh, dpg, col, acc_row(vec, 2, C))
    column_to_rows(col, row, n)
    swap = remote(row, got, s_t.at[0], r_t.at[0], OTHER)
    swap.start()
    tick(x3[0], x3[1])
    swap.wait()
    scale_columns(row, got, col, n, width, lambda v: v / width)
    ends = []
    for sq in range(seqs):
        ends.append(backward_scan_one(sq, length, dm, h, pf, pg, low, hgain, link, rh, col, gl, tail))
        tick(z1[2 + sq] if sq < 2 else (lambda: None))
    pay[4:8, :] = ids[...]
    for sq in range(seqs):
        pay[sq:sq + 1, :] = ends[sq][1]
        pay[2 + sq:3 + sq, :] = ends[sq][0]
    cps = spread(Z, z, pay, box, s_c, r_c)
    tick(x3[2], x3[3])
    spread_wait(Z, z, pay, box, s_c, r_c, cps)
    end[...] = suffix_state(Z, z, box)
    backward_last(seqs, length, gl, tail, end, h, start, pi, pf, low, link, dpi, dpf, acc_row(vec, 3, C))
    tick(z2[0])
    w3_start(0, 0)
    p4(4, n1v, dpi)
    tick(x4[0], x4[1], z2[1])
    p4(5, n1v, dpf)
    tick(x4[2], x4[3], z2[2])
    p4(6, n1v, dpg)
    tick(z2[3], x5[0], x5[1])
    p5(0, NC // 2)
    tick(x5[2], x5[3], z3[0], z3[1])
    p5(NC // 2, NC)
    tick(z3[2], z3[3], *x6)
    po_load(0)
    outs = [[z4[0]], [], [z4[1]], [], [z4[2]], [], [z4[3]], []]
    for k in range(NP):
        if k + 1 < NP:
            po_load(k + 1)
        p_out(k)
        tick(*(outs[k] if k < len(outs) else []))
    for k in (NP - 2, NP - 1):
        o_store(k).wait()
    for j in range(NC):
        p6a(j)
        if j % 4 == 3 and j // 4 < 2:
            tick(z5[j // 4])
    p6b()
    for j in range(NC):
        p6c(j)
        if j % 4 == 3 and j // 4 < 2:
            tick(z5[2 + j // 4])
    for j in (NC - 2, NC - 1):
        dx_copy(j).wait()
    first = remote(vec, vgot.at[0], v_s.at[0], v_r.at[0], sc.C)
    first.start()
    tick(z6[0])
    first.wait()
    vec[...] = vec[...] + vgot[0]
    second = remote(vec, vgot.at[1], v_s.at[1], v_r.at[1], sc.X)
    second.start()
    tick(z6[1])
    second.wait()
    vec[...] = vec[...] + vgot[1]
    cps = spread(Z, z, vec, vbox, vz_s, vz_r)
    tick(z6[2], z6[3])
    spread_wait(Z, z, vec, vbox, vz_s, vz_r, cps)
    total = vbox[0]
    for k in range(1, Z):
        total = total + vbox[k]
    vec_out[...] = total
    for k in range(NP):
        pn_copy(k).wait_send()
        po_copy(k).wait_send()
    for j in range(NC):
        n_copy(j).wait_send()
    for w in range(7):
        sc.drain(w, 7)


def acc_row(vec, k, C):
    return vec.at[k:k + 1, pl.ds(0, C)]


def back_all(Z, seqs, length, gd, gg, gu, pn, po, x, mid, cot, n1, m, w_out, w_in, w_f, w_g, pi, pf, pg, h,
             rh, start, ids, link, gain1, gain2, low, hgain, cid=1):
    n, width = x.shape
    C = pi.shape[1]
    dma = pltpu.SemaphoreType.DMA
    bf, f = jnp.bfloat16, jnp.float32
    sh = jax.ShapeDtypeStruct
    anyw, vmem = pl.BlockSpec(memory_space=pl.ANY), pl.BlockSpec(memory_space=pltpu.VMEM)
    shapes = [gd.shape, gg.shape, gu.shape] + [(width, C)] * 4
    R = [s[0] // (4 * Z) for s in shapes]
    N = [s[1] for s in shapes]
    Rm, Nm = max(R), max(N)
    NP, NC = n // TR, width // TC
    out_shape = ([sh((n, width), f), sh((n, width), f), sh((8, width), f)]
                 + [sh((r, k), f) for r, k in zip(R, N)]
                 + [sh((width, C), bf)] * 4
                 + [sh((n, width), bf)] * 2
                 + [sh((2 * Z * r, k), bf) for r, k in zip(R, N)]
                 + [sh((Z * r, k), bf) for r, k in zip(R, N)]
                 + [sh((Z * r, k), bf) for r, k in zip(R, N)]
                 + [sh((Z * r, k), bf) for r, k in zip(R, N)]
                 + [sh((r // 2, k), bf) for r, k in zip(R, N)])
    V = pltpu.VMEM
    scratch = [
        V((2, Z, Rm, Nm), bf), V((2, Z - 1, Rm, Nm), bf), V((2, 3, Rm, Nm), bf), V((5, Rm, Nm), bf), V((Rm, Nm), f),
        V((n, width), f), V((n, width), bf), V((n, C), f), V((n, C), f), V((n, C), f), V((n, C), f), V((n, C), f),
        V((n, C), f), V((n, C), f), V((n, C), bf), V((n, C), bf), V((n, C), bf), V((n, width), bf), V((n, C), bf),
        V((2, width, TC), bf), V((2, 3, TC, C), bf), V((2, TC, C), bf), V((NC, n, TC), bf), V((NC, n, TC), bf),
        V((2, 2, TR, width), f), V((2, 2, TR, width), bf), V((8, width), f), V((2, 8, width), f), V((Z, 8, width), f),
        V((n, 1), f), V((seqs, C), f), V((8, C), f), V((Z, 8, C), f), V((n // 128, 128), f), V((n // 128, 128), f),
        V((2, n, 128), f),
        dma((6,)), dma((1,)), dma((4, 3)), dma((2,)), dma((NP,)), dma((NP,)), dma((NP,)), dma((NP,)), dma((NC,)), dma((NC,)),
        dma((2, 4)), dma((2,)), dma((2,)), dma((2,)), dma((Z - 1,)), dma((Z,)), dma((Z - 1,)), dma((Z,)), dma((1,)), dma((1,)),
        dma((7, 2)), dma((7, 2)), dma((7, Z)), dma((7, Z)), dma((7, Z - 1)), dma((7, Z)), dma((7, Z)),
        dma((7,)), dma((7,)), dma((3, 5)), dma((7,)),
    ]
    res = pl.pallas_call(
        functools.partial(back_body, Z, seqs, length),
        out_shape=out_shape,
        in_specs=[anyw] * 18 + [vmem] * 8,
        out_specs=[anyw, anyw, vmem] + [anyw] * (len(out_shape) - 3),
        scratch_shapes=scratch,
        compiler_params=pltpu.CompilerParams(collective_id=cid, has_side_effects=True, vmem_limit_bytes=66_000_000),
        name="backward",
    )(gd, gg, gu, pn, po, x, mid, cot, n1, m, w_out, w_in, w_f, w_g, pi, pf, pg, h, rh, start, ids, link, gain1, gain2, low, hgain)
    return res[0], res[1], res[2], res[3:10]


def carried_in(x, axis, combine, identity, reverse):
    size, position = (lax.axis_size(axis), lax.axis_index(axis))
    everything = jax.tree.map(lambda part: lax.all_gather(part, axis), x)
    start = jax.tree.map(
        lambda part, zero: jnp.broadcast_to(jnp.asarray(zero, part.dtype), part.shape), x, identity
    )

    def turn(k, before):
        at = size - 1 - k if reverse else k
        reached = at > position if reverse else at < position
        new = combine(before, jax.tree.map(lambda part: part[at], everything))
        return jax.tree.map(lambda a, b: jnp.where(reached, a, b), new, before)

    return lax.fori_loop(0, size, turn, start)


def inverse_rms(inputs):
    return lax.rsqrt(jnp.mean(inputs * inputs, axis=-1, keepdims=True) + epsilon)


def rms_backward(inputs, row_scale, gain_vec, upstream):
    weighted = upstream * gain_vec
    inner_sum = jnp.mean(weighted * inputs, axis=-1, keepdims=True)
    return weighted * row_scale - inputs * (row_scale * row_scale * row_scale) * inner_sum


def silu_slope(inputs):
    sig_part = jax.nn.sigmoid(inputs)
    return sig_part * (1.0 + inputs * (1.0 - sig_part))


def times_back(left_mat, right_mat):
    return lax.dot_general(
        left_mat, right_mat, (((1,), (1,)), ((), ())), preferred_element_type=jnp.float32
    )


def outer_sum(left_mat, right_mat):
    return lax.dot_general(
        left_mat, right_mat, (((0,), (0,)), ((), ())), preferred_element_type=jnp.float32
    )


def linear_step(first_part, second_part):
    return (first_part[0] * second_part[0], second_part[0] * first_part[1] + second_part[1])


def joined_ids(last_ids, first_ids):
    return jnp.where((last_ids == first_ids) | (last_ids < 0.0) | (first_ids < 0.0), 1.0, 0.0)


def forward_join(first_part, second_part):
    linked = joined_ids(first_part[3], second_part[2])[:, None]
    return (
        first_part[0] * second_part[0] * linked,
        second_part[0] * linked * first_part[1] + second_part[1],
        jnp.where(first_part[2] < 0.0, second_part[2], first_part[2]),
        jnp.where(second_part[3] < 0.0, first_part[3], second_part[3]),
    )


def backward_join(first_part, second_part):
    linked = joined_ids(second_part[3], first_part[2])[:, None]
    return (
        second_part[0] * linked * first_part[0],
        second_part[0] * linked * first_part[1] + second_part[1],
        jnp.where(second_part[2] < 0.0, first_part[2], second_part[2]),
        jnp.where(first_part[3] < 0.0, second_part[3], first_part[3]),
    )


def mixer_forward_plain(seqs, length, width, pi, pf, pg, lower, gain, segs):
    channels = pi.shape[1]
    forget = lower + (1.0 - lower) * jax.nn.sigmoid(pf)
    candidate = jax.nn.silu(pi) * (1.0 - forget)
    inner_link = jnp.concatenate(
        [jnp.ones((seqs, 1), jnp.float32), jnp.where(segs[:, 1:] == segs[:, :-1], 1.0, 0.0)], axis=1
    )
    decay = forget.reshape(seqs, length, channels) * inner_link[:, :, None]
    prod, local = lax.associative_scan(
        linear_step, (decay, candidate.reshape(seqs, length, channels)), axis=1
    )
    first, last = segs[:, 0], segs[:, -1]
    ones, zero = jnp.ones((seqs, channels), jnp.float32), jnp.zeros((seqs, channels), jnp.float32)
    minus = -jnp.ones((seqs,), jnp.float32)
    prefix = carried_in(
        (prod[:, -1], local[:, -1], first, last), "ctx", forward_join, (ones, zero, minus, minus), False
    )
    start = joined_ids(prefix[3], first)[:, None] * prefix[1]
    h = (local + prod * start[:, None, :]).reshape(seqs * length, channels)
    squares = lax.psum(jnp.sum(h * h, axis=1), "tp")
    rh = lax.rsqrt(squares / width + epsilon)[:, None]
    m = (h * rh * gain * jax.nn.silu(pg)).astype(jnp.bfloat16)
    return h, m, rh, start


def mixer_backward_plain(seqs, length, width, dm, h, pi, pf, pg, lower, gain, segs, rh, start):
    channels = pi.shape[1]
    s = jax.nn.sigmoid(pf)
    forget = lower + (1.0 - lower) * s
    inner_link = jnp.concatenate(
        [jnp.ones((seqs, 1), jnp.float32), jnp.where(segs[:, 1:] == segs[:, :-1], 1.0, 0.0)], axis=1
    )
    forget_seq = forget.reshape(seqs, length, channels)
    decay = forget_seq * inner_link[:, :, None]
    silu_gate = jax.nn.silu(pg)
    weighted = dm * gain * silu_gate
    inner = lax.psum(jnp.sum(weighted * h, axis=1), "tp")
    dh = weighted * rh - h * (rh * rh * rh) * (inner / width)[:, None]
    gain_grad = jnp.sum(dm * h * rh * silu_gate, axis=0)
    dpg = (dm * h * rh * gain * silu_slope(pg)).astype(jnp.bfloat16)
    ones_row = jnp.ones((seqs, 1, channels), jnp.float32)
    following = jnp.concatenate([decay[:, 1:], ones_row], axis=1)
    tail, local = lax.associative_scan(
        linear_step, (following, dh.reshape(seqs, length, channels)), reverse=True, axis=1
    )
    first, last = segs[:, 0], segs[:, -1]
    ones, zero = jnp.ones((seqs, channels), jnp.float32), jnp.zeros((seqs, channels), jnp.float32)
    minus = -jnp.ones((seqs,), jnp.float32)
    suffix = carried_in(
        (decay[:, 0] * tail[:, 0], forget_seq[:, 0] * local[:, 0], first, last),
        "ctx", backward_join, (ones, zero, minus, minus), True,
    )
    end = joined_ids(last, suffix[2])[:, None] * suffix[1]
    g = (local + tail * end[:, None, :]).reshape(seqs * length, channels)
    states = h.reshape(seqs, length, channels)
    previous = jnp.concatenate(
        [start[:, None, :], inner_link[:, 1:, None] * states[:, :-1]], axis=1
    ).reshape(seqs * length, channels)
    dforget = g * (previous - jax.nn.silu(pi))
    dpi = (g * (1.0 - forget) * silu_slope(pi)).astype(jnp.bfloat16)
    dpf = (dforget * (1.0 - lower) * s * (1.0 - s)).astype(jnp.bfloat16)
    return dpi, dpf, dpg, gain_grad, jnp.sum(dforget * (1.0 - s), axis=0)


def on_device(
    block_input,
    segment_ids,
    norm_gain,
    lower,
    w_input,
    w_forget,
    w_gate,
    hidden_gain,
    w_out,
    mlp_gain,
    w_mlp_gate,
    w_mlp_up,
    w_down,
    cotangent,
):
    bfloat, f32 = jnp.bfloat16, jnp.float32
    seqs, length, width = block_input.shape
    rows_all = seqs * length
    small = lax.axis_size("shard") == 4
    Z = lax.axis_size("ctx")
    shards = [
        w.astype(bfloat) for w in (w_input, w_forget, w_gate, w_out, w_mlp_gate, w_mlp_up, w_down)
    ]
    if small:
        wide = gather_all(shards, 4, Z)
    else:
        wide = [lax.all_gather(w, ("shard", "ctx"), axis=0, tiled=True) for w in shards]
    wide_input, wide_forget, wide_gate, wide_out, wide_mgate, wide_mup, wide_down = wide
    segs = segment_ids.astype(f32)
    link = jnp.concatenate(
        [jnp.ones((seqs, 1), f32), jnp.where(segs[:, 1:] == segs[:, :-1], 1.0, 0.0)], axis=1
    ).reshape(rows_all, 1)
    residual_in = block_input.reshape(rows_all, width)
    scale_one = inverse_rms(residual_in)
    normed_one = (residual_in * scale_one * norm_gain).astype(bfloat)
    pi = jnp.dot(normed_one, wide_input, preferred_element_type=f32)
    pf = jnp.dot(normed_one, wide_forget, preferred_element_type=f32)
    pg = jnp.dot(normed_one, wide_gate, preferred_element_type=f32)
    channels = pi.shape[1]
    ids = jnp.broadcast_to(
        jnp.concatenate([segs[:, 0], segs[:, -1]])[:, None], (2 * seqs, channels)
    )
    low_row, gain_row = lower[None, :], hidden_gain[None, :]
    if small:
        h, mixed_in, rh, start = mixer_forward(
            Z, seqs, length, width, pi, pf, pg, low_row, gain_row, link, ids
        )
    else:
        h, mixed_in, rh, start = mixer_forward_plain(
            seqs, length, width, pi, pf, pg, lower, hidden_gain, segs
        )
    mixer_out = lax.psum(times_back(mixed_in, wide_out).astype(bfloat), "tp").astype(f32)
    middle = residual_in + mixer_out
    scale_two = inverse_rms(middle)
    normed_two = (middle * scale_two * mlp_gain).astype(bfloat)
    gate_pre = jnp.dot(normed_two, wide_mgate, preferred_element_type=f32)
    up_pre = jnp.dot(normed_two, wide_mup, preferred_element_type=f32)
    silu_mlp = jax.nn.silu(gate_pre)
    activated = (silu_mlp * up_pre).astype(bfloat)
    upstream = cotangent.reshape(rows_all, width)
    upstream_low = upstream.astype(bfloat)
    grad_activ = jnp.dot(upstream_low, wide_down, preferred_element_type=f32)
    grad_down = outer_sum(upstream_low, activated).astype(bfloat)
    grad_gate_pre = (grad_activ * up_pre * silu_slope(gate_pre)).astype(bfloat)
    grad_up_pre = (grad_activ * silu_mlp).astype(bfloat)
    grad_mgate = outer_sum(normed_two, grad_gate_pre).astype(bfloat)
    grad_mup = outer_sum(normed_two, grad_up_pre).astype(bfloat)
    down_part = times_back(activated, wide_down).astype(bfloat)
    normed_part = (times_back(grad_gate_pre, wide_mgate) + times_back(grad_up_pre, wide_mup)).astype(bfloat)
    if small:
        output, grad_resid, vectors, sums = back_all(
            Z, seqs, length, grad_down, grad_mgate, grad_mup, normed_part, down_part, residual_in, middle, upstream,
            normed_one, mixed_in, wide_out, wide_input, wide_forget, wide_gate, pi, pf, pg, h,
            rh, start, ids, link, norm_gain[None, :], mlp_gain[None, :], low_row, gain_row
        )
        grad_norm_gain, grad_mlp_gain = vectors[0], vectors[1]
        grad_hidden_gain, grad_lower = vectors[2, :channels], vectors[3, :channels]
    else:
        output = middle + lax.psum(down_part, "tp").astype(f32)
        grad_normed_two = lax.psum(normed_part, "tp").astype(f32)
        grad_mlp_gain = jnp.sum(grad_normed_two * middle * scale_two, axis=0)
        grad_middle = upstream + rms_backward(middle, scale_two, mlp_gain, grad_normed_two)
        middle_low = grad_middle.astype(bfloat)
        dm = jnp.dot(middle_low, wide_out, preferred_element_type=f32)
        grad_out = outer_sum(middle_low, mixed_in).astype(bfloat)
        dpi, dpf, dpg, grad_hidden_gain, grad_lower = mixer_backward_plain(
            seqs, length, width, dm, h, pi, pf, pg, lower, hidden_gain, segs, rh, start
        )
        grad_w_input = outer_sum(normed_one, dpi).astype(bfloat)
        grad_w_forget = outer_sum(normed_one, dpf).astype(bfloat)
        grad_w_gate = outer_sum(normed_one, dpg).astype(bfloat)
        grad_normed_one = lax.psum(
            (
                times_back(dpi, wide_input) + times_back(dpf, wide_forget) + times_back(dpg, wide_gate)
            ).astype(bfloat),
            "tp",
        ).astype(f32)
        grad_norm_gain = jnp.sum(grad_normed_one * residual_in * scale_one, axis=0)
        grad_resid = grad_middle + rms_backward(residual_in, scale_one, norm_gain, grad_normed_one)
        vectors = lax.psum(
            jnp.concatenate([grad_norm_gain, grad_mlp_gain, grad_lower, grad_hidden_gain]), ("shard", "ctx")
        )
        grad_norm_gain, grad_mlp_gain = vectors[:width], vectors[width : 2 * width]
        grad_lower = vectors[2 * width : 2 * width + channels]
        grad_hidden_gain = vectors[2 * width + channels :]
        sums = [
            lax.psum_scatter(p, ("shard", "ctx"), scatter_dimension=0, tiled=True).astype(f32)
            for p in (grad_down, grad_mgate, grad_mup, grad_out, grad_w_input, grad_w_forget, grad_w_gate)
        ]
    return (
        output.reshape(block_input.shape),
        grad_resid.reshape(block_input.shape),
        grad_norm_gain,
        grad_lower,
        sums[4],
        sums[5],
        sums[6],
        grad_hidden_gain,
        sums[3],
        grad_mlp_gain,
        sums[1],
        sums[2],
        sums[0],
    )


def solution(mesh):
    return jax.shard_map(
        on_device,
        mesh=mesh,
        in_specs=(
            P("shard", "ctx", None),
            P("shard", "ctx"),
            P(),
            P("tp"),
            P(("shard", "ctx"), "tp"),
            P(("shard", "ctx"), "tp"),
            P(("shard", "ctx"), "tp"),
            P("tp"),
            P(("shard", "ctx"), "tp"),
            P(),
            P(("shard", "ctx"), "tp"),
            P(("shard", "ctx"), "tp"),
            P(("shard", "ctx"), "tp"),
            P("shard", "ctx", None),
        ),
        out_specs=(
            P("shard", "ctx", None),
            P("shard", "ctx", None),
            P(),
            P("tp"),
            P(("shard", "ctx"), "tp"),
            P(("shard", "ctx"), "tp"),
            P(("shard", "ctx"), "tp"),
            P("tp"),
            P(("shard", "ctx"), "tp"),
            P(),
            P(("shard", "ctx"), "tp"),
            P(("shard", "ctx"), "tp"),
            P(("shard", "ctx"), "tp"),
        ),
        check_vma=False,
    )
```

```python
import functools
import jax
import jax.numpy as jnp
from jax import lax
from jax.experimental import pallas as pl
from jax.experimental.pallas import tpu as pltpu
from jax.sharding import PartitionSpec as P

epsilon = 1e-06
MESH = pl.DeviceIdType.MESH


def remote(src, dst, send_sem, recv_sem, device):
    return pltpu.make_async_remote_copy(
        src_ref=src, dst_ref=dst, send_sem=send_sem, recv_sem=recv_sem,
        device_id=device, device_id_type=MESH)


def pick(z, values):
    out = jnp.int32(values[-1])
    for k in range(len(values) - 2, -1, -1):
        out = jnp.where(z == k, values[k], out)
    return out


def far_first(Z):
    table = []
    for z in range(Z):
        ups, dns, mine, turn = list(range(Z - 1, z, -1)), list(range(0, z)), [], z < Z // 2
        while ups or dns:
            if (turn and ups) or not dns:
                mine.append(ups.pop(0))
            else:
                mine.append(dns.pop(0))
            turn = not turn
        table.append(mine + [z])
    return table


class Scatter:
    def __init__(self, Z, parts, rc, xr, zu, zd, hr, outs, xs, zs, stage, fin, sems):
        self.Z, self.parts, self.rc, self.xr, self.zu, self.zd, self.hr, self.outs = Z, parts, rc, xr, zu, zd, hr, outs
        self.xs, self.zs, self.stage, self.fin = xs, zs, stage, fin
        (self.c_s, self.c_r, self.x_s, self.x_r, self.z_s, self.u_r, self.d_r, self.h_s, self.h_r, self.l_s, self.f_s) = sems
        s, z = lax.axis_index("shard"), lax.axis_index("ctx")
        q, c = s // 2, lax.rem(s, 2)
        self.z, self.q, self.c = z, q, c
        self.even = lax.rem(z, 2) == 0
        self.zp = jnp.where(self.even, z + 1, z - 1)
        self.X = {"shard": (1 - q) * 2 + c}
        self.C = {"shard": q * 2 + (1 - c)}
        self.UP, self.DN, self.ZP = {"ctx": z + 1}, {"ctx": z - 1}, {"ctx": self.zp}
        self.R = [p.shape[0] // (4 * Z) for p in parts]
        self.N = [p.shape[1] for p in parts]
        self.ffirst = far_first(Z)

    def part(self, w, q, c, z, n=1):
        R = self.R[w]
        return self.parts[w].at[pl.ds(pl.multiple_of(((2 * q + c) * self.Z + z) * R, R), n * R), :]

    def rows(self, ref, i, w):
        R = self.R[w]
        return ref.at[pl.ds(pl.multiple_of(i * R, R), R), :]

    def hrows(self, ref, i, w, h):
        H = self.R[w] // 2
        return ref.at[pl.ds(pl.multiple_of(i * 2 * H + h * H, H), H), :]

    def c_copy(self, w, k):
        Z, R = self.Z, self.R[w]
        q = self.q if k == 1 else 1 - self.q
        return remote(self.part(w, q, 1 - self.c, 0, Z), self.rc[w].at[pl.ds(k * Z * R, Z * R), :],
                      self.c_s.at[w, k], self.c_r.at[w, k], self.C)

    def c_send(self, w):
        for k in (0, 1):
            self.c_copy(w, k).start()

    def stage_of(self, slot):
        return self.stage[0].at[slot] if slot < 2 else self.stage[1]

    def load_waits(self, w, srcs, slot):
        cps = []
        for i, src in enumerate(srcs):
            if src is not None:
                n = src.shape[0]
                cps.append(pltpu.make_async_copy(
                    src, self.stage_of(slot).at[i, pl.ds(0, n), pl.ds(0, self.N[w])], self.l_s.at[slot, i]))
        return cps

    def load(self, w, srcs, slot):
        cps = self.load_waits(w, srcs, slot)
        for cp in cps:
            cp.start()
        return cps

    def add(self, w, slot, idx, store, lo=0, hi=None, off=None):
        N = self.N[w]
        hi = self.R[w] if hi is None else hi
        G = 16

        def go(i, _):
            r = pl.multiple_of(lo + i * G, G)
            tot = None
            for k in idx:
                rk = r
                if off is not None and k in off:
                    rk = pl.multiple_of(r + off[k], G)
                v = self.stage_of(slot)[k, pl.ds(rk, G), pl.ds(0, N)].astype(jnp.float32)
                tot = v if tot is None else tot + v
            store(r, tot)
            return 0

        lax.fori_loop(0, (hi - lo) // G, go, 0)

    def x_slot(self, w, n):
        return self.xs.at[w % 2, n, :, pl.ds(0, self.N[w])]

    def order(self, n):
        return pick(self.z, [t[n] for t in self.ffirst])

    def x_copy(self, w, n, half=None):
        zt = self.order(n)
        src = self.x_slot(w, n)
        H = self.R[w] // 2
        if half is None:
            return remote(src, self.rows(self.xr[w], zt, w), self.x_s.at[w, n], self.x_r.at[w, n], self.X)
        return remote(src.at[pl.ds(half * H, H), :], self.hrows(self.xr[w], zt, w, half), self.x_s.at[w, n], self.x_r.at[w, n], self.X)

    def h_copy(self, w, n=0):
        H = self.R[w] // 2
        return remote(self.x_slot(w, n).at[pl.ds(0, H), :], self.hr[w], self.h_s.at[w], self.h_r.at[w], self.ZP)

    def on_pair(self, n, yes, no):
        if n == self.Z - 1:
            no()
            return
        paired = self.order(n) == self.zp

        @pl.when(paired)
        def _():
            yes()

        @pl.when(jnp.logical_not(paired))
        def _():
            no()

    def x_load(self, w, n):
        zt = self.order(n)
        return self.load(w, [self.part(w, 1 - self.q, self.c, zt), self.rows(self.rc[w], zt, w)], n % 2)

    def x_phase(self, w, n):
        Z, H = self.Z, self.R[w] // 2
        last = n == Z - 1
        if n == 0:
            self.c_copy(w, 0).wait_recv()
            self.x_load(w, 0)
        if not last:
            self.x_load(w, n + 1)
        if last:
            self.h_copy(w).wait_recv()
            for cp in self.load(w, [None, None, self.hr[w]], n % 2):
                cp.wait()
        if w >= 2:
            self.x_wait_send(w - 2, n)
        zt = self.order(n)
        for cp in self.load_waits(w, [self.part(w, 1 - self.q, self.c, zt), self.rows(self.rc[w], zt, w)], n % 2):
            cp.wait()
        dst = self.x_slot(w, n)

        def store(r, v):
            dst[pl.ds(r, 16), :] = v.astype(jnp.bfloat16)

        if last:
            self.add(w, n % 2, (0, 1, 2), store, 0, H)
            self.add(w, n % 2, (0, 1), store, H, 2 * H)
            self.x_copy(w, n).start()
        else:
            self.add(w, n % 2, (0, 1), store)

            def yes():
                self.h_copy(w, n).start()
                self.x_copy(w, n, 1).start()

            self.on_pair(n, yes, lambda: self.x_copy(w, n).start())

    def x_wait_send(self, w, n):
        def yes():
            self.h_copy(w, n).wait_send()
            self.x_copy(w, n, 1).wait_send()

        self.on_pair(n, yes, lambda: self.x_copy(w, n).wait_send())

    def z_copy(self, w, n, dest, up):
        src = self.zs.at[w % 2, n, :, pl.ds(0, self.N[w])]
        if up:
            return remote(src, self.rows(self.zu[w], dest, w), self.z_s.at[w, n], self.u_r.at[w, dest], self.UP)
        return remote(src, self.rows(self.zd[w], dest, w), self.z_s.at[w, n], self.d_r.at[w, dest], self.DN)

    def x_wait(self, w, n):
        self.on_pair(n, lambda: self.x_copy(w, n, 1).wait_recv(), lambda: self.x_copy(w, n).wait_recv())

    def z_phase(self, w, n):
        Z, H = self.Z, self.R[w] // 2
        z = self.z
        last = n == Z - 1
        dest = z if last else pick(z, [t[n] for t in self.ffirst])
        if n == 0:
            self.c_copy(w, 1).wait_recv()
        self.x_wait(w, n)
        cps = self.load(w, [self.part(w, self.q, self.c, dest), self.rows(self.rc[w], dest + Z, w),
                            self.rows(self.xr[w], dest, w)], 2)
        if not last:
            up = dest > z
            down = dest < z
            has_in = (up & (z > 0)) | (down & (z < Z - 1))

            @pl.when(up & (z > 0))
            def _():
                self.z_copy(w, n, dest, True).wait_recv()
                cp = self.load(w, [None] * 3 + [self.rows(self.zu[w], dest, w)], 2)
                cp[0].wait()

            @pl.when(down & (z < Z - 1))
            def _():
                self.z_copy(w, n, dest, False).wait_recv()
                cp = self.load(w, [None] * 3 + [self.rows(self.zd[w], dest, w)], 2)
                cp[0].wait()

            if w >= 2:
                self.z_wait_send(w - 2, n)
            for cp in cps:
                cp.wait()
            dst = self.zs.at[w % 2, n, :, pl.ds(0, self.N[w])]

            def store(r, v):
                dst[pl.ds(r, 16), :] = v.astype(jnp.bfloat16)

            paired = dest == self.zp
            self.sum_parts(w, paired, has_in, (3,), store)

            @pl.when(up)
            def _():
                self.z_copy(w, n, dest, True).start()

            @pl.when(down)
            def _():
                self.z_copy(w, n, dest, False).start()
        else:
            @pl.when(z > 0)
            def _():
                self.z_copy(w, 0, dest, True).wait_recv()
                cp = self.load(w, [None] * 3 + [self.rows(self.zu[w], dest, w)], 2)
                cp[0].wait()

            @pl.when(z < Z - 1)
            def _():
                self.z_copy(w, 0, dest, False).wait_recv()
                cp = self.load(w, [None] * 4 + [self.rows(self.zd[w], dest, w)], 2)
                cp[0].wait()

            for cp in cps:
                cp.wait()
            if w >= 1:
                self.f_copy(w - 1).wait()
            dst = self.fin.at[:, pl.ds(0, self.N[w])]

            def store(r, v):
                dst[pl.ds(r, 16), :] = v

            @pl.when((z > 0) & (z < Z - 1))
            def _():
                self.add(w, 2, (0, 1, 2, 3, 4), store)

            @pl.when(z == 0)
            def _():
                self.add(w, 2, (0, 1, 2, 4), store)

            @pl.when(z == Z - 1)
            def _():
                self.add(w, 2, (0, 1, 2, 3), store)

            self.f_copy(w).start()

    def sum_parts(self, w, paired, has_in, extra, store):
        H = self.R[w] // 2
        for p in (False, True):
            for e in (False, True):
                cond = (paired if p else jnp.logical_not(paired)) & (has_in if e else jnp.logical_not(has_in))

                @pl.when(cond)
                def _(p=p, e=e):
                    ex = extra if e else ()
                    if p:
                        self.add(w, 2, (0, 1) + ex, store, 0, H)
                        self.add(w, 2, (0, 1, 2) + ex, store, H, 2 * H)
                    else:
                        self.add(w, 2, (0, 1, 2) + ex, store)

    def z_wait_send(self, w, n):
        z = self.z
        dest = pick(z, [t[n] for t in self.ffirst])
        self.z_copy_any(w, n).wait_send()

    def z_copy_any(self, w, n):
        src = self.zs.at[w % 2, n, :, pl.ds(0, self.N[w])]
        return remote(src, self.rows(self.zu[w], 0, w), self.z_s.at[w, n], self.u_r.at[w, 0],
                      {"ctx": jnp.where(pick(self.z, [t[n] for t in self.ffirst]) > self.z, self.z + 1, self.z - 1)})

    def f_copy(self, w):
        return pltpu.make_async_copy(self.fin.at[:, pl.ds(0, self.N[w])], self.outs[w], self.f_s.at[w])

    def drain(self, w, nw):
        for k in (0, 1):
            self.c_copy(w, k).wait_send()
        if w >= nw - 2:
            for n in range(self.Z):
                self.x_wait_send(w, n)
            for n in range(self.Z - 1):
                self.z_wait_send(w, n)
        if w == nw - 1:
            self.f_copy(w).wait()


T8 = 8


def spread(Z, z, pay, box, s_sem, r_sem):
    cps = []
    for o in range(1, Z):
        to = lax.rem(z + o, Z)
        cp = remote(pay, box.at[z], s_sem.at[o - 1], r_sem.at[z], {"ctx": to})
        cp.start()
        cps.append(cp)
    box[z] = pay[...]
    return cps


def spread_wait(Z, z, pay, box, s_sem, r_sem, cps):
    for o in range(1, Z):
        frm = lax.rem(z + o, Z)
        remote(pay, box.at[frm], s_sem.at[o - 1], r_sem.at[frm], {"ctx": frm}).wait_recv()
    for cp in cps:
        cp.wait_send()


def joined(box, k):
    last, first = box[k, 6:8, :], box[k + 1, 4:6, :]
    return jnp.where(last == first, 1.0, 0.0)


def prefix_state(Z, z, box):
    state = jnp.zeros(box.shape[2:][:0] + (2, box.shape[2]), jnp.float32)
    mine = state
    for k in range(Z - 1):
        state = joined(box, k) * (box[k, 2:4, :] + box[k, 0:2, :] * state)
        mine = jnp.where(z == k + 1, state, mine)
    return mine


def suffix_state(Z, z, box):
    state = jnp.zeros((2, box.shape[2]), jnp.float32)
    mine = state
    for k in range(Z - 2, -1, -1):
        state = joined(box, k) * (box[k + 1, 2:4, :] + box[k + 1, 0:2, :] * state)
        mine = jnp.where(z == k, state, mine)
    return mine


def diagonal():
    return lax.broadcasted_iota(jnp.int32, (128, 128), 0) == lax.broadcasted_iota(jnp.int32, (128, 128), 1)


def column_to_rows(col_ref, row_ref, n):
    eye = diagonal()
    for k in range(n // 128):
        col = col_ref[pl.ds(k * 128, 128), :]
        row_ref[k:k + 1, :] = jnp.sum(jnp.where(eye, jnp.broadcast_to(col, (128, 128)), 0.0), axis=0, keepdims=True)


def rows_to_column(row, k):
    return jnp.sum(jnp.where(diagonal(), jnp.broadcast_to(row, (128, 128)), 0.0), axis=1, keepdims=True)


def sigmoid(v):
    return jax.nn.sigmoid(v)


def row_at(ref, t):
    return pl.ds(pl.multiple_of(t, T8), T8)


def forward_scan_one(sq, length, pi, pf, lower, link, h, cum):
    C = pi.shape[1]
    low = lower[...]
    iota = lax.broadcasted_iota(jnp.int32, (T8, C), 0)

    def tile(i, carry):
        hl, pr = carry
        r = row_at(pi, sq * length + i * T8)
        s = sigmoid(pf[r, :])
        forget = low + (1.0 - low) * s
        x = pi[r, :]
        b = x * sigmoid(x) * (1.0 - forget)
        a = forget * link[r, :]
        for sh in (1, 2, 4):
            keep = iota >= sh
            b = b + jnp.where(keep, a * pltpu.roll(b, sh, 0), 0.0)
            a = jnp.where(keep, a * pltpu.roll(a, sh, 0), a)
        b = b + a * hl
        a = a * pr
        h[r, :] = b
        cum[r, :] = a
        return b[T8 - 1:T8, :], a[T8 - 1:T8, :]

    return lax.fori_loop(0, length // T8, tile, (jnp.zeros((1, C), jnp.float32), jnp.ones((1, C), jnp.float32)), unroll=2)


def forward_finish(seqs, length, h, cum, start, col):
    def tile(i, _, sq):
        r = row_at(h, sq * length + i * T8)
        v = h[r, :] + cum[r, :] * start[sq:sq + 1, :]
        h[r, :] = v
        col[r, :] = jnp.sum(v * v, axis=1, keepdims=True)
        return 0

    for sq in range(seqs):
        lax.fori_loop(0, length // T8, functools.partial(tile, sq=sq), 0, unroll=2)


def swap_columns(col, row, got, s_sem, r_sem, other, n):
    column_to_rows(col, row, n)
    cp = remote(row, got, s_sem, r_sem, {"tp": other})
    cp.start()
    cp.wait()


def scale_columns(row, got, col, n, width, fn):
    for k in range(n // 128):
        col[pl.ds(k * 128, 128), :] = fn(rows_to_column(row[k:k + 1, :] + got[k:k + 1, :], k))


def mixed(h, rh, gain, pg, m, step=16):
    g = gain[...]

    def tile(i, _):
        r = pl.ds(pl.multiple_of(i * step, step), step)
        p = pg[r, :]
        m[r, :] = (h[r, :] * rh[r, :] * g * (p * sigmoid(p))).astype(m.dtype)
        return 0

    lax.fori_loop(0, h.shape[0] // step, tile, 0)


def backward_first(n, dm, h, pg, gain, rh, dpg, col, gsum, step=16):
    g = gain[...]

    def tile(i, acc):
        r = pl.ds(pl.multiple_of(i * step, step), step)
        d, hv, p, rv = dm[r, :], h[r, :], pg[r, :], rh[r, :]
        s = sigmoid(p)
        sl = p * s
        q = d * g * sl
        col[r, :] = jnp.sum(q * hv, axis=1, keepdims=True)
        hr = d * hv * rv
        dpg[r, :] = (hr * g * (s * (1.0 + p * (1.0 - s)))).astype(dpg.dtype)
        return acc + jnp.sum(hr * sl, axis=0, keepdims=True)

    gsum[...] = lax.fori_loop(0, n // step, tile, jnp.zeros(gsum.shape, jnp.float32))


def backward_scan_one(sq, length, dm, h, pf, pg, lower, gain, link, rh, inner, gl, tail):
    C = dm.shape[1]
    low, g = lower[...], gain[...]
    iota = lax.broadcasted_iota(jnp.int32, (T8, C), 0)
    nt = length // T8
    def tile(k, carry):
        vl, pr = carry
        r = row_at(dm, sq * length + (nt - 1 - k) * T8)
        rv = rh[r, :]
        p = pg[r, :]
        q = dm[r, :] * g * (p * sigmoid(p))
        dh = q * rv - h[r, :] * (rv * rv * rv) * inner[r, :]
        a = (low + (1.0 - low) * sigmoid(pf[r, :])) * link[r, :]
        b = a * dh
        for sh in (1, 2, 4):
            keep = iota < T8 - sh
            b = b + jnp.where(keep, a * pltpu.roll(b, T8 - sh, 0), 0.0)
            a = jnp.where(keep, a * pltpu.roll(a, T8 - sh, 0), a)
        v = b + a * vl
        pa = a * pr
        last = iota == T8 - 1
        gl[r, :] = dh + jnp.where(last, vl, pltpu.roll(v, T8 - 1, 0))
        tail[r, :] = jnp.where(last, pr, pltpu.roll(pa, T8 - 1, 0))
        return v[0:1, :], pa[0:1, :]

    return lax.fori_loop(0, nt, tile, (jnp.zeros((1, C), jnp.float32), jnp.ones((1, C), jnp.float32)), unroll=2)


def backward_last(seqs, length, gl, tail, end, h, start, pi, pf, lower, link, dpi, dpf, lsum):
    C = gl.shape[1]
    low = lower[...]
    iota = lax.broadcasted_iota(jnp.int32, (T8, C), 0)
    total = jnp.zeros((1, C), jnp.float32)
    for sq in range(seqs):
        def tile(i, carry):
            acc, hp = carry
            halves = []
            for half in (0, 1):
                r = row_at(gl, sq * length + i * 16 + half * T8)
                gv = gl[r, :] + tail[r, :] * end[sq:sq + 1, :]
                hv = h[r, :]
                prev = jnp.where(iota == 0, hp, pltpu.roll(hv, 1, 0) * link[r, :])
                if half == 1:
                    prev = jnp.where(iota == 0, prev * link[r, :], prev)
                else:
                    prev = jnp.where((iota == 0) & (i > 0), prev * link[r, :], prev)
                s = sigmoid(pf[r, :])
                forget = low + (1.0 - low) * s
                x = pi[r, :]
                sx = sigmoid(x)
                df = gv * (prev - x * sx)
                halves.append((gv * (1.0 - forget) * (sx * (1.0 + x * (1.0 - sx))), df * (1.0 - low) * s * (1.0 - s)))
                acc = acc + jnp.sum(df * (1.0 - s), axis=0, keepdims=True)
                hp = hv[T8 - 1:T8, :]
            r = pl.ds(pl.multiple_of(sq * length + i * 16, 16), 16)
            dpi[r, :] = jnp.concatenate([halves[0][0], halves[1][0]], axis=0).astype(dpi.dtype)
            dpf[r, :] = jnp.concatenate([halves[0][1], halves[1][1]], axis=0).astype(dpf.dtype)
            return acc, hp

        total, _ = lax.fori_loop(0, length // 16, tile, (total, start[sq:sq + 1, :]))
    lsum[...] = total


def gather_steps(nw, Z, ahead, relay, own, out, sems):
    (s_up, r_up, s_dn, r_dn, s_x, r_x, s_c, r_c, s_h, r_h, l_sem) = sems
    s, z = lax.axis_index("shard"), lax.axis_index("ctx")
    q, c = s // 2, lax.rem(s, 2)
    sx, sc = (1 - q) * 2 + c, q * 2 + (1 - c)
    sxc = (1 - q) * 2 + (1 - c)
    even = lax.rem(z, 2) == 0
    zp = jnp.where(even, z + 1, z - 1)
    rows = [r.shape[0] for r in own]

    def block(w, s_, z_, part=0):
        R = rows[w]
        start = pl.multiple_of((s_ * Z + z_) * R, R)
        if part == 0:
            return out[w].at[pl.ds(start, R), :]
        H = R // 2
        return out[w].at[pl.ds(pl.multiple_of(start + (part - 1) * H, H), H), :]

    UP, DN, XX, CC, ZP = {"ctx": z + 1}, {"ctx": z - 1}, {"shard": sx}, {"shard": sc}, {"ctx": zp}

    def up(w, k, src=None):
        b = block(w, s, z - k)
        return remote(b if src is None else src, b, s_up.at[w, k], r_up.at[w, k], UP)

    def dn(w, k, src=None):
        b = block(w, s, z + k)
        return remote(b if src is None else src, b, s_dn.at[w, k], r_dn.at[w, k], DN)

    def origin(j):
        return z if j == 0 else (z - j if j < Z else z + j - Z + 1)

    def valid(j):
        return (z >= j) if j < Z else (z + j - Z + 1 <= Z - 1)

    def xx(w, j, part, src=None):
        b = block(w, s, origin(j), part)
        return remote(b if src is None else src, b, s_x.at[w, j], r_x.at[w, j], XX)

    def xx_in(w, j, part):
        b = block(w, sx, origin(j), part)
        return remote(b, b, s_x.at[w, j], r_x.at[w, j], XX)

    def cc(w, j, src=None):
        b = block(w, s if j < 2 * Z - 1 else sx, origin(j % (2 * Z - 1)))
        return remote(b if src is None else src, b, s_c.at[w, j], r_c.at[w, j], CC)

    def cc_in(w, j):
        b = block(w, sc if j < 2 * Z - 1 else sxc, origin(j % (2 * Z - 1)))
        return remote(b, b, s_c.at[w, j], r_c.at[w, j], CC)

    def half(w):
        b = block(w, sx, z, 1)
        return remote(b, b, s_h.at[w], r_h.at[w], ZP)

    def half_in(w):
        b = block(w, sx, zp, 1)
        return remote(b, b, s_h.at[w], r_h.at[w], ZP)

    local = []
    for w in range(nw):
        local.append(pltpu.make_async_copy(own[w], block(w, s, z), l_sem.at[w]))

    def begin(w):
        local[w].start()

        @pl.when(z < Z - 1)
        def _():
            up(w, 0, own[w]).start()

        @pl.when(z > 0)
        def _():
            dn(w, 0, own[w]).start()

        xx(w, 0, 0, own[w]).start()
        cc(w, 0, own[w]).start()

    def is_pair(j):
        if j == 1:
            return jnp.logical_not(even)
        if j == Z:
            return even
        return None

    def for_part(w, j, fn):
        pair = is_pair(j) if relay else None
        if pair is None:
            fn(0)
        else:
            @pl.when(pair)
            def _():
                fn(2)

            @pl.when(jnp.logical_not(pair))
            def _():
                fn(0)

    def step(w, k):
        @pl.when(z >= k)
        def _():
            remote(block(w, s, z - k), block(w, s, z - k), s_up.at[w, k - 1], r_up.at[w, k - 1], UP).wait_recv()
            if k < Z - 1:
                @pl.when(z < Z - 1)
                def _():
                    up(w, k).start()
            for_part(w, k, lambda p: xx(w, k, p).start())
            cc(w, k).start()

        @pl.when(z + k <= Z - 1)
        def _():
            remote(block(w, s, z + k), block(w, s, z + k), s_dn.at[w, k - 1], r_dn.at[w, k - 1], DN).wait_recv()
            if k < Z - 1:
                @pl.when(z > 0)
                def _():
                    dn(w, k).start()
            for_part(w, Z - 1 + k, lambda p: xx(w, Z - 1 + k, p).start())
            cc(w, Z - 1 + k).start()

    def xstep(w, j):
        @pl.when(valid(j))
        def _():
            for_part(w, j, lambda p: xx_in(w, j, p).wait_recv())
            if j == 0:
                if relay:
                    half(w).start()
                cc(w, 2 * Z - 1).start()
            else:
                if relay and is_pair(j) is not None:
                    @pl.when(is_pair(j))
                    def _():
                        half_in(w).wait_recv()
                cc(w, 2 * Z - 1 + j).start()

    def finish(w):
        for j in range(4 * Z - 2):
            @pl.when(valid(j % (2 * Z - 1)))
            def _():
                cc_in(w, j).wait_recv()
                cc(w, j).wait_send()
        for j in range(2 * Z - 1):
            @pl.when(valid(j))
            def _():
                for_part(w, j, lambda p: xx(w, j, p).wait_send())
        for k in range(Z - 1):
            @pl.when((z >= k) & (z < Z - 1))
            def _():
                up(w, k).wait_send()

            @pl.when((z + k <= Z - 1) & (z > 0))
            def _():
                dn(w, k).wait_send()
        if relay:
            half(w).wait_send()
        local[w].wait()

    def tick(w, k):
        step(w, k)
        if k == 1:
            xstep(w, 0)
            if w + ahead < nw:
                begin(w + ahead)
        else:
            xstep(w, k - 1)
            xstep(w, Z - 1 + k - 1)
        if w > 0 and k == 1:
            xstep(w - 1, Z - 1)
            xstep(w - 1, 2 * Z - 2)

    def last():
        xstep(nw - 1, Z - 1)
        xstep(nw - 1, 2 * Z - 2)

    return begin, tick, last, finish


def front_body(Z, seqs, length, ahead, *refs):
    nw = 7
    own = refs[:nw]
    x, cot, gain1, gain2, low, hgain, link, ids = refs[nw:nw + 8]
    k0 = nw + 8
    wide = refs[k0:k0 + nw]
    k0 += nw
    n1_o, pi_o, pf_o, pg_o, h_o, m_o, mid_o, n2_o, gate_o, up_o, act_o, gy_o, gd_o, rh, start = refs[k0:k0 + 15]
    k0 += 15
    (xv, n1, n2, pi, pf, pg, h, cum, m, wbuf, wob, pn, rn, gate, up, act, gy, stg, e_f,
     pay, box, row, got) = refs[k0:k0 + 23]
    k0 += 23
    s_c, r_c, s_t, r_t, n_s, n_r, w_s, o_s, e_s, g_s, x_s = refs[k0:k0 + 11]
    sems = refs[k0 + 11:]
    w_in, w_f, w_g, w_out, w_mg, w_mu, w_dn = wide
    n, width = x.shape
    C, F = pi.shape[1], gate.shape[1]
    s, z, t = lax.axis_index("shard"), lax.axis_index("ctx"), lax.axis_index("tp")
    q, c = s // 2, lax.rem(s, 2)
    OTHER = {"tp": 1 - t}
    begin, tick, last, finish = gather_steps(nw, Z, ahead, True, own, wide, sems)
    NP, NF, NW, NC = n // TR, F // TC, C // TC, width // TC

    barrier = pltpu.get_barrier_semaphore()
    for d in [{"shard": (1 - q) * 2 + c}, {"shard": q * 2 + (1 - c)}, OTHER] + [{"ctx": lax.rem(z + o, Z)} for o in range(1, Z)]:
        pl.semaphore_signal(barrier, inc=1, device_id=d, device_id_type=MESH)
    pl.semaphore_wait(barrier, 2 + Z)

    for w in range(ahead):
        begin(w)
    load_x = pltpu.make_async_copy(x, xv, x_s.at[0])
    load_x.start()
    done = []

    def put(src, dst, k):
        cp = pltpu.make_async_copy(src, dst, o_s.at[k])
        cp.start()
        done.append(cp)

    def norm_in():
        load_x.wait()
        g = gain1[...]

        def go(i, _):
            r = pl.ds(pl.multiple_of(i * 16, 16), 16)
            v = xv[r, :]
            n1[r, :] = (v * lax.rsqrt(jnp.mean(v * v, axis=1, keepdims=True) + epsilon) * g).astype(jnp.bfloat16)
            return 0

        lax.fori_loop(0, n // 16, go, 0, unroll=2)
        put(n1, n1_o, 0)

    def times(lhs, w, dst, tiles, after=None):
        def load(j, s):
            return pltpu.make_async_copy(w.at[:, pl.ds(pl.multiple_of(j * TC, TC), TC)], wbuf.at[s], w_s.at[s])

        load(0, 0).start()

        def go(j, _):
            s = lax.rem(j, 2)

            @pl.when(j + 1 < tiles)
            def _():
                load(j + 1, 1 - s).start()

            load(j, s).wait()
            dst[:, pl.ds(pl.multiple_of(j * TC, TC), TC)] = jnp.dot(lhs[...], wbuf[s], preferred_element_type=jnp.float32)
            if after is not None:
                after(j)
            return 0

        lax.fori_loop(0, tiles, go, 0)

    def rows_of(k):
        return pl.ds(k * TR, TR)

    def pn_copy(k):
        return remote(pn.at[rows_of(k), :], rn.at[rows_of(k), :], n_s.at[k], n_r.at[k], OTHER)

    def out_product():
        def load(j, s):
            return pltpu.make_async_copy(w_out.at[pl.ds(pl.multiple_of(j * TC, TC), TC), :], wob.at[s], w_s.at[s])

        load(0, 0).start()

        def go(j, _):
            s = lax.rem(j, 2)

            @pl.when(j + 1 < NC)
            def _():
                load(j + 1, 1 - s).start()

            load(j, s).wait()
            pn[:, pl.ds(pl.multiple_of(j * TC, TC), TC)] = dot_t(m[...], wob[s]).astype(jnp.bfloat16)
            return 0

        lax.fori_loop(0, NC, go, 0)
        for k in range(NP):
            pn_copy(k).start()

    def middle(k):
        pn_copy(k).wait_recv()
        g = gain2[...]

        def go(i, _):
            r = pl.ds(pl.multiple_of(k * TR + i * 16, 16), 16)
            v = xv[r, :] + (pn[r, :].astype(jnp.float32) + rn[r, :].astype(jnp.float32))
            xv[r, :] = v
            n2[r, :] = (v * lax.rsqrt(jnp.mean(v * v, axis=1, keepdims=True) + epsilon) * g).astype(jnp.bfloat16)
            return 0

        lax.fori_loop(0, TR // 16, go, 0)

    def cot_load(k):
        return pltpu.make_async_copy(cot.at[rows_of(k), :], e_f.at[k % 2], e_s.at[k % 2])

    def cot_low():
        cot_load(0).start()
        for k in range(NP):
            if k + 1 < NP:
                cot_load(k + 1).start()
            cot_load(k).wait()
            gy[rows_of(k), :] = e_f[k % 2].astype(jnp.bfloat16)

    def activate(j):
        cols = pl.ds(pl.multiple_of(j * TC, TC), TC)

        def go(i, _):
            r = pl.ds(pl.multiple_of(i * 32, 32), 32)
            v = gate[r, cols]
            act[r, cols] = (v * sigmoid(v) * up[r, cols]).astype(jnp.bfloat16)
            return 0

        lax.fori_loop(0, n // 32, go, 0)

    def gd_copy(j, s):
        return pltpu.make_async_copy(stg.at[s], gd_o.at[pl.ds(pl.multiple_of(j * TC, TC), TC), :], g_s.at[s])

    def down_grad(j0, j1):
        def go(j, _):
            s = lax.rem(j, 2)

            @pl.when(j >= 2)
            def _():
                gd_copy(j - 2, s).wait()

            stg[s] = dot_o(gy[:, pl.ds(pl.multiple_of(j * TC, TC), TC)], act[...]).astype(jnp.bfloat16)
            gd_copy(j, s).start()
            return 0

        lax.fori_loop(j0, j1, go, 0)

    norm_in()
    for w, src, dst, o, k in ((0, w_in, pi, pi_o, 1), (1, w_f, pf, pf_o, 2), (2, w_g, pg, pg_o, 3)):
        if w == 0:
            tick(0, 1)
            tick(0, 2)
            tick(0, 3)
        tick(w + 1, 1)
        tick(w + 1, 2)
        finish(w)
        times(n1, src, dst, NW)
        put(dst, o, k)
        if w < 2:
            tick(w + 1, 3)
    ends = [forward_scan_one(0, length, pi, pf, low, link, h, cum)]
    tick(3, 3)
    for sq in range(1, seqs):
        ends.append(forward_scan_one(sq, length, pi, pf, low, link, h, cum))
    pay[4:8, :] = ids[...]
    for sq in range(seqs):
        pay[sq:sq + 1, :] = ends[sq][1]
        pay[2 + sq:3 + sq, :] = ends[sq][0]
    cps = spread(Z, z, pay, box, s_c, r_c)
    tick(4, 1)
    cot_low()
    put(gy, gy_o, 4)
    spread_wait(Z, z, pay, box, s_c, r_c, cps)
    start[...] = prefix_state(Z, z, box)
    forward_finish(seqs, length, h, cum, start, rh)
    put(h, h_o, 5)
    swap_columns(rh, row, got, s_t.at[0], r_t.at[0], 1 - t, n)
    scale_columns(row, got, rh, n, width, lambda v: lax.rsqrt(v / width + epsilon))
    mixed(h, rh, hgain, pg, m)
    put(m, m_o, 6)
    tick(4, 2)
    finish(3)
    out_product()
    tick(4, 3)
    for k in range(NP // 2):
        middle(k)
    tick(5, 1)
    for k in range(NP // 2, NP):
        middle(k)
    put(xv, mid_o, 7)
    put(n2, n2_o, 8)
    tick(5, 2)
    finish(4)
    times(n2, w_mg, gate, NF)
    put(gate, gate_o, 9)
    tick(5, 3)
    tick(6, 1)
    finish(5)
    times(n2, w_mu, up, NF, activate)
    put(up, up_o, 10)
    put(act, act_o, 11)
    tick(6, 2)
    down_grad(0, NC // 2)
    tick(6, 3)
    down_grad(NC // 2, NC)
    last()
    finish(6)
    gd_copy(NC - 2, NC % 2).wait()
    gd_copy(NC - 1, (NC - 1) % 2).wait()
    for k in range(NP):
        pn_copy(k).wait_send()
    for cp in done:
        cp.wait()


def front_all(Z, seqs, length, shards, x, cot, gain1, gain2, low, hgain, link, ids, cid=0, ahead=2):
    nw = len(shards)
    n, width = x.shape
    C, F = shards[0].shape[1], shards[4].shape[1]
    dma = pltpu.SemaphoreType.DMA
    bf, f = jnp.bfloat16, jnp.float32
    sh = jax.ShapeDtypeStruct
    anyw, vmem = pl.BlockSpec(memory_space=pl.ANY), pl.BlockSpec(memory_space=pltpu.VMEM)
    NP = n // TR
    V = pltpu.VMEM
    out_shape = ([sh((a.shape[0] * 4 * Z, a.shape[1]), bf) for a in shards]
                 + [sh((n, width), bf)] + [sh((n, C), f)] * 4 + [sh((n, C), bf)] + [sh((n, width), f), sh((n, width), bf)]
                 + [sh((n, F), f)] * 2 + [sh((n, F), bf), sh((n, width), bf), sh((width, F), bf), sh((n, 1), f), sh((seqs, C), f)])
    scratch = [
        V((n, width), f), V((n, width), bf), V((n, width), bf), V((n, C), f), V((n, C), f), V((n, C), f), V((n, C), f), V((n, C), f),
        V((n, C), bf), V((2, width, TC), bf), V((2, TC, C), bf), V((n, width), bf), V((n, width), bf), V((n, F), f), V((n, F), f),
        V((n, F), bf), V((n, width), bf), V((2, TC, F), bf), V((2, TR, width), f),
        V((8, C), f), V((Z, 8, C), f), V((n // 128, 128), f), V((n // 128, 128), f),
        dma((Z - 1,)), dma((Z,)), dma((1,)), dma((1,)), dma((NP,)), dma((NP,)), dma((2,)), dma((12,)), dma((2,)), dma((2,)), dma((1,)),
        dma((nw, Z - 1)), dma((nw, Z - 1)), dma((nw, Z - 1)), dma((nw, Z - 1)),
        dma((nw, 2 * Z - 1)), dma((nw, 2 * Z - 1)),
        dma((nw, 4 * Z - 2)), dma((nw, 4 * Z - 2)), dma((nw,)), dma((nw,)), dma((nw,)),
    ]
    res = pl.pallas_call(
        functools.partial(front_body, Z, seqs, length, ahead),
        out_shape=out_shape,
        in_specs=[vmem] * nw + [anyw] * 2 + [vmem] * 6,
        out_specs=[anyw] * (len(out_shape) - 2) + [vmem] * 2,
        scratch_shapes=scratch,
        compiler_params=pltpu.CompilerParams(collective_id=cid, has_side_effects=True, vmem_limit_bytes=66_000_000),
        name="forward",
    )(*shards, x, cot, gain1, gain2, low, hgain, link, ids)
    return res[:nw], res[nw:]


TR = 64
TC = 256


def dot_t(a, b):
    return lax.dot_general(a, b, (((1,), (1,)), ((), ())), preferred_element_type=jnp.float32)


def dot_o(a, b):
    return lax.dot_general(a, b, (((0,), (0,)), ((), ())), preferred_element_type=jnp.float32)


def back_body(Z, seqs, length, *refs):
    (gd, gg, gu, pn, po, x, mid, cot, n1, m, w_out, w_in, w_f, w_g, pi_h, pf_h, pg_h, h_h,
     rh, start, ids, link, gain1, gain2, low, hgain) = refs[:26]
    out, dx, vec_out = refs[26:29]
    grads = refs[29:36]
    mparts = refs[36:40]
    rn, ro = refs[40:42]
    k0 = 42
    rc, xr, zu, zd, hr = (refs[k0 + 7 * i:k0 + 7 * (i + 1)] for i in range(5))
    k0 += 35
    (xs, zs, stage, stage_z, fin, dmid, gm, dm, h, pi, pf, pg, gl, tail, dpi, dpf, dpg, n1v, mv, wbuf, wbuf3, stg, sn, rn1,
     e_f, e_b, vec, vgot, vbox, col, end, pay, box, row, got, acc) = refs[k0:k0 + 36]
    k0 += 36
    (l_h, l_n, w_s, g_s, n_s, n_r, o_s, o_r, t_s, t_r, e_s, eo_s, v_s, v_r, vz_s, vz_r, s_c, r_c, s_t, r_t) = refs[k0:k0 + 20]
    sems = refs[k0 + 20:]
    n, width = x.shape
    C = dm.shape[1]
    parts = (gd, gg, gu) + tuple(mparts)
    sc = Scatter(Z, parts, rc, xr, zu, zd, hr, grads, xs, zs, (stage, stage_z), fin, sems)
    z = sc.z
    t = lax.axis_index("tp")
    OTHER = {"tp": 1 - t}

    barrier = pltpu.get_barrier_semaphore()
    for d in [sc.X, sc.C, OTHER] + [{"ctx": lax.rem(z + o, Z)} for o in range(1, Z)]:
        pl.semaphore_signal(barrier, inc=1, device_id=d, device_id_type=MESH)
    pl.semaphore_wait(barrier, 2 + Z)

    for w in range(3):
        sc.c_send(w)

    NP = n // TR
    NC = width // TC

    def rows_of(k):
        return pl.ds(k * TR, TR)

    def pn_copy(k):
        return remote(pn.at[rows_of(k), :], rn.at[rows_of(k), :], n_s.at[k], n_r.at[k], OTHER)

    def po_copy(k):
        return remote(po.at[rows_of(k), :], ro.at[rows_of(k), :], o_s.at[k], o_r.at[k], OTHER)

    for k in range(NP):
        pn_copy(k).start()
    for k in range(NP):
        po_copy(k).start()
    early = [pltpu.make_async_copy(a, b, l_h.at[i]) for i, (a, b) in enumerate(
        ((pi_h, pi), (pf_h, pf), (pg_h, pg), (h_h, h), (n1, n1v), (m, mv)))]
    for cp in early:
        cp.start()
    vec[...] = jnp.zeros_like(vec)

    steps = []

    def X(w):
        return [functools.partial(sc.x_phase, w, k) for k in range(Z)]

    def Zs(w):
        return [functools.partial(sc.z_phase, w, k) for k in range(Z)]

    def tick(*todo):
        for s in todo:
            s()

    def piece(k, s, f_src, b_src):
        r = rows_of(k)
        return ([pltpu.make_async_copy(a.at[r, :], e_f.at[s, i], e_s.at[s, i]) for i, a in enumerate(f_src)]
                + [pltpu.make_async_copy(a.at[r, :], e_b.at[s, i], e_s.at[s, 2 + i]) for i, a in enumerate(b_src)])

    def p1_load(k):
        pn_copy(k).wait_recv()
        for cp in piece(k, k % 2, (mid, cot), (pn, rn)):
            cp.start()

    def p1(k):
        s = k % 2
        for cp in piece(k, s, (mid, cot), (pn, rn)):
            cp.wait()
        g = gain2[...]

        def go(i, a):
            r = pl.ds(pl.multiple_of(i * 16, 16), 16)
            v, ct = e_f[s, 0, r, :], e_f[s, 1, r, :]
            d = e_b[s, 0, r, :].astype(jnp.float32) + e_b[s, 1, r, :].astype(jnp.float32)
            r2 = lax.rsqrt(jnp.mean(v * v, axis=1, keepdims=True) + epsilon)
            gdn = d * g
            inner = jnp.mean(gdn * v, axis=1, keepdims=True)
            o = ct + gdn * r2 - v * (r2 * r2 * r2 * inner)
            rr = pl.ds(pl.multiple_of(k * TR + i * 16, 16), 16)
            dmid[rr, :] = o
            gm[rr, :] = o.astype(jnp.bfloat16)
            return a + jnp.sum(d * v * r2, axis=0, keepdims=True)

        vec[1:2, :] = vec[1:2, :] + lax.fori_loop(0, TR // 16, go, jnp.zeros((1, width), jnp.float32))

    def po_load(k):
        po_copy(k).wait_recv()
        for cp in piece(k, k % 2, (mid,), (po, ro)):
            if cp is not None:
                cp.start()

    def o_store(k):
        return pltpu.make_async_copy(e_f.at[k % 2, 1], out.at[rows_of(k), :], eo_s.at[k % 2])

    def p_out(k):
        s = k % 2
        for cp in piece(k, s, (mid,), (po, ro)):
            cp.wait()
        if k >= 2:
            o_store(k - 2).wait()

        def go(i, _):
            r = pl.ds(pl.multiple_of(i * 16, 16), 16)
            e_f[s, 1, r, :] = e_f[s, 0, r, :] + (e_b[s, 0, r, :].astype(jnp.float32) + e_b[s, 1, r, :].astype(jnp.float32))
            return 0

        lax.fori_loop(0, TR // 16, go, 0)
        o_store(k).start()

    NW = C // TC

    def w_load(j, s):
        return pltpu.make_async_copy(w_out.at[:, pl.ds(pl.multiple_of(j * TC, TC), TC)], wbuf.at[s], w_s.at[s, 0])

    def p2():
        w_load(0, 0).start()

        def go(j, _):
            s = lax.rem(j, 2)

            @pl.when(j + 1 < NW)
            def _():
                w_load(j + 1, 1 - s).start()

            w_load(j, s).wait()
            dm[:, pl.ds(pl.multiple_of(j * TC, TC), TC)] = jnp.dot(gm[...], wbuf[s], preferred_element_type=jnp.float32)
            return 0

        lax.fori_loop(0, NW, go, 0)

    def g_copy(dst, j, s):
        return pltpu.make_async_copy(stg.at[s], dst.at[pl.ds(pl.multiple_of(j * TC, TC), TC), :], g_s.at[s])

    def p4(w, lhs, rhs):
        dst = mparts[w - 3]

        def go(j, _):
            s = lax.rem(j, 2)

            @pl.when(j >= 2)
            def _():
                g_copy(dst, j - 2, s).wait()

            stg[s] = dot_o(lhs[:, pl.ds(pl.multiple_of(j * TC, TC), TC)], rhs[...]).astype(jnp.bfloat16)
            g_copy(dst, j, s).start()
            return 0

        lax.fori_loop(0, NC, go, 0)
        g_copy(dst, NC - 2, NC % 2).wait()
        g_copy(dst, NC - 1, (NC - 1) % 2).wait()
        sc.c_send(w)

    def w3_start(j, s):
        for i, a in enumerate((w_in, w_f, w_g)):
            pltpu.make_async_copy(a.at[pl.ds(pl.multiple_of(j * TC, TC), TC), :], wbuf3.at[s, i], w_s.at[2 + s, i]).start()

    def w3_wait(j, s):
        for i, a in enumerate((w_in, w_f, w_g)):
            pltpu.make_async_copy(a.at[pl.ds(pl.multiple_of(j * TC, TC), TC), :], wbuf3.at[s, i], w_s.at[2 + s, i]).wait()

    def n_copy(j):
        return remote(sn.at[j], rn1.at[j], t_s.at[j], t_r.at[j], OTHER)

    def p5(j0, j1):
        def go(j, _):
            s = lax.rem(j, 2)

            @pl.when(j + 1 < NC)
            def _():
                w3_start(j + 1, 1 - s)

            w3_wait(j, s)
            o = dot_t(dpi[...], wbuf3[s, 0]) + dot_t(dpf[...], wbuf3[s, 1]) + dot_t(dpg[...], wbuf3[s, 2])
            sn[j] = o.astype(jnp.bfloat16)
            n_copy(j).start()
            return 0

        lax.fori_loop(j0, j1, go, 0)

    def x_load(j, s):
        return pltpu.make_async_copy(x.at[:, pl.ds(j * TC, TC)], tail.at[:, pl.ds(s * TC, TC)], e_s.at[s, 0])

    def p6a(j):
        s = j % 2
        if j == 0:
            x_load(0, 0).start()
        if j + 1 < NC:
            x_load(j + 1, 1 - s).start()
        x_load(j, s).wait()
        n_copy(j).wait_recv()
        g = gain1[:, j * TC:(j + 1) * TC]

        def go(i, _):
            r = pl.ds(pl.multiple_of(i * 16, 16), 16)
            v = tail[r, s * TC:(s + 1) * TC]
            d = sn[j, r, :].astype(jnp.float32) + rn1[j, r, :].astype(jnp.float32)
            a, b = v * v, d * g * v
            a, b = a[:, :128] + a[:, 128:], b[:, :128] + b[:, 128:]
            if j == 0:
                acc[0, r, :] = a
                acc[1, r, :] = b
            else:
                acc[0, r, :] = acc[0, r, :] + a
                acc[1, r, :] = acc[1, r, :] + b
            return 0

        lax.fori_loop(0, n // 16, go, 0, unroll=2)

    def p6b():
        def go(i, _):
            r = pl.ds(pl.multiple_of(i * 16, 16), 16)
            r1 = lax.rsqrt(jnp.sum(acc[0, r, :], axis=1, keepdims=True) / width + epsilon)
            inner = jnp.sum(acc[1, r, :], axis=1, keepdims=True) / width
            acc[0, r, :] = jnp.broadcast_to(r1, (16, 128))
            acc[1, r, :] = jnp.broadcast_to(r1 * r1 * r1 * inner, (16, 128))
            return 0

        lax.fori_loop(0, n // 16, go, 0, unroll=2)

    def dx_copy(j):
        s = j % 2
        return pltpu.make_async_copy(gl.at[:, pl.ds(s * TC, TC)], dx.at[:, pl.ds(j * TC, TC)], eo_s.at[s])

    def p6c(j):
        s = j % 2
        if j == 0:
            x_load(0, 0).start()
        if j + 1 < NC:
            x_load(j + 1, 1 - s).start()
        x_load(j, s).wait()
        if j >= 2:
            dx_copy(j - 2).wait()
        g = gain1[:, j * TC:(j + 1) * TC]

        def go(i, total):
            r = pl.ds(pl.multiple_of(i * 16, 16), 16)
            v = tail[r, s * TC:(s + 1) * TC]
            d = sn[j, r, :].astype(jnp.float32) + rn1[j, r, :].astype(jnp.float32)
            r1 = jnp.concatenate([acc[0, r, :], acc[0, r, :]], axis=1)
            ri = jnp.concatenate([acc[1, r, :], acc[1, r, :]], axis=1)
            gl[r, s * TC:(s + 1) * TC] = dmid[r, j * TC:(j + 1) * TC] + d * g * r1 - v * ri
            return total + jnp.sum(d * v * r1, axis=0, keepdims=True)

        vec[0:1, j * TC:(j + 1) * TC] = lax.fori_loop(0, n // 16, go, jnp.zeros((1, TC), jnp.float32), unroll=2)
        dx_copy(j).start()

    x0, x1, x2, z0, z1, z2 = X(0), X(1), X(2), Zs(0), Zs(1), Zs(2)
    x3, x4, x5, x6 = X(3), X(4), X(5), X(6)
    z3, z4, z5, z6 = Zs(3), Zs(4), Zs(5), Zs(6)
    tick(*x0, x1[0])
    p1_load(0)
    tick(x1[1])
    between = [[z0[0], x1[2]], [x1[3]], [z0[1]], [], [z0[2], x2[0]], [], [z0[3], x2[1]], [x2[2]]]
    for k in range(NP):
        if k + 1 < NP:
            p1_load(k + 1)
        p1(k)
        tick(*(between[k] if k < len(between) else []))
    p2()
    tick(x2[3], z1[0])
    for cp in early:
        cp.wait()
    p4(3, gm, mv)
    tick(z1[1])
    backward_first(n, dm, h, pg, hgain, rh, dpg, col, acc_row(vec, 2, C))
    column_to_rows(col, row, n)
    swap = remote(row, got, s_t.at[0], r_t.at[0], OTHER)
    swap.start()
    tick(x3[0], x3[1])
    swap.wait()
    scale_columns(row, got, col, n, width, lambda v: v / width)
    ends = []
    for sq in range(seqs):
        ends.append(backward_scan_one(sq, length, dm, h, pf, pg, low, hgain, link, rh, col, gl, tail))
        tick(z1[2 + sq] if sq < 2 else (lambda: None))
    pay[4:8, :] = ids[...]
    for sq in range(seqs):
        pay[sq:sq + 1, :] = ends[sq][1]
        pay[2 + sq:3 + sq, :] = ends[sq][0]
    cps = spread(Z, z, pay, box, s_c, r_c)
    tick(x3[2], x3[3])
    spread_wait(Z, z, pay, box, s_c, r_c, cps)
    end[...] = suffix_state(Z, z, box)
    backward_last(seqs, length, gl, tail, end, h, start, pi, pf, low, link, dpi, dpf, acc_row(vec, 3, C))
    tick(z2[0])
    w3_start(0, 0)
    p4(4, n1v, dpi)
    tick(x4[0], x4[1], z2[1])
    p4(5, n1v, dpf)
    tick(x4[2], x4[3], z2[2])
    p4(6, n1v, dpg)
    tick(z2[3], x5[0], x5[1])
    p5(0, NC // 2)
    tick(x5[2], x5[3], z3[0], z3[1])
    p5(NC // 2, NC)
    tick(z3[2], z3[3], *x6)
    po_load(0)
    outs = [[z4[0]], [], [z4[1]], [], [z4[2]], [], [z4[3]], []]
    for k in range(NP):
        if k + 1 < NP:
            po_load(k + 1)
        p_out(k)
        tick(*(outs[k] if k < len(outs) else []))
    for k in (NP - 2, NP - 1):
        o_store(k).wait()
    for j in range(NC):
        p6a(j)
        if j % 4 == 3 and j // 4 < 2:
            tick(z5[j // 4])
    p6b()
    for j in range(NC):
        p6c(j)
        if j % 4 == 3 and j // 4 < 2:
            tick(z5[2 + j // 4])
    for j in (NC - 2, NC - 1):
        dx_copy(j).wait()
    first = remote(vec, vgot.at[0], v_s.at[0], v_r.at[0], sc.C)
    first.start()
    tick(z6[0])
    first.wait()
    vec[...] = vec[...] + vgot[0]
    second = remote(vec, vgot.at[1], v_s.at[1], v_r.at[1], sc.X)
    second.start()
    tick(z6[1])
    second.wait()
    vec[...] = vec[...] + vgot[1]
    cps = spread(Z, z, vec, vbox, vz_s, vz_r)
    tick(z6[2], z6[3])
    spread_wait(Z, z, vec, vbox, vz_s, vz_r, cps)
    total = vbox[0]
    for k in range(1, Z):
        total = total + vbox[k]
    vec_out[...] = total
    for k in range(NP):
        pn_copy(k).wait_send()
        po_copy(k).wait_send()
    for j in range(NC):
        n_copy(j).wait_send()
    for w in range(7):
        sc.drain(w, 7)


def acc_row(vec, k, C):
    return vec.at[k:k + 1, pl.ds(0, C)]


def back_all(Z, seqs, length, gd, gg, gu, pn, po, x, mid, cot, n1, m, w_out, w_in, w_f, w_g, pi, pf, pg, h,
             rh, start, ids, link, gain1, gain2, low, hgain, cid=1):
    n, width = x.shape
    C = pi.shape[1]
    dma = pltpu.SemaphoreType.DMA
    bf, f = jnp.bfloat16, jnp.float32
    sh = jax.ShapeDtypeStruct
    anyw, vmem = pl.BlockSpec(memory_space=pl.ANY), pl.BlockSpec(memory_space=pltpu.VMEM)
    shapes = [gd.shape, gg.shape, gu.shape] + [(width, C)] * 4
    R = [s[0] // (4 * Z) for s in shapes]
    N = [s[1] for s in shapes]
    Rm, Nm = max(R), max(N)
    NP, NC = n // TR, width // TC
    out_shape = ([sh((n, width), f), sh((n, width), f), sh((8, width), f)]
                 + [sh((r, k), f) for r, k in zip(R, N)]
                 + [sh((width, C), bf)] * 4
                 + [sh((n, width), bf)] * 2
                 + [sh((2 * Z * r, k), bf) for r, k in zip(R, N)]
                 + [sh((Z * r, k), bf) for r, k in zip(R, N)]
                 + [sh((Z * r, k), bf) for r, k in zip(R, N)]
                 + [sh((Z * r, k), bf) for r, k in zip(R, N)]
                 + [sh((r // 2, k), bf) for r, k in zip(R, N)])
    V = pltpu.VMEM
    scratch = [
        V((2, Z, Rm, Nm), bf), V((2, Z - 1, Rm, Nm), bf), V((2, 3, Rm, Nm), bf), V((5, Rm, Nm), bf), V((Rm, Nm), f),
        V((n, width), f), V((n, width), bf), V((n, C), f), V((n, C), f), V((n, C), f), V((n, C), f), V((n, C), f),
        V((n, C), f), V((n, C), f), V((n, C), bf), V((n, C), bf), V((n, C), bf), V((n, width), bf), V((n, C), bf),
        V((2, width, TC), bf), V((2, 3, TC, C), bf), V((2, TC, C), bf), V((NC, n, TC), bf), V((NC, n, TC), bf),
        V((2, 2, TR, width), f), V((2, 2, TR, width), bf), V((8, width), f), V((2, 8, width), f), V((Z, 8, width), f),
        V((n, 1), f), V((seqs, C), f), V((8, C), f), V((Z, 8, C), f), V((n // 128, 128), f), V((n // 128, 128), f),
        V((2, n, 128), f),
        dma((6,)), dma((1,)), dma((4, 3)), dma((2,)), dma((NP,)), dma((NP,)), dma((NP,)), dma((NP,)), dma((NC,)), dma((NC,)),
        dma((2, 4)), dma((2,)), dma((2,)), dma((2,)), dma((Z - 1,)), dma((Z,)), dma((Z - 1,)), dma((Z,)), dma((1,)), dma((1,)),
        dma((7, 2)), dma((7, 2)), dma((7, Z)), dma((7, Z)), dma((7, Z - 1)), dma((7, Z)), dma((7, Z)),
        dma((7,)), dma((7,)), dma((3, 5)), dma((7,)),
    ]
    res = pl.pallas_call(
        functools.partial(back_body, Z, seqs, length),
        out_shape=out_shape,
        in_specs=[anyw] * 18 + [vmem] * 8,
        out_specs=[anyw, anyw, vmem] + [anyw] * (len(out_shape) - 3),
        scratch_shapes=scratch,
        compiler_params=pltpu.CompilerParams(collective_id=cid, has_side_effects=True, vmem_limit_bytes=66_000_000),
        name="backward",
    )(gd, gg, gu, pn, po, x, mid, cot, n1, m, w_out, w_in, w_f, w_g, pi, pf, pg, h, rh, start, ids, link, gain1, gain2, low, hgain)
    return res[0], res[1], res[2], res[3:10]


def carried_in(x, axis, combine, identity, reverse):
    size, position = (lax.axis_size(axis), lax.axis_index(axis))
    everything = jax.tree.map(lambda part: lax.all_gather(part, axis), x)
    start = jax.tree.map(
        lambda part, zero: jnp.broadcast_to(jnp.asarray(zero, part.dtype), part.shape), x, identity
    )

    def turn(k, before):
        at = size - 1 - k if reverse else k
        reached = at > position if reverse else at < position
        new = combine(before, jax.tree.map(lambda part: part[at], everything))
        return jax.tree.map(lambda a, b: jnp.where(reached, a, b), new, before)

    return lax.fori_loop(0, size, turn, start)


def inverse_rms(inputs):
    return lax.rsqrt(jnp.mean(inputs * inputs, axis=-1, keepdims=True) + epsilon)


def rms_backward(inputs, row_scale, gain_vec, upstream):
    weighted = upstream * gain_vec
    inner_sum = jnp.mean(weighted * inputs, axis=-1, keepdims=True)
    return weighted * row_scale - inputs * (row_scale * row_scale * row_scale) * inner_sum


def silu_slope(inputs):
    sig_part = jax.nn.sigmoid(inputs)
    return sig_part * (1.0 + inputs * (1.0 - sig_part))


def times_back(left_mat, right_mat):
    return lax.dot_general(
        left_mat, right_mat, (((1,), (1,)), ((), ())), preferred_element_type=jnp.float32
    )


def outer_sum(left_mat, right_mat):
    return lax.dot_general(
        left_mat, right_mat, (((0,), (0,)), ((), ())), preferred_element_type=jnp.float32
    )


def linear_step(first_part, second_part):
    return (first_part[0] * second_part[0], second_part[0] * first_part[1] + second_part[1])


def joined_ids(last_ids, first_ids):
    return jnp.where((last_ids == first_ids) | (last_ids < 0.0) | (first_ids < 0.0), 1.0, 0.0)


def forward_join(first_part, second_part):
    linked = joined_ids(first_part[3], second_part[2])[:, None]
    return (
        first_part[0] * second_part[0] * linked,
        second_part[0] * linked * first_part[1] + second_part[1],
        jnp.where(first_part[2] < 0.0, second_part[2], first_part[2]),
        jnp.where(second_part[3] < 0.0, first_part[3], second_part[3]),
    )


def backward_join(first_part, second_part):
    linked = joined_ids(second_part[3], first_part[2])[:, None]
    return (
        second_part[0] * linked * first_part[0],
        second_part[0] * linked * first_part[1] + second_part[1],
        jnp.where(second_part[2] < 0.0, first_part[2], second_part[2]),
        jnp.where(first_part[3] < 0.0, second_part[3], first_part[3]),
    )


def mixer_forward_plain(seqs, length, width, pi, pf, pg, lower, gain, segs):
    channels = pi.shape[1]
    forget = lower + (1.0 - lower) * jax.nn.sigmoid(pf)
    candidate = jax.nn.silu(pi) * (1.0 - forget)
    inner_link = jnp.concatenate(
        [jnp.ones((seqs, 1), jnp.float32), jnp.where(segs[:, 1:] == segs[:, :-1], 1.0, 0.0)], axis=1
    )
    decay = forget.reshape(seqs, length, channels) * inner_link[:, :, None]
    prod, local = lax.associative_scan(
        linear_step, (decay, candidate.reshape(seqs, length, channels)), axis=1
    )
    first, last = segs[:, 0], segs[:, -1]
    ones, zero = jnp.ones((seqs, channels), jnp.float32), jnp.zeros((seqs, channels), jnp.float32)
    minus = -jnp.ones((seqs,), jnp.float32)
    prefix = carried_in(
        (prod[:, -1], local[:, -1], first, last), "ctx", forward_join, (ones, zero, minus, minus), False
    )
    start = joined_ids(prefix[3], first)[:, None] * prefix[1]
    h = (local + prod * start[:, None, :]).reshape(seqs * length, channels)
    squares = lax.psum(jnp.sum(h * h, axis=1), "tp")
    rh = lax.rsqrt(squares / width + epsilon)[:, None]
    m = (h * rh * gain * jax.nn.silu(pg)).astype(jnp.bfloat16)
    return h, m, rh, start


def mixer_backward_plain(seqs, length, width, dm, h, pi, pf, pg, lower, gain, segs, rh, start):
    channels = pi.shape[1]
    s = jax.nn.sigmoid(pf)
    forget = lower + (1.0 - lower) * s
    inner_link = jnp.concatenate(
        [jnp.ones((seqs, 1), jnp.float32), jnp.where(segs[:, 1:] == segs[:, :-1], 1.0, 0.0)], axis=1
    )
    forget_seq = forget.reshape(seqs, length, channels)
    decay = forget_seq * inner_link[:, :, None]
    silu_gate = jax.nn.silu(pg)
    weighted = dm * gain * silu_gate
    inner = lax.psum(jnp.sum(weighted * h, axis=1), "tp")
    dh = weighted * rh - h * (rh * rh * rh) * (inner / width)[:, None]
    gain_grad = jnp.sum(dm * h * rh * silu_gate, axis=0)
    dpg = (dm * h * rh * gain * silu_slope(pg)).astype(jnp.bfloat16)
    ones_row = jnp.ones((seqs, 1, channels), jnp.float32)
    following = jnp.concatenate([decay[:, 1:], ones_row], axis=1)
    tail, local = lax.associative_scan(
        linear_step, (following, dh.reshape(seqs, length, channels)), reverse=True, axis=1
    )
    first, last = segs[:, 0], segs[:, -1]
    ones, zero = jnp.ones((seqs, channels), jnp.float32), jnp.zeros((seqs, channels), jnp.float32)
    minus = -jnp.ones((seqs,), jnp.float32)
    suffix = carried_in(
        (decay[:, 0] * tail[:, 0], forget_seq[:, 0] * local[:, 0], first, last),
        "ctx", backward_join, (ones, zero, minus, minus), True,
    )
    end = joined_ids(last, suffix[2])[:, None] * suffix[1]
    g = (local + tail * end[:, None, :]).reshape(seqs * length, channels)
    states = h.reshape(seqs, length, channels)
    previous = jnp.concatenate(
        [start[:, None, :], inner_link[:, 1:, None] * states[:, :-1]], axis=1
    ).reshape(seqs * length, channels)
    dforget = g * (previous - jax.nn.silu(pi))
    dpi = (g * (1.0 - forget) * silu_slope(pi)).astype(jnp.bfloat16)
    dpf = (dforget * (1.0 - lower) * s * (1.0 - s)).astype(jnp.bfloat16)
    return dpi, dpf, dpg, gain_grad, jnp.sum(dforget * (1.0 - s), axis=0)


def on_device(
    block_input,
    segment_ids,
    norm_gain,
    lower,
    w_input,
    w_forget,
    w_gate,
    hidden_gain,
    w_out,
    mlp_gain,
    w_mlp_gate,
    w_mlp_up,
    w_down,
    cotangent,
):
    bfloat, f32 = jnp.bfloat16, jnp.float32
    seqs, length, width = block_input.shape
    rows_all = seqs * length
    small = lax.axis_size("shard") == 4
    Z = lax.axis_size("ctx")
    shards = [
        w.astype(bfloat) for w in (w_input, w_forget, w_gate, w_out, w_mlp_gate, w_mlp_up, w_down)
    ]
    segs = segment_ids.astype(f32)
    residual_in = block_input.reshape(rows_all, width)
    upstream = cotangent.reshape(rows_all, width)
    channels = lower.shape[0]
    if small:
        link = jnp.concatenate(
            [jnp.ones((seqs, 1), f32), jnp.where(segs[:, 1:] == segs[:, :-1], 1.0, 0.0)], axis=1
        ).reshape(rows_all, 1)
        ids = jnp.broadcast_to(
            jnp.concatenate([segs[:, 0], segs[:, -1]])[:, None], (2 * seqs, channels)
        )
        low_row, gain_row = lower[None, :], hidden_gain[None, :]
        gain_one, gain_two = norm_gain[None, :], mlp_gain[None, :]
        wide, kept = front_all(
            Z, seqs, length, shards, residual_in, upstream, gain_one, gain_two, low_row, gain_row, link, ids
        )
        (normed_one, pi, pf, pg, h, mixed_in, middle, normed_two, gate_pre, up_pre, activated, upstream_low,
         grad_down, rh, start) = kept
        wide_input, wide_forget, wide_gate, wide_out, wide_mgate, wide_mup, wide_down = wide
        silu_mlp = jax.nn.silu(gate_pre)
    else:
        wide = [lax.all_gather(w, ("shard", "ctx"), axis=0, tiled=True) for w in shards]
        wide_input, wide_forget, wide_gate, wide_out, wide_mgate, wide_mup, wide_down = wide
        scale_one = inverse_rms(residual_in)
        normed_one = (residual_in * scale_one * norm_gain).astype(bfloat)
        pi = jnp.dot(normed_one, wide_input, preferred_element_type=f32)
        pf = jnp.dot(normed_one, wide_forget, preferred_element_type=f32)
        pg = jnp.dot(normed_one, wide_gate, preferred_element_type=f32)
        h, mixed_in, rh, start = mixer_forward_plain(
            seqs, length, width, pi, pf, pg, lower, hidden_gain, segs
        )
        mixer_out = lax.psum(times_back(mixed_in, wide_out).astype(bfloat), "tp").astype(f32)
        middle = residual_in + mixer_out
        scale_two = inverse_rms(middle)
        normed_two = (middle * scale_two * mlp_gain).astype(bfloat)
        gate_pre = jnp.dot(normed_two, wide_mgate, preferred_element_type=f32)
        up_pre = jnp.dot(normed_two, wide_mup, preferred_element_type=f32)
        silu_mlp = jax.nn.silu(gate_pre)
        activated = (silu_mlp * up_pre).astype(bfloat)
        upstream_low = upstream.astype(bfloat)
        grad_down = outer_sum(upstream_low, activated).astype(bfloat)
    grad_activ = jnp.dot(upstream_low, wide_down, preferred_element_type=f32)
    grad_gate_pre = (grad_activ * up_pre * silu_slope(gate_pre)).astype(bfloat)
    grad_up_pre = (grad_activ * silu_mlp).astype(bfloat)
    grad_mgate = outer_sum(normed_two, grad_gate_pre).astype(bfloat)
    grad_mup = outer_sum(normed_two, grad_up_pre).astype(bfloat)
    down_part = times_back(activated, wide_down).astype(bfloat)
    normed_part = (times_back(grad_gate_pre, wide_mgate) + times_back(grad_up_pre, wide_mup)).astype(bfloat)
    if small:
        output, grad_resid, vectors, sums = back_all(
            Z, seqs, length, grad_down, grad_mgate, grad_mup, normed_part, down_part, residual_in, middle, upstream,
            normed_one, mixed_in, wide_out, wide_input, wide_forget, wide_gate, pi, pf, pg, h,
            rh, start, ids, link, gain_one, gain_two, low_row, gain_row
        )
        grad_norm_gain, grad_mlp_gain = vectors[0], vectors[1]
        grad_hidden_gain, grad_lower = vectors[2, :channels], vectors[3, :channels]
    else:
        output = middle + lax.psum(down_part, "tp").astype(f32)
        grad_normed_two = lax.psum(normed_part, "tp").astype(f32)
        grad_mlp_gain = jnp.sum(grad_normed_two * middle * scale_two, axis=0)
        grad_middle = upstream + rms_backward(middle, scale_two, mlp_gain, grad_normed_two)
        middle_low = grad_middle.astype(bfloat)
        dm = jnp.dot(middle_low, wide_out, preferred_element_type=f32)
        grad_out = outer_sum(middle_low, mixed_in).astype(bfloat)
        dpi, dpf, dpg, grad_hidden_gain, grad_lower = mixer_backward_plain(
            seqs, length, width, dm, h, pi, pf, pg, lower, hidden_gain, segs, rh, start
        )
        grad_w_input = outer_sum(normed_one, dpi).astype(bfloat)
        grad_w_forget = outer_sum(normed_one, dpf).astype(bfloat)
        grad_w_gate = outer_sum(normed_one, dpg).astype(bfloat)
        grad_normed_one = lax.psum(
            (
                times_back(dpi, wide_input) + times_back(dpf, wide_forget) + times_back(dpg, wide_gate)
            ).astype(bfloat),
            "tp",
        ).astype(f32)
        grad_norm_gain = jnp.sum(grad_normed_one * residual_in * scale_one, axis=0)
        grad_resid = grad_middle + rms_backward(residual_in, scale_one, norm_gain, grad_normed_one)
        vectors = lax.psum(
            jnp.concatenate([grad_norm_gain, grad_mlp_gain, grad_lower, grad_hidden_gain]), ("shard", "ctx")
        )
        grad_norm_gain, grad_mlp_gain = vectors[:width], vectors[width : 2 * width]
        grad_lower = vectors[2 * width : 2 * width + channels]
        grad_hidden_gain = vectors[2 * width + channels :]
        sums = [
            lax.psum_scatter(p, ("shard", "ctx"), scatter_dimension=0, tiled=True).astype(f32)
            for p in (grad_down, grad_mgate, grad_mup, grad_out, grad_w_input, grad_w_forget, grad_w_gate)
        ]
    return (
        output.reshape(block_input.shape),
        grad_resid.reshape(block_input.shape),
        grad_norm_gain,
        grad_lower,
        sums[4],
        sums[5],
        sums[6],
        grad_hidden_gain,
        sums[3],
        grad_mlp_gain,
        sums[1],
        sums[2],
        sums[0],
    )


def solution(mesh):
    return jax.shard_map(
        on_device,
        mesh=mesh,
        in_specs=(
            P("shard", "ctx", None),
            P("shard", "ctx"),
            P(),
            P("tp"),
            P(("shard", "ctx"), "tp"),
            P(("shard", "ctx"), "tp"),
            P(("shard", "ctx"), "tp"),
            P("tp"),
            P(("shard", "ctx"), "tp"),
            P(),
            P(("shard", "ctx"), "tp"),
            P(("shard", "ctx"), "tp"),
            P(("shard", "ctx"), "tp"),
            P("shard", "ctx", None),
        ),
        out_specs=(
            P("shard", "ctx", None),
            P("shard", "ctx", None),
            P(),
            P("tp"),
            P(("shard", "ctx"), "tp"),
            P(("shard", "ctx"), "tp"),
            P(("shard", "ctx"), "tp"),
            P("tp"),
            P(("shard", "ctx"), "tp"),
            P(),
            P(("shard", "ctx"), "tp"),
            P(("shard", "ctx"), "tp"),
            P(("shard", "ctx"), "tp"),
        ),
        check_vma=False,
    )
```

```python
import functools
import jax
import jax.numpy as jnp
from jax import lax
from jax.experimental import pallas as pl
from jax.experimental.pallas import tpu as pltpu
from jax.sharding import PartitionSpec as P

epsilon = 1e-06
MESH = pl.DeviceIdType.MESH


def remote(src, dst, send_sem, recv_sem, device):
    return pltpu.make_async_remote_copy(
        src_ref=src, dst_ref=dst, send_sem=send_sem, recv_sem=recv_sem,
        device_id=device, device_id_type=MESH)


def pick(z, values):
    out = jnp.int32(values[-1])
    for k in range(len(values) - 2, -1, -1):
        out = jnp.where(z == k, values[k], out)
    return out


def far_first(Z):
    table = []
    for z in range(Z):
        ups, dns, mine, turn = list(range(Z - 1, z, -1)), list(range(0, z)), [], z < Z // 2
        while ups or dns:
            if (turn and ups) or not dns:
                mine.append(ups.pop(0))
            else:
                mine.append(dns.pop(0))
            turn = not turn
        table.append(mine + [z])
    return table


class Scatter:
    def __init__(self, Z, parts, rc, xr, zu, zd, hr, outs, xs, zs, stage, fin, sems):
        self.Z, self.parts, self.rc, self.xr, self.zu, self.zd, self.hr, self.outs = Z, parts, rc, xr, zu, zd, hr, outs
        self.xs, self.zs, self.stage, self.fin = xs, zs, stage, fin
        (self.c_s, self.c_r, self.x_s, self.x_r, self.z_s, self.u_r, self.d_r, self.h_s, self.h_r, self.l_s, self.f_s) = sems
        s, z = lax.axis_index("shard"), lax.axis_index("ctx")
        q, c = s // 2, lax.rem(s, 2)
        self.z, self.q, self.c = z, q, c
        self.even = lax.rem(z, 2) == 0
        self.zp = jnp.where(self.even, z + 1, z - 1)
        self.X = {"shard": (1 - q) * 2 + c}
        self.C = {"shard": q * 2 + (1 - c)}
        self.UP, self.DN, self.ZP = {"ctx": z + 1}, {"ctx": z - 1}, {"ctx": self.zp}
        self.R = [p.shape[0] // (4 * Z) for p in parts]
        self.N = [p.shape[1] for p in parts]
        self.ffirst = far_first(Z)

    def part(self, w, q, c, z, n=1):
        R = self.R[w]
        return self.parts[w].at[pl.ds(pl.multiple_of(((2 * q + c) * self.Z + z) * R, R), n * R), :]

    def rows(self, ref, i, w):
        R = self.R[w]
        return ref.at[pl.ds(pl.multiple_of(i * R, R), R), :]

    def hrows(self, ref, i, w, h):
        H = self.R[w] // 2
        return ref.at[pl.ds(pl.multiple_of(i * 2 * H + h * H, H), H), :]

    def c_copy(self, w, k):
        Z, R = self.Z, self.R[w]
        q = self.q if k == 1 else 1 - self.q
        return remote(self.part(w, q, 1 - self.c, 0, Z), self.rc[w].at[pl.ds(k * Z * R, Z * R), :],
                      self.c_s.at[w, k], self.c_r.at[w, k], self.C)

    def c_send(self, w):
        for k in (0, 1):
            self.c_copy(w, k).start()

    def stage_of(self, slot):
        return self.stage[0].at[slot] if slot < 2 else self.stage[1]

    def load_waits(self, w, srcs, slot):
        cps = []
        for i, src in enumerate(srcs):
            if src is not None:
                n = src.shape[0]
                cps.append(pltpu.make_async_copy(
                    src, self.stage_of(slot).at[i, pl.ds(0, n), pl.ds(0, self.N[w])], self.l_s.at[slot, i]))
        return cps

    def load(self, w, srcs, slot):
        cps = self.load_waits(w, srcs, slot)
        for cp in cps:
            cp.start()
        return cps

    def add(self, w, slot, idx, store, lo=0, hi=None, off=None):
        N = self.N[w]
        hi = self.R[w] if hi is None else hi
        G = 16

        def go(i, _):
            r = pl.multiple_of(lo + i * G, G)
            tot = None
            for k in idx:
                rk = r
                if off is not None and k in off:
                    rk = pl.multiple_of(r + off[k], G)
                v = self.stage_of(slot)[k, pl.ds(rk, G), pl.ds(0, N)].astype(jnp.float32)
                tot = v if tot is None else tot + v
            store(r, tot)
            return 0

        lax.fori_loop(0, (hi - lo) // G, go, 0)

    def x_slot(self, w, n):
        return self.xs.at[w % 2, n, :, pl.ds(0, self.N[w])]

    def order(self, n):
        return pick(self.z, [t[n] for t in self.ffirst])

    def x_copy(self, w, n, half=None):
        zt = self.order(n)
        src = self.x_slot(w, n)
        H = self.R[w] // 2
        if half is None:
            return remote(src, self.rows(self.xr[w], zt, w), self.x_s.at[w, n], self.x_r.at[w, n], self.X)
        return remote(src.at[pl.ds(half * H, H), :], self.hrows(self.xr[w], zt, w, half), self.x_s.at[w, n], self.x_r.at[w, n], self.X)

    def h_copy(self, w, n=0):
        H = self.R[w] // 2
        return remote(self.x_slot(w, n).at[pl.ds(0, H), :], self.hr[w], self.h_s.at[w], self.h_r.at[w], self.ZP)

    def on_pair(self, n, yes, no):
        if n == self.Z - 1:
            no()
            return
        paired = self.order(n) == self.zp

        @pl.when(paired)
        def _():
            yes()

        @pl.when(jnp.logical_not(paired))
        def _():
            no()

    def x_load(self, w, n):
        zt = self.order(n)
        return self.load(w, [self.part(w, 1 - self.q, self.c, zt), self.rows(self.rc[w], zt, w)], n % 2)

    def x_phase(self, w, n):
        Z, H = self.Z, self.R[w] // 2
        last = n == Z - 1
        if n == 0:
            self.c_copy(w, 0).wait_recv()
            self.x_load(w, 0)
        if not last:
            self.x_load(w, n + 1)
        if last:
            self.h_copy(w).wait_recv()
            for cp in self.load(w, [None, None, self.hr[w]], n % 2):
                cp.wait()
        if w >= 2:
            self.x_wait_send(w - 2, n)
        zt = self.order(n)
        for cp in self.load_waits(w, [self.part(w, 1 - self.q, self.c, zt), self.rows(self.rc[w], zt, w)], n % 2):
            cp.wait()
        dst = self.x_slot(w, n)

        def store(r, v):
            dst[pl.ds(r, 16), :] = v.astype(jnp.bfloat16)

        if last:
            self.add(w, n % 2, (0, 1, 2), store, 0, H)
            self.add(w, n % 2, (0, 1), store, H, 2 * H)
            self.x_copy(w, n).start()
        else:
            self.add(w, n % 2, (0, 1), store)

            def yes():
                self.h_copy(w, n).start()
                self.x_copy(w, n, 1).start()

            self.on_pair(n, yes, lambda: self.x_copy(w, n).start())

    def x_wait_send(self, w, n):
        def yes():
            self.h_copy(w, n).wait_send()
            self.x_copy(w, n, 1).wait_send()

        self.on_pair(n, yes, lambda: self.x_copy(w, n).wait_send())

    def z_copy(self, w, n, dest, up):
        src = self.zs.at[w % 2, n, :, pl.ds(0, self.N[w])]
        if up:
            return remote(src, self.rows(self.zu[w], dest, w), self.z_s.at[w, n], self.u_r.at[w, dest], self.UP)
        return remote(src, self.rows(self.zd[w], dest, w), self.z_s.at[w, n], self.d_r.at[w, dest], self.DN)

    def x_wait(self, w, n):
        self.on_pair(n, lambda: self.x_copy(w, n, 1).wait_recv(), lambda: self.x_copy(w, n).wait_recv())

    def z_phase(self, w, n):
        Z, H = self.Z, self.R[w] // 2
        z = self.z
        last = n == Z - 1
        dest = z if last else pick(z, [t[n] for t in self.ffirst])
        if n == 0:
            self.c_copy(w, 1).wait_recv()
        self.x_wait(w, n)
        cps = self.load(w, [self.part(w, self.q, self.c, dest), self.rows(self.rc[w], dest + Z, w),
                            self.rows(self.xr[w], dest, w)], 2)
        if not last:
            up = dest > z
            down = dest < z
            has_in = (up & (z > 0)) | (down & (z < Z - 1))

            @pl.when(up & (z > 0))
            def _():
                self.z_copy(w, n, dest, True).wait_recv()
                cp = self.load(w, [None] * 3 + [self.rows(self.zu[w], dest, w)], 2)
                cp[0].wait()

            @pl.when(down & (z < Z - 1))
            def _():
                self.z_copy(w, n, dest, False).wait_recv()
                cp = self.load(w, [None] * 3 + [self.rows(self.zd[w], dest, w)], 2)
                cp[0].wait()

            if w >= 2:
                self.z_wait_send(w - 2, n)
            for cp in cps:
                cp.wait()
            dst = self.zs.at[w % 2, n, :, pl.ds(0, self.N[w])]

            def store(r, v):
                dst[pl.ds(r, 16), :] = v.astype(jnp.bfloat16)

            paired = dest == self.zp
            self.sum_parts(w, paired, has_in, (3,), store)

            @pl.when(up)
            def _():
                self.z_copy(w, n, dest, True).start()

            @pl.when(down)
            def _():
                self.z_copy(w, n, dest, False).start()
        else:
            @pl.when(z > 0)
            def _():
                self.z_copy(w, 0, dest, True).wait_recv()
                cp = self.load(w, [None] * 3 + [self.rows(self.zu[w], dest, w)], 2)
                cp[0].wait()

            @pl.when(z < Z - 1)
            def _():
                self.z_copy(w, 0, dest, False).wait_recv()
                cp = self.load(w, [None] * 4 + [self.rows(self.zd[w], dest, w)], 2)
                cp[0].wait()

            for cp in cps:
                cp.wait()
            if w >= 1:
                self.f_copy(w - 1).wait()
            dst = self.fin.at[:, pl.ds(0, self.N[w])]

            def store(r, v):
                dst[pl.ds(r, 16), :] = v

            @pl.when((z > 0) & (z < Z - 1))
            def _():
                self.add(w, 2, (0, 1, 2, 3, 4), store)

            @pl.when(z == 0)
            def _():
                self.add(w, 2, (0, 1, 2, 4), store)

            @pl.when(z == Z - 1)
            def _():
                self.add(w, 2, (0, 1, 2, 3), store)

            self.f_copy(w).start()

    def sum_parts(self, w, paired, has_in, extra, store):
        H = self.R[w] // 2
        for p in (False, True):
            for e in (False, True):
                cond = (paired if p else jnp.logical_not(paired)) & (has_in if e else jnp.logical_not(has_in))

                @pl.when(cond)
                def _(p=p, e=e):
                    ex = extra if e else ()
                    if p:
                        self.add(w, 2, (0, 1) + ex, store, 0, H)
                        self.add(w, 2, (0, 1, 2) + ex, store, H, 2 * H)
                    else:
                        self.add(w, 2, (0, 1, 2) + ex, store)

    def z_wait_send(self, w, n):
        z = self.z
        dest = pick(z, [t[n] for t in self.ffirst])
        self.z_copy_any(w, n).wait_send()

    def z_copy_any(self, w, n):
        src = self.zs.at[w % 2, n, :, pl.ds(0, self.N[w])]
        return remote(src, self.rows(self.zu[w], 0, w), self.z_s.at[w, n], self.u_r.at[w, 0],
                      {"ctx": jnp.where(pick(self.z, [t[n] for t in self.ffirst]) > self.z, self.z + 1, self.z - 1)})

    def f_copy(self, w):
        return pltpu.make_async_copy(self.fin.at[:, pl.ds(0, self.N[w])], self.outs[w], self.f_s.at[w])

    def drain(self, w, nw):
        for k in (0, 1):
            self.c_copy(w, k).wait_send()
        if w >= nw - 2:
            for n in range(self.Z):
                self.x_wait_send(w, n)
            for n in range(self.Z - 1):
                self.z_wait_send(w, n)
        if w == nw - 1:
            self.f_copy(w).wait()


T8 = 8


def spread(Z, z, pay, box, s_sem, r_sem):
    cps = []
    for o in range(1, Z):
        to = lax.rem(z + o, Z)
        cp = remote(pay, box.at[z], s_sem.at[o - 1], r_sem.at[z], {"ctx": to})
        cp.start()
        cps.append(cp)
    box[z] = pay[...]
    return cps


def spread_wait(Z, z, pay, box, s_sem, r_sem, cps):
    for o in range(1, Z):
        frm = lax.rem(z + o, Z)
        remote(pay, box.at[frm], s_sem.at[o - 1], r_sem.at[frm], {"ctx": frm}).wait_recv()
    for cp in cps:
        cp.wait_send()


def joined(box, k):
    last, first = box[k, 6:8, :], box[k + 1, 4:6, :]
    return jnp.where(last == first, 1.0, 0.0)


def prefix_state(Z, z, box):
    state = jnp.zeros(box.shape[2:][:0] + (2, box.shape[2]), jnp.float32)
    mine = state
    for k in range(Z - 1):
        state = joined(box, k) * (box[k, 2:4, :] + box[k, 0:2, :] * state)
        mine = jnp.where(z == k + 1, state, mine)
    return mine


def suffix_state(Z, z, box):
    state = jnp.zeros((2, box.shape[2]), jnp.float32)
    mine = state
    for k in range(Z - 2, -1, -1):
        state = joined(box, k) * (box[k + 1, 2:4, :] + box[k + 1, 0:2, :] * state)
        mine = jnp.where(z == k, state, mine)
    return mine


def diagonal():
    return lax.broadcasted_iota(jnp.int32, (128, 128), 0) == lax.broadcasted_iota(jnp.int32, (128, 128), 1)


def column_to_rows(col_ref, row_ref, n):
    eye = diagonal()
    for k in range(n // 128):
        col = col_ref[pl.ds(k * 128, 128), :]
        row_ref[k:k + 1, :] = jnp.sum(jnp.where(eye, jnp.broadcast_to(col, (128, 128)), 0.0), axis=0, keepdims=True)


def rows_to_column(row, k):
    return jnp.sum(jnp.where(diagonal(), jnp.broadcast_to(row, (128, 128)), 0.0), axis=1, keepdims=True)


def sigmoid(v):
    return jax.nn.sigmoid(v)


def row_at(ref, t):
    return pl.ds(pl.multiple_of(t, T8), T8)


def forward_scan_one(sq, length, pi, pf, lower, link, h, cum):
    C = pi.shape[1]
    low = lower[...]
    iota = lax.broadcasted_iota(jnp.int32, (T8, C), 0)

    def tile(i, carry):
        hl, pr = carry
        r = row_at(pi, sq * length + i * T8)
        s = sigmoid(pf[r, :])
        forget = low + (1.0 - low) * s
        x = pi[r, :]
        b = x * sigmoid(x) * (1.0 - forget)
        a = forget * link[r, :]
        for sh in (1, 2, 4):
            keep = iota >= sh
            b = b + jnp.where(keep, a * pltpu.roll(b, sh, 0), 0.0)
            a = jnp.where(keep, a * pltpu.roll(a, sh, 0), a)
        b = b + a * hl
        a = a * pr
        h[r, :] = b
        cum[r, :] = a
        return b[T8 - 1:T8, :], a[T8 - 1:T8, :]

    return lax.fori_loop(0, length // T8, tile, (jnp.zeros((1, C), jnp.float32), jnp.ones((1, C), jnp.float32)), unroll=2)


def forward_finish(seqs, length, h, cum, start, col):
    def tile(i, _, sq):
        r = row_at(h, sq * length + i * T8)
        v = h[r, :] + cum[r, :] * start[sq:sq + 1, :]
        h[r, :] = v
        col[r, :] = jnp.sum(v * v, axis=1, keepdims=True)
        return 0

    for sq in range(seqs):
        lax.fori_loop(0, length // T8, functools.partial(tile, sq=sq), 0, unroll=2)


def swap_columns(col, row, got, s_sem, r_sem, other, n):
    column_to_rows(col, row, n)
    cp = remote(row, got, s_sem, r_sem, {"tp": other})
    cp.start()
    cp.wait()


def scale_columns(row, got, col, n, width, fn):
    for k in range(n // 128):
        col[pl.ds(k * 128, 128), :] = fn(rows_to_column(row[k:k + 1, :] + got[k:k + 1, :], k))


def mixed(h, rh, gain, pg, m, step=16):
    g = gain[...]

    def tile(i, _):
        r = pl.ds(pl.multiple_of(i * step, step), step)
        p = pg[r, :]
        m[r, :] = (h[r, :] * rh[r, :] * g * (p * sigmoid(p))).astype(m.dtype)
        return 0

    lax.fori_loop(0, h.shape[0] // step, tile, 0)


def backward_first(n, dm, h, pg, gain, rh, dpg, col, gsum, step=16):
    g = gain[...]

    def tile(i, acc):
        r = pl.ds(pl.multiple_of(i * step, step), step)
        d, hv, p, rv = dm[r, :], h[r, :], pg[r, :], rh[r, :]
        s = sigmoid(p)
        sl = p * s
        q = d * g * sl
        col[r, :] = jnp.sum(q * hv, axis=1, keepdims=True)
        hr = d * hv * rv
        dpg[r, :] = (hr * g * (s * (1.0 + p * (1.0 - s)))).astype(dpg.dtype)
        return acc + jnp.sum(hr * sl, axis=0, keepdims=True)

    gsum[...] = lax.fori_loop(0, n // step, tile, jnp.zeros(gsum.shape, jnp.float32))


def backward_scan_one(sq, length, dm, h, pf, pg, lower, gain, link, rh, inner, gl, tail):
    C = dm.shape[1]
    low, g = lower[...], gain[...]
    iota = lax.broadcasted_iota(jnp.int32, (T8, C), 0)
    nt = length // T8
    def tile(k, carry):
        vl, pr = carry
        r = row_at(dm, sq * length + (nt - 1 - k) * T8)
        rv = rh[r, :]
        p = pg[r, :]
        q = dm[r, :] * g * (p * sigmoid(p))
        dh = q * rv - h[r, :] * (rv * rv * rv) * inner[r, :]
        a = (low + (1.0 - low) * sigmoid(pf[r, :])) * link[r, :]
        b = a * dh
        for sh in (1, 2, 4):
            keep = iota < T8 - sh
            b = b + jnp.where(keep, a * pltpu.roll(b, T8 - sh, 0), 0.0)
            a = jnp.where(keep, a * pltpu.roll(a, T8 - sh, 0), a)
        v = b + a * vl
        pa = a * pr
        last = iota == T8 - 1
        gl[r, :] = dh + jnp.where(last, vl, pltpu.roll(v, T8 - 1, 0))
        tail[r, :] = jnp.where(last, pr, pltpu.roll(pa, T8 - 1, 0))
        return v[0:1, :], pa[0:1, :]

    return lax.fori_loop(0, nt, tile, (jnp.zeros((1, C), jnp.float32), jnp.ones((1, C), jnp.float32)), unroll=2)


def backward_last(seqs, length, gl, tail, end, h, start, pi, pf, lower, link, dpi, dpf, lsum):
    C = gl.shape[1]
    low = lower[...]
    iota = lax.broadcasted_iota(jnp.int32, (T8, C), 0)
    total = jnp.zeros((1, C), jnp.float32)
    for sq in range(seqs):
        def tile(i, carry):
            acc, hp = carry
            halves = []
            for half in (0, 1):
                r = row_at(gl, sq * length + i * 16 + half * T8)
                gv = gl[r, :] + tail[r, :] * end[sq:sq + 1, :]
                hv = h[r, :]
                prev = jnp.where(iota == 0, hp, pltpu.roll(hv, 1, 0) * link[r, :])
                if half == 1:
                    prev = jnp.where(iota == 0, prev * link[r, :], prev)
                else:
                    prev = jnp.where((iota == 0) & (i > 0), prev * link[r, :], prev)
                s = sigmoid(pf[r, :])
                forget = low + (1.0 - low) * s
                x = pi[r, :]
                sx = sigmoid(x)
                df = gv * (prev - x * sx)
                halves.append((gv * (1.0 - forget) * (sx * (1.0 + x * (1.0 - sx))), df * (1.0 - low) * s * (1.0 - s)))
                acc = acc + jnp.sum(df * (1.0 - s), axis=0, keepdims=True)
                hp = hv[T8 - 1:T8, :]
            r = pl.ds(pl.multiple_of(sq * length + i * 16, 16), 16)
            dpi[r, :] = jnp.concatenate([halves[0][0], halves[1][0]], axis=0).astype(dpi.dtype)
            dpf[r, :] = jnp.concatenate([halves[0][1], halves[1][1]], axis=0).astype(dpf.dtype)
            return acc, hp

        total, _ = lax.fori_loop(0, length // 16, tile, (total, start[sq:sq + 1, :]))
    lsum[...] = total


def gather_steps(nw, Z, ahead, relay, own, out, sems):
    (s_up, r_up, s_dn, r_dn, s_x, r_x, s_c, r_c, s_h, r_h, l_sem) = sems
    s, z = lax.axis_index("shard"), lax.axis_index("ctx")
    q, c = s // 2, lax.rem(s, 2)
    sx, sc = (1 - q) * 2 + c, q * 2 + (1 - c)
    sxc = (1 - q) * 2 + (1 - c)
    even = lax.rem(z, 2) == 0
    zp = jnp.where(even, z + 1, z - 1)
    rows = [r.shape[0] for r in own]

    def block(w, s_, z_, part=0):
        R = rows[w]
        start = pl.multiple_of((s_ * Z + z_) * R, R)
        if part == 0:
            return out[w].at[pl.ds(start, R), :]
        H = R // 2
        return out[w].at[pl.ds(pl.multiple_of(start + (part - 1) * H, H), H), :]

    UP, DN, XX, CC, ZP = {"ctx": z + 1}, {"ctx": z - 1}, {"shard": sx}, {"shard": sc}, {"ctx": zp}

    def up(w, k, src=None):
        b = block(w, s, z - k)
        return remote(b if src is None else src, b, s_up.at[w, k], r_up.at[w, k], UP)

    def dn(w, k, src=None):
        b = block(w, s, z + k)
        return remote(b if src is None else src, b, s_dn.at[w, k], r_dn.at[w, k], DN)

    def origin(j):
        return z if j == 0 else (z - j if j < Z else z + j - Z + 1)

    def valid(j):
        return (z >= j) if j < Z else (z + j - Z + 1 <= Z - 1)

    def xx(w, j, part, src=None):
        b = block(w, s, origin(j), part)
        return remote(b if src is None else src, b, s_x.at[w, j], r_x.at[w, j], XX)

    def xx_in(w, j, part):
        b = block(w, sx, origin(j), part)
        return remote(b, b, s_x.at[w, j], r_x.at[w, j], XX)

    def cc(w, j, src=None):
        b = block(w, s if j < 2 * Z - 1 else sx, origin(j % (2 * Z - 1)))
        return remote(b if src is None else src, b, s_c.at[w, j], r_c.at[w, j], CC)

    def cc_in(w, j):
        b = block(w, sc if j < 2 * Z - 1 else sxc, origin(j % (2 * Z - 1)))
        return remote(b, b, s_c.at[w, j], r_c.at[w, j], CC)

    def half(w):
        b = block(w, sx, z, 1)
        return remote(b, b, s_h.at[w], r_h.at[w], ZP)

    def half_in(w):
        b = block(w, sx, zp, 1)
        return remote(b, b, s_h.at[w], r_h.at[w], ZP)

    local = []
    for w in range(nw):
        local.append(pltpu.make_async_copy(own[w], block(w, s, z), l_sem.at[w]))

    def begin(w):
        local[w].start()

        @pl.when(z < Z - 1)
        def _():
            up(w, 0, own[w]).start()

        @pl.when(z > 0)
        def _():
            dn(w, 0, own[w]).start()

        xx(w, 0, 0, own[w]).start()
        cc(w, 0, own[w]).start()

    def is_pair(j):
        if j == 1:
            return jnp.logical_not(even)
        if j == Z:
            return even
        return None

    def for_part(w, j, fn):
        pair = is_pair(j) if relay else None
        if pair is None:
            fn(0)
        else:
            @pl.when(pair)
            def _():
                fn(2)

            @pl.when(jnp.logical_not(pair))
            def _():
                fn(0)

    def step(w, k):
        @pl.when(z >= k)
        def _():
            remote(block(w, s, z - k), block(w, s, z - k), s_up.at[w, k - 1], r_up.at[w, k - 1], UP).wait_recv()
            if k < Z - 1:
                @pl.when(z < Z - 1)
                def _():
                    up(w, k).start()
            for_part(w, k, lambda p: xx(w, k, p).start())
            cc(w, k).start()

        @pl.when(z + k <= Z - 1)
        def _():
            remote(block(w, s, z + k), block(w, s, z + k), s_dn.at[w, k - 1], r_dn.at[w, k - 1], DN).wait_recv()
            if k < Z - 1:
                @pl.when(z > 0)
                def _():
                    dn(w, k).start()
            for_part(w, Z - 1 + k, lambda p: xx(w, Z - 1 + k, p).start())
            cc(w, Z - 1 + k).start()

    def xstep(w, j):
        @pl.when(valid(j))
        def _():
            for_part(w, j, lambda p: xx_in(w, j, p).wait_recv())
            if j == 0:
                if relay:
                    half(w).start()
                cc(w, 2 * Z - 1).start()
            else:
                if relay and is_pair(j) is not None:
                    @pl.when(is_pair(j))
                    def _():
                        half_in(w).wait_recv()
                cc(w, 2 * Z - 1 + j).start()

    def finish(w):
        for j in range(4 * Z - 2):
            @pl.when(valid(j % (2 * Z - 1)))
            def _():
                cc_in(w, j).wait_recv()
                cc(w, j).wait_send()
        for j in range(2 * Z - 1):
            @pl.when(valid(j))
            def _():
                for_part(w, j, lambda p: xx(w, j, p).wait_send())
        for k in range(Z - 1):
            @pl.when((z >= k) & (z < Z - 1))
            def _():
                up(w, k).wait_send()

            @pl.when((z + k <= Z - 1) & (z > 0))
            def _():
                dn(w, k).wait_send()
        if relay:
            half(w).wait_send()
        local[w].wait()

    def tick(w, k):
        step(w, k)
        if k == 1:
            xstep(w, 0)
            if w + ahead < nw:
                begin(w + ahead)
        else:
            xstep(w, k - 1)
            xstep(w, Z - 1 + k - 1)
        if w > 0 and k == 1:
            xstep(w - 1, Z - 1)
            xstep(w - 1, 2 * Z - 2)

    def last():
        xstep(nw - 1, Z - 1)
        xstep(nw - 1, 2 * Z - 2)

    return begin, tick, last, finish


def front_body(Z, seqs, length, ahead, *refs):
    nw = 7
    wide_own = refs[:nw]
    x, cot, gain1, gain2, low, hgain, link, ids = refs[nw:nw + 8]
    k0 = nw + 8
    wide = refs[k0:k0 + nw]
    k0 += nw
    n1_o, pi_o, pf_o, pg_o, h_o, m_o, mid_o, n2_o, gate_o, up_o, act_o, gy_o, gd_o, rh, start = refs[k0:k0 + 15]
    k0 += 15
    (xv, n1, n2, pi, pf, pg, h, cum, m, wbuf, wob, pn, rn, gate, up, act, gy, stg, e_f,
     pay, box, row, got, wst) = refs[k0:k0 + 24]
    own = refs[k0 + 24:k0 + 24 + nw]
    k0 += 24 + nw
    s_c, r_c, s_t, r_t, n_s, n_r, w_s, o_s, e_s, g_s, x_s, f_s = refs[k0:k0 + 12]
    sems = refs[k0 + 12:]
    w_in, w_f, w_g, w_out, w_mg, w_mu, w_dn = wide
    n, width = x.shape
    C, F = pi.shape[1], gate.shape[1]
    s, z, t = lax.axis_index("shard"), lax.axis_index("ctx"), lax.axis_index("tp")
    q, c = s // 2, lax.rem(s, 2)
    OTHER = {"tp": 1 - t}
    begin, tick, last, finish = gather_steps(nw, Z, ahead, True, own, wide, sems)
    NP, NF, NW, NC = n // TR, F // TC, C // TC, width // TC

    def own_load(w):
        return pltpu.make_async_copy(wide_own[w], wst.at[w % 2, :, pl.ds(0, own[w].shape[1])], f_s.at[w % 2])

    def own_low(w):
        own_load(w).wait()
        cols = own[w].shape[1]

        def go(i, _):
            r = pl.ds(pl.multiple_of(i * 16, 16), 16)
            own[w][r, :] = wst[w % 2, r, :cols].astype(jnp.bfloat16)
            return 0

        lax.fori_loop(0, own[w].shape[0] // 16, go, 0)
        if w + 2 < nw:
            own_load(w + 2).start()

    own_load(0).start()
    own_load(1).start()
    barrier = pltpu.get_barrier_semaphore()
    for d in [{"shard": (1 - q) * 2 + c}, {"shard": q * 2 + (1 - c)}, OTHER] + [{"ctx": lax.rem(z + o, Z)} for o in range(1, Z)]:
        pl.semaphore_signal(barrier, inc=1, device_id=d, device_id_type=MESH)
    pl.semaphore_wait(barrier, 2 + Z)

    for w in range(ahead):
        own_low(w)
        begin(w)
    load_x = pltpu.make_async_copy(x, xv, x_s.at[0])
    load_x.start()
    done = []

    def put(src, dst, k):
        cp = pltpu.make_async_copy(src, dst, o_s.at[k])
        cp.start()
        done.append(cp)

    def norm_in():
        load_x.wait()
        g = gain1[...]

        def go(i, _):
            r = pl.ds(pl.multiple_of(i * 16, 16), 16)
            v = xv[r, :]
            n1[r, :] = (v * lax.rsqrt(jnp.mean(v * v, axis=1, keepdims=True) + epsilon) * g).astype(jnp.bfloat16)
            return 0

        lax.fori_loop(0, n // 16, go, 0, unroll=2)
        put(n1, n1_o, 0)

    def times(lhs, w, dst, tiles, after=None):
        def load(j, s):
            return pltpu.make_async_copy(w.at[:, pl.ds(pl.multiple_of(j * TC, TC), TC)], wbuf.at[s], w_s.at[s])

        load(0, 0).start()

        def go(j, _):
            s = lax.rem(j, 2)

            @pl.when(j + 1 < tiles)
            def _():
                load(j + 1, 1 - s).start()

            load(j, s).wait()
            dst[:, pl.ds(pl.multiple_of(j * TC, TC), TC)] = jnp.dot(lhs[...], wbuf[s], preferred_element_type=jnp.float32)
            if after is not None:
                after(j)
            return 0

        lax.fori_loop(0, tiles, go, 0)

    def rows_of(k):
        return pl.ds(k * TR, TR)

    def pn_copy(k):
        return remote(pn.at[rows_of(k), :], rn.at[rows_of(k), :], n_s.at[k], n_r.at[k], OTHER)

    def out_product():
        def load(j, s):
            return pltpu.make_async_copy(w_out.at[pl.ds(pl.multiple_of(j * TC, TC), TC), :], wob.at[s], w_s.at[s])

        load(0, 0).start()

        def go(j, _):
            s = lax.rem(j, 2)

            @pl.when(j + 1 < NC)
            def _():
                load(j + 1, 1 - s).start()

            load(j, s).wait()
            pn[:, pl.ds(pl.multiple_of(j * TC, TC), TC)] = dot_t(m[...], wob[s]).astype(jnp.bfloat16)
            return 0

        lax.fori_loop(0, NC, go, 0)
        for k in range(NP):
            pn_copy(k).start()

    def middle(k):
        pn_copy(k).wait_recv()
        g = gain2[...]

        def go(i, _):
            r = pl.ds(pl.multiple_of(k * TR + i * 16, 16), 16)
            v = xv[r, :] + (pn[r, :].astype(jnp.float32) + rn[r, :].astype(jnp.float32))
            xv[r, :] = v
            n2[r, :] = (v * lax.rsqrt(jnp.mean(v * v, axis=1, keepdims=True) + epsilon) * g).astype(jnp.bfloat16)
            return 0

        lax.fori_loop(0, TR // 16, go, 0)

    def cot_load(k):
        return pltpu.make_async_copy(cot.at[rows_of(k), :], e_f.at[k % 2], e_s.at[k % 2])

    def cot_low():
        cot_load(0).start()
        for k in range(NP):
            if k + 1 < NP:
                cot_load(k + 1).start()
            cot_load(k).wait()
            gy[rows_of(k), :] = e_f[k % 2].astype(jnp.bfloat16)

    def activate(j):
        cols = pl.ds(pl.multiple_of(j * TC, TC), TC)

        def go(i, _):
            r = pl.ds(pl.multiple_of(i * 32, 32), 32)
            v = gate[r, cols]
            act[r, cols] = (v * sigmoid(v) * up[r, cols]).astype(jnp.bfloat16)
            return 0

        lax.fori_loop(0, n // 32, go, 0)

    def gd_copy(j, s):
        return pltpu.make_async_copy(stg.at[s], gd_o.at[pl.ds(pl.multiple_of(j * TC, TC), TC), :], g_s.at[s])

    def down_grad(j0, j1):
        def go(j, _):
            s = lax.rem(j, 2)

            @pl.when(j >= 2)
            def _():
                gd_copy(j - 2, s).wait()

            stg[s] = dot_o(gy[:, pl.ds(pl.multiple_of(j * TC, TC), TC)], act[...]).astype(jnp.bfloat16)
            gd_copy(j, s).start()
            return 0

        lax.fori_loop(j0, j1, go, 0)

    own_low(2)
    norm_in()
    for w in range(3, nw):
        own_low(w)
    for w, src, dst, o, k in ((0, w_in, pi, pi_o, 1), (1, w_f, pf, pf_o, 2), (2, w_g, pg, pg_o, 3)):
        if w == 0:
            tick(0, 1)
            tick(0, 2)
            tick(0, 3)
        tick(w + 1, 1)
        tick(w + 1, 2)
        finish(w)
        times(n1, src, dst, NW)
        put(dst, o, k)
        if w < 2:
            tick(w + 1, 3)
    ends = [forward_scan_one(0, length, pi, pf, low, link, h, cum)]
    tick(3, 3)
    for sq in range(1, seqs):
        ends.append(forward_scan_one(sq, length, pi, pf, low, link, h, cum))
    pay[4:8, :] = ids[...]
    for sq in range(seqs):
        pay[sq:sq + 1, :] = ends[sq][1]
        pay[2 + sq:3 + sq, :] = ends[sq][0]
    cps = spread(Z, z, pay, box, s_c, r_c)
    tick(4, 1)
    cot_low()
    put(gy, gy_o, 4)
    spread_wait(Z, z, pay, box, s_c, r_c, cps)
    start[...] = prefix_state(Z, z, box)
    forward_finish(seqs, length, h, cum, start, rh)
    put(h, h_o, 5)
    swap_columns(rh, row, got, s_t.at[0], r_t.at[0], 1 - t, n)
    scale_columns(row, got, rh, n, width, lambda v: lax.rsqrt(v / width + epsilon))
    mixed(h, rh, hgain, pg, m)
    put(m, m_o, 6)
    tick(4, 2)
    finish(3)
    out_product()
    tick(4, 3)
    for k in range(NP // 2):
        middle(k)
    tick(5, 1)
    for k in range(NP // 2, NP):
        middle(k)
    put(xv, mid_o, 7)
    put(n2, n2_o, 8)
    tick(5, 2)
    finish(4)
    times(n2, w_mg, gate, NF)
    put(gate, gate_o, 9)
    tick(5, 3)
    tick(6, 1)
    finish(5)
    times(n2, w_mu, up, NF, activate)
    put(up, up_o, 10)
    put(act, act_o, 11)
    tick(6, 2)
    down_grad(0, NC // 2)
    tick(6, 3)
    down_grad(NC // 2, NC)
    last()
    finish(6)
    gd_copy(NC - 2, NC % 2).wait()
    gd_copy(NC - 1, (NC - 1) % 2).wait()
    for k in range(NP):
        pn_copy(k).wait_send()
    for cp in done:
        cp.wait()


def front_all(Z, seqs, length, shards, x, cot, gain1, gain2, low, hgain, link, ids, cid=0, ahead=2):
    nw = len(shards)
    n, width = x.shape
    C, F = shards[0].shape[1], shards[4].shape[1]
    dma = pltpu.SemaphoreType.DMA
    bf, f = jnp.bfloat16, jnp.float32
    sh = jax.ShapeDtypeStruct
    anyw, vmem = pl.BlockSpec(memory_space=pl.ANY), pl.BlockSpec(memory_space=pltpu.VMEM)
    NP = n // TR
    V = pltpu.VMEM
    out_shape = ([sh((a.shape[0] * 4 * Z, a.shape[1]), bf) for a in shards]
                 + [sh((n, width), bf)] + [sh((n, C), f)] * 4 + [sh((n, C), bf)] + [sh((n, width), f), sh((n, width), bf)]
                 + [sh((n, F), f)] * 2 + [sh((n, F), bf), sh((n, width), bf), sh((width, F), bf), sh((n, 1), f), sh((seqs, C), f)])
    scratch = [
        V((n, width), f), V((n, width), bf), V((n, width), bf), V((n, C), f), V((n, C), f), V((n, C), f), V((n, C), f), V((n, C), f),
        V((n, C), bf), V((2, width, TC), bf), V((2, TC, C), bf), V((n, width), bf), V((n, width), bf), V((n, F), f), V((n, F), f),
        V((n, F), bf), V((n, width), bf), V((2, TC, F), bf), V((2, TR, width), f),
        V((8, C), f), V((Z, 8, C), f), V((n // 128, 128), f), V((n // 128, 128), f),
        V((2, shards[0].shape[0], F), f),
    ] + [V(a.shape, bf) for a in shards] + [
        dma((Z - 1,)), dma((Z,)), dma((1,)), dma((1,)), dma((NP,)), dma((NP,)), dma((2,)), dma((12,)), dma((2,)), dma((2,)), dma((1,)), dma((2,)),
        dma((nw, Z - 1)), dma((nw, Z - 1)), dma((nw, Z - 1)), dma((nw, Z - 1)),
        dma((nw, 2 * Z - 1)), dma((nw, 2 * Z - 1)),
        dma((nw, 4 * Z - 2)), dma((nw, 4 * Z - 2)), dma((nw,)), dma((nw,)), dma((nw,)),
    ]
    res = pl.pallas_call(
        functools.partial(front_body, Z, seqs, length, ahead),
        out_shape=out_shape,
        in_specs=[anyw] * (nw + 2) + [vmem] * 6,
        out_specs=[anyw] * (len(out_shape) - 2) + [vmem] * 2,
        scratch_shapes=scratch,
        compiler_params=pltpu.CompilerParams(collective_id=cid, has_side_effects=True, vmem_limit_bytes=66_000_000),
        name="forward",
    )(*shards, x, cot, gain1, gain2, low, hgain, link, ids)
    return res[:nw], res[nw:]


TR = 64
TC = 256


def dot_t(a, b):
    return lax.dot_general(a, b, (((1,), (1,)), ((), ())), preferred_element_type=jnp.float32)


def dot_o(a, b):
    return lax.dot_general(a, b, (((0,), (0,)), ((), ())), preferred_element_type=jnp.float32)


def back_body(Z, seqs, length, *refs):
    (gd, gy_h, n2_h, act_h, gate_h, up_h, w_dn, w_mg, w_mu, x, mid, cot, n1, m, w_out, w_in, w_f, w_g,
     pi_h, pf_h, pg_h, h_h, rh, start, ids, link, gain1, gain2, low, hgain) = refs[:30]
    dx, vec_out = refs[30:32]
    grads = refs[32:39]
    mparts = refs[39:45]
    pn, po, rn, ro = refs[45:49]
    k0 = 49
    rc, xr, zu, zd, hr = (refs[k0 + 7 * i:k0 + 7 * (i + 1)] for i in range(5))
    k0 += 35
    (xs, zs, stage, stage_z, fin, dmid, gm, dm, h, pi, pf, pg, gl, tail, dpi, dpf, dpg, n1v, mv, wbuf, tb, du, sn, rn1,
     e_f, e_b, vec, vgot, vbox, col, end, pay, box, row, got) = refs[k0:k0 + 35]
    k0 += 35
    (l_h, l_n, w_s, g_s, n_s, n_r, o_s, o_r, t_s, t_r, e_s, eo_s, v_s, v_r, vz_s, vz_r, s_c, r_c, s_t, r_t, b_s) = refs[k0:k0 + 21]
    sems = refs[k0 + 21:]
    n, width = x.shape
    C = dm.shape[1]
    F = du.shape[1]
    parts = (gd,) + tuple(mparts)
    sc = Scatter(Z, parts, rc, xr, zu, zd, hr, grads, xs, zs, (stage, stage_z), fin, sems)
    z = sc.z
    t = lax.axis_index("tp")
    OTHER = {"tp": 1 - t}

    barrier = pltpu.get_barrier_semaphore()
    for d in [sc.X, sc.C, OTHER] + [{"ctx": lax.rem(z + o, Z)} for o in range(1, Z)]:
        pl.semaphore_signal(barrier, inc=1, device_id=d, device_id_type=MESH)
    pl.semaphore_wait(barrier, 2 + Z)

    sc.c_send(0)

    NP = n // TR
    NC = width // TC

    def rows_of(k):
        return pl.ds(k * TR, TR)

    def pn_copy(k):
        return remote(pn.at[rows_of(k), :], rn.at[rows_of(k), :], n_s.at[k], n_r.at[k], OTHER)

    def po_copy(k):
        return remote(po.at[rows_of(k), :], ro.at[rows_of(k), :], o_s.at[k], o_r.at[k], OTHER)

    early = [pltpu.make_async_copy(a, b, l_h.at[i]) for i, (a, b) in enumerate(
        ((pi_h, pi), (pf_h, pf), (pg_h, pg), (h_h, h), (m, mv), (gy_h, n1v), (n2_h, gm), (mid, dmid)))]
    for cp in early:
        cp.start()
    vec[...] = jnp.zeros_like(vec)

    steps = []

    def X(w):
        return [functools.partial(sc.x_phase, w, k) for k in range(Z)]

    def Zs(w):
        return [functools.partial(sc.z_phase, w, k) for k in range(Z)]

    def tick(*todo):
        for s in todo:
            s()

    def piece(k, s, f_src, b_src):
        r = rows_of(k)
        return ([pltpu.make_async_copy(a.at[r, :], e_f.at[s, i], e_s.at[s, i]) for i, a in enumerate(f_src)]
                + [pltpu.make_async_copy(a.at[r, :], e_b.at[s, i], e_s.at[s, 2 + i]) for i, a in enumerate(b_src)])

    def p1_load(k):
        pn_copy(k).wait_recv()
        for cp in piece(k, k % 2, (cot,), (pn, rn)):
            cp.start()

    def p1(k):
        s = k % 2
        for cp in piece(k, s, (cot,), (pn, rn)):
            cp.wait()
        g = gain2[...]

        def go(i, a):
            r = pl.ds(pl.multiple_of(i * 16, 16), 16)
            rr = pl.ds(pl.multiple_of(k * TR + i * 16, 16), 16)
            v, ct = dmid[rr, :], e_f[s, 0, r, :]
            d = e_b[s, 0, r, :].astype(jnp.float32) + e_b[s, 1, r, :].astype(jnp.float32)
            r2 = lax.rsqrt(jnp.mean(v * v, axis=1, keepdims=True) + epsilon)
            gdn = d * g
            inner = jnp.mean(gdn * v, axis=1, keepdims=True)
            o = ct + gdn * r2 - v * (r2 * r2 * r2 * inner)
            dmid[rr, :] = o
            gm[rr, :] = o.astype(jnp.bfloat16)
            return a + jnp.sum(d * v * r2, axis=0, keepdims=True)

        vec[1:2, :] = vec[1:2, :] + lax.fori_loop(0, TR // 16, go, jnp.zeros((1, width), jnp.float32))

    segments = [(b, a, min(C, F - a)) for b, a in ((dpi, 0), (dpf, C), (dpg, 2 * C))]

    def tile_of(j):
        return pl.ds(pl.multiple_of(j * TC, TC), TC)

    def glu_loads(j, s):
        return [pltpu.make_async_copy(a.at[:, tile_of(j)], b, w_s.at[s, i]) for i, (a, b) in enumerate(
            ((w_dn, wbuf.at[s]), (gate_h, gl.at[:, tile_of(s)]), (up_h, tail.at[:, tile_of(s)])))]

    def glu_cols(g):
        buf, first, size = segments[g]

        def go(j, _):
            s = lax.rem(j, 2)

            @pl.when(j + 1 < F // TC)
            def _():
                for cp in glu_loads(j + 1, 1 - s):
                    cp.start()

            for cp in glu_loads(j, s):
                cp.wait()
            dm[:, :TC] = jnp.dot(n1v[...], wbuf[s], preferred_element_type=jnp.float32)
            here, there = tile_of(s), tile_of(j)
            inside = tile_of(j - first // TC)

            def rows(i, _):
                r = pl.ds(pl.multiple_of(i * 32, 32), 32)
                v, u, d = gl[r, here], tail[r, here], dm[r, :TC]
                sg = sigmoid(v)
                buf[r, inside] = (d * u * (sg * (1.0 + v * (1.0 - sg)))).astype(jnp.bfloat16)
                du[r, there] = (d * (v * sg)).astype(jnp.bfloat16)
                return 0

            lax.fori_loop(0, n // 32, rows, 0)
            return 0

        lax.fori_loop(first // TC, (first + size) // TC, go, 0)

    def w_rows(w, j, s):
        return pltpu.make_async_copy(w.at[tile_of(j), :], tb.at[s, :, pl.ds(0, F)], w_s.at[2 + s, 0])

    def sn_out(dst, j):
        return pltpu.make_async_copy(sn.at[j], dst.at[:, tile_of(j)], b_s.at[j])

    def normed(j0, j1):
        def go(j, _):
            w_rows(w_mg, j, 0).wait()
            o = None
            for buf, first, size in segments:
                v = dot_t(buf[:, :size], tb[0, :, first:first + size])
                o = v if o is None else o + v

            @pl.when(j + 1 < NC)
            def _():
                w_rows(w_mg, j + 1, 0).start()

            w_rows(w_mu, j, 1).wait()
            o = o + dot_t(du[...], tb[1, :, :F])

            @pl.when(j + 1 < NC)
            def _():
                w_rows(w_mu, j + 1, 1).start()

            sn[j] = o.astype(jnp.bfloat16)
            sn_out(pn, j).start()
            return 0

        lax.fori_loop(j0, j1, go, 0)

    def t_copy(dst, j, s):
        return pltpu.make_async_copy(tb.at[s, :, pl.ds(0, dst.shape[1])], dst.at[tile_of(j), :], g_s.at[s])

    def glu_grad(w, cols, j0, j1):
        dst = parts[w]

        def go(j, _):
            s = lax.rem(j, 2)

            @pl.when(j >= 2)
            def _():
                t_copy(dst, j - 2, s).wait()

            lhs = gm[:, tile_of(j)]
            for buf, first, size in cols:
                tb[s, :, first:first + size] = dot_o(lhs, buf[:, :size]).astype(jnp.bfloat16)
            t_copy(dst, j, s).start()
            return 0

        lax.fori_loop(j0, j1, go, 0)
        if j1 == NC:
            t_copy(dst, NC - 2, NC % 2).wait()
            t_copy(dst, NC - 1, (NC - 1) % 2).wait()
            sc.c_send(w)

    def down(j0, j1):
        def go(j, _):
            s = lax.rem(j, 2)

            @pl.when(j + 1 < NC)
            def _():
                w_rows(w_dn, j + 1, 1 - s).start()

            w_rows(w_dn, j, s).wait()
            sn[j] = dot_t(du[...], tb[s, :, :F]).astype(jnp.bfloat16)
            sn_out(po, j).start()
            return 0

        lax.fori_loop(j0, j1, go, 0)

    NW = C // TC

    def w_load(j, s):
        return pltpu.make_async_copy(w_out.at[:, pl.ds(pl.multiple_of(j * TC, TC), TC)], wbuf.at[s], w_s.at[s, 0])

    def p2():
        w_load(0, 0).start()

        def go(j, _):
            s = lax.rem(j, 2)

            @pl.when(j + 1 < NW)
            def _():
                w_load(j + 1, 1 - s).start()

            w_load(j, s).wait()
            dm[:, pl.ds(pl.multiple_of(j * TC, TC), TC)] = jnp.dot(gm[...], wbuf[s], preferred_element_type=jnp.float32)
            return 0

        lax.fori_loop(0, NW, go, 0)

    def p4(w, lhs, rhs):
        dst = parts[w]

        def go(j, _):
            s = lax.rem(j, 2)

            @pl.when(j >= 2)
            def _():
                t_copy(dst, j - 2, s).wait()

            tb[s, :, :C] = dot_o(lhs[:, tile_of(j)], rhs[...]).astype(jnp.bfloat16)
            t_copy(dst, j, s).start()
            return 0

        lax.fori_loop(0, NC, go, 0)
        t_copy(dst, NC - 2, NC % 2).wait()
        t_copy(dst, NC - 1, (NC - 1) % 2).wait()
        sc.c_send(w)

    def w3(j, s):
        return [pltpu.make_async_copy(a.at[tile_of(j), :], tb.at[s, :, pl.ds(i * C, C)], w_s.at[2 + s, i])
                for i, a in enumerate((w_in, w_f, w_g))]

    def w3_start(j, s):
        for cp in w3(j, s):
            cp.start()

    def w3_wait(j, s):
        for cp in w3(j, s):
            cp.wait()

    def n_copy(j):
        return remote(sn.at[j], rn1.at[j], t_s.at[j], t_r.at[j], OTHER)

    def p5(j0, j1):
        def go(j, _):
            s = lax.rem(j, 2)

            @pl.when(j + 1 < NC)
            def _():
                w3_start(j + 1, 1 - s)

            w3_wait(j, s)
            o = dot_t(dpi[...], tb[s, :, :C]) + dot_t(dpf[...], tb[s, :, C:2 * C]) + dot_t(dpg[...], tb[s, :, 2 * C:3 * C])
            sn[j] = o.astype(jnp.bfloat16)
            n_copy(j).start()
            return 0

        lax.fori_loop(j0, j1, go, 0)

    def x_load(j, s):
        return pltpu.make_async_copy(x.at[:, pl.ds(j * TC, TC)], tail.at[:, pl.ds(s * TC, TC)], e_s.at[s, 0])

    def p6a(j):
        s = j % 2
        if j == 0:
            x_load(0, 0).start()
        if j + 1 < NC:
            x_load(j + 1, 1 - s).start()
        x_load(j, s).wait()
        n_copy(j).wait_recv()
        g = gain1[:, j * TC:(j + 1) * TC]

        def go(i, _):
            r = pl.ds(pl.multiple_of(i * 16, 16), 16)
            v = tail[r, s * TC:(s + 1) * TC]
            d = sn[j, r, :].astype(jnp.float32) + rn1[j, r, :].astype(jnp.float32)
            a, b = v * v, d * g * v
            a, b = a[:, :128] + a[:, 128:], b[:, :128] + b[:, 128:]
            if j == 0:
                dm[r, :128] = a
                dm[r, 128:256] = b
            else:
                dm[r, :128] = dm[r, :128] + a
                dm[r, 128:256] = dm[r, 128:256] + b
            return 0

        lax.fori_loop(0, n // 16, go, 0, unroll=2)

    def p6b():
        def go(i, _):
            r = pl.ds(pl.multiple_of(i * 16, 16), 16)
            r1 = lax.rsqrt(jnp.sum(dm[r, :128], axis=1, keepdims=True) / width + epsilon)
            inner = jnp.sum(dm[r, 128:256], axis=1, keepdims=True) / width
            dm[r, :128] = jnp.broadcast_to(r1, (16, 128))
            dm[r, 128:256] = jnp.broadcast_to(r1 * r1 * r1 * inner, (16, 128))
            return 0

        lax.fori_loop(0, n // 16, go, 0, unroll=2)

    def dx_copy(j):
        s = j % 2
        return pltpu.make_async_copy(gl.at[:, pl.ds(s * TC, TC)], dx.at[:, pl.ds(j * TC, TC)], eo_s.at[s])

    def p6c(j):
        s = j % 2
        if j == 0:
            x_load(0, 0).start()
        if j + 1 < NC:
            x_load(j + 1, 1 - s).start()
        x_load(j, s).wait()
        if j >= 2:
            dx_copy(j - 2).wait()
        g = gain1[:, j * TC:(j + 1) * TC]

        def go(i, total):
            r = pl.ds(pl.multiple_of(i * 16, 16), 16)
            v = tail[r, s * TC:(s + 1) * TC]
            d = sn[j, r, :].astype(jnp.float32) + rn1[j, r, :].astype(jnp.float32)
            r1 = jnp.concatenate([dm[r, :128], dm[r, :128]], axis=1)
            ri = jnp.concatenate([dm[r, 128:256], dm[r, 128:256]], axis=1)
            gl[r, s * TC:(s + 1) * TC] = dmid[r, j * TC:(j + 1) * TC] + d * g * r1 - v * ri
            return total + jnp.sum(d * v * r1, axis=0, keepdims=True)

        vec[0:1, j * TC:(j + 1) * TC] = lax.fori_loop(0, n // 16, go, jnp.zeros((1, TC), jnp.float32), unroll=2)
        dx_copy(j).start()

    x0, x1, x2, z0, z1, z2 = X(0), X(1), X(2), Zs(0), Zs(1), Zs(2)
    x3, x4, x5, x6 = X(3), X(4), X(5), X(6)
    z3, z4, z5, z6 = Zs(3), Zs(4), Zs(5), Zs(6)
    for cp in glu_loads(0, 0):
        cp.start()
    early[5].wait()
    glu_cols(0)
    tick(x0[0])
    glu_cols(1)
    tick(x0[1])
    w_rows(w_mg, 0, 0).start()
    w_rows(w_mu, 0, 1).start()
    glu_cols(2)
    tick(x0[2])
    load_n1 = pltpu.make_async_copy(n1, n1v, l_h.at[5])
    load_n1.start()
    normed(0, NC // 2)
    tick(x0[3], z0[0])
    normed(NC // 2, NC)
    for j in range(NC):
        sn_out(pn, j).wait()
    for k in range(NP):
        pn_copy(k).start()
    tick(z0[1])
    early[6].wait()
    glu_grad(1, segments, 0, NC // 2)
    tick(z0[2])
    glu_grad(1, segments, NC // 2, NC)
    tick(z0[3])
    glu_grad(2, [(du, 0, F)], 0, NC // 2)
    tick(x1[0])
    glu_grad(2, [(du, 0, F)], NC // 2, NC)
    load_act = pltpu.make_async_copy(act_h, du, l_h.at[6])
    load_act.start()
    w_rows(w_dn, 0, 0).start()
    tick(x1[1])
    load_act.wait()
    down(0, NC // 2)
    tick(x1[2])
    down(NC // 2, NC)
    for j in range(NC):
        sn_out(po, j).wait()
    for k in range(NP):
        po_copy(k).start()
    p1_load(0)
    tick(x1[3], z1[0])
    early[7].wait()
    between = [[z1[1]], [x2[0]], [x2[1]], [z1[2]], [x2[2]], [], [z1[3]], [x2[3]]]
    for k in range(NP):
        if k + 1 < NP:
            p1_load(k + 1)
        p1(k)
        tick(*(between[k] if k < len(between) else []))
    p2()
    tick(z2[0])
    for cp in early[:5]:
        cp.wait()
    load_n1.wait()
    p4(3, gm, mv)
    tick(z2[1])
    backward_first(n, dm, h, pg, hgain, rh, dpg, col, acc_row(vec, 2, C))
    column_to_rows(col, row, n)
    swap = remote(row, got, s_t.at[0], r_t.at[0], OTHER)
    swap.start()
    tick(x3[0], x3[1])
    swap.wait()
    scale_columns(row, got, col, n, width, lambda v: v / width)
    ends = []
    for sq in range(seqs):
        ends.append(backward_scan_one(sq, length, dm, h, pf, pg, low, hgain, link, rh, col, gl, tail))
        if sq == 0:
            tick(z2[2])
    pay[4:8, :] = ids[...]
    for sq in range(seqs):
        pay[sq:sq + 1, :] = ends[sq][1]
        pay[2 + sq:3 + sq, :] = ends[sq][0]
    cps = spread(Z, z, pay, box, s_c, r_c)
    tick(x3[2], x3[3], z2[3])
    spread_wait(Z, z, pay, box, s_c, r_c, cps)
    end[...] = suffix_state(Z, z, box)
    backward_last(seqs, length, gl, tail, end, h, start, pi, pf, low, link, dpi, dpf, acc_row(vec, 3, C))
    tick(z3[0])
    p4(4, n1v, dpi)
    tick(z3[1], x4[0], x4[1])
    p4(5, n1v, dpf)
    tick(x4[2], x4[3], z3[2])
    p4(6, n1v, dpg)
    w3_start(0, 0)
    tick(z3[3], x5[0], x5[1])
    p5(0, NC // 2)
    tick(x5[2], x5[3], z4[0], z4[1])
    p5(NC // 2, NC)
    tick(z4[2], z4[3], *x6)
    for j in range(NC):
        p6a(j)
        if j % 4 == 3 and j // 4 < 2:
            tick(z5[j // 4])
    p6b()
    for j in range(NC):
        p6c(j)
        if j % 4 == 3 and j // 4 < 2:
            tick(z5[2 + j // 4])
    for j in (NC - 2, NC - 1):
        dx_copy(j).wait()
    first = remote(vec, vgot.at[0], v_s.at[0], v_r.at[0], sc.C)
    first.start()
    tick(z6[0])
    first.wait()
    vec[...] = vec[...] + vgot[0]
    second = remote(vec, vgot.at[1], v_s.at[1], v_r.at[1], sc.X)
    second.start()
    tick(z6[1])
    second.wait()
    vec[...] = vec[...] + vgot[1]
    cps = spread(Z, z, vec, vbox, vz_s, vz_r)
    tick(z6[2], z6[3])
    spread_wait(Z, z, vec, vbox, vz_s, vz_r, cps)
    total = vbox[0]
    for k in range(1, Z):
        total = total + vbox[k]
    vec_out[...] = total
    for k in range(NP):
        pn_copy(k).wait_send()
        po_copy(k).wait_send()
        po_copy(k).wait_recv()
    for j in range(NC):
        n_copy(j).wait_send()
    for w in range(7):
        sc.drain(w, 7)


def acc_row(vec, k, C):
    return vec.at[k:k + 1, pl.ds(0, C)]


def back_all(Z, seqs, length, gd, gy, n2, act, gate, up, w_dn, w_mg, w_mu, x, mid, cot, n1, m, w_out, w_in, w_f, w_g,
             pi, pf, pg, h, rh, start, ids, link, gain1, gain2, low, hgain, cid=1):
    n, width = x.shape
    C, F = pi.shape[1], gate.shape[1]
    dma = pltpu.SemaphoreType.DMA
    bf, f = jnp.bfloat16, jnp.float32
    sh = jax.ShapeDtypeStruct
    anyw, vmem = pl.BlockSpec(memory_space=pl.ANY), pl.BlockSpec(memory_space=pltpu.VMEM)
    shapes = [(width, F)] * 3 + [(width, C)] * 4
    R = [s[0] // (4 * Z) for s in shapes]
    N = [s[1] for s in shapes]
    Rm, Nm = max(R), max(N)
    NP, NC = n // TR, width // TC
    out_shape = ([sh((n, width), f), sh((8, width), f)]
                 + [sh((r, k), f) for r, k in zip(R, N)]
                 + [sh((width, F), bf)] * 2 + [sh((width, C), bf)] * 4
                 + [sh((n, width), bf)] * 4
                 + [sh((2 * Z * r, k), bf) for r, k in zip(R, N)]
                 + [sh((Z * r, k), bf) for r, k in zip(R, N)]
                 + [sh((Z * r, k), bf) for r, k in zip(R, N)]
                 + [sh((Z * r, k), bf) for r, k in zip(R, N)]
                 + [sh((r // 2, k), bf) for r, k in zip(R, N)])
    V = pltpu.VMEM
    scratch = [
        V((2, Z, Rm, Nm), bf), V((2, Z - 1, Rm, Nm), bf), V((2, 3, Rm, Nm), bf), V((5, Rm, Nm), bf), V((Rm, Nm), f),
        V((n, width), f), V((n, width), bf), V((n, C), f), V((n, C), f), V((n, C), f), V((n, C), f), V((n, C), f),
        V((n, C), f), V((n, C), f), V((n, C), bf), V((n, C), bf), V((n, C), bf), V((n, width), bf), V((n, C), bf),
        V((2, width, TC), bf), V((2, TC, 3 * C), bf), V((n, F), bf), V((NC, n, TC), bf), V((NC, n, TC), bf),
        V((2, 1, TR, width), f), V((2, 2, TR, width), bf), V((8, width), f), V((2, 8, width), f), V((Z, 8, width), f),
        V((n, 1), f), V((seqs, C), f), V((8, C), f), V((Z, 8, C), f), V((n // 128, 128), f), V((n // 128, 128), f),
        dma((8,)), dma((1,)), dma((4, 3)), dma((2,)), dma((NP,)), dma((NP,)), dma((NP,)), dma((NP,)), dma((NC,)), dma((NC,)),
        dma((2, 4)), dma((2,)), dma((2,)), dma((2,)), dma((Z - 1,)), dma((Z,)), dma((Z - 1,)), dma((Z,)), dma((1,)), dma((1,)),
        dma((NC,)),
        dma((7, 2)), dma((7, 2)), dma((7, Z)), dma((7, Z)), dma((7, Z - 1)), dma((7, Z)), dma((7, Z)),
        dma((7,)), dma((7,)), dma((3, 5)), dma((7,)),
    ]
    res = pl.pallas_call(
        functools.partial(back_body, Z, seqs, length),
        out_shape=out_shape,
        in_specs=[anyw] * 22 + [vmem] * 8,
        out_specs=[anyw, vmem] + [anyw] * (len(out_shape) - 2),
        scratch_shapes=scratch,
        compiler_params=pltpu.CompilerParams(collective_id=cid, has_side_effects=True, vmem_limit_bytes=66_000_000),
        name="backward",
    )(gd, gy, n2, act, gate, up, w_dn, w_mg, w_mu, x, mid, cot, n1, m, w_out, w_in, w_f, w_g, pi, pf, pg, h,
      rh, start, ids, link, gain1, gain2, low, hgain)
    return res[0], res[1], res[2:9], res[16], res[18]


def carried_in(x, axis, combine, identity, reverse):
    size, position = (lax.axis_size(axis), lax.axis_index(axis))
    everything = jax.tree.map(lambda part: lax.all_gather(part, axis), x)
    start = jax.tree.map(
        lambda part, zero: jnp.broadcast_to(jnp.asarray(zero, part.dtype), part.shape), x, identity
    )

    def turn(k, before):
        at = size - 1 - k if reverse else k
        reached = at > position if reverse else at < position
        new = combine(before, jax.tree.map(lambda part: part[at], everything))
        return jax.tree.map(lambda a, b: jnp.where(reached, a, b), new, before)

    return lax.fori_loop(0, size, turn, start)


def inverse_rms(inputs):
    return lax.rsqrt(jnp.mean(inputs * inputs, axis=-1, keepdims=True) + epsilon)


def rms_backward(inputs, row_scale, gain_vec, upstream):
    weighted = upstream * gain_vec
    inner_sum = jnp.mean(weighted * inputs, axis=-1, keepdims=True)
    return weighted * row_scale - inputs * (row_scale * row_scale * row_scale) * inner_sum


def silu_slope(inputs):
    sig_part = jax.nn.sigmoid(inputs)
    return sig_part * (1.0 + inputs * (1.0 - sig_part))


def times_back(left_mat, right_mat):
    return lax.dot_general(
        left_mat, right_mat, (((1,), (1,)), ((), ())), preferred_element_type=jnp.float32
    )


def outer_sum(left_mat, right_mat):
    return lax.dot_general(
        left_mat, right_mat, (((0,), (0,)), ((), ())), preferred_element_type=jnp.float32
    )


def linear_step(first_part, second_part):
    return (first_part[0] * second_part[0], second_part[0] * first_part[1] + second_part[1])


def joined_ids(last_ids, first_ids):
    return jnp.where((last_ids == first_ids) | (last_ids < 0.0) | (first_ids < 0.0), 1.0, 0.0)


def forward_join(first_part, second_part):
    linked = joined_ids(first_part[3], second_part[2])[:, None]
    return (
        first_part[0] * second_part[0] * linked,
        second_part[0] * linked * first_part[1] + second_part[1],
        jnp.where(first_part[2] < 0.0, second_part[2], first_part[2]),
        jnp.where(second_part[3] < 0.0, first_part[3], second_part[3]),
    )


def backward_join(first_part, second_part):
    linked = joined_ids(second_part[3], first_part[2])[:, None]
    return (
        second_part[0] * linked * first_part[0],
        second_part[0] * linked * first_part[1] + second_part[1],
        jnp.where(second_part[2] < 0.0, first_part[2], second_part[2]),
        jnp.where(first_part[3] < 0.0, second_part[3], first_part[3]),
    )


def mixer_forward_plain(seqs, length, width, pi, pf, pg, lower, gain, segs):
    channels = pi.shape[1]
    forget = lower + (1.0 - lower) * jax.nn.sigmoid(pf)
    candidate = jax.nn.silu(pi) * (1.0 - forget)
    inner_link = jnp.concatenate(
        [jnp.ones((seqs, 1), jnp.float32), jnp.where(segs[:, 1:] == segs[:, :-1], 1.0, 0.0)], axis=1
    )
    decay = forget.reshape(seqs, length, channels) * inner_link[:, :, None]
    prod, local = lax.associative_scan(
        linear_step, (decay, candidate.reshape(seqs, length, channels)), axis=1
    )
    first, last = segs[:, 0], segs[:, -1]
    ones, zero = jnp.ones((seqs, channels), jnp.float32), jnp.zeros((seqs, channels), jnp.float32)
    minus = -jnp.ones((seqs,), jnp.float32)
    prefix = carried_in(
        (prod[:, -1], local[:, -1], first, last), "ctx", forward_join, (ones, zero, minus, minus), False
    )
    start = joined_ids(prefix[3], first)[:, None] * prefix[1]
    h = (local + prod * start[:, None, :]).reshape(seqs * length, channels)
    squares = lax.psum(jnp.sum(h * h, axis=1), "tp")
    rh = lax.rsqrt(squares / width + epsilon)[:, None]
    m = (h * rh * gain * jax.nn.silu(pg)).astype(jnp.bfloat16)
    return h, m, rh, start


def mixer_backward_plain(seqs, length, width, dm, h, pi, pf, pg, lower, gain, segs, rh, start):
    channels = pi.shape[1]
    s = jax.nn.sigmoid(pf)
    forget = lower + (1.0 - lower) * s
    inner_link = jnp.concatenate(
        [jnp.ones((seqs, 1), jnp.float32), jnp.where(segs[:, 1:] == segs[:, :-1], 1.0, 0.0)], axis=1
    )
    forget_seq = forget.reshape(seqs, length, channels)
    decay = forget_seq * inner_link[:, :, None]
    silu_gate = jax.nn.silu(pg)
    weighted = dm * gain * silu_gate
    inner = lax.psum(jnp.sum(weighted * h, axis=1), "tp")
    dh = weighted * rh - h * (rh * rh * rh) * (inner / width)[:, None]
    gain_grad = jnp.sum(dm * h * rh * silu_gate, axis=0)
    dpg = (dm * h * rh * gain * silu_slope(pg)).astype(jnp.bfloat16)
    ones_row = jnp.ones((seqs, 1, channels), jnp.float32)
    following = jnp.concatenate([decay[:, 1:], ones_row], axis=1)
    tail, local = lax.associative_scan(
        linear_step, (following, dh.reshape(seqs, length, channels)), reverse=True, axis=1
    )
    first, last = segs[:, 0], segs[:, -1]
    ones, zero = jnp.ones((seqs, channels), jnp.float32), jnp.zeros((seqs, channels), jnp.float32)
    minus = -jnp.ones((seqs,), jnp.float32)
    suffix = carried_in(
        (decay[:, 0] * tail[:, 0], forget_seq[:, 0] * local[:, 0], first, last),
        "ctx", backward_join, (ones, zero, minus, minus), True,
    )
    end = joined_ids(last, suffix[2])[:, None] * suffix[1]
    g = (local + tail * end[:, None, :]).reshape(seqs * length, channels)
    states = h.reshape(seqs, length, channels)
    previous = jnp.concatenate(
        [start[:, None, :], inner_link[:, 1:, None] * states[:, :-1]], axis=1
    ).reshape(seqs * length, channels)
    dforget = g * (previous - jax.nn.silu(pi))
    dpi = (g * (1.0 - forget) * silu_slope(pi)).astype(jnp.bfloat16)
    dpf = (dforget * (1.0 - lower) * s * (1.0 - s)).astype(jnp.bfloat16)
    return dpi, dpf, dpg, gain_grad, jnp.sum(dforget * (1.0 - s), axis=0)


def on_device(
    block_input,
    segment_ids,
    norm_gain,
    lower,
    w_input,
    w_forget,
    w_gate,
    hidden_gain,
    w_out,
    mlp_gain,
    w_mlp_gate,
    w_mlp_up,
    w_down,
    cotangent,
):
    bfloat, f32 = jnp.bfloat16, jnp.float32
    seqs, length, width = block_input.shape
    rows_all = seqs * length
    small = lax.axis_size("shard") == 4
    Z = lax.axis_size("ctx")
    shards = [w_input, w_forget, w_gate, w_out, w_mlp_gate, w_mlp_up, w_down]
    segs = segment_ids.astype(f32)
    residual_in = block_input.reshape(rows_all, width)
    upstream = cotangent.reshape(rows_all, width)
    channels = lower.shape[0]
    if small:
        link = jnp.concatenate(
            [jnp.ones((seqs, 1), f32), jnp.where(segs[:, 1:] == segs[:, :-1], 1.0, 0.0)], axis=1
        ).reshape(rows_all, 1)
        ids = jnp.broadcast_to(
            jnp.concatenate([segs[:, 0], segs[:, -1]])[:, None], (2 * seqs, channels)
        )
        low_row, gain_row = lower[None, :], hidden_gain[None, :]
        gain_one, gain_two = norm_gain[None, :], mlp_gain[None, :]
        wide, kept = front_all(
            Z, seqs, length, shards, residual_in, upstream, gain_one, gain_two, low_row, gain_row, link, ids
        )
        (normed_one, pi, pf, pg, h, mixed_in, middle, normed_two, gate_pre, up_pre, activated, upstream_low,
         grad_down, rh, start) = kept
        wide_input, wide_forget, wide_gate, wide_out, wide_mgate, wide_mup, wide_down = wide
        grad_resid, vectors, sums, down_mine, down_other = back_all(
            Z, seqs, length, grad_down, upstream_low, normed_two, activated, gate_pre, up_pre, wide_down, wide_mgate,
            wide_mup, residual_in, middle, upstream, normed_one, mixed_in, wide_out, wide_input, wide_forget, wide_gate,
            pi, pf, pg, h, rh, start, ids, link, gain_one, gain_two, low_row, gain_row
        )
        output = middle + (down_mine.astype(f32) + down_other.astype(f32))
        grad_norm_gain, grad_mlp_gain = vectors[0], vectors[1]
        grad_hidden_gain, grad_lower = vectors[2, :channels], vectors[3, :channels]
    else:
        wide = [lax.all_gather(w.astype(bfloat), ("shard", "ctx"), axis=0, tiled=True) for w in shards]
        wide_input, wide_forget, wide_gate, wide_out, wide_mgate, wide_mup, wide_down = wide
        scale_one = inverse_rms(residual_in)
        normed_one = (residual_in * scale_one * norm_gain).astype(bfloat)
        pi = jnp.dot(normed_one, wide_input, preferred_element_type=f32)
        pf = jnp.dot(normed_one, wide_forget, preferred_element_type=f32)
        pg = jnp.dot(normed_one, wide_gate, preferred_element_type=f32)
        h, mixed_in, rh, start = mixer_forward_plain(
            seqs, length, width, pi, pf, pg, lower, hidden_gain, segs
        )
        mixer_out = lax.psum(times_back(mixed_in, wide_out).astype(bfloat), "tp").astype(f32)
        middle = residual_in + mixer_out
        scale_two = inverse_rms(middle)
        normed_two = (middle * scale_two * mlp_gain).astype(bfloat)
        gate_pre = jnp.dot(normed_two, wide_mgate, preferred_element_type=f32)
        up_pre = jnp.dot(normed_two, wide_mup, preferred_element_type=f32)
        silu_mlp = jax.nn.silu(gate_pre)
        activated = (silu_mlp * up_pre).astype(bfloat)
        upstream_low = upstream.astype(bfloat)
        grad_down = outer_sum(upstream_low, activated).astype(bfloat)
        grad_activ = jnp.dot(upstream_low, wide_down, preferred_element_type=f32)
        grad_gate_pre = (grad_activ * up_pre * silu_slope(gate_pre)).astype(bfloat)
        grad_up_pre = (grad_activ * silu_mlp).astype(bfloat)
        grad_mgate = outer_sum(normed_two, grad_gate_pre).astype(bfloat)
        grad_mup = outer_sum(normed_two, grad_up_pre).astype(bfloat)
        down_part = times_back(activated, wide_down).astype(bfloat)
        normed_part = (times_back(grad_gate_pre, wide_mgate) + times_back(grad_up_pre, wide_mup)).astype(bfloat)
        output = middle + lax.psum(down_part, "tp").astype(f32)
        grad_normed_two = lax.psum(normed_part, "tp").astype(f32)
        grad_mlp_gain = jnp.sum(grad_normed_two * middle * scale_two, axis=0)
        grad_middle = upstream + rms_backward(middle, scale_two, mlp_gain, grad_normed_two)
        middle_low = grad_middle.astype(bfloat)
        dm = jnp.dot(middle_low, wide_out, preferred_element_type=f32)
        grad_out = outer_sum(middle_low, mixed_in).astype(bfloat)
        dpi, dpf, dpg, grad_hidden_gain, grad_lower = mixer_backward_plain(
            seqs, length, width, dm, h, pi, pf, pg, lower, hidden_gain, segs, rh, start
        )
        grad_w_input = outer_sum(normed_one, dpi).astype(bfloat)
        grad_w_forget = outer_sum(normed_one, dpf).astype(bfloat)
        grad_w_gate = outer_sum(normed_one, dpg).astype(bfloat)
        grad_normed_one = lax.psum(
            (
                times_back(dpi, wide_input) + times_back(dpf, wide_forget) + times_back(dpg, wide_gate)
            ).astype(bfloat),
            "tp",
        ).astype(f32)
        grad_norm_gain = jnp.sum(grad_normed_one * residual_in * scale_one, axis=0)
        grad_resid = grad_middle + rms_backward(residual_in, scale_one, norm_gain, grad_normed_one)
        vectors = lax.psum(
            jnp.concatenate([grad_norm_gain, grad_mlp_gain, grad_lower, grad_hidden_gain]), ("shard", "ctx")
        )
        grad_norm_gain, grad_mlp_gain = vectors[:width], vectors[width : 2 * width]
        grad_lower = vectors[2 * width : 2 * width + channels]
        grad_hidden_gain = vectors[2 * width + channels :]
        sums = [
            lax.psum_scatter(p, ("shard", "ctx"), scatter_dimension=0, tiled=True).astype(f32)
            for p in (grad_down, grad_mgate, grad_mup, grad_out, grad_w_input, grad_w_forget, grad_w_gate)
        ]
    return (
        output.reshape(block_input.shape),
        grad_resid.reshape(block_input.shape),
        grad_norm_gain,
        grad_lower,
        sums[4],
        sums[5],
        sums[6],
        grad_hidden_gain,
        sums[3],
        grad_mlp_gain,
        sums[1],
        sums[2],
        sums[0],
    )


def solution(mesh):
    return jax.shard_map(
        on_device,
        mesh=mesh,
        in_specs=(
            P("shard", "ctx", None),
            P("shard", "ctx"),
            P(),
            P("tp"),
            P(("shard", "ctx"), "tp"),
            P(("shard", "ctx"), "tp"),
            P(("shard", "ctx"), "tp"),
            P("tp"),
            P(("shard", "ctx"), "tp"),
            P(),
            P(("shard", "ctx"), "tp"),
            P(("shard", "ctx"), "tp"),
            P(("shard", "ctx"), "tp"),
            P("shard", "ctx", None),
        ),
        out_specs=(
            P("shard", "ctx", None),
            P("shard", "ctx", None),
            P(),
            P("tp"),
            P(("shard", "ctx"), "tp"),
            P(("shard", "ctx"), "tp"),
            P(("shard", "ctx"), "tp"),
            P("tp"),
            P(("shard", "ctx"), "tp"),
            P(),
            P(("shard", "ctx"), "tp"),
            P(("shard", "ctx"), "tp"),
            P(("shard", "ctx"), "tp"),
        ),
        check_vma=False,
    )
```

```python
import functools
import jax
import jax.numpy as jnp
from jax import lax
from jax.experimental import pallas as pl
from jax.experimental.pallas import tpu as pltpu
from jax.sharding import PartitionSpec as P

epsilon = 1e-06
MESH = pl.DeviceIdType.MESH


def remote(src, dst, send_sem, recv_sem, device):
    return pltpu.make_async_remote_copy(
        src_ref=src, dst_ref=dst, send_sem=send_sem, recv_sem=recv_sem,
        device_id=device, device_id_type=MESH)


def pick(z, values):
    out = jnp.int32(values[-1])
    for k in range(len(values) - 2, -1, -1):
        out = jnp.where(z == k, values[k], out)
    return out


def far_first(Z):
    table = []
    for z in range(Z):
        ups, dns, mine, turn = list(range(Z - 1, z, -1)), list(range(0, z)), [], z < Z // 2
        while ups or dns:
            if (turn and ups) or not dns:
                mine.append(ups.pop(0))
            else:
                mine.append(dns.pop(0))
            turn = not turn
        table.append(mine + [z])
    return table


class Scatter:
    def __init__(self, Z, parts, rc, xr, zu, zd, hr, outs, xs, zs, stage, fin, sems):
        self.Z, self.parts, self.rc, self.xr, self.zu, self.zd, self.hr, self.outs = Z, parts, rc, xr, zu, zd, hr, outs
        self.xs, self.zs, self.stage, self.fin = xs, zs, stage, fin
        (self.c_s, self.c_r, self.x_s, self.x_r, self.z_s, self.u_r, self.d_r, self.h_s, self.h_r, self.l_s, self.f_s) = sems
        s, z = lax.axis_index("shard"), lax.axis_index("ctx")
        q, c = s // 2, lax.rem(s, 2)
        self.z, self.q, self.c = z, q, c
        self.even = lax.rem(z, 2) == 0
        self.zp = jnp.where(self.even, z + 1, z - 1)
        self.X = {"shard": (1 - q) * 2 + c}
        self.C = {"shard": q * 2 + (1 - c)}
        self.UP, self.DN, self.ZP = {"ctx": z + 1}, {"ctx": z - 1}, {"ctx": self.zp}
        self.R = [p.shape[0] // (4 * Z) for p in parts]
        self.N = [p.shape[1] for p in parts]
        self.ffirst = far_first(Z)

    def part(self, w, q, c, z, n=1):
        R = self.R[w]
        return self.parts[w].at[pl.ds(pl.multiple_of(((2 * q + c) * self.Z + z) * R, R), n * R), :]

    def rows(self, ref, i, w):
        R = self.R[w]
        return ref.at[pl.ds(pl.multiple_of(i * R, R), R), :]

    def hrows(self, ref, i, w, h):
        H = self.R[w] // 2
        return ref.at[pl.ds(pl.multiple_of(i * 2 * H + h * H, H), H), :]

    def c_copy(self, w, k):
        Z, R = self.Z, self.R[w]
        q = self.q if k == 1 else 1 - self.q
        return remote(self.part(w, q, 1 - self.c, 0, Z), self.rc[w].at[pl.ds(k * Z * R, Z * R), :],
                      self.c_s.at[w, k], self.c_r.at[w, k], self.C)

    def c_send(self, w):
        for k in (0, 1):
            self.c_copy(w, k).start()

    def stage_of(self, slot):
        return self.stage[0].at[slot] if slot < 2 else self.stage[1]

    def load_waits(self, w, srcs, slot):
        cps = []
        for i, src in enumerate(srcs):
            if src is not None:
                n = src.shape[0]
                cps.append(pltpu.make_async_copy(
                    src, self.stage_of(slot).at[i, pl.ds(0, n), pl.ds(0, self.N[w])], self.l_s.at[slot, i]))
        return cps

    def load(self, w, srcs, slot):
        cps = self.load_waits(w, srcs, slot)
        for cp in cps:
            cp.start()
        return cps

    def add(self, w, slot, idx, store, lo=0, hi=None, off=None):
        N = self.N[w]
        hi = self.R[w] if hi is None else hi
        G = 16

        def go(i, _):
            r = pl.multiple_of(lo + i * G, G)
            tot = None
            for k in idx:
                rk = r
                if off is not None and k in off:
                    rk = pl.multiple_of(r + off[k], G)
                v = self.stage_of(slot)[k, pl.ds(rk, G), pl.ds(0, N)].astype(jnp.float32)
                tot = v if tot is None else tot + v
            store(r, tot)
            return 0

        lax.fori_loop(0, (hi - lo) // G, go, 0)

    def x_slot(self, w, n):
        return self.xs.at[w % 2, n, :, pl.ds(0, self.N[w])]

    def order(self, n):
        return pick(self.z, [t[n] for t in self.ffirst])

    def x_copy(self, w, n, half=None):
        zt = self.order(n)
        src = self.x_slot(w, n)
        H = self.R[w] // 2
        if half is None:
            return remote(src, self.rows(self.xr[w], zt, w), self.x_s.at[w, n], self.x_r.at[w, n], self.X)
        return remote(src.at[pl.ds(half * H, H), :], self.hrows(self.xr[w], zt, w, half), self.x_s.at[w, n], self.x_r.at[w, n], self.X)

    def h_copy(self, w, n=0):
        H = self.R[w] // 2
        return remote(self.x_slot(w, n).at[pl.ds(0, H), :], self.hr[w], self.h_s.at[w], self.h_r.at[w], self.ZP)

    def on_pair(self, n, yes, no):
        if n == self.Z - 1:
            no()
            return
        paired = self.order(n) == self.zp

        @pl.when(paired)
        def _():
            yes()

        @pl.when(jnp.logical_not(paired))
        def _():
            no()

    def x_load(self, w, n):
        zt = self.order(n)
        return self.load(w, [self.part(w, 1 - self.q, self.c, zt), self.rows(self.rc[w], zt, w)], n % 2)

    def x_phase(self, w, n):
        Z, H = self.Z, self.R[w] // 2
        last = n == Z - 1
        if n == 0:
            self.c_copy(w, 0).wait_recv()
            self.x_load(w, 0)
        if not last:
            self.x_load(w, n + 1)
        if last:
            self.h_copy(w).wait_recv()
            for cp in self.load(w, [None, None, self.hr[w]], n % 2):
                cp.wait()
        if w >= 2:
            self.x_wait_send(w - 2, n)
        zt = self.order(n)
        for cp in self.load_waits(w, [self.part(w, 1 - self.q, self.c, zt), self.rows(self.rc[w], zt, w)], n % 2):
            cp.wait()
        dst = self.x_slot(w, n)

        def store(r, v):
            dst[pl.ds(r, 16), :] = v.astype(jnp.bfloat16)

        if last:
            self.add(w, n % 2, (0, 1, 2), store, 0, H)
            self.add(w, n % 2, (0, 1), store, H, 2 * H)
            self.x_copy(w, n).start()
        else:
            self.add(w, n % 2, (0, 1), store)

            def yes():
                self.h_copy(w, n).start()
                self.x_copy(w, n, 1).start()

            self.on_pair(n, yes, lambda: self.x_copy(w, n).start())

    def x_wait_send(self, w, n):
        def yes():
            self.h_copy(w, n).wait_send()
            self.x_copy(w, n, 1).wait_send()

        self.on_pair(n, yes, lambda: self.x_copy(w, n).wait_send())

    def z_copy(self, w, n, dest, up):
        src = self.zs.at[w % 2, n, :, pl.ds(0, self.N[w])]
        if up:
            return remote(src, self.rows(self.zu[w], dest, w), self.z_s.at[w, n], self.u_r.at[w, dest], self.UP)
        return remote(src, self.rows(self.zd[w], dest, w), self.z_s.at[w, n], self.d_r.at[w, dest], self.DN)

    def x_wait(self, w, n):
        self.on_pair(n, lambda: self.x_copy(w, n, 1).wait_recv(), lambda: self.x_copy(w, n).wait_recv())

    def z_step(self, w, n, end):
        at_end = (self.z == 0) | (self.z == self.Z - 1)

        @pl.when(at_end if end else jnp.logical_not(at_end))
        def _():
            self.z_phase(w, n, end)

    def z_in(self, w, dest, up, k):
        self.z_copy(w, 0, dest, up).wait_recv()
        self.load(w, [None] * k + [self.rows((self.zu if up else self.zd)[w], dest, w)], 2)[0].wait()

    def z_phase(self, w, n, end):
        Z, H = self.Z, self.R[w] // 2
        z = self.z
        last = n == Z - 1
        dest = z if last else self.order(n)
        if n == 0:
            self.c_copy(w, 1).wait_recv()
        self.x_wait(w, n)
        cps = self.load(w, [self.part(w, self.q, self.c, dest), self.rows(self.rc[w], dest + Z, w),
                            self.rows(self.xr[w], dest, w)], 2)
        if last:
            if end:
                @pl.when(z > 0)
                def _():
                    self.z_in(w, dest, True, 3)

                @pl.when(z == 0)
                def _():
                    self.z_in(w, dest, False, 3)
            else:
                self.z_in(w, dest, True, 3)
                self.z_in(w, dest, False, 4)
            for cp in cps:
                cp.wait()
            if w >= 1:
                self.f_copy(w - 1).wait()
            dst = self.fin.at[:, pl.ds(0, self.N[w])]

            def store(r, v):
                dst[pl.ds(r, 16), :] = v

            self.add(w, 2, (0, 1, 2, 3) if end else (0, 1, 2, 3, 4), store)
            self.f_copy(w).start()
            return
        up = dest > z
        if not end:
            @pl.when(up)
            def _():
                self.z_in(w, dest, True, 3)

            @pl.when(jnp.logical_not(up))
            def _():
                self.z_in(w, dest, False, 3)
        if w >= 2:
            self.z_wait_send(w - 2, n)
        for cp in cps:
            cp.wait()
        dst = self.zs.at[w % 2, n, :, pl.ds(0, self.N[w])]

        def store(r, v):
            dst[pl.ds(r, 16), :] = v.astype(jnp.bfloat16)

        more = () if end else (3,)
        paired = dest == self.zp

        @pl.when(paired)
        def _():
            self.add(w, 2, (0, 1) + more, store, 0, H)
            self.add(w, 2, (0, 1, 2) + more, store, H, 2 * H)

        @pl.when(jnp.logical_not(paired))
        def _():
            self.add(w, 2, (0, 1, 2) + more, store)

        @pl.when(up)
        def _():
            self.z_copy(w, n, dest, True).start()

        @pl.when(jnp.logical_not(up))
        def _():
            self.z_copy(w, n, dest, False).start()

    def z_wait_send(self, w, n):
        z = self.z
        dest = pick(z, [t[n] for t in self.ffirst])
        self.z_copy_any(w, n).wait_send()

    def z_copy_any(self, w, n):
        src = self.zs.at[w % 2, n, :, pl.ds(0, self.N[w])]
        return remote(src, self.rows(self.zu[w], 0, w), self.z_s.at[w, n], self.u_r.at[w, 0],
                      {"ctx": jnp.where(pick(self.z, [t[n] for t in self.ffirst]) > self.z, self.z + 1, self.z - 1)})

    def f_copy(self, w):
        return pltpu.make_async_copy(self.fin.at[:, pl.ds(0, self.N[w])], self.outs[w], self.f_s.at[w])

    def drain(self, w, nw):
        for k in (0, 1):
            self.c_copy(w, k).wait_send()
        if w >= nw - 2:
            for n in range(self.Z):
                self.x_wait_send(w, n)
            for n in range(self.Z - 1):
                self.z_wait_send(w, n)
        if w == nw - 1:
            self.f_copy(w).wait()


T8 = 8


def spread(Z, z, pay, box, s_sem, r_sem):
    cps = []
    for o in range(1, Z):
        to = lax.rem(z + o, Z)
        cp = remote(pay, box.at[z], s_sem.at[o - 1], r_sem.at[z], {"ctx": to})
        cp.start()
        cps.append(cp)
    box[z] = pay[...]
    return cps


def spread_wait(Z, z, pay, box, s_sem, r_sem, cps):
    for o in range(1, Z):
        frm = lax.rem(z + o, Z)
        remote(pay, box.at[frm], s_sem.at[o - 1], r_sem.at[frm], {"ctx": frm}).wait_recv()
    for cp in cps:
        cp.wait_send()


def joined(box, k):
    last, first = box[k, 6:8, :], box[k + 1, 4:6, :]
    return jnp.where(last == first, 1.0, 0.0)


def prefix_state(Z, z, box):
    state = jnp.zeros(box.shape[2:][:0] + (2, box.shape[2]), jnp.float32)
    mine = state
    for k in range(Z - 1):
        state = joined(box, k) * (box[k, 2:4, :] + box[k, 0:2, :] * state)
        mine = jnp.where(z == k + 1, state, mine)
    return mine


def suffix_state(Z, z, box):
    state = jnp.zeros((2, box.shape[2]), jnp.float32)
    mine = state
    for k in range(Z - 2, -1, -1):
        state = joined(box, k) * (box[k + 1, 2:4, :] + box[k + 1, 0:2, :] * state)
        mine = jnp.where(z == k, state, mine)
    return mine


def diagonal():
    return lax.broadcasted_iota(jnp.int32, (128, 128), 0) == lax.broadcasted_iota(jnp.int32, (128, 128), 1)


def column_to_rows(col_ref, row_ref, n):
    eye = diagonal()
    for k in range(n // 128):
        col = col_ref[pl.ds(k * 128, 128), :]
        row_ref[k:k + 1, :] = jnp.sum(jnp.where(eye, jnp.broadcast_to(col, (128, 128)), 0.0), axis=0, keepdims=True)


def rows_to_column(row, k):
    return jnp.sum(jnp.where(diagonal(), jnp.broadcast_to(row, (128, 128)), 0.0), axis=1, keepdims=True)


def sigmoid(v):
    return jax.nn.sigmoid(v)


def row_at(ref, t):
    return pl.ds(pl.multiple_of(t, T8), T8)


def forward_scan_one(sq, length, pi, pf, lower, link, h, cum):
    C = pi.shape[1]
    low = lower[...]
    iota = lax.broadcasted_iota(jnp.int32, (T8, C), 0)

    def tile(i, carry):
        hl, pr = carry
        r = row_at(pi, sq * length + i * T8)
        s = sigmoid(pf[r, :])
        forget = low + (1.0 - low) * s
        x = pi[r, :]
        b = x * sigmoid(x) * (1.0 - forget)
        a = forget * link[r, :]
        for sh in (1, 2, 4):
            keep = iota >= sh
            b = b + jnp.where(keep, a * pltpu.roll(b, sh, 0), 0.0)
            a = jnp.where(keep, a * pltpu.roll(a, sh, 0), a)
        b = b + a * hl
        a = a * pr
        h[r, :] = b
        cum[r, :] = a
        return b[T8 - 1:T8, :], a[T8 - 1:T8, :]

    return lax.fori_loop(0, length // T8, tile, (jnp.zeros((1, C), jnp.float32), jnp.ones((1, C), jnp.float32)), unroll=2)


def forward_finish(seqs, length, h, cum, start, col):
    def tile(i, _, sq):
        r = row_at(h, sq * length + i * T8)
        v = h[r, :] + cum[r, :] * start[sq:sq + 1, :]
        h[r, :] = v
        col[r, :] = jnp.sum(v * v, axis=1, keepdims=True)
        return 0

    for sq in range(seqs):
        lax.fori_loop(0, length // T8, functools.partial(tile, sq=sq), 0, unroll=2)


def swap_columns(col, row, got, s_sem, r_sem, other, n):
    column_to_rows(col, row, n)
    cp = remote(row, got, s_sem, r_sem, {"tp": other})
    cp.start()
    cp.wait()


def scale_columns(row, got, col, n, width, fn):
    for k in range(n // 128):
        col[pl.ds(k * 128, 128), :] = fn(rows_to_column(row[k:k + 1, :] + got[k:k + 1, :], k))


def mixed(h, rh, gain, pg, m, step=16):
    g = gain[...]

    def tile(i, _):
        r = pl.ds(pl.multiple_of(i * step, step), step)
        p = pg[r, :]
        m[r, :] = (h[r, :] * rh[r, :] * g * (p * sigmoid(p))).astype(m.dtype)
        return 0

    lax.fori_loop(0, h.shape[0] // step, tile, 0)


def backward_first(n, dm, h, pg, gain, rh, dpg, col, gsum, step=16):
    g = gain[...]

    def tile(i, acc):
        r = pl.ds(pl.multiple_of(i * step, step), step)
        d, hv, p, rv = dm[r, :], h[r, :], pg[r, :], rh[r, :]
        s = sigmoid(p)
        sl = p * s
        q = d * g * sl
        col[r, :] = jnp.sum(q * hv, axis=1, keepdims=True)
        hr = d * hv * rv
        dpg[r, :] = (hr * g * (s * (1.0 + p * (1.0 - s)))).astype(dpg.dtype)
        return acc + jnp.sum(hr * sl, axis=0, keepdims=True)

    gsum[...] = lax.fori_loop(0, n // step, tile, jnp.zeros(gsum.shape, jnp.float32))


def backward_scan_one(sq, length, dm, h, pf, pg, lower, gain, link, rh, inner, gl, tail):
    C = dm.shape[1]
    low, g = lower[...], gain[...]
    iota = lax.broadcasted_iota(jnp.int32, (T8, C), 0)
    nt = length // T8
    def tile(k, carry):
        vl, pr = carry
        r = row_at(dm, sq * length + (nt - 1 - k) * T8)
        rv = rh[r, :]
        p = pg[r, :]
        q = dm[r, :] * g * (p * sigmoid(p))
        dh = q * rv - h[r, :] * (rv * rv * rv) * inner[r, :]
        a = (low + (1.0 - low) * sigmoid(pf[r, :])) * link[r, :]
        b = a * dh
        for sh in (1, 2, 4):
            keep = iota < T8 - sh
            b = b + jnp.where(keep, a * pltpu.roll(b, T8 - sh, 0), 0.0)
            a = jnp.where(keep, a * pltpu.roll(a, T8 - sh, 0), a)
        v = b + a * vl
        pa = a * pr
        last = iota == T8 - 1
        gl[r, :] = dh + jnp.where(last, vl, pltpu.roll(v, T8 - 1, 0))
        tail[r, :] = jnp.where(last, pr, pltpu.roll(pa, T8 - 1, 0))
        return v[0:1, :], pa[0:1, :]

    return lax.fori_loop(0, nt, tile, (jnp.zeros((1, C), jnp.float32), jnp.ones((1, C), jnp.float32)), unroll=2)


def backward_last(seqs, length, gl, tail, end, h, start, pi, pf, lower, link, dpi, dpf, lsum):
    C = gl.shape[1]
    low = lower[...]
    iota = lax.broadcasted_iota(jnp.int32, (T8, C), 0)
    total = jnp.zeros((1, C), jnp.float32)
    for sq in range(seqs):
        def tile(i, carry):
            acc, hp = carry
            halves = []
            for half in (0, 1):
                r = row_at(gl, sq * length + i * 16 + half * T8)
                gv = gl[r, :] + tail[r, :] * end[sq:sq + 1, :]
                hv = h[r, :]
                prev = jnp.where(iota == 0, hp, pltpu.roll(hv, 1, 0) * link[r, :])
                if half == 1:
                    prev = jnp.where(iota == 0, prev * link[r, :], prev)
                else:
                    prev = jnp.where((iota == 0) & (i > 0), prev * link[r, :], prev)
                s = sigmoid(pf[r, :])
                forget = low + (1.0 - low) * s
                x = pi[r, :]
                sx = sigmoid(x)
                df = gv * (prev - x * sx)
                halves.append((gv * (1.0 - forget) * (sx * (1.0 + x * (1.0 - sx))), df * (1.0 - low) * s * (1.0 - s)))
                acc = acc + jnp.sum(df * (1.0 - s), axis=0, keepdims=True)
                hp = hv[T8 - 1:T8, :]
            r = pl.ds(pl.multiple_of(sq * length + i * 16, 16), 16)
            dpi[r, :] = jnp.concatenate([halves[0][0], halves[1][0]], axis=0).astype(dpi.dtype)
            dpf[r, :] = jnp.concatenate([halves[0][1], halves[1][1]], axis=0).astype(dpf.dtype)
            return acc, hp

        total, _ = lax.fori_loop(0, length // 16, tile, (total, start[sq:sq + 1, :]))
    lsum[...] = total


def gather_steps(nw, Z, ahead, relay, own, out, sems):
    (s_up, r_up, s_dn, r_dn, s_x, r_x, s_c, r_c, s_h, r_h, l_sem) = sems
    s, z = lax.axis_index("shard"), lax.axis_index("ctx")
    q, c = s // 2, lax.rem(s, 2)
    sx, sc = (1 - q) * 2 + c, q * 2 + (1 - c)
    sxc = (1 - q) * 2 + (1 - c)
    even = lax.rem(z, 2) == 0
    zp = jnp.where(even, z + 1, z - 1)
    rows = [r.shape[0] for r in own]

    def block(w, s_, z_, part=0):
        R = rows[w]
        start = pl.multiple_of((s_ * Z + z_) * R, R)
        if part == 0:
            return out[w].at[pl.ds(start, R), :]
        H = R // 2
        return out[w].at[pl.ds(pl.multiple_of(start + (part - 1) * H, H), H), :]

    UP, DN, XX, CC, ZP = {"ctx": z + 1}, {"ctx": z - 1}, {"shard": sx}, {"shard": sc}, {"ctx": zp}

    def up(w, k, src=None):
        b = block(w, s, z - k)
        return remote(b if src is None else src, b, s_up.at[w, k], r_up.at[w, k], UP)

    def dn(w, k, src=None):
        b = block(w, s, z + k)
        return remote(b if src is None else src, b, s_dn.at[w, k], r_dn.at[w, k], DN)

    def origin(j):
        return z if j == 0 else (z - j if j < Z else z + j - Z + 1)

    def valid(j):
        return (z >= j) if j < Z else (z + j - Z + 1 <= Z - 1)

    def xx(w, j, part, src=None):
        b = block(w, s, origin(j), part)
        return remote(b if src is None else src, b, s_x.at[w, j], r_x.at[w, j], XX)

    def xx_in(w, j, part):
        b = block(w, sx, origin(j), part)
        return remote(b, b, s_x.at[w, j], r_x.at[w, j], XX)

    def cc(w, j, src=None):
        b = block(w, s if j < 2 * Z - 1 else sx, origin(j % (2 * Z - 1)))
        return remote(b if src is None else src, b, s_c.at[w, j], r_c.at[w, j], CC)

    def cc_in(w, j):
        b = block(w, sc if j < 2 * Z - 1 else sxc, origin(j % (2 * Z - 1)))
        return remote(b, b, s_c.at[w, j], r_c.at[w, j], CC)

    def half(w):
        b = block(w, sx, z, 1)
        return remote(b, b, s_h.at[w], r_h.at[w], ZP)

    def half_in(w):
        b = block(w, sx, zp, 1)
        return remote(b, b, s_h.at[w], r_h.at[w], ZP)

    local = []
    for w in range(nw):
        local.append(pltpu.make_async_copy(own[w], block(w, s, z), l_sem.at[w]))

    def begin(w):
        local[w].start()

        @pl.when(z < Z - 1)
        def _():
            up(w, 0, own[w]).start()

        @pl.when(z > 0)
        def _():
            dn(w, 0, own[w]).start()

        xx(w, 0, 0, own[w]).start()
        cc(w, 0, own[w]).start()

    def is_pair(j):
        if j == 1:
            return jnp.logical_not(even)
        if j == Z:
            return even
        return None

    def for_part(w, j, fn):
        pair = is_pair(j) if relay else None
        if pair is None:
            fn(0)
        else:
            @pl.when(pair)
            def _():
                fn(2)

            @pl.when(jnp.logical_not(pair))
            def _():
                fn(0)

    def step(w, k):
        @pl.when(z >= k)
        def _():
            remote(block(w, s, z - k), block(w, s, z - k), s_up.at[w, k - 1], r_up.at[w, k - 1], UP).wait_recv()
            if k < Z - 1:
                @pl.when(z < Z - 1)
                def _():
                    up(w, k).start()
            for_part(w, k, lambda p: xx(w, k, p).start())
            cc(w, k).start()

        @pl.when(z + k <= Z - 1)
        def _():
            remote(block(w, s, z + k), block(w, s, z + k), s_dn.at[w, k - 1], r_dn.at[w, k - 1], DN).wait_recv()
            if k < Z - 1:
                @pl.when(z > 0)
                def _():
                    dn(w, k).start()
            for_part(w, Z - 1 + k, lambda p: xx(w, Z - 1 + k, p).start())
            cc(w, Z - 1 + k).start()

    def xstep(w, j):
        @pl.when(valid(j))
        def _():
            for_part(w, j, lambda p: xx_in(w, j, p).wait_recv())
            if j == 0:
                if relay:
                    half(w).start()
                cc(w, 2 * Z - 1).start()
            else:
                if relay and is_pair(j) is not None:
                    @pl.when(is_pair(j))
                    def _():
                        half_in(w).wait_recv()
                cc(w, 2 * Z - 1 + j).start()

    def finish(w):
        for j in range(4 * Z - 2):
            @pl.when(valid(j % (2 * Z - 1)))
            def _():
                cc_in(w, j).wait_recv()
                cc(w, j).wait_send()
        for j in range(2 * Z - 1):
            @pl.when(valid(j))
            def _():
                for_part(w, j, lambda p: xx(w, j, p).wait_send())
        for k in range(Z - 1):
            @pl.when((z >= k) & (z < Z - 1))
            def _():
                up(w, k).wait_send()

            @pl.when((z + k <= Z - 1) & (z > 0))
            def _():
                dn(w, k).wait_send()
        if relay:
            half(w).wait_send()
        local[w].wait()

    def tick(w, k):
        step(w, k)
        if k == 1:
            xstep(w, 0)
            if w + ahead < nw:
                begin(w + ahead)
        else:
            xstep(w, k - 1)
            xstep(w, Z - 1 + k - 1)
        if w > 0 and k == 1:
            xstep(w - 1, Z - 1)
            xstep(w - 1, 2 * Z - 2)

    def last():
        xstep(nw - 1, Z - 1)
        xstep(nw - 1, 2 * Z - 2)

    return begin, tick, last, finish


def front_body(Z, seqs, length, ahead, *refs):
    nw = 7
    wide_own = refs[:nw]
    x, cot, gain1, gain2, low, hgain, link, ids = refs[nw:nw + 8]
    k0 = nw + 8
    wide = refs[k0:k0 + nw]
    k0 += nw
    n1_o, pi_o, pf_o, pg_o, h_o, m_o, mid_o, n2_o, gate_o, up_o, act_o, gy_o, gd_o, rh, start = refs[k0:k0 + 15]
    k0 += 15
    (xv, n1, n2, pi, pf, pg, h, cum, m, wbuf, wob, pn, rn, gate, up, act, gy, stg, e_f,
     pay, box, row, got, wst) = refs[k0:k0 + 24]
    own = refs[k0 + 24:k0 + 24 + nw]
    k0 += 24 + nw
    s_c, r_c, s_t, r_t, n_s, n_r, w_s, o_s, e_s, g_s, x_s, f_s = refs[k0:k0 + 12]
    sems = refs[k0 + 12:]
    w_in, w_f, w_g, w_out, w_mg, w_mu, w_dn = wide
    n, width = x.shape
    C, F = pi.shape[1], gate.shape[1]
    s, z, t = lax.axis_index("shard"), lax.axis_index("ctx"), lax.axis_index("tp")
    q, c = s // 2, lax.rem(s, 2)
    OTHER = {"tp": 1 - t}
    begin, tick, last, finish = gather_steps(nw, Z, ahead, True, own, wide, sems)
    NP, NF, NW, NC = n // TR, F // TC, C // TC, width // TC

    def own_load(w):
        return pltpu.make_async_copy(wide_own[w], wst.at[w % 2, :, pl.ds(0, own[w].shape[1])], f_s.at[w % 2])

    def own_low(w):
        own_load(w).wait()
        cols = own[w].shape[1]

        def go(i, _):
            r = pl.ds(pl.multiple_of(i * 16, 16), 16)
            own[w][r, :] = wst[w % 2, r, :cols].astype(jnp.bfloat16)
            return 0

        lax.fori_loop(0, own[w].shape[0] // 16, go, 0)
        if w + 2 < nw:
            own_load(w + 2).start()

    own_load(0).start()
    own_load(1).start()
    barrier = pltpu.get_barrier_semaphore()
    for d in [{"shard": (1 - q) * 2 + c}, {"shard": q * 2 + (1 - c)}, OTHER] + [{"ctx": lax.rem(z + o, Z)} for o in range(1, Z)]:
        pl.semaphore_signal(barrier, inc=1, device_id=d, device_id_type=MESH)
    pl.semaphore_wait(barrier, 2 + Z)

    for w in range(ahead):
        own_low(w)
        begin(w)
    load_x = pltpu.make_async_copy(x, xv, x_s.at[0])
    load_x.start()
    done = []

    def put(src, dst, k):
        cp = pltpu.make_async_copy(src, dst, o_s.at[k])
        cp.start()
        done.append(cp)

    def norm_in():
        load_x.wait()
        g = gain1[...]

        def go(i, _):
            r = pl.ds(pl.multiple_of(i * 16, 16), 16)
            v = xv[r, :]
            n1[r, :] = (v * lax.rsqrt(jnp.mean(v * v, axis=1, keepdims=True) + epsilon) * g).astype(jnp.bfloat16)
            return 0

        lax.fori_loop(0, n // 16, go, 0, unroll=2)
        put(n1, n1_o, 0)

    def times(lhs, w, dst, tiles, after=None):
        def load(j, s):
            return pltpu.make_async_copy(w.at[:, pl.ds(pl.multiple_of(j * TC, TC), TC)], wbuf.at[s], w_s.at[s])

        load(0, 0).start()

        def go(j, _):
            s = lax.rem(j, 2)

            @pl.when(j + 1 < tiles)
            def _():
                load(j + 1, 1 - s).start()

            load(j, s).wait()
            dst[:, pl.ds(pl.multiple_of(j * TC, TC), TC)] = jnp.dot(lhs[...], wbuf[s], preferred_element_type=jnp.float32)
            if after is not None:
                after(j)
            return 0

        lax.fori_loop(0, tiles, go, 0)

    def rows_of(k):
        return pl.ds(k * TR, TR)

    def pn_copy(k):
        return remote(pn.at[rows_of(k), :], rn.at[rows_of(k), :], n_s.at[k], n_r.at[k], OTHER)

    def out_product():
        def load(j, s):
            return pltpu.make_async_copy(w_out.at[pl.ds(pl.multiple_of(j * TC, TC), TC), :], wob.at[s], w_s.at[s])

        load(0, 0).start()

        def go(j, _):
            s = lax.rem(j, 2)

            @pl.when(j + 1 < NC)
            def _():
                load(j + 1, 1 - s).start()

            load(j, s).wait()
            pn[:, pl.ds(pl.multiple_of(j * TC, TC), TC)] = dot_t(m[...], wob[s]).astype(jnp.bfloat16)
            return 0

        lax.fori_loop(0, NC, go, 0)
        for k in range(NP):
            pn_copy(k).start()

    def middle(k):
        pn_copy(k).wait_recv()
        g = gain2[...]

        def go(i, _):
            r = pl.ds(pl.multiple_of(k * TR + i * 16, 16), 16)
            v = xv[r, :] + (pn[r, :].astype(jnp.float32) + rn[r, :].astype(jnp.float32))
            xv[r, :] = v
            n2[r, :] = (v * lax.rsqrt(jnp.mean(v * v, axis=1, keepdims=True) + epsilon) * g).astype(jnp.bfloat16)
            return 0

        lax.fori_loop(0, TR // 16, go, 0)

    def cot_load(k):
        return pltpu.make_async_copy(cot.at[rows_of(k), :], e_f.at[k % 2], e_s.at[k % 2])

    def cot_low():
        cot_load(0).start()
        for k in range(NP):
            if k + 1 < NP:
                cot_load(k + 1).start()
            cot_load(k).wait()
            gy[rows_of(k), :] = e_f[k % 2].astype(jnp.bfloat16)

    def activate(j):
        cols = pl.ds(pl.multiple_of(j * TC, TC), TC)

        def go(i, _):
            r = pl.ds(pl.multiple_of(i * 32, 32), 32)
            v = gate[r, cols]
            act[r, cols] = (v * sigmoid(v) * up[r, cols]).astype(jnp.bfloat16)
            return 0

        lax.fori_loop(0, n // 32, go, 0)

    def gd_copy(j, s):
        return pltpu.make_async_copy(stg.at[s], gd_o.at[pl.ds(pl.multiple_of(j * TC, TC), TC), :], g_s.at[s])

    def down_grad(j0, j1):
        def go(j, _):
            s = lax.rem(j, 2)

            @pl.when(j >= 2)
            def _():
                gd_copy(j - 2, s).wait()

            stg[s] = dot_o(gy[:, pl.ds(pl.multiple_of(j * TC, TC), TC)], act[...]).astype(jnp.bfloat16)
            gd_copy(j, s).start()
            return 0

        lax.fori_loop(j0, j1, go, 0)

    own_low(2)
    norm_in()
    for w in range(3, nw):
        own_low(w)
    for w, src, dst, o, k in ((0, w_in, pi, pi_o, 1), (1, w_f, pf, pf_o, 2), (2, w_g, pg, pg_o, 3)):
        if w == 0:
            tick(0, 1)
            tick(0, 2)
            tick(0, 3)
        tick(w + 1, 1)
        tick(w + 1, 2)
        finish(w)
        times(n1, src, dst, NW)
        put(dst, o, k)
        if w < 2:
            tick(w + 1, 3)
    ends = [forward_scan_one(0, length, pi, pf, low, link, h, cum)]
    tick(3, 3)
    for sq in range(1, seqs):
        ends.append(forward_scan_one(sq, length, pi, pf, low, link, h, cum))
    pay[4:8, :] = ids[...]
    for sq in range(seqs):
        pay[sq:sq + 1, :] = ends[sq][1]
        pay[2 + sq:3 + sq, :] = ends[sq][0]
    cps = spread(Z, z, pay, box, s_c, r_c)
    tick(4, 1)
    cot_low()
    put(gy, gy_o, 4)
    spread_wait(Z, z, pay, box, s_c, r_c, cps)
    start[...] = prefix_state(Z, z, box)
    forward_finish(seqs, length, h, cum, start, rh)
    put(h, h_o, 5)
    swap_columns(rh, row, got, s_t.at[0], r_t.at[0], 1 - t, n)
    scale_columns(row, got, rh, n, width, lambda v: lax.rsqrt(v / width + epsilon))
    mixed(h, rh, hgain, pg, m)
    put(m, m_o, 6)
    tick(4, 2)
    finish(3)
    out_product()
    tick(4, 3)
    for k in range(NP // 2):
        middle(k)
    tick(5, 1)
    for k in range(NP // 2, NP):
        middle(k)
    put(xv, mid_o, 7)
    put(n2, n2_o, 8)
    tick(5, 2)
    finish(4)
    times(n2, w_mg, gate, NF)
    put(gate, gate_o, 9)
    tick(5, 3)
    tick(6, 1)
    finish(5)
    times(n2, w_mu, up, NF, activate)
    put(up, up_o, 10)
    put(act, act_o, 11)
    tick(6, 2)
    down_grad(0, NC // 2)
    tick(6, 3)
    down_grad(NC // 2, NC)
    last()
    finish(6)
    gd_copy(NC - 2, NC % 2).wait()
    gd_copy(NC - 1, (NC - 1) % 2).wait()
    for k in range(NP):
        pn_copy(k).wait_send()
    for cp in done:
        cp.wait()


def front_all(Z, seqs, length, shards, x, cot, gain1, gain2, low, hgain, link, ids, cid=0, ahead=2):
    nw = len(shards)
    n, width = x.shape
    C, F = shards[0].shape[1], shards[4].shape[1]
    dma = pltpu.SemaphoreType.DMA
    bf, f = jnp.bfloat16, jnp.float32
    sh = jax.ShapeDtypeStruct
    anyw, vmem = pl.BlockSpec(memory_space=pl.ANY), pl.BlockSpec(memory_space=pltpu.VMEM)
    NP = n // TR
    V = pltpu.VMEM
    out_shape = ([sh((a.shape[0] * 4 * Z, a.shape[1]), bf) for a in shards]
                 + [sh((n, width), bf)] + [sh((n, C), f)] * 4 + [sh((n, C), bf)] + [sh((n, width), f), sh((n, width), bf)]
                 + [sh((n, F), f)] * 2 + [sh((n, F), bf), sh((n, width), bf), sh((width, F), bf), sh((n, 1), f), sh((seqs, C), f)])
    scratch = [
        V((n, width), f), V((n, width), bf), V((n, width), bf), V((n, C), f), V((n, C), f), V((n, C), f), V((n, C), f), V((n, C), f),
        V((n, C), bf), V((2, width, TC), bf), V((2, TC, C), bf), V((n, width), bf), V((n, width), bf), V((n, F), f), V((n, F), f),
        V((n, F), bf), V((n, width), bf), V((2, TC, F), bf), V((2, TR, width), f),
        V((8, C), f), V((Z, 8, C), f), V((n // 128, 128), f), V((n // 128, 128), f),
        V((2, shards[0].shape[0], F), f),
    ] + [V(a.shape, bf) for a in shards] + [
        dma((Z - 1,)), dma((Z,)), dma((1,)), dma((1,)), dma((NP,)), dma((NP,)), dma((2,)), dma((12,)), dma((2,)), dma((2,)), dma((1,)), dma((2,)),
        dma((nw, Z - 1)), dma((nw, Z - 1)), dma((nw, Z - 1)), dma((nw, Z - 1)),
        dma((nw, 2 * Z - 1)), dma((nw, 2 * Z - 1)),
        dma((nw, 4 * Z - 2)), dma((nw, 4 * Z - 2)), dma((nw,)), dma((nw,)), dma((nw,)),
    ]
    res = pl.pallas_call(
        functools.partial(front_body, Z, seqs, length, ahead),
        out_shape=out_shape,
        in_specs=[anyw] * (nw + 2) + [vmem] * 6,
        out_specs=[anyw] * (len(out_shape) - 2) + [vmem] * 2,
        scratch_shapes=scratch,
        compiler_params=pltpu.CompilerParams(collective_id=cid, has_side_effects=True, vmem_limit_bytes=66_000_000),
        name="forward",
    )(*shards, x, cot, gain1, gain2, low, hgain, link, ids)
    return res[:nw], res[nw:]


TR = 64
TC = 256


def dot_t(a, b):
    return lax.dot_general(a, b, (((1,), (1,)), ((), ())), preferred_element_type=jnp.float32)


def dot_o(a, b):
    return lax.dot_general(a, b, (((0,), (0,)), ((), ())), preferred_element_type=jnp.float32)


def back_body(Z, seqs, length, *refs):
    (gd, gy_h, n2_h, act_h, gate_h, up_h, w_dn, w_mg, w_mu, x, mid, cot, n1, m, w_out, w_in, w_f, w_g,
     pi_h, pf_h, pg_h, h_h, rh, start, ids, link, gain1, gain2, low, hgain) = refs[:30]
    dx, vec_out = refs[30:32]
    grads = refs[32:39]
    mparts = refs[39:45]
    pn, po, rn, ro = refs[45:49]
    k0 = 49
    rc, xr, zu, zd, hr = (refs[k0 + 7 * i:k0 + 7 * (i + 1)] for i in range(5))
    k0 += 35
    (xs, zs, stage, stage_z, fin, dmid, gm, dm, h, pi, pf, pg, gl, tail, dpi, dpf, dpg, n1v, mv, wbuf, tb, du, sn, rn1,
     e_f, e_b, vec, vgot, vbox, col, end, pay, box, row, got) = refs[k0:k0 + 35]
    k0 += 35
    (l_h, l_n, w_s, g_s, n_s, n_r, o_s, o_r, t_s, t_r, e_s, eo_s, v_s, v_r, vz_s, vz_r, s_c, r_c, s_t, r_t, b_s) = refs[k0:k0 + 21]
    sems = refs[k0 + 21:]
    n, width = x.shape
    C = dm.shape[1]
    F = du.shape[1]
    parts = (gd,) + tuple(mparts)
    sc = Scatter(Z, parts, rc, xr, zu, zd, hr, grads, xs, zs, (stage, stage_z), fin, sems)
    z = sc.z
    t = lax.axis_index("tp")
    OTHER = {"tp": 1 - t}

    barrier = pltpu.get_barrier_semaphore()
    for d in [sc.X, sc.C, OTHER] + [{"ctx": lax.rem(z + o, Z)} for o in range(1, Z)]:
        pl.semaphore_signal(barrier, inc=1, device_id=d, device_id_type=MESH)
    pl.semaphore_wait(barrier, 2 + Z)

    sc.c_send(0)

    NP = n // TR
    NC = width // TC

    def rows_of(k):
        return pl.ds(k * TR, TR)

    def pn_copy(k):
        return remote(pn.at[rows_of(k), :], rn.at[rows_of(k), :], n_s.at[k], n_r.at[k], OTHER)

    def po_copy(k):
        return remote(po.at[rows_of(k), :], ro.at[rows_of(k), :], o_s.at[k], o_r.at[k], OTHER)

    early = [pltpu.make_async_copy(a, b, l_h.at[i]) for i, (a, b) in enumerate(
        ((pi_h, pi), (pf_h, pf), (pg_h, pg), (h_h, h), (m, mv), (gy_h, n1v), (n2_h, gm), (mid, dmid)))]
    for cp in early:
        cp.start()
    vec[...] = jnp.zeros_like(vec)

    steps = []

    def X(w):
        return [functools.partial(sc.x_phase, w, k) for k in range(Z)]

    def E(w, k):
        return functools.partial(sc.z_step, w, k, True)

    def M(w, k):
        return functools.partial(sc.z_step, w, k, False)

    def tick(*todo):
        for s in todo:
            s()

    def piece(k, s, f_src, b_src):
        r = rows_of(k)
        return ([pltpu.make_async_copy(a.at[r, :], e_f.at[s, i], e_s.at[s, i]) for i, a in enumerate(f_src)]
                + [pltpu.make_async_copy(a.at[r, :], e_b.at[s, i], e_s.at[s, 2 + i]) for i, a in enumerate(b_src)])

    def p1_load(k):
        pn_copy(k).wait_recv()
        for cp in piece(k, k % 2, (cot,), (pn, rn)):
            cp.start()

    def p1(k):
        s = k % 2
        for cp in piece(k, s, (cot,), (pn, rn)):
            cp.wait()
        g = gain2[...]

        def go(i, a):
            r = pl.ds(pl.multiple_of(i * 16, 16), 16)
            rr = pl.ds(pl.multiple_of(k * TR + i * 16, 16), 16)
            v, ct = dmid[rr, :], e_f[s, 0, r, :]
            d = e_b[s, 0, r, :].astype(jnp.float32) + e_b[s, 1, r, :].astype(jnp.float32)
            r2 = lax.rsqrt(jnp.mean(v * v, axis=1, keepdims=True) + epsilon)
            gdn = d * g
            inner = jnp.mean(gdn * v, axis=1, keepdims=True)
            o = ct + gdn * r2 - v * (r2 * r2 * r2 * inner)
            dmid[rr, :] = o
            gm[rr, :] = o.astype(jnp.bfloat16)
            return a + jnp.sum(d * v * r2, axis=0, keepdims=True)

        vec[1:2, :] = vec[1:2, :] + lax.fori_loop(0, TR // 16, go, jnp.zeros((1, width), jnp.float32))

    segments = [(b, a, min(C, F - a)) for b, a in ((dpi, 0), (dpf, C), (dpg, 2 * C))]

    def tile_of(j):
        return pl.ds(pl.multiple_of(j * TC, TC), TC)

    def glu_loads(j, s):
        return [pltpu.make_async_copy(a.at[:, tile_of(j)], b, w_s.at[s, i]) for i, (a, b) in enumerate(
            ((w_dn, wbuf.at[s]), (gate_h, gl.at[:, tile_of(s)]), (up_h, tail.at[:, tile_of(s)])))]

    def glu_cols(g):
        buf, first, size = segments[g]

        def go(j, _):
            s = lax.rem(j, 2)

            @pl.when(j + 1 < F // TC)
            def _():
                for cp in glu_loads(j + 1, 1 - s):
                    cp.start()

            for cp in glu_loads(j, s):
                cp.wait()
            dm[:, :TC] = jnp.dot(n1v[...], wbuf[s], preferred_element_type=jnp.float32)
            here, there = tile_of(s), tile_of(j)
            inside = tile_of(j - first // TC)

            def rows(i, _):
                r = pl.ds(pl.multiple_of(i * 32, 32), 32)
                v, u, d = gl[r, here], tail[r, here], dm[r, :TC]
                sg = sigmoid(v)
                buf[r, inside] = (d * u * (sg * (1.0 + v * (1.0 - sg)))).astype(jnp.bfloat16)
                du[r, there] = (d * (v * sg)).astype(jnp.bfloat16)
                return 0

            lax.fori_loop(0, n // 32, rows, 0)
            return 0

        lax.fori_loop(first // TC, (first + size) // TC, go, 0)

    def w_rows(w, j, s):
        return pltpu.make_async_copy(w.at[tile_of(j), :], tb.at[s, :, pl.ds(0, F)], w_s.at[2 + s, 0])

    def sn_out(dst, j):
        return pltpu.make_async_copy(sn.at[j], dst.at[:, tile_of(j)], b_s.at[j])

    def normed(j0, j1):
        def go(j, _):
            w_rows(w_mg, j, 0).wait()
            o = None
            for buf, first, size in segments:
                v = dot_t(buf[:, :size], tb[0, :, first:first + size])
                o = v if o is None else o + v

            @pl.when(j + 1 < NC)
            def _():
                w_rows(w_mg, j + 1, 0).start()

            w_rows(w_mu, j, 1).wait()
            o = o + dot_t(du[...], tb[1, :, :F])

            @pl.when(j + 1 < NC)
            def _():
                w_rows(w_mu, j + 1, 1).start()

            sn[j] = o.astype(jnp.bfloat16)
            sn_out(pn, j).start()
            return 0

        lax.fori_loop(j0, j1, go, 0)

    def t_copy(dst, j, s):
        return pltpu.make_async_copy(tb.at[s, :, pl.ds(0, dst.shape[1])], dst.at[tile_of(j), :], g_s.at[s])

    def glu_grad(w, cols, j0, j1):
        dst = parts[w]

        def go(j, _):
            s = lax.rem(j, 2)

            @pl.when(j >= 2)
            def _():
                t_copy(dst, j - 2, s).wait()

            lhs = gm[:, tile_of(j)]
            for buf, first, size in cols:
                tb[s, :, first:first + size] = dot_o(lhs, buf[:, :size]).astype(jnp.bfloat16)
            t_copy(dst, j, s).start()
            return 0

        lax.fori_loop(j0, j1, go, 0)
        if j1 == NC:
            t_copy(dst, NC - 2, NC % 2).wait()
            t_copy(dst, NC - 1, (NC - 1) % 2).wait()
            sc.c_send(w)

    def down(j0, j1):
        def go(j, _):
            s = lax.rem(j, 2)

            @pl.when(j + 1 < NC)
            def _():
                w_rows(w_dn, j + 1, 1 - s).start()

            w_rows(w_dn, j, s).wait()
            sn[j] = dot_t(du[...], tb[s, :, :F]).astype(jnp.bfloat16)
            sn_out(po, j).start()
            return 0

        lax.fori_loop(j0, j1, go, 0)

    NW = C // TC

    def w_load(j, s):
        return pltpu.make_async_copy(w_out.at[:, pl.ds(pl.multiple_of(j * TC, TC), TC)], wbuf.at[s], w_s.at[s, 0])

    def p2():
        w_load(0, 0).start()

        def go(j, _):
            s = lax.rem(j, 2)

            @pl.when(j + 1 < NW)
            def _():
                w_load(j + 1, 1 - s).start()

            w_load(j, s).wait()
            dm[:, pl.ds(pl.multiple_of(j * TC, TC), TC)] = jnp.dot(gm[...], wbuf[s], preferred_element_type=jnp.float32)
            return 0

        lax.fori_loop(0, NW, go, 0)

    def p4(w, lhs, rhs):
        dst = parts[w]

        def go(j, _):
            s = lax.rem(j, 2)

            @pl.when(j >= 2)
            def _():
                t_copy(dst, j - 2, s).wait()

            tb[s, :, :C] = dot_o(lhs[:, tile_of(j)], rhs[...]).astype(jnp.bfloat16)
            t_copy(dst, j, s).start()
            return 0

        lax.fori_loop(0, NC, go, 0)
        t_copy(dst, NC - 2, NC % 2).wait()
        t_copy(dst, NC - 1, (NC - 1) % 2).wait()
        sc.c_send(w)

    def w3(j, s):
        return [pltpu.make_async_copy(a.at[tile_of(j), :], tb.at[s, :, pl.ds(i * C, C)], w_s.at[2 + s, i])
                for i, a in enumerate((w_in, w_f, w_g))]

    def w3_start(j, s):
        for cp in w3(j, s):
            cp.start()

    def w3_wait(j, s):
        for cp in w3(j, s):
            cp.wait()

    def n_copy(j):
        return remote(sn.at[j], rn1.at[j], t_s.at[j], t_r.at[j], OTHER)

    def p5(j0, j1):
        def go(j, _):
            s = lax.rem(j, 2)

            @pl.when(j + 1 < NC)
            def _():
                w3_start(j + 1, 1 - s)

            w3_wait(j, s)
            o = dot_t(dpi[...], tb[s, :, :C]) + dot_t(dpf[...], tb[s, :, C:2 * C]) + dot_t(dpg[...], tb[s, :, 2 * C:3 * C])
            sn[j] = o.astype(jnp.bfloat16)
            n_copy(j).start()
            return 0

        lax.fori_loop(j0, j1, go, 0)

    def x_load(j, s):
        return pltpu.make_async_copy(x.at[:, pl.ds(j * TC, TC)], tail.at[:, pl.ds(s * TC, TC)], e_s.at[s, 0])

    def p6a(j):
        s = j % 2
        if j == 0:
            x_load(0, 0).start()
        if j + 1 < NC:
            x_load(j + 1, 1 - s).start()
        x_load(j, s).wait()
        n_copy(j).wait_recv()
        g = gain1[:, j * TC:(j + 1) * TC]

        def go(i, _):
            r = pl.ds(pl.multiple_of(i * 16, 16), 16)
            v = tail[r, s * TC:(s + 1) * TC]
            d = sn[j, r, :].astype(jnp.float32) + rn1[j, r, :].astype(jnp.float32)
            a, b = v * v, d * g * v
            a, b = a[:, :128] + a[:, 128:], b[:, :128] + b[:, 128:]
            if j == 0:
                dm[r, :128] = a
                dm[r, 128:256] = b
            else:
                dm[r, :128] = dm[r, :128] + a
                dm[r, 128:256] = dm[r, 128:256] + b
            return 0

        lax.fori_loop(0, n // 16, go, 0, unroll=2)

    def p6b():
        def go(i, _):
            r = pl.ds(pl.multiple_of(i * 16, 16), 16)
            r1 = lax.rsqrt(jnp.sum(dm[r, :128], axis=1, keepdims=True) / width + epsilon)
            inner = jnp.sum(dm[r, 128:256], axis=1, keepdims=True) / width
            dm[r, :128] = jnp.broadcast_to(r1, (16, 128))
            dm[r, 128:256] = jnp.broadcast_to(r1 * r1 * r1 * inner, (16, 128))
            return 0

        lax.fori_loop(0, n // 16, go, 0, unroll=2)

    def dx_copy(j):
        s = j % 2
        return pltpu.make_async_copy(gl.at[:, pl.ds(s * TC, TC)], dx.at[:, pl.ds(j * TC, TC)], eo_s.at[s])

    def p6c(j):
        s = j % 2
        if j == 0:
            x_load(0, 0).start()
        if j + 1 < NC:
            x_load(j + 1, 1 - s).start()
        x_load(j, s).wait()
        if j >= 2:
            dx_copy(j - 2).wait()
        g = gain1[:, j * TC:(j + 1) * TC]

        def go(i, total):
            r = pl.ds(pl.multiple_of(i * 16, 16), 16)
            v = tail[r, s * TC:(s + 1) * TC]
            d = sn[j, r, :].astype(jnp.float32) + rn1[j, r, :].astype(jnp.float32)
            r1 = jnp.concatenate([dm[r, :128], dm[r, :128]], axis=1)
            ri = jnp.concatenate([dm[r, 128:256], dm[r, 128:256]], axis=1)
            gl[r, s * TC:(s + 1) * TC] = dmid[r, j * TC:(j + 1) * TC] + d * g * r1 - v * ri
            return total + jnp.sum(d * v * r1, axis=0, keepdims=True)

        vec[0:1, j * TC:(j + 1) * TC] = lax.fori_loop(0, n // 16, go, jnp.zeros((1, TC), jnp.float32), unroll=2)
        dx_copy(j).start()

    x0, x1, x2, x3, x4, x5, x6 = (X(w) for w in range(7))
    for cp in glu_loads(0, 0):
        cp.start()
    early[5].wait()
    glu_cols(0)
    tick(x0[0])
    glu_cols(1)
    tick(x0[1])
    glu_cols(2)
    tick(x0[2])
    load_n1 = pltpu.make_async_copy(n1, n1v, l_h.at[5])
    load_n1.start()
    early[6].wait()
    glu_grad(1, segments, 0, NC // 2)
    tick(E(0, 0))
    glu_grad(1, segments, NC // 2, NC)
    w_rows(w_mg, 0, 0).start()
    w_rows(w_mu, 0, 1).start()
    tick(x0[3], M(0, 0), E(0, 1))
    normed(0, NC // 2)
    tick(x1[0], M(0, 1), E(0, 2))
    normed(NC // 2, NC)
    for j in range(NC):
        sn_out(pn, j).wait()
    for k in range(NP):
        pn_copy(k).start()
    tick(x1[1], M(0, 2), E(0, 3))
    glu_grad(2, [(du, 0, F)], 0, NC // 2)
    tick(x1[2], M(0, 3))
    glu_grad(2, [(du, 0, F)], NC // 2, NC)
    load_act = pltpu.make_async_copy(act_h, du, l_h.at[6])
    load_act.start()
    w_rows(w_dn, 0, 0).start()
    tick(E(1, 0))
    load_act.wait()
    down(0, NC // 2)
    tick(x1[3], M(1, 0), E(1, 1))
    down(NC // 2, NC)
    for j in range(NC):
        sn_out(po, j).wait()
    for k in range(NP):
        po_copy(k).start()
    p1_load(0)
    tick(x2[0], M(1, 1), E(1, 2))
    early[7].wait()
    between = [[], [x2[1]], [], [M(1, 2), E(1, 3)], [], [x2[2]], [], [M(1, 3)]]
    for k in range(NP):
        if k + 1 < NP:
            p1_load(k + 1)
        p1(k)
        tick(*(between[k] if k < len(between) else []))
    p2()
    tick(x2[3], E(2, 0))
    for cp in early[:5]:
        cp.wait()
    load_n1.wait()
    p4(3, gm, mv)
    tick(M(2, 0), E(2, 1))
    backward_first(n, dm, h, pg, hgain, rh, dpg, col, acc_row(vec, 2, C))
    column_to_rows(col, row, n)
    swap = remote(row, got, s_t.at[0], r_t.at[0], OTHER)
    swap.start()
    tick(x3[0], x3[1])
    swap.wait()
    scale_columns(row, got, col, n, width, lambda v: v / width)
    ends = []
    for sq in range(seqs):
        ends.append(backward_scan_one(sq, length, dm, h, pf, pg, low, hgain, link, rh, col, gl, tail))
        if sq == 0:
            tick(x3[2], M(2, 1), E(2, 2))
    pay[4:8, :] = ids[...]
    for sq in range(seqs):
        pay[sq:sq + 1, :] = ends[sq][1]
        pay[2 + sq:3 + sq, :] = ends[sq][0]
    cps = spread(Z, z, pay, box, s_c, r_c)
    tick(x3[3], M(2, 2), E(2, 3))
    spread_wait(Z, z, pay, box, s_c, r_c, cps)
    end[...] = suffix_state(Z, z, box)
    backward_last(seqs, length, gl, tail, end, h, start, pi, pf, low, link, dpi, dpf, acc_row(vec, 3, C))
    tick(M(2, 3), E(3, 0))
    p4(4, n1v, dpi)
    tick(x4[0], x4[1], M(3, 0), E(3, 1))
    p4(5, n1v, dpf)
    tick(x4[2], x4[3], M(3, 1), E(3, 2))
    p4(6, n1v, dpg)
    w3_start(0, 0)
    tick(x5[0], x5[1], M(3, 2), E(3, 3))
    p5(0, NC // 2)
    tick(x5[2], M(3, 3), E(4, 0))
    p5(NC // 2, NC)
    tick(x5[3], x6[0], x6[1], M(4, 0), E(4, 1))
    late = {3: [x6[2], M(4, 1), E(4, 2)], 7: [x6[3], M(4, 2), E(4, 3)]}
    for j in range(NC):
        p6a(j)
        tick(*late.get(j, []))
    p6b()
    tick(M(4, 3), E(5, 0))
    late = {1: [M(5, 0), E(5, 1)], 3: [M(5, 1), E(5, 2)], 5: [M(5, 2), E(5, 3)], 7: [M(5, 3), E(6, 0)]}
    for j in range(NC):
        p6c(j)
        tick(*late.get(j, []))
    for j in (NC - 2, NC - 1):
        dx_copy(j).wait()
    first = remote(vec, vgot.at[0], v_s.at[0], v_r.at[0], sc.C)
    first.start()
    tick(M(6, 0), E(6, 1))
    first.wait()
    vec[...] = vec[...] + vgot[0]
    second = remote(vec, vgot.at[1], v_s.at[1], v_r.at[1], sc.X)
    second.start()
    tick(M(6, 1), E(6, 2))
    second.wait()
    vec[...] = vec[...] + vgot[1]
    cps = spread(Z, z, vec, vbox, vz_s, vz_r)
    tick(M(6, 2), E(6, 3), M(6, 3))
    spread_wait(Z, z, vec, vbox, vz_s, vz_r, cps)
    total = vbox[0]
    for k in range(1, Z):
        total = total + vbox[k]
    vec_out[...] = total
    for k in range(NP):
        pn_copy(k).wait_send()
        po_copy(k).wait_send()
        po_copy(k).wait_recv()
    for j in range(NC):
        n_copy(j).wait_send()
    for w in range(7):
        sc.drain(w, 7)


def acc_row(vec, k, C):
    return vec.at[k:k + 1, pl.ds(0, C)]


def back_all(Z, seqs, length, gd, gy, n2, act, gate, up, w_dn, w_mg, w_mu, x, mid, cot, n1, m, w_out, w_in, w_f, w_g,
             pi, pf, pg, h, rh, start, ids, link, gain1, gain2, low, hgain, cid=1):
    n, width = x.shape
    C, F = pi.shape[1], gate.shape[1]
    dma = pltpu.SemaphoreType.DMA
    bf, f = jnp.bfloat16, jnp.float32
    sh = jax.ShapeDtypeStruct
    anyw, vmem = pl.BlockSpec(memory_space=pl.ANY), pl.BlockSpec(memory_space=pltpu.VMEM)
    shapes = [(width, F)] * 3 + [(width, C)] * 4
    R = [s[0] // (4 * Z) for s in shapes]
    N = [s[1] for s in shapes]
    Rm, Nm = max(R), max(N)
    NP, NC = n // TR, width // TC
    out_shape = ([sh((n, width), f), sh((8, width), f)]
                 + [sh((r, k), f) for r, k in zip(R, N)]
                 + [sh((width, F), bf)] * 2 + [sh((width, C), bf)] * 4
                 + [sh((n, width), bf)] * 4
                 + [sh((2 * Z * r, k), bf) for r, k in zip(R, N)]
                 + [sh((Z * r, k), bf) for r, k in zip(R, N)]
                 + [sh((Z * r, k), bf) for r, k in zip(R, N)]
                 + [sh((Z * r, k), bf) for r, k in zip(R, N)]
                 + [sh((r // 2, k), bf) for r, k in zip(R, N)])
    V = pltpu.VMEM
    scratch = [
        V((2, Z, Rm, Nm), bf), V((2, Z - 1, Rm, Nm), bf), V((2, 3, Rm, Nm), bf), V((5, Rm, Nm), bf), V((Rm, Nm), f),
        V((n, width), f), V((n, width), bf), V((n, C), f), V((n, C), f), V((n, C), f), V((n, C), f), V((n, C), f),
        V((n, C), f), V((n, C), f), V((n, C), bf), V((n, C), bf), V((n, C), bf), V((n, width), bf), V((n, C), bf),
        V((2, width, TC), bf), V((2, TC, 3 * C), bf), V((n, F), bf), V((NC, n, TC), bf), V((NC, n, TC), bf),
        V((2, 1, TR, width), f), V((2, 2, TR, width), bf), V((8, width), f), V((2, 8, width), f), V((Z, 8, width), f),
        V((n, 1), f), V((seqs, C), f), V((8, C), f), V((Z, 8, C), f), V((n // 128, 128), f), V((n // 128, 128), f),
        dma((8,)), dma((1,)), dma((4, 3)), dma((2,)), dma((NP,)), dma((NP,)), dma((NP,)), dma((NP,)), dma((NC,)), dma((NC,)),
        dma((2, 4)), dma((2,)), dma((2,)), dma((2,)), dma((Z - 1,)), dma((Z,)), dma((Z - 1,)), dma((Z,)), dma((1,)), dma((1,)),
        dma((NC,)),
        dma((7, 2)), dma((7, 2)), dma((7, Z)), dma((7, Z)), dma((7, Z - 1)), dma((7, Z)), dma((7, Z)),
        dma((7,)), dma((7,)), dma((3, 5)), dma((7,)),
    ]
    res = pl.pallas_call(
        functools.partial(back_body, Z, seqs, length),
        out_shape=out_shape,
        in_specs=[anyw] * 22 + [vmem] * 8,
        out_specs=[anyw, vmem] + [anyw] * (len(out_shape) - 2),
        scratch_shapes=scratch,
        compiler_params=pltpu.CompilerParams(collective_id=cid, has_side_effects=True, vmem_limit_bytes=66_000_000),
        name="backward",
    )(gd, gy, n2, act, gate, up, w_dn, w_mg, w_mu, x, mid, cot, n1, m, w_out, w_in, w_f, w_g, pi, pf, pg, h,
      rh, start, ids, link, gain1, gain2, low, hgain)
    return res[0], res[1], res[2:9], res[16], res[18]


def carried_in(x, axis, combine, identity, reverse):
    size, position = (lax.axis_size(axis), lax.axis_index(axis))
    everything = jax.tree.map(lambda part: lax.all_gather(part, axis), x)
    start = jax.tree.map(
        lambda part, zero: jnp.broadcast_to(jnp.asarray(zero, part.dtype), part.shape), x, identity
    )

    def turn(k, before):
        at = size - 1 - k if reverse else k
        reached = at > position if reverse else at < position
        new = combine(before, jax.tree.map(lambda part: part[at], everything))
        return jax.tree.map(lambda a, b: jnp.where(reached, a, b), new, before)

    return lax.fori_loop(0, size, turn, start)


def inverse_rms(inputs):
    return lax.rsqrt(jnp.mean(inputs * inputs, axis=-1, keepdims=True) + epsilon)


def rms_backward(inputs, row_scale, gain_vec, upstream):
    weighted = upstream * gain_vec
    inner_sum = jnp.mean(weighted * inputs, axis=-1, keepdims=True)
    return weighted * row_scale - inputs * (row_scale * row_scale * row_scale) * inner_sum


def silu_slope(inputs):
    sig_part = jax.nn.sigmoid(inputs)
    return sig_part * (1.0 + inputs * (1.0 - sig_part))


def times_back(left_mat, right_mat):
    return lax.dot_general(
        left_mat, right_mat, (((1,), (1,)), ((), ())), preferred_element_type=jnp.float32
    )


def outer_sum(left_mat, right_mat):
    return lax.dot_general(
        left_mat, right_mat, (((0,), (0,)), ((), ())), preferred_element_type=jnp.float32
    )


def linear_step(first_part, second_part):
    return (first_part[0] * second_part[0], second_part[0] * first_part[1] + second_part[1])


def joined_ids(last_ids, first_ids):
    return jnp.where((last_ids == first_ids) | (last_ids < 0.0) | (first_ids < 0.0), 1.0, 0.0)


def forward_join(first_part, second_part):
    linked = joined_ids(first_part[3], second_part[2])[:, None]
    return (
        first_part[0] * second_part[0] * linked,
        second_part[0] * linked * first_part[1] + second_part[1],
        jnp.where(first_part[2] < 0.0, second_part[2], first_part[2]),
        jnp.where(second_part[3] < 0.0, first_part[3], second_part[3]),
    )


def backward_join(first_part, second_part):
    linked = joined_ids(second_part[3], first_part[2])[:, None]
    return (
        second_part[0] * linked * first_part[0],
        second_part[0] * linked * first_part[1] + second_part[1],
        jnp.where(second_part[2] < 0.0, first_part[2], second_part[2]),
        jnp.where(first_part[3] < 0.0, second_part[3], first_part[3]),
    )


def mixer_forward_plain(seqs, length, width, pi, pf, pg, lower, gain, segs):
    channels = pi.shape[1]
    forget = lower + (1.0 - lower) * jax.nn.sigmoid(pf)
    candidate = jax.nn.silu(pi) * (1.0 - forget)
    inner_link = jnp.concatenate(
        [jnp.ones((seqs, 1), jnp.float32), jnp.where(segs[:, 1:] == segs[:, :-1], 1.0, 0.0)], axis=1
    )
    decay = forget.reshape(seqs, length, channels) * inner_link[:, :, None]
    prod, local = lax.associative_scan(
        linear_step, (decay, candidate.reshape(seqs, length, channels)), axis=1
    )
    first, last = segs[:, 0], segs[:, -1]
    ones, zero = jnp.ones((seqs, channels), jnp.float32), jnp.zeros((seqs, channels), jnp.float32)
    minus = -jnp.ones((seqs,), jnp.float32)
    prefix = carried_in(
        (prod[:, -1], local[:, -1], first, last), "ctx", forward_join, (ones, zero, minus, minus), False
    )
    start = joined_ids(prefix[3], first)[:, None] * prefix[1]
    h = (local + prod * start[:, None, :]).reshape(seqs * length, channels)
    squares = lax.psum(jnp.sum(h * h, axis=1), "tp")
    rh = lax.rsqrt(squares / width + epsilon)[:, None]
    m = (h * rh * gain * jax.nn.silu(pg)).astype(jnp.bfloat16)
    return h, m, rh, start


def mixer_backward_plain(seqs, length, width, dm, h, pi, pf, pg, lower, gain, segs, rh, start):
    channels = pi.shape[1]
    s = jax.nn.sigmoid(pf)
    forget = lower + (1.0 - lower) * s
    inner_link = jnp.concatenate(
        [jnp.ones((seqs, 1), jnp.float32), jnp.where(segs[:, 1:] == segs[:, :-1], 1.0, 0.0)], axis=1
    )
    forget_seq = forget.reshape(seqs, length, channels)
    decay = forget_seq * inner_link[:, :, None]
    silu_gate = jax.nn.silu(pg)
    weighted = dm * gain * silu_gate
    inner = lax.psum(jnp.sum(weighted * h, axis=1), "tp")
    dh = weighted * rh - h * (rh * rh * rh) * (inner / width)[:, None]
    gain_grad = jnp.sum(dm * h * rh * silu_gate, axis=0)
    dpg = (dm * h * rh * gain * silu_slope(pg)).astype(jnp.bfloat16)
    ones_row = jnp.ones((seqs, 1, channels), jnp.float32)
    following = jnp.concatenate([decay[:, 1:], ones_row], axis=1)
    tail, local = lax.associative_scan(
        linear_step, (following, dh.reshape(seqs, length, channels)), reverse=True, axis=1
    )
    first, last = segs[:, 0], segs[:, -1]
    ones, zero = jnp.ones((seqs, channels), jnp.float32), jnp.zeros((seqs, channels), jnp.float32)
    minus = -jnp.ones((seqs,), jnp.float32)
    suffix = carried_in(
        (decay[:, 0] * tail[:, 0], forget_seq[:, 0] * local[:, 0], first, last),
        "ctx", backward_join, (ones, zero, minus, minus), True,
    )
    end = joined_ids(last, suffix[2])[:, None] * suffix[1]
    g = (local + tail * end[:, None, :]).reshape(seqs * length, channels)
    states = h.reshape(seqs, length, channels)
    previous = jnp.concatenate(
        [start[:, None, :], inner_link[:, 1:, None] * states[:, :-1]], axis=1
    ).reshape(seqs * length, channels)
    dforget = g * (previous - jax.nn.silu(pi))
    dpi = (g * (1.0 - forget) * silu_slope(pi)).astype(jnp.bfloat16)
    dpf = (dforget * (1.0 - lower) * s * (1.0 - s)).astype(jnp.bfloat16)
    return dpi, dpf, dpg, gain_grad, jnp.sum(dforget * (1.0 - s), axis=0)


def on_device(
    block_input,
    segment_ids,
    norm_gain,
    lower,
    w_input,
    w_forget,
    w_gate,
    hidden_gain,
    w_out,
    mlp_gain,
    w_mlp_gate,
    w_mlp_up,
    w_down,
    cotangent,
):
    bfloat, f32 = jnp.bfloat16, jnp.float32
    seqs, length, width = block_input.shape
    rows_all = seqs * length
    small = lax.axis_size("shard") == 4
    Z = lax.axis_size("ctx")
    shards = [w_input, w_forget, w_gate, w_out, w_mlp_gate, w_mlp_up, w_down]
    segs = segment_ids.astype(f32)
    residual_in = block_input.reshape(rows_all, width)
    upstream = cotangent.reshape(rows_all, width)
    channels = lower.shape[0]
    if small:
        link = jnp.concatenate(
            [jnp.ones((seqs, 1), f32), jnp.where(segs[:, 1:] == segs[:, :-1], 1.0, 0.0)], axis=1
        ).reshape(rows_all, 1)
        ids = jnp.broadcast_to(
            jnp.concatenate([segs[:, 0], segs[:, -1]])[:, None], (2 * seqs, channels)
        )
        low_row, gain_row = lower[None, :], hidden_gain[None, :]
        gain_one, gain_two = norm_gain[None, :], mlp_gain[None, :]
        wide, kept = front_all(
            Z, seqs, length, shards, residual_in, upstream, gain_one, gain_two, low_row, gain_row, link, ids
        )
        (normed_one, pi, pf, pg, h, mixed_in, middle, normed_two, gate_pre, up_pre, activated, upstream_low,
         grad_down, rh, start) = kept
        wide_input, wide_forget, wide_gate, wide_out, wide_mgate, wide_mup, wide_down = wide
        grad_resid, vectors, sums, down_mine, down_other = back_all(
            Z, seqs, length, grad_down, upstream_low, normed_two, activated, gate_pre, up_pre, wide_down, wide_mgate,
            wide_mup, residual_in, middle, upstream, normed_one, mixed_in, wide_out, wide_input, wide_forget, wide_gate,
            pi, pf, pg, h, rh, start, ids, link, gain_one, gain_two, low_row, gain_row
        )
        output = middle + (down_mine.astype(f32) + down_other.astype(f32))
        grad_norm_gain, grad_mlp_gain = vectors[0], vectors[1]
        grad_hidden_gain, grad_lower = vectors[2, :channels], vectors[3, :channels]
    else:
        wide = [lax.all_gather(w.astype(bfloat), ("shard", "ctx"), axis=0, tiled=True) for w in shards]
        wide_input, wide_forget, wide_gate, wide_out, wide_mgate, wide_mup, wide_down = wide
        scale_one = inverse_rms(residual_in)
        normed_one = (residual_in * scale_one * norm_gain).astype(bfloat)
        pi = jnp.dot(normed_one, wide_input, preferred_element_type=f32)
        pf = jnp.dot(normed_one, wide_forget, preferred_element_type=f32)
        pg = jnp.dot(normed_one, wide_gate, preferred_element_type=f32)
        h, mixed_in, rh, start = mixer_forward_plain(
            seqs, length, width, pi, pf, pg, lower, hidden_gain, segs
        )
        mixer_out = lax.psum(times_back(mixed_in, wide_out).astype(bfloat), "tp").astype(f32)
        middle = residual_in + mixer_out
        scale_two = inverse_rms(middle)
        normed_two = (middle * scale_two * mlp_gain).astype(bfloat)
        gate_pre = jnp.dot(normed_two, wide_mgate, preferred_element_type=f32)
        up_pre = jnp.dot(normed_two, wide_mup, preferred_element_type=f32)
        silu_mlp = jax.nn.silu(gate_pre)
        activated = (silu_mlp * up_pre).astype(bfloat)
        upstream_low = upstream.astype(bfloat)
        grad_down = outer_sum(upstream_low, activated).astype(bfloat)
        grad_activ = jnp.dot(upstream_low, wide_down, preferred_element_type=f32)
        grad_gate_pre = (grad_activ * up_pre * silu_slope(gate_pre)).astype(bfloat)
        grad_up_pre = (grad_activ * silu_mlp).astype(bfloat)
        grad_mgate = outer_sum(normed_two, grad_gate_pre).astype(bfloat)
        grad_mup = outer_sum(normed_two, grad_up_pre).astype(bfloat)
        down_part = times_back(activated, wide_down).astype(bfloat)
        normed_part = (times_back(grad_gate_pre, wide_mgate) + times_back(grad_up_pre, wide_mup)).astype(bfloat)
        output = middle + lax.psum(down_part, "tp").astype(f32)
        grad_normed_two = lax.psum(normed_part, "tp").astype(f32)
        grad_mlp_gain = jnp.sum(grad_normed_two * middle * scale_two, axis=0)
        grad_middle = upstream + rms_backward(middle, scale_two, mlp_gain, grad_normed_two)
        middle_low = grad_middle.astype(bfloat)
        dm = jnp.dot(middle_low, wide_out, preferred_element_type=f32)
        grad_out = outer_sum(middle_low, mixed_in).astype(bfloat)
        dpi, dpf, dpg, grad_hidden_gain, grad_lower = mixer_backward_plain(
            seqs, length, width, dm, h, pi, pf, pg, lower, hidden_gain, segs, rh, start
        )
        grad_w_input = outer_sum(normed_one, dpi).astype(bfloat)
        grad_w_forget = outer_sum(normed_one, dpf).astype(bfloat)
        grad_w_gate = outer_sum(normed_one, dpg).astype(bfloat)
        grad_normed_one = lax.psum(
            (
                times_back(dpi, wide_input) + times_back(dpf, wide_forget) + times_back(dpg, wide_gate)
            ).astype(bfloat),
            "tp",
        ).astype(f32)
        grad_norm_gain = jnp.sum(grad_normed_one * residual_in * scale_one, axis=0)
        grad_resid = grad_middle + rms_backward(residual_in, scale_one, norm_gain, grad_normed_one)
        vectors = lax.psum(
            jnp.concatenate([grad_norm_gain, grad_mlp_gain, grad_lower, grad_hidden_gain]), ("shard", "ctx")
        )
        grad_norm_gain, grad_mlp_gain = vectors[:width], vectors[width : 2 * width]
        grad_lower = vectors[2 * width : 2 * width + channels]
        grad_hidden_gain = vectors[2 * width + channels :]
        sums = [
            lax.psum_scatter(p, ("shard", "ctx"), scatter_dimension=0, tiled=True).astype(f32)
            for p in (grad_down, grad_mgate, grad_mup, grad_out, grad_w_input, grad_w_forget, grad_w_gate)
        ]
    return (
        output.reshape(block_input.shape),
        grad_resid.reshape(block_input.shape),
        grad_norm_gain,
        grad_lower,
        sums[4],
        sums[5],
        sums[6],
        grad_hidden_gain,
        sums[3],
        grad_mlp_gain,
        sums[1],
        sums[2],
        sums[0],
    )


def solution(mesh):
    return jax.shard_map(
        on_device,
        mesh=mesh,
        in_specs=(
            P("shard", "ctx", None),
            P("shard", "ctx"),
            P(),
            P("tp"),
            P(("shard", "ctx"), "tp"),
            P(("shard", "ctx"), "tp"),
            P(("shard", "ctx"), "tp"),
            P("tp"),
            P(("shard", "ctx"), "tp"),
            P(),
            P(("shard", "ctx"), "tp"),
            P(("shard", "ctx"), "tp"),
            P(("shard", "ctx"), "tp"),
            P("shard", "ctx", None),
        ),
        out_specs=(
            P("shard", "ctx", None),
            P("shard", "ctx", None),
            P(),
            P("tp"),
            P(("shard", "ctx"), "tp"),
            P(("shard", "ctx"), "tp"),
            P(("shard", "ctx"), "tp"),
            P("tp"),
            P(("shard", "ctx"), "tp"),
            P(),
            P(("shard", "ctx"), "tp"),
            P(("shard", "ctx"), "tp"),
            P(("shard", "ctx"), "tp"),
        ),
        check_vma=False,
    )
```

```python
import functools
import jax
import jax.numpy as jnp
from jax import lax
from jax.experimental import pallas as pl
from jax.experimental.pallas import tpu as pltpu
from jax.sharding import PartitionSpec as P

epsilon = 1e-06
MESH = pl.DeviceIdType.MESH


def remote(src, dst, send_sem, recv_sem, device):
    return pltpu.make_async_remote_copy(
        src_ref=src, dst_ref=dst, send_sem=send_sem, recv_sem=recv_sem,
        device_id=device, device_id_type=MESH)


def pick(z, values):
    out = jnp.int32(values[-1])
    for k in range(len(values) - 2, -1, -1):
        out = jnp.where(z == k, values[k], out)
    return out


def far_first(Z):
    table = []
    for z in range(Z):
        ups, dns, mine, turn = list(range(Z - 1, z, -1)), list(range(0, z)), [], z < Z // 2
        while ups or dns:
            if (turn and ups) or not dns:
                mine.append(ups.pop(0))
            else:
                mine.append(dns.pop(0))
            turn = not turn
        table.append(mine + [z])
    return table


class Scatter:
    def __init__(self, Z, parts, rc, xr, zu, zd, hr, outs, xs, zs, stage, fin, sems):
        self.Z, self.parts, self.rc, self.xr, self.zu, self.zd, self.hr, self.outs = Z, parts, rc, xr, zu, zd, hr, outs
        self.xs, self.zs, self.stage, self.fin = xs, zs, stage, fin
        (self.c_s, self.c_r, self.x_s, self.x_r, self.z_s, self.u_r, self.d_r, self.h_s, self.h_r, self.l_s, self.f_s) = sems
        s, z = lax.axis_index("shard"), lax.axis_index("ctx")
        q, c = s // 2, lax.rem(s, 2)
        self.z, self.q, self.c = z, q, c
        self.even = lax.rem(z, 2) == 0
        self.zp = jnp.where(self.even, z + 1, z - 1)
        self.X = {"shard": (1 - q) * 2 + c}
        self.C = {"shard": q * 2 + (1 - c)}
        self.UP, self.DN, self.ZP = {"ctx": z + 1}, {"ctx": z - 1}, {"ctx": self.zp}
        self.R = [p.shape[0] // (4 * Z) for p in parts]
        self.N = [p.shape[1] for p in parts]
        self.ffirst = far_first(Z)

    def part(self, w, q, c, z, n=1):
        R = self.R[w]
        return self.parts[w].at[pl.ds(pl.multiple_of(((2 * q + c) * self.Z + z) * R, R), n * R), :]

    def rows(self, ref, i, w):
        R = self.R[w]
        return ref.at[pl.ds(pl.multiple_of(i * R, R), R), :]

    def hrows(self, ref, i, w, h):
        H = self.R[w] // 2
        return ref.at[pl.ds(pl.multiple_of(i * 2 * H + h * H, H), H), :]

    def c_copy(self, w, k):
        Z, R = self.Z, self.R[w]
        q = self.q if k == 1 else 1 - self.q
        return remote(self.part(w, q, 1 - self.c, 0, Z), self.rc[w].at[pl.ds(k * Z * R, Z * R), :],
                      self.c_s.at[w, k], self.c_r.at[w, k], self.C)

    def c_send(self, w):
        for k in (0, 1):
            self.c_copy(w, k).start()

    def stage_of(self, slot):
        return self.stage[0].at[slot] if slot < 2 else self.stage[1]

    def load_waits(self, w, srcs, slot):
        cps = []
        for i, src in enumerate(srcs):
            if src is not None:
                n = src.shape[0]
                cps.append(pltpu.make_async_copy(
                    src, self.stage_of(slot).at[i, pl.ds(0, n), pl.ds(0, self.N[w])], self.l_s.at[slot, i]))
        return cps

    def load(self, w, srcs, slot):
        cps = self.load_waits(w, srcs, slot)
        for cp in cps:
            cp.start()
        return cps

    def add(self, w, slot, idx, store, lo=0, hi=None, off=None):
        N = self.N[w]
        hi = self.R[w] if hi is None else hi
        G = 16

        def go(i, _):
            r = pl.multiple_of(lo + i * G, G)
            tot = None
            for k in idx:
                rk = r
                if off is not None and k in off:
                    rk = pl.multiple_of(r + off[k], G)
                v = self.stage_of(slot)[k, pl.ds(rk, G), pl.ds(0, N)].astype(jnp.float32)
                tot = v if tot is None else tot + v
            store(r, tot)
            return 0

        lax.fori_loop(0, (hi - lo) // G, go, 0)

    def x_slot(self, w, n):
        return self.xs.at[w % 2, n, :, pl.ds(0, self.N[w])]

    def order(self, n):
        return pick(self.z, [t[n] for t in self.ffirst])

    def x_copy(self, w, n, half=None):
        zt = self.order(n)
        src = self.x_slot(w, n)
        H = self.R[w] // 2
        if half is None:
            return remote(src, self.rows(self.xr[w], zt, w), self.x_s.at[w, n], self.x_r.at[w, n], self.X)
        return remote(src.at[pl.ds(half * H, H), :], self.hrows(self.xr[w], zt, w, half), self.x_s.at[w, n], self.x_r.at[w, n], self.X)

    def h_copy(self, w, n=0):
        H = self.R[w] // 2
        return remote(self.x_slot(w, n).at[pl.ds(0, H), :], self.hr[w], self.h_s.at[w], self.h_r.at[w], self.ZP)

    def on_pair(self, n, yes, no):
        if n == self.Z - 1:
            no()
            return
        paired = self.order(n) == self.zp

        @pl.when(paired)
        def _():
            yes()

        @pl.when(jnp.logical_not(paired))
        def _():
            no()

    def x_load(self, w, n):
        zt = self.order(n)
        return self.load(w, [self.part(w, 1 - self.q, self.c, zt), self.rows(self.rc[w], zt, w)], n % 2)

    def x_phase(self, w, n):
        Z, H = self.Z, self.R[w] // 2
        last = n == Z - 1
        if n == 0:
            self.c_copy(w, 0).wait_recv()
            self.x_load(w, 0)
        if not last:
            self.x_load(w, n + 1)
        if last:
            self.h_copy(w).wait_recv()
            for cp in self.load(w, [None, None, self.hr[w]], n % 2):
                cp.wait()
        if w >= 2:
            self.x_wait_send(w - 2, n)
        zt = self.order(n)
        for cp in self.load_waits(w, [self.part(w, 1 - self.q, self.c, zt), self.rows(self.rc[w], zt, w)], n % 2):
            cp.wait()
        dst = self.x_slot(w, n)

        def store(r, v):
            dst[pl.ds(r, 16), :] = v.astype(jnp.bfloat16)

        if last:
            self.add(w, n % 2, (0, 1, 2), store, 0, H)
            self.add(w, n % 2, (0, 1), store, H, 2 * H)
            self.x_copy(w, n).start()
        else:
            self.add(w, n % 2, (0, 1), store)

            def yes():
                self.h_copy(w, n).start()
                self.x_copy(w, n, 1).start()

            self.on_pair(n, yes, lambda: self.x_copy(w, n).start())

    def x_wait_send(self, w, n):
        def yes():
            self.h_copy(w, n).wait_send()
            self.x_copy(w, n, 1).wait_send()

        self.on_pair(n, yes, lambda: self.x_copy(w, n).wait_send())

    def z_copy(self, w, n, dest, up):
        src = self.zs.at[w % 2, n, :, pl.ds(0, self.N[w])]
        if up:
            return remote(src, self.rows(self.zu[w], dest, w), self.z_s.at[w, n], self.u_r.at[w, dest], self.UP)
        return remote(src, self.rows(self.zd[w], dest, w), self.z_s.at[w, n], self.d_r.at[w, dest], self.DN)

    def x_wait(self, w, n):
        self.on_pair(n, lambda: self.x_copy(w, n, 1).wait_recv(), lambda: self.x_copy(w, n).wait_recv())

    def z_step(self, w, n, end):
        at_end = (self.z == 0) | (self.z == self.Z - 1)

        @pl.when(at_end if end else jnp.logical_not(at_end))
        def _():
            self.z_phase(w, n, end)

    def z_in(self, w, dest, up, k):
        self.z_copy(w, 0, dest, up).wait_recv()
        self.load(w, [None] * k + [self.rows((self.zu if up else self.zd)[w], dest, w)], 2)[0].wait()

    def z_phase(self, w, n, end):
        Z, H = self.Z, self.R[w] // 2
        z = self.z
        last = n == Z - 1
        dest = z if last else self.order(n)
        if n == 0:
            self.c_copy(w, 1).wait_recv()
        self.x_wait(w, n)
        cps = self.load(w, [self.part(w, self.q, self.c, dest), self.rows(self.rc[w], dest + Z, w),
                            self.rows(self.xr[w], dest, w)], 2)
        if last:
            if end:
                @pl.when(z > 0)
                def _():
                    self.z_in(w, dest, True, 3)

                @pl.when(z == 0)
                def _():
                    self.z_in(w, dest, False, 3)
            else:
                self.z_in(w, dest, True, 3)
                self.z_in(w, dest, False, 4)
            for cp in cps:
                cp.wait()
            if w >= 1:
                self.f_copy(w - 1).wait()
            dst = self.fin.at[:, pl.ds(0, self.N[w])]

            def store(r, v):
                dst[pl.ds(r, 16), :] = v

            self.add(w, 2, (0, 1, 2, 3) if end else (0, 1, 2, 3, 4), store)
            self.f_copy(w).start()
            return
        up = dest > z
        if not end:
            @pl.when(up)
            def _():
                self.z_in(w, dest, True, 3)

            @pl.when(jnp.logical_not(up))
            def _():
                self.z_in(w, dest, False, 3)
        if w >= 2:
            self.z_wait_send(w - 2, n)
        for cp in cps:
            cp.wait()
        dst = self.zs.at[w % 2, n, :, pl.ds(0, self.N[w])]

        def store(r, v):
            dst[pl.ds(r, 16), :] = v.astype(jnp.bfloat16)

        more = () if end else (3,)
        paired = dest == self.zp

        @pl.when(paired)
        def _():
            self.add(w, 2, (0, 1) + more, store, 0, H)
            self.add(w, 2, (0, 1, 2) + more, store, H, 2 * H)

        @pl.when(jnp.logical_not(paired))
        def _():
            self.add(w, 2, (0, 1, 2) + more, store)

        @pl.when(up)
        def _():
            self.z_copy(w, n, dest, True).start()

        @pl.when(jnp.logical_not(up))
        def _():
            self.z_copy(w, n, dest, False).start()

    def z_wait_send(self, w, n):
        z = self.z
        dest = pick(z, [t[n] for t in self.ffirst])
        self.z_copy_any(w, n).wait_send()

    def z_copy_any(self, w, n):
        src = self.zs.at[w % 2, n, :, pl.ds(0, self.N[w])]
        return remote(src, self.rows(self.zu[w], 0, w), self.z_s.at[w, n], self.u_r.at[w, 0],
                      {"ctx": jnp.where(pick(self.z, [t[n] for t in self.ffirst]) > self.z, self.z + 1, self.z - 1)})

    def f_copy(self, w):
        return pltpu.make_async_copy(self.fin.at[:, pl.ds(0, self.N[w])], self.outs[w], self.f_s.at[w])

    def drain(self, w, nw):
        for k in (0, 1):
            self.c_copy(w, k).wait_send()
        if w >= nw - 2:
            for n in range(self.Z):
                self.x_wait_send(w, n)
            for n in range(self.Z - 1):
                self.z_wait_send(w, n)
        if w == nw - 1:
            self.f_copy(w).wait()


T8 = 8


def spread(Z, z, pay, box, s_sem, r_sem):
    cps = []
    for o in range(1, Z):
        to = lax.rem(z + o, Z)
        cp = remote(pay, box.at[z], s_sem.at[o - 1], r_sem.at[z], {"ctx": to})
        cp.start()
        cps.append(cp)
    box[z] = pay[...]
    return cps


def spread_wait(Z, z, pay, box, s_sem, r_sem, cps):
    for o in range(1, Z):
        frm = lax.rem(z + o, Z)
        remote(pay, box.at[frm], s_sem.at[o - 1], r_sem.at[frm], {"ctx": frm}).wait_recv()
    for cp in cps:
        cp.wait_send()


def joined(box, k):
    last, first = box[k, 6:8, :], box[k + 1, 4:6, :]
    return jnp.where(last == first, 1.0, 0.0)


def prefix_state(Z, z, box):
    state = jnp.zeros(box.shape[2:][:0] + (2, box.shape[2]), jnp.float32)
    mine = state
    for k in range(Z - 1):
        state = joined(box, k) * (box[k, 2:4, :] + box[k, 0:2, :] * state)
        mine = jnp.where(z == k + 1, state, mine)
    return mine


def suffix_state(Z, z, box):
    state = jnp.zeros((2, box.shape[2]), jnp.float32)
    mine = state
    for k in range(Z - 2, -1, -1):
        state = joined(box, k) * (box[k + 1, 2:4, :] + box[k + 1, 0:2, :] * state)
        mine = jnp.where(z == k, state, mine)
    return mine


def diagonal():
    return lax.broadcasted_iota(jnp.int32, (128, 128), 0) == lax.broadcasted_iota(jnp.int32, (128, 128), 1)


def column_to_rows(col_ref, row_ref, n):
    eye = diagonal()
    for k in range(n // 128):
        col = col_ref[pl.ds(k * 128, 128), :]
        row_ref[k:k + 1, :] = jnp.sum(jnp.where(eye, jnp.broadcast_to(col, (128, 128)), 0.0), axis=0, keepdims=True)


def rows_to_column(row, k):
    return jnp.sum(jnp.where(diagonal(), jnp.broadcast_to(row, (128, 128)), 0.0), axis=1, keepdims=True)


def sigmoid(v):
    return jax.nn.sigmoid(v)


def row_at(ref, t):
    return pl.ds(pl.multiple_of(t, T8), T8)


def forward_scan_one(sq, length, pi, pf, lower, link, h, cum):
    C = pi.shape[1]
    low = lower[...]
    iota = lax.broadcasted_iota(jnp.int32, (T8, C), 0)

    def tile(i, carry):
        hl, pr = carry
        r = row_at(pi, sq * length + i * T8)
        s = sigmoid(pf[r, :])
        forget = low + (1.0 - low) * s
        x = pi[r, :]
        b = x * sigmoid(x) * (1.0 - forget)
        a = forget * link[r, :]
        for sh in (1, 2, 4):
            keep = iota >= sh
            b = b + jnp.where(keep, a * pltpu.roll(b, sh, 0), 0.0)
            a = jnp.where(keep, a * pltpu.roll(a, sh, 0), a)
        b = b + a * hl
        a = a * pr
        h[r, :] = b
        cum[r, :] = a
        return b[T8 - 1:T8, :], a[T8 - 1:T8, :]

    return lax.fori_loop(0, length // T8, tile, (jnp.zeros((1, C), jnp.float32), jnp.ones((1, C), jnp.float32)), unroll=2)


def forward_finish(seqs, length, h, cum, start, col):
    def tile(i, _, sq):
        r = row_at(h, sq * length + i * T8)
        v = h[r, :] + cum[r, :] * start[sq:sq + 1, :]
        h[r, :] = v
        col[r, :] = jnp.sum(v * v, axis=1, keepdims=True)
        return 0

    for sq in range(seqs):
        lax.fori_loop(0, length // T8, functools.partial(tile, sq=sq), 0, unroll=2)


def swap_columns(col, row, got, s_sem, r_sem, other, n):
    column_to_rows(col, row, n)
    cp = remote(row, got, s_sem, r_sem, {"tp": other})
    cp.start()
    cp.wait()


def scale_columns(row, got, col, n, width, fn):
    for k in range(n // 128):
        col[pl.ds(k * 128, 128), :] = fn(rows_to_column(row[k:k + 1, :] + got[k:k + 1, :], k))


def mixed(h, rh, gain, pg, m, step=16):
    g = gain[...]

    def tile(i, _):
        r = pl.ds(pl.multiple_of(i * step, step), step)
        p = pg[r, :]
        m[r, :] = (h[r, :] * rh[r, :] * g * (p * sigmoid(p))).astype(m.dtype)
        return 0

    lax.fori_loop(0, h.shape[0] // step, tile, 0)


def backward_first(n, dm, h, pg, gain, rh, dpg, col, gsum, step=16):
    g = gain[...]

    def tile(i, acc):
        r = pl.ds(pl.multiple_of(i * step, step), step)
        d, hv, p, rv = dm[r, :], h[r, :], pg[r, :], rh[r, :]
        s = sigmoid(p)
        sl = p * s
        q = d * g * sl
        col[r, :] = jnp.sum(q * hv, axis=1, keepdims=True)
        hr = d * hv * rv
        dpg[r, :] = (hr * g * (s * (1.0 + p * (1.0 - s)))).astype(dpg.dtype)
        return acc + jnp.sum(hr * sl, axis=0, keepdims=True)

    gsum[...] = lax.fori_loop(0, n // step, tile, jnp.zeros(gsum.shape, jnp.float32))


def backward_scan_one(sq, length, dm, h, pf, pg, lower, gain, link, rh, inner, gl, tail):
    C = dm.shape[1]
    low, g = lower[...], gain[...]
    iota = lax.broadcasted_iota(jnp.int32, (T8, C), 0)
    nt = length // T8
    def tile(k, carry):
        vl, pr = carry
        r = row_at(dm, sq * length + (nt - 1 - k) * T8)
        rv = rh[r, :]
        p = pg[r, :]
        q = dm[r, :] * g * (p * sigmoid(p))
        dh = q * rv - h[r, :] * (rv * rv * rv) * inner[r, :]
        a = (low + (1.0 - low) * sigmoid(pf[r, :])) * link[r, :]
        b = a * dh
        for sh in (1, 2, 4):
            keep = iota < T8 - sh
            b = b + jnp.where(keep, a * pltpu.roll(b, T8 - sh, 0), 0.0)
            a = jnp.where(keep, a * pltpu.roll(a, T8 - sh, 0), a)
        v = b + a * vl
        pa = a * pr
        last = iota == T8 - 1
        gl[r, :] = dh + jnp.where(last, vl, pltpu.roll(v, T8 - 1, 0))
        tail[r, :] = jnp.where(last, pr, pltpu.roll(pa, T8 - 1, 0))
        return v[0:1, :], pa[0:1, :]

    return lax.fori_loop(0, nt, tile, (jnp.zeros((1, C), jnp.float32), jnp.ones((1, C), jnp.float32)), unroll=2)


def backward_last(seqs, length, gl, tail, end, h, start, pi, pf, lower, link, dpi, dpf, lsum):
    C = gl.shape[1]
    low = lower[...]
    iota = lax.broadcasted_iota(jnp.int32, (T8, C), 0)
    total = jnp.zeros((1, C), jnp.float32)
    for sq in range(seqs):
        def tile(i, carry):
            acc, hp = carry
            halves = []
            for half in (0, 1):
                r = row_at(gl, sq * length + i * 16 + half * T8)
                gv = gl[r, :] + tail[r, :] * end[sq:sq + 1, :]
                hv = h[r, :]
                prev = jnp.where(iota == 0, hp, pltpu.roll(hv, 1, 0) * link[r, :])
                if half == 1:
                    prev = jnp.where(iota == 0, prev * link[r, :], prev)
                else:
                    prev = jnp.where((iota == 0) & (i > 0), prev * link[r, :], prev)
                s = sigmoid(pf[r, :])
                forget = low + (1.0 - low) * s
                x = pi[r, :]
                sx = sigmoid(x)
                df = gv * (prev - x * sx)
                halves.append((gv * (1.0 - forget) * (sx * (1.0 + x * (1.0 - sx))), df * (1.0 - low) * s * (1.0 - s)))
                acc = acc + jnp.sum(df * (1.0 - s), axis=0, keepdims=True)
                hp = hv[T8 - 1:T8, :]
            r = pl.ds(pl.multiple_of(sq * length + i * 16, 16), 16)
            dpi[r, :] = jnp.concatenate([halves[0][0], halves[1][0]], axis=0).astype(dpi.dtype)
            dpf[r, :] = jnp.concatenate([halves[0][1], halves[1][1]], axis=0).astype(dpf.dtype)
            return acc, hp

        total, _ = lax.fori_loop(0, length // 16, tile, (total, start[sq:sq + 1, :]))
    lsum[...] = total


def gather_steps(nw, Z, ahead, relay, own, out, sems):
    (s_up, r_up, s_dn, r_dn, s_x, r_x, s_c, r_c, s_h, r_h, l_sem) = sems
    s, z = lax.axis_index("shard"), lax.axis_index("ctx")
    q, c = s // 2, lax.rem(s, 2)
    sx, sc = (1 - q) * 2 + c, q * 2 + (1 - c)
    sxc = (1 - q) * 2 + (1 - c)
    even = lax.rem(z, 2) == 0
    zp = jnp.where(even, z + 1, z - 1)
    rows = [r.shape[0] for r in own]

    def block(w, s_, z_, part=0):
        R = rows[w]
        start = pl.multiple_of((s_ * Z + z_) * R, R)
        if part == 0:
            return out[w].at[pl.ds(start, R), :]
        H = R // 2
        return out[w].at[pl.ds(pl.multiple_of(start + (part - 1) * H, H), H), :]

    UP, DN, XX, CC, ZP = {"ctx": z + 1}, {"ctx": z - 1}, {"shard": sx}, {"shard": sc}, {"ctx": zp}

    def up(w, k, src=None):
        b = block(w, s, z - k)
        return remote(b if src is None else src, b, s_up.at[w, k], r_up.at[w, k], UP)

    def dn(w, k, src=None):
        b = block(w, s, z + k)
        return remote(b if src is None else src, b, s_dn.at[w, k], r_dn.at[w, k], DN)

    def origin(j):
        return z if j == 0 else (z - j if j < Z else z + j - Z + 1)

    def valid(j):
        return (z >= j) if j < Z else (z + j - Z + 1 <= Z - 1)

    def xx(w, j, part, src=None):
        b = block(w, s, origin(j), part)
        return remote(b if src is None else src, b, s_x.at[w, j], r_x.at[w, j], XX)

    def xx_in(w, j, part):
        b = block(w, sx, origin(j), part)
        return remote(b, b, s_x.at[w, j], r_x.at[w, j], XX)

    def cc(w, j, src=None):
        b = block(w, s if j < 2 * Z - 1 else sx, origin(j % (2 * Z - 1)))
        return remote(b if src is None else src, b, s_c.at[w, j], r_c.at[w, j], CC)

    def cc_in(w, j):
        b = block(w, sc if j < 2 * Z - 1 else sxc, origin(j % (2 * Z - 1)))
        return remote(b, b, s_c.at[w, j], r_c.at[w, j], CC)

    def half(w):
        b = block(w, sx, z, 1)
        return remote(b, b, s_h.at[w], r_h.at[w], ZP)

    def half_in(w):
        b = block(w, sx, zp, 1)
        return remote(b, b, s_h.at[w], r_h.at[w], ZP)

    local = []
    for w in range(nw):
        local.append(pltpu.make_async_copy(own[w], block(w, s, z), l_sem.at[w]))

    def begin(w):
        local[w].start()

        @pl.when(z < Z - 1)
        def _():
            up(w, 0, own[w]).start()

        @pl.when(z > 0)
        def _():
            dn(w, 0, own[w]).start()

        xx(w, 0, 0, own[w]).start()
        cc(w, 0, own[w]).start()

    def is_pair(j):
        if j == 1:
            return jnp.logical_not(even)
        if j == Z:
            return even
        return None

    def for_part(w, j, fn):
        pair = is_pair(j) if relay else None
        if pair is None:
            fn(0)
        else:
            @pl.when(pair)
            def _():
                fn(2)

            @pl.when(jnp.logical_not(pair))
            def _():
                fn(0)

    def step(w, k):
        @pl.when(z >= k)
        def _():
            remote(block(w, s, z - k), block(w, s, z - k), s_up.at[w, k - 1], r_up.at[w, k - 1], UP).wait_recv()
            if k < Z - 1:
                @pl.when(z < Z - 1)
                def _():
                    up(w, k).start()
            for_part(w, k, lambda p: xx(w, k, p).start())
            cc(w, k).start()

        @pl.when(z + k <= Z - 1)
        def _():
            remote(block(w, s, z + k), block(w, s, z + k), s_dn.at[w, k - 1], r_dn.at[w, k - 1], DN).wait_recv()
            if k < Z - 1:
                @pl.when(z > 0)
                def _():
                    dn(w, k).start()
            for_part(w, Z - 1 + k, lambda p: xx(w, Z - 1 + k, p).start())
            cc(w, Z - 1 + k).start()

    def xstep(w, j):
        @pl.when(valid(j))
        def _():
            for_part(w, j, lambda p: xx_in(w, j, p).wait_recv())
            if j == 0:
                if relay:
                    half(w).start()
                cc(w, 2 * Z - 1).start()
            else:
                if relay and is_pair(j) is not None:
                    @pl.when(is_pair(j))
                    def _():
                        half_in(w).wait_recv()
                cc(w, 2 * Z - 1 + j).start()

    def finish(w):
        for j in range(4 * Z - 2):
            @pl.when(valid(j % (2 * Z - 1)))
            def _():
                cc_in(w, j).wait_recv()
                cc(w, j).wait_send()
        for j in range(2 * Z - 1):
            @pl.when(valid(j))
            def _():
                for_part(w, j, lambda p: xx(w, j, p).wait_send())
        for k in range(Z - 1):
            @pl.when((z >= k) & (z < Z - 1))
            def _():
                up(w, k).wait_send()

            @pl.when((z + k <= Z - 1) & (z > 0))
            def _():
                dn(w, k).wait_send()
        if relay:
            half(w).wait_send()
        local[w].wait()

    def tick(w, k):
        step(w, k)
        if k == 1:
            xstep(w, 0)
            if w + ahead < nw:
                begin(w + ahead)
        else:
            xstep(w, k - 1)
            xstep(w, Z - 1 + k - 1)
        if w > 0 and k == 1:
            xstep(w - 1, Z - 1)
            xstep(w - 1, 2 * Z - 2)

    def last():
        xstep(nw - 1, Z - 1)
        xstep(nw - 1, 2 * Z - 2)

    return begin, tick, last, finish


def front_body(Z, seqs, length, ahead, *refs):
    nw = 7
    wide_own = refs[:nw]
    x, cot, gain1, gain2, low, hgain, link, ids = refs[nw:nw + 8]
    k0 = nw + 8
    wide = refs[k0:k0 + nw]
    k0 += nw
    n1_o, pi_o, pf_o, pg_o, h_o, m_o, mid_o, n2_o, gate_o, up_o, act_o, gy_o, gd_o, rh, start = refs[k0:k0 + 15]
    k0 += 15
    (xv, n1, n2, pi, pf, pg, h, cum, m, wbuf, wob, pn, rn, gate, up, act, gy, stg, e_f,
     pay, box, row, got, wst) = refs[k0:k0 + 24]
    own = refs[k0 + 24:k0 + 24 + nw]
    k0 += 24 + nw
    s_c, r_c, s_t, r_t, n_s, n_r, w_s, o_s, e_s, g_s, x_s, f_s = refs[k0:k0 + 12]
    sems = refs[k0 + 12:]
    w_in, w_f, w_g, w_out, w_mg, w_mu, w_dn = wide
    n, width = x.shape
    C, F = pi.shape[1], gate.shape[1]
    s, z, t = lax.axis_index("shard"), lax.axis_index("ctx"), lax.axis_index("tp")
    q, c = s // 2, lax.rem(s, 2)
    OTHER = {"tp": 1 - t}
    begin, tick, last, finish = gather_steps(nw, Z, ahead, True, own, wide, sems)
    NP, NF, NW, NC = n // TR, F // TC, C // TC, width // TC

    def own_load(w):
        return pltpu.make_async_copy(wide_own[w], wst.at[w % 2, :, pl.ds(0, own[w].shape[1])], f_s.at[w % 2])

    def own_low(w):
        own_load(w).wait()
        cols = own[w].shape[1]

        def go(i, _):
            r = pl.ds(pl.multiple_of(i * 16, 16), 16)
            own[w][r, :] = wst[w % 2, r, :cols].astype(jnp.bfloat16)
            return 0

        lax.fori_loop(0, own[w].shape[0] // 16, go, 0)
        if w + 2 < nw:
            own_load(w + 2).start()

    own_load(0).start()
    own_load(1).start()
    barrier = pltpu.get_barrier_semaphore()
    for d in [{"shard": (1 - q) * 2 + c}, {"shard": q * 2 + (1 - c)}, OTHER] + [{"ctx": lax.rem(z + o, Z)} for o in range(1, Z)]:
        pl.semaphore_signal(barrier, inc=1, device_id=d, device_id_type=MESH)
    pl.semaphore_wait(barrier, 2 + Z)

    for w in range(ahead):
        own_low(w)
        begin(w)
    load_x = pltpu.make_async_copy(x, xv, x_s.at[0])
    load_x.start()
    done = []

    def put(src, dst, k):
        cp = pltpu.make_async_copy(src, dst, o_s.at[k])
        cp.start()
        done.append(cp)

    def norm_in():
        load_x.wait()
        g = gain1[...]

        def go(i, _):
            r = pl.ds(pl.multiple_of(i * 16, 16), 16)
            v = xv[r, :]
            n1[r, :] = (v * lax.rsqrt(jnp.mean(v * v, axis=1, keepdims=True) + epsilon) * g).astype(jnp.bfloat16)
            return 0

        lax.fori_loop(0, n // 16, go, 0, unroll=2)
        put(n1, n1_o, 0)

    def times(lhs, w, dst, tiles, after=None):
        def load(j, s):
            return pltpu.make_async_copy(w.at[:, pl.ds(pl.multiple_of(j * TC, TC), TC)], wbuf.at[s], w_s.at[s])

        load(0, 0).start()

        def go(j, _):
            s = lax.rem(j, 2)

            @pl.when(j + 1 < tiles)
            def _():
                load(j + 1, 1 - s).start()

            load(j, s).wait()
            dst[:, pl.ds(pl.multiple_of(j * TC, TC), TC)] = jnp.dot(lhs[...], wbuf[s], preferred_element_type=jnp.float32)
            if after is not None:
                after(j)
            return 0

        lax.fori_loop(0, tiles, go, 0)

    def rows_of(k):
        return pl.ds(k * TR, TR)

    def pn_copy(k):
        return remote(pn.at[rows_of(k), :], rn.at[rows_of(k), :], n_s.at[k], n_r.at[k], OTHER)

    def out_product():
        def load(j, s):
            return pltpu.make_async_copy(w_out.at[pl.ds(pl.multiple_of(j * TC, TC), TC), :], wob.at[s], w_s.at[s])

        load(0, 0).start()

        def go(j, _):
            s = lax.rem(j, 2)

            @pl.when(j + 1 < NC)
            def _():
                load(j + 1, 1 - s).start()

            load(j, s).wait()
            pn[:, pl.ds(pl.multiple_of(j * TC, TC), TC)] = dot_t(m[...], wob[s]).astype(jnp.bfloat16)
            return 0

        lax.fori_loop(0, NC, go, 0)
        for k in range(NP):
            pn_copy(k).start()

    def middle(k):
        pn_copy(k).wait_recv()
        g = gain2[...]

        def go(i, _):
            r = pl.ds(pl.multiple_of(k * TR + i * 16, 16), 16)
            v = xv[r, :] + (pn[r, :].astype(jnp.float32) + rn[r, :].astype(jnp.float32))
            xv[r, :] = v
            n2[r, :] = (v * lax.rsqrt(jnp.mean(v * v, axis=1, keepdims=True) + epsilon) * g).astype(jnp.bfloat16)
            return 0

        lax.fori_loop(0, TR // 16, go, 0)

    def cot_load(k):
        return pltpu.make_async_copy(cot.at[rows_of(k), :], e_f.at[k % 2], e_s.at[k % 2])

    def cot_low():
        cot_load(0).start()
        for k in range(NP):
            if k + 1 < NP:
                cot_load(k + 1).start()
            cot_load(k).wait()
            gy[rows_of(k), :] = e_f[k % 2].astype(jnp.bfloat16)

    def activate(j):
        cols = pl.ds(pl.multiple_of(j * TC, TC), TC)

        def go(i, _):
            r = pl.ds(pl.multiple_of(i * 32, 32), 32)
            v = gate[r, cols]
            act[r, cols] = (v * sigmoid(v) * up[r, cols]).astype(jnp.bfloat16)
            return 0

        lax.fori_loop(0, n // 32, go, 0)

    def gd_copy(j, s):
        return pltpu.make_async_copy(stg.at[s], gd_o.at[pl.ds(pl.multiple_of(j * TC, TC), TC), :], g_s.at[s])

    def down_grad(j0, j1):
        def go(j, _):
            s = lax.rem(j, 2)

            @pl.when(j >= 2)
            def _():
                gd_copy(j - 2, s).wait()

            stg[s] = dot_o(gy[:, pl.ds(pl.multiple_of(j * TC, TC), TC)], act[...]).astype(jnp.bfloat16)
            gd_copy(j, s).start()
            return 0

        lax.fori_loop(j0, j1, go, 0)

    own_low(2)
    norm_in()
    for w in range(3, nw):
        own_low(w)
    for w, src, dst, o, k in ((0, w_in, pi, pi_o, 1), (1, w_f, pf, pf_o, 2), (2, w_g, pg, pg_o, 3)):
        if w == 0:
            tick(0, 1)
            tick(0, 2)
            tick(0, 3)
        tick(w + 1, 1)
        tick(w + 1, 2)
        finish(w)
        times(n1, src, dst, NW)
        put(dst, o, k)
        if w < 2:
            tick(w + 1, 3)
    ends = [forward_scan_one(0, length, pi, pf, low, link, h, cum)]
    tick(3, 3)
    for sq in range(1, seqs):
        ends.append(forward_scan_one(sq, length, pi, pf, low, link, h, cum))
    pay[4:8, :] = ids[...]
    for sq in range(seqs):
        pay[sq:sq + 1, :] = ends[sq][1]
        pay[2 + sq:3 + sq, :] = ends[sq][0]
    cps = spread(Z, z, pay, box, s_c, r_c)
    tick(4, 1)
    cot_low()
    put(gy, gy_o, 4)
    spread_wait(Z, z, pay, box, s_c, r_c, cps)
    start[...] = prefix_state(Z, z, box)
    forward_finish(seqs, length, h, cum, start, rh)
    put(h, h_o, 5)
    swap_columns(rh, row, got, s_t.at[0], r_t.at[0], 1 - t, n)
    scale_columns(row, got, rh, n, width, lambda v: lax.rsqrt(v / width + epsilon))
    mixed(h, rh, hgain, pg, m)
    put(m, m_o, 6)
    tick(4, 2)
    finish(3)
    out_product()
    tick(4, 3)
    for k in range(NP // 2):
        middle(k)
    tick(5, 1)
    for k in range(NP // 2, NP):
        middle(k)
    put(xv, mid_o, 7)
    put(n2, n2_o, 8)
    tick(5, 2)
    finish(4)
    times(n2, w_mg, gate, NF)
    put(gate, gate_o, 9)
    tick(5, 3)
    tick(6, 1)
    finish(5)
    times(n2, w_mu, up, NF, activate)
    put(up, up_o, 10)
    put(act, act_o, 11)
    tick(6, 2)
    down_grad(0, NC // 2)
    tick(6, 3)
    down_grad(NC // 2, NC)
    last()
    finish(6)
    gd_copy(NC - 2, NC % 2).wait()
    gd_copy(NC - 1, (NC - 1) % 2).wait()
    for k in range(NP):
        pn_copy(k).wait_send()
    for cp in done:
        cp.wait()


def front_all(Z, seqs, length, shards, x, cot, gain1, gain2, low, hgain, link, ids, cid=0, ahead=2):
    nw = len(shards)
    n, width = x.shape
    C, F = shards[0].shape[1], shards[4].shape[1]
    dma = pltpu.SemaphoreType.DMA
    bf, f = jnp.bfloat16, jnp.float32
    sh = jax.ShapeDtypeStruct
    anyw, vmem = pl.BlockSpec(memory_space=pl.ANY), pl.BlockSpec(memory_space=pltpu.VMEM)
    NP = n // TR
    V = pltpu.VMEM
    out_shape = ([sh((a.shape[0] * 4 * Z, a.shape[1]), bf) for a in shards]
                 + [sh((n, width), bf)] + [sh((n, C), f)] * 4 + [sh((n, C), bf)] + [sh((n, width), f), sh((n, width), bf)]
                 + [sh((n, F), f)] * 2 + [sh((n, F), bf), sh((n, width), bf), sh((width, F), bf), sh((n, 1), f), sh((seqs, C), f)])
    scratch = [
        V((n, width), f), V((n, width), bf), V((n, width), bf), V((n, C), f), V((n, C), f), V((n, C), f), V((n, C), f), V((n, C), f),
        V((n, C), bf), V((2, width, TC), bf), V((2, TC, C), bf), V((n, width), bf), V((n, width), bf), V((n, F), f), V((n, F), f),
        V((n, F), bf), V((n, width), bf), V((2, TC, F), bf), V((2, TR, width), f),
        V((8, C), f), V((Z, 8, C), f), V((n // 128, 128), f), V((n // 128, 128), f),
        V((2, shards[0].shape[0], F), f),
    ] + [V(a.shape, bf) for a in shards] + [
        dma((Z - 1,)), dma((Z,)), dma((1,)), dma((1,)), dma((NP,)), dma((NP,)), dma((2,)), dma((12,)), dma((2,)), dma((2,)), dma((1,)), dma((2,)),
        dma((nw, Z - 1)), dma((nw, Z - 1)), dma((nw, Z - 1)), dma((nw, Z - 1)),
        dma((nw, 2 * Z - 1)), dma((nw, 2 * Z - 1)),
        dma((nw, 4 * Z - 2)), dma((nw, 4 * Z - 2)), dma((nw,)), dma((nw,)), dma((nw,)),
    ]
    res = pl.pallas_call(
        functools.partial(front_body, Z, seqs, length, ahead),
        out_shape=out_shape,
        in_specs=[anyw] * (nw + 2) + [vmem] * 6,
        out_specs=[anyw] * (len(out_shape) - 2) + [vmem] * 2,
        scratch_shapes=scratch,
        compiler_params=pltpu.CompilerParams(collective_id=cid, has_side_effects=True, vmem_limit_bytes=66_000_000),
        name="forward",
    )(*shards, x, cot, gain1, gain2, low, hgain, link, ids)
    return res[:nw], res[nw:]


TR = 64
TC = 256


def dot_t(a, b):
    return lax.dot_general(a, b, (((1,), (1,)), ((), ())), preferred_element_type=jnp.float32)


def dot_o(a, b):
    return lax.dot_general(a, b, (((0,), (0,)), ((), ())), preferred_element_type=jnp.float32)


def back_body(Z, seqs, length, *refs):
    (gd, gy_h, n2_h, act_h, gate_h, up_h, w_dn, w_mg, w_mu, x, mid, cot, n1, m, w_out, w_in, w_f, w_g,
     pi_h, pf_h, pg_h, h_h, rh, start, ids, link, gain1, gain2, low, hgain) = refs[:30]
    dx, vec_out = refs[30:32]
    grads = refs[32:39]
    mparts = refs[39:45]
    pn, po, rn, ro = refs[45:49]
    k0 = 49
    rc, xr, zu, zd, hr = (refs[k0 + 7 * i:k0 + 7 * (i + 1)] for i in range(5))
    k0 += 35
    (xs, zs, stage, stage_z, fin, dmid, gm, dm, h, pi, pf, pg, gl, tail, dpi, dpf, dpg, n1v, mv, wbuf, tb, du, sn, rn1,
     e_f, e_b, vec, vgot, vbox, col, end, pay, box, row, got) = refs[k0:k0 + 35]
    k0 += 35
    (l_h, l_n, w_s, g_s, n_s, n_r, o_s, o_r, t_s, t_r, e_s, eo_s, v_s, v_r, vz_s, vz_r, s_c, r_c, s_t, r_t, b_s) = refs[k0:k0 + 21]
    sems = refs[k0 + 21:]
    n, width = x.shape
    C = dm.shape[1]
    F = du.shape[1]
    parts = (gd,) + tuple(mparts)
    sc = Scatter(Z, parts, rc, xr, zu, zd, hr, grads, xs, zs, (stage, stage_z), fin, sems)
    z = sc.z
    t = lax.axis_index("tp")
    OTHER = {"tp": 1 - t}

    barrier = pltpu.get_barrier_semaphore()
    for d in [sc.X, sc.C, OTHER] + [{"ctx": lax.rem(z + o, Z)} for o in range(1, Z)]:
        pl.semaphore_signal(barrier, inc=1, device_id=d, device_id_type=MESH)
    pl.semaphore_wait(barrier, 2 + Z)

    sc.c_send(0)

    NP = n // TR
    NC = width // TC

    def rows_of(k):
        return pl.ds(k * TR, TR)

    def pn_copy(k):
        return remote(pn.at[rows_of(k), :], rn.at[rows_of(k), :], n_s.at[k], n_r.at[k], OTHER)

    def po_copy(k):
        return remote(po.at[rows_of(k), :], ro.at[rows_of(k), :], o_s.at[k], o_r.at[k], OTHER)

    early = [pltpu.make_async_copy(a, b, l_h.at[i]) for i, (a, b) in enumerate(
        ((pi_h, pi), (pf_h, pf), (pg_h, pg), (h_h, h), (m, mv), (gy_h, n1v), (n2_h, gm), (mid, dmid)))]
    for cp in early:
        cp.start()
    vec[...] = jnp.zeros_like(vec)

    steps = []

    def X(w):
        return [functools.partial(sc.x_phase, w, k) for k in range(Z)]

    def E(w, k):
        return functools.partial(sc.z_step, w, k, True)

    def M(w, k):
        return functools.partial(sc.z_step, w, k, False)

    def tick(*todo):
        for s in todo:
            s()

    def piece(k, s, f_src, b_src):
        r = rows_of(k)
        return ([pltpu.make_async_copy(a.at[r, :], e_f.at[s, i], e_s.at[s, i]) for i, a in enumerate(f_src)]
                + [pltpu.make_async_copy(a.at[r, :], e_b.at[s, i], e_s.at[s, 2 + i]) for i, a in enumerate(b_src)])

    def p1_load(k):
        pn_copy(k).wait_recv()
        for cp in piece(k, k % 2, (cot,), (pn, rn)):
            cp.start()

    def p1(k):
        s = k % 2
        for cp in piece(k, s, (cot,), (pn, rn)):
            cp.wait()
        g = gain2[...]

        def go(i, a):
            r = pl.ds(pl.multiple_of(i * 16, 16), 16)
            rr = pl.ds(pl.multiple_of(k * TR + i * 16, 16), 16)
            v, ct = dmid[rr, :], e_f[s, 0, r, :]
            d = e_b[s, 0, r, :].astype(jnp.float32) + e_b[s, 1, r, :].astype(jnp.float32)
            r2 = lax.rsqrt(jnp.mean(v * v, axis=1, keepdims=True) + epsilon)
            gdn = d * g
            inner = jnp.mean(gdn * v, axis=1, keepdims=True)
            o = ct + gdn * r2 - v * (r2 * r2 * r2 * inner)
            dmid[rr, :] = o
            gm[rr, :] = o.astype(jnp.bfloat16)
            return a + jnp.sum(d * v * r2, axis=0, keepdims=True)

        vec[1:2, :] = vec[1:2, :] + lax.fori_loop(0, TR // 16, go, jnp.zeros((1, width), jnp.float32))

    segments = [(b, a, min(C, F - a)) for b, a in ((dpi, 0), (dpf, C), (dpg, 2 * C))]

    def tile_of(j):
        return pl.ds(pl.multiple_of(j * TC, TC), TC)

    def glu_loads(j, s):
        return [pltpu.make_async_copy(a.at[:, tile_of(j)], b, w_s.at[s, i]) for i, (a, b) in enumerate(
            ((w_dn, wbuf.at[s]), (gate_h, gl.at[:, tile_of(s)]), (up_h, tail.at[:, tile_of(s)])))]

    def glu_cols(g):
        buf, first, size = segments[g]

        def go(j, _):
            s = lax.rem(j, 2)

            @pl.when(j + 1 < F // TC)
            def _():
                for cp in glu_loads(j + 1, 1 - s):
                    cp.start()

            for cp in glu_loads(j, s):
                cp.wait()
            dm[:, :TC] = jnp.dot(n1v[...], wbuf[s], preferred_element_type=jnp.float32)
            here, there = tile_of(s), tile_of(j)
            inside = tile_of(j - first // TC)

            def rows(i, _):
                r = pl.ds(pl.multiple_of(i * 32, 32), 32)
                v, u, d = gl[r, here], tail[r, here], dm[r, :TC]
                sg = sigmoid(v)
                buf[r, inside] = (d * u * (sg * (1.0 + v * (1.0 - sg)))).astype(jnp.bfloat16)
                du[r, there] = (d * (v * sg)).astype(jnp.bfloat16)
                return 0

            lax.fori_loop(0, n // 32, rows, 0)
            return 0

        lax.fori_loop(first // TC, (first + size) // TC, go, 0)

    def w_rows(w, j, s):
        return pltpu.make_async_copy(w.at[tile_of(j), :], tb.at[s, :, pl.ds(0, F)], w_s.at[2 + s, 0])

    def sn_out(dst, j):
        return pltpu.make_async_copy(sn.at[j], dst.at[:, tile_of(j)], b_s.at[j])

    def normed(j0, j1):
        def go(j, _):
            w_rows(w_mg, j, 0).wait()
            o = None
            for buf, first, size in segments:
                v = dot_t(buf[:, :size], tb[0, :, first:first + size])
                o = v if o is None else o + v

            @pl.when(j + 1 < NC)
            def _():
                w_rows(w_mg, j + 1, 0).start()

            w_rows(w_mu, j, 1).wait()
            o = o + dot_t(du[...], tb[1, :, :F])

            @pl.when(j + 1 < NC)
            def _():
                w_rows(w_mu, j + 1, 1).start()

            sn[j] = o.astype(jnp.bfloat16)
            sn_out(pn, j).start()
            return 0

        lax.fori_loop(j0, j1, go, 0)

    def t_copy(dst, j, s):
        return pltpu.make_async_copy(tb.at[s, :, pl.ds(0, dst.shape[1])], dst.at[tile_of(j), :], g_s.at[s])

    def glu_grad(w, cols, j0, j1):
        dst = parts[w]

        def go(j, _):
            s = lax.rem(j, 2)

            @pl.when(j >= 2)
            def _():
                t_copy(dst, j - 2, s).wait()

            lhs = gm[:, tile_of(j)]
            for buf, first, size in cols:
                tb[s, :, first:first + size] = dot_o(lhs, buf[:, :size]).astype(jnp.bfloat16)
            t_copy(dst, j, s).start()
            return 0

        lax.fori_loop(j0, j1, go, 0)
        if j1 == NC:
            t_copy(dst, NC - 2, NC % 2).wait()
            t_copy(dst, NC - 1, (NC - 1) % 2).wait()
            sc.c_send(w)

    def down(j0, j1):
        def go(j, _):
            s = lax.rem(j, 2)

            @pl.when(j + 1 < NC)
            def _():
                w_rows(w_dn, j + 1, 1 - s).start()

            w_rows(w_dn, j, s).wait()
            sn[j] = dot_t(du[...], tb[s, :, :F]).astype(jnp.bfloat16)
            sn_out(po, j).start()
            return 0

        lax.fori_loop(j0, j1, go, 0)

    NW = C // TC

    def w_load(j, s):
        return pltpu.make_async_copy(w_out.at[:, pl.ds(pl.multiple_of(j * TC, TC), TC)], wbuf.at[s], w_s.at[s, 0])

    def p2():
        w_load(0, 0).start()

        def go(j, _):
            s = lax.rem(j, 2)

            @pl.when(j + 1 < NW)
            def _():
                w_load(j + 1, 1 - s).start()

            w_load(j, s).wait()
            dm[:, pl.ds(pl.multiple_of(j * TC, TC), TC)] = jnp.dot(gm[...], wbuf[s], preferred_element_type=jnp.float32)
            return 0

        lax.fori_loop(0, NW, go, 0)

    def p4(w, lhs, rhs):
        dst = parts[w]

        def go(j, _):
            s = lax.rem(j, 2)

            @pl.when(j >= 2)
            def _():
                t_copy(dst, j - 2, s).wait()

            tb[s, :, :C] = dot_o(lhs[:, tile_of(j)], rhs[...]).astype(jnp.bfloat16)
            t_copy(dst, j, s).start()
            return 0

        lax.fori_loop(0, NC, go, 0)
        t_copy(dst, NC - 2, NC % 2).wait()
        t_copy(dst, NC - 1, (NC - 1) % 2).wait()
        sc.c_send(w)

    def w3(j, s):
        return [pltpu.make_async_copy(a.at[tile_of(j), :], tb.at[s, :, pl.ds(i * C, C)], w_s.at[2 + s, i])
                for i, a in enumerate((w_in, w_f, w_g))]

    def w3_start(j, s):
        for cp in w3(j, s):
            cp.start()

    def w3_wait(j, s):
        for cp in w3(j, s):
            cp.wait()

    def n_copy(j):
        return remote(sn.at[j], rn1.at[j], t_s.at[j], t_r.at[j], OTHER)

    def p5(j0, j1):
        def go(j, _):
            s = lax.rem(j, 2)

            @pl.when(j + 1 < NC)
            def _():
                w3_start(j + 1, 1 - s)

            w3_wait(j, s)
            o = dot_t(dpi[...], tb[s, :, :C]) + dot_t(dpf[...], tb[s, :, C:2 * C]) + dot_t(dpg[...], tb[s, :, 2 * C:3 * C])
            sn[j] = o.astype(jnp.bfloat16)
            n_copy(j).start()
            return 0

        lax.fori_loop(j0, j1, go, 0)

    def x_load(j, s):
        return pltpu.make_async_copy(x.at[:, pl.ds(j * TC, TC)], tail.at[:, pl.ds(s * TC, TC)], e_s.at[s, 0])

    def p6a(j):
        s = j % 2
        if j == 0:
            x_load(0, 0).start()
        if j + 1 < NC:
            x_load(j + 1, 1 - s).start()
        x_load(j, s).wait()
        n_copy(j).wait_recv()
        g = gain1[:, j * TC:(j + 1) * TC]

        def go(i, _):
            r = pl.ds(pl.multiple_of(i * 16, 16), 16)
            v = tail[r, s * TC:(s + 1) * TC]
            d = sn[j, r, :].astype(jnp.float32) + rn1[j, r, :].astype(jnp.float32)
            a, b = v * v, d * g * v
            a, b = a[:, :128] + a[:, 128:], b[:, :128] + b[:, 128:]
            if j == 0:
                dm[r, :128] = a
                dm[r, 128:256] = b
            else:
                dm[r, :128] = dm[r, :128] + a
                dm[r, 128:256] = dm[r, 128:256] + b
            return 0

        lax.fori_loop(0, n // 16, go, 0, unroll=2)

    def p6b():
        def go(i, _):
            r = pl.ds(pl.multiple_of(i * 16, 16), 16)
            r1 = lax.rsqrt(jnp.sum(dm[r, :128], axis=1, keepdims=True) / width + epsilon)
            inner = jnp.sum(dm[r, 128:256], axis=1, keepdims=True) / width
            dm[r, :128] = jnp.broadcast_to(r1, (16, 128))
            dm[r, 128:256] = jnp.broadcast_to(r1 * r1 * r1 * inner, (16, 128))
            return 0

        lax.fori_loop(0, n // 16, go, 0, unroll=2)

    def dx_copy(j):
        s = j % 2
        return pltpu.make_async_copy(gl.at[:, pl.ds(s * TC, TC)], dx.at[:, pl.ds(j * TC, TC)], eo_s.at[s])

    def p6c(j):
        s = j % 2
        if j == 0:
            x_load(0, 0).start()
        if j + 1 < NC:
            x_load(j + 1, 1 - s).start()
        x_load(j, s).wait()
        if j >= 2:
            dx_copy(j - 2).wait()
        g = gain1[:, j * TC:(j + 1) * TC]

        def go(i, total):
            r = pl.ds(pl.multiple_of(i * 16, 16), 16)
            v = tail[r, s * TC:(s + 1) * TC]
            d = sn[j, r, :].astype(jnp.float32) + rn1[j, r, :].astype(jnp.float32)
            r1 = jnp.concatenate([dm[r, :128], dm[r, :128]], axis=1)
            ri = jnp.concatenate([dm[r, 128:256], dm[r, 128:256]], axis=1)
            gl[r, s * TC:(s + 1) * TC] = dmid[r, j * TC:(j + 1) * TC] + d * g * r1 - v * ri
            return total + jnp.sum(d * v * r1, axis=0, keepdims=True)

        vec[0:1, j * TC:(j + 1) * TC] = lax.fori_loop(0, n // 16, go, jnp.zeros((1, TC), jnp.float32), unroll=2)
        dx_copy(j).start()

    x0, x1, x2, x3, x4, x5, x6 = (X(w) for w in range(7))
    for cp in glu_loads(0, 0):
        cp.start()
    early[5].wait()
    glu_cols(0)
    tick(x0[0])
    glu_cols(1)
    tick(x0[1])
    glu_cols(2)
    tick(x0[2])
    load_n1 = pltpu.make_async_copy(n1, n1v, l_h.at[5])
    load_n1.start()
    early[6].wait()
    glu_grad(1, segments, 0, NC // 2)
    tick(E(0, 0))
    glu_grad(1, segments, NC // 2, NC)
    w_rows(w_mg, 0, 0).start()
    w_rows(w_mu, 0, 1).start()
    tick(x0[3], M(0, 0), E(0, 1))
    normed(0, NC // 2)
    tick(x1[0], M(0, 1), E(0, 2))
    normed(NC // 2, NC)
    for j in range(NC):
        sn_out(pn, j).wait()
    for k in range(NP):
        pn_copy(k).start()
    tick(x1[1], M(0, 2), E(0, 3))
    glu_grad(2, [(du, 0, F)], 0, NC // 2)
    tick(x1[2], M(0, 3))
    glu_grad(2, [(du, 0, F)], NC // 2, NC)
    load_act = pltpu.make_async_copy(act_h, du, l_h.at[6])
    load_act.start()
    w_rows(w_dn, 0, 0).start()
    tick(E(1, 0))
    load_act.wait()
    down(0, NC // 2)
    tick(x1[3], M(1, 0), E(1, 1))
    down(NC // 2, NC)
    for j in range(NC):
        sn_out(po, j).wait()
    for k in range(NP):
        po_copy(k).start()
    p1_load(0)
    tick(x2[0], M(1, 1), E(1, 2))
    early[7].wait()
    between = [[], [x2[1]], [], [M(1, 2), E(1, 3)], [], [x2[2]], [], [M(1, 3)]]
    for k in range(NP):
        if k + 1 < NP:
            p1_load(k + 1)
        p1(k)
        tick(*(between[k] if k < len(between) else []))
    p2()
    tick(x2[3], E(2, 0))
    for cp in early[:5]:
        cp.wait()
    load_n1.wait()
    p4(3, gm, mv)
    tick(M(2, 0))
    backward_first(n, dm, h, pg, hgain, rh, dpg, col, acc_row(vec, 2, C))
    column_to_rows(col, row, n)
    swap = remote(row, got, s_t.at[0], r_t.at[0], OTHER)
    swap.start()
    tick(x3[0], x3[1])
    swap.wait()
    scale_columns(row, got, col, n, width, lambda v: v / width)
    ends = []
    for sq in range(seqs):
        ends.append(backward_scan_one(sq, length, dm, h, pf, pg, low, hgain, link, rh, col, gl, tail))
        if sq == 0:
            tick(x3[2])
    pay[4:8, :] = ids[...]
    for sq in range(seqs):
        pay[sq:sq + 1, :] = ends[sq][1]
        pay[2 + sq:3 + sq, :] = ends[sq][0]
    cps = spread(Z, z, pay, box, s_c, r_c)
    w3_start(0, 0)
    tick(E(2, 1), x3[3], M(2, 1), E(2, 2))
    spread_wait(Z, z, pay, box, s_c, r_c, cps)
    end[...] = suffix_state(Z, z, box)
    backward_last(seqs, length, gl, tail, end, h, start, pi, pf, low, link, dpi, dpf, acc_row(vec, 3, C))
    tick(M(2, 2), E(2, 3))
    p5(0, NC // 2)
    tick(M(2, 3), E(3, 0))
    p5(NC // 2, NC)
    tick(M(3, 0), E(3, 1))
    p4(4, n1v, dpi)
    tick(M(3, 1), E(3, 2), x4[0], x4[1])
    p4(5, n1v, dpf)
    tick(M(3, 2), E(3, 3), x4[2], x4[3])
    p4(6, n1v, dpg)
    tick(M(3, 3), E(4, 0), x5[0], x5[1])
    late = [[M(4, 0), E(4, 1)], [x5[2], x5[3]], [M(4, 1), E(4, 2)], [x6[0], x6[1]], [M(4, 2), E(4, 3)], [x6[2]],
            [M(4, 3), E(5, 0)], [x6[3]]]
    for j in range(NC):
        p6a(j)
        tick(*(late[j] if j < len(late) else []))
    p6b()
    tick(M(5, 0), E(5, 1))
    late = {1: [M(5, 1), E(5, 2)], 3: [M(5, 2), E(5, 3)], 5: [M(5, 3), E(6, 0)], 7: [M(6, 0), E(6, 1)]}
    for j in range(NC):
        p6c(j)
        tick(*late.get(j, []))
    for j in (NC - 2, NC - 1):
        dx_copy(j).wait()
    first = remote(vec, vgot.at[0], v_s.at[0], v_r.at[0], sc.C)
    first.start()
    tick(M(6, 1), E(6, 2))
    first.wait()
    vec[...] = vec[...] + vgot[0]
    second = remote(vec, vgot.at[1], v_s.at[1], v_r.at[1], sc.X)
    second.start()
    tick(M(6, 2), E(6, 3))
    second.wait()
    vec[...] = vec[...] + vgot[1]
    cps = spread(Z, z, vec, vbox, vz_s, vz_r)
    tick(M(6, 3))
    spread_wait(Z, z, vec, vbox, vz_s, vz_r, cps)
    total = vbox[0]
    for k in range(1, Z):
        total = total + vbox[k]
    vec_out[...] = total
    for k in range(NP):
        pn_copy(k).wait_send()
        po_copy(k).wait_send()
        po_copy(k).wait_recv()
    for j in range(NC):
        n_copy(j).wait_send()
    for w in range(7):
        sc.drain(w, 7)


def acc_row(vec, k, C):
    return vec.at[k:k + 1, pl.ds(0, C)]


def back_all(Z, seqs, length, gd, gy, n2, act, gate, up, w_dn, w_mg, w_mu, x, mid, cot, n1, m, w_out, w_in, w_f, w_g,
             pi, pf, pg, h, rh, start, ids, link, gain1, gain2, low, hgain, cid=1):
    n, width = x.shape
    C, F = pi.shape[1], gate.shape[1]
    dma = pltpu.SemaphoreType.DMA
    bf, f = jnp.bfloat16, jnp.float32
    sh = jax.ShapeDtypeStruct
    anyw, vmem = pl.BlockSpec(memory_space=pl.ANY), pl.BlockSpec(memory_space=pltpu.VMEM)
    shapes = [(width, F)] * 3 + [(width, C)] * 4
    R = [s[0] // (4 * Z) for s in shapes]
    N = [s[1] for s in shapes]
    Rm, Nm = max(R), max(N)
    NP, NC = n // TR, width // TC
    out_shape = ([sh((n, width), f), sh((8, width), f)]
                 + [sh((r, k), f) for r, k in zip(R, N)]
                 + [sh((width, F), bf)] * 2 + [sh((width, C), bf)] * 4
                 + [sh((n, width), bf)] * 4
                 + [sh((2 * Z * r, k), bf) for r, k in zip(R, N)]
                 + [sh((Z * r, k), bf) for r, k in zip(R, N)]
                 + [sh((Z * r, k), bf) for r, k in zip(R, N)]
                 + [sh((Z * r, k), bf) for r, k in zip(R, N)]
                 + [sh((r // 2, k), bf) for r, k in zip(R, N)])
    V = pltpu.VMEM
    scratch = [
        V((2, Z, Rm, Nm), bf), V((2, Z - 1, Rm, Nm), bf), V((2, 3, Rm, Nm), bf), V((5, Rm, Nm), bf), V((Rm, Nm), f),
        V((n, width), f), V((n, width), bf), V((n, C), f), V((n, C), f), V((n, C), f), V((n, C), f), V((n, C), f),
        V((n, C), f), V((n, C), f), V((n, C), bf), V((n, C), bf), V((n, C), bf), V((n, width), bf), V((n, C), bf),
        V((2, width, TC), bf), V((2, TC, 3 * C), bf), V((n, F), bf), V((NC, n, TC), bf), V((NC, n, TC), bf),
        V((2, 1, TR, width), f), V((2, 2, TR, width), bf), V((8, width), f), V((2, 8, width), f), V((Z, 8, width), f),
        V((n, 1), f), V((seqs, C), f), V((8, C), f), V((Z, 8, C), f), V((n // 128, 128), f), V((n // 128, 128), f),
        dma((8,)), dma((1,)), dma((4, 3)), dma((2,)), dma((NP,)), dma((NP,)), dma((NP,)), dma((NP,)), dma((NC,)), dma((NC,)),
        dma((2, 4)), dma((2,)), dma((2,)), dma((2,)), dma((Z - 1,)), dma((Z,)), dma((Z - 1,)), dma((Z,)), dma((1,)), dma((1,)),
        dma((NC,)),
        dma((7, 2)), dma((7, 2)), dma((7, Z)), dma((7, Z)), dma((7, Z - 1)), dma((7, Z)), dma((7, Z)),
        dma((7,)), dma((7,)), dma((3, 5)), dma((7,)),
    ]
    res = pl.pallas_call(
        functools.partial(back_body, Z, seqs, length),
        out_shape=out_shape,
        in_specs=[anyw] * 22 + [vmem] * 8,
        out_specs=[anyw, vmem] + [anyw] * (len(out_shape) - 2),
        scratch_shapes=scratch,
        compiler_params=pltpu.CompilerParams(collective_id=cid, has_side_effects=True, vmem_limit_bytes=66_000_000),
        name="backward",
    )(gd, gy, n2, act, gate, up, w_dn, w_mg, w_mu, x, mid, cot, n1, m, w_out, w_in, w_f, w_g, pi, pf, pg, h,
      rh, start, ids, link, gain1, gain2, low, hgain)
    return res[0], res[1], res[2:9], res[16], res[18]


def carried_in(x, axis, combine, identity, reverse):
    size, position = (lax.axis_size(axis), lax.axis_index(axis))
    everything = jax.tree.map(lambda part: lax.all_gather(part, axis), x)
    start = jax.tree.map(
        lambda part, zero: jnp.broadcast_to(jnp.asarray(zero, part.dtype), part.shape), x, identity
    )

    def turn(k, before):
        at = size - 1 - k if reverse else k
        reached = at > position if reverse else at < position
        new = combine(before, jax.tree.map(lambda part: part[at], everything))
        return jax.tree.map(lambda a, b: jnp.where(reached, a, b), new, before)

    return lax.fori_loop(0, size, turn, start)


def inverse_rms(inputs):
    return lax.rsqrt(jnp.mean(inputs * inputs, axis=-1, keepdims=True) + epsilon)


def rms_backward(inputs, row_scale, gain_vec, upstream):
    weighted = upstream * gain_vec
    inner_sum = jnp.mean(weighted * inputs, axis=-1, keepdims=True)
    return weighted * row_scale - inputs * (row_scale * row_scale * row_scale) * inner_sum


def silu_slope(inputs):
    sig_part = jax.nn.sigmoid(inputs)
    return sig_part * (1.0 + inputs * (1.0 - sig_part))


def times_back(left_mat, right_mat):
    return lax.dot_general(
        left_mat, right_mat, (((1,), (1,)), ((), ())), preferred_element_type=jnp.float32
    )


def outer_sum(left_mat, right_mat):
    return lax.dot_general(
        left_mat, right_mat, (((0,), (0,)), ((), ())), preferred_element_type=jnp.float32
    )


def linear_step(first_part, second_part):
    return (first_part[0] * second_part[0], second_part[0] * first_part[1] + second_part[1])


def joined_ids(last_ids, first_ids):
    return jnp.where((last_ids == first_ids) | (last_ids < 0.0) | (first_ids < 0.0), 1.0, 0.0)


def forward_join(first_part, second_part):
    linked = joined_ids(first_part[3], second_part[2])[:, None]
    return (
        first_part[0] * second_part[0] * linked,
        second_part[0] * linked * first_part[1] + second_part[1],
        jnp.where(first_part[2] < 0.0, second_part[2], first_part[2]),
        jnp.where(second_part[3] < 0.0, first_part[3], second_part[3]),
    )


def backward_join(first_part, second_part):
    linked = joined_ids(second_part[3], first_part[2])[:, None]
    return (
        second_part[0] * linked * first_part[0],
        second_part[0] * linked * first_part[1] + second_part[1],
        jnp.where(second_part[2] < 0.0, first_part[2], second_part[2]),
        jnp.where(first_part[3] < 0.0, second_part[3], first_part[3]),
    )


def mixer_forward_plain(seqs, length, width, pi, pf, pg, lower, gain, segs):
    channels = pi.shape[1]
    forget = lower + (1.0 - lower) * jax.nn.sigmoid(pf)
    candidate = jax.nn.silu(pi) * (1.0 - forget)
    inner_link = jnp.concatenate(
        [jnp.ones((seqs, 1), jnp.float32), jnp.where(segs[:, 1:] == segs[:, :-1], 1.0, 0.0)], axis=1
    )
    decay = forget.reshape(seqs, length, channels) * inner_link[:, :, None]
    prod, local = lax.associative_scan(
        linear_step, (decay, candidate.reshape(seqs, length, channels)), axis=1
    )
    first, last = segs[:, 0], segs[:, -1]
    ones, zero = jnp.ones((seqs, channels), jnp.float32), jnp.zeros((seqs, channels), jnp.float32)
    minus = -jnp.ones((seqs,), jnp.float32)
    prefix = carried_in(
        (prod[:, -1], local[:, -1], first, last), "ctx", forward_join, (ones, zero, minus, minus), False
    )
    start = joined_ids(prefix[3], first)[:, None] * prefix[1]
    h = (local + prod * start[:, None, :]).reshape(seqs * length, channels)
    squares = lax.psum(jnp.sum(h * h, axis=1), "tp")
    rh = lax.rsqrt(squares / width + epsilon)[:, None]
    m = (h * rh * gain * jax.nn.silu(pg)).astype(jnp.bfloat16)
    return h, m, rh, start


def mixer_backward_plain(seqs, length, width, dm, h, pi, pf, pg, lower, gain, segs, rh, start):
    channels = pi.shape[1]
    s = jax.nn.sigmoid(pf)
    forget = lower + (1.0 - lower) * s
    inner_link = jnp.concatenate(
        [jnp.ones((seqs, 1), jnp.float32), jnp.where(segs[:, 1:] == segs[:, :-1], 1.0, 0.0)], axis=1
    )
    forget_seq = forget.reshape(seqs, length, channels)
    decay = forget_seq * inner_link[:, :, None]
    silu_gate = jax.nn.silu(pg)
    weighted = dm * gain * silu_gate
    inner = lax.psum(jnp.sum(weighted * h, axis=1), "tp")
    dh = weighted * rh - h * (rh * rh * rh) * (inner / width)[:, None]
    gain_grad = jnp.sum(dm * h * rh * silu_gate, axis=0)
    dpg = (dm * h * rh * gain * silu_slope(pg)).astype(jnp.bfloat16)
    ones_row = jnp.ones((seqs, 1, channels), jnp.float32)
    following = jnp.concatenate([decay[:, 1:], ones_row], axis=1)
    tail, local = lax.associative_scan(
        linear_step, (following, dh.reshape(seqs, length, channels)), reverse=True, axis=1
    )
    first, last = segs[:, 0], segs[:, -1]
    ones, zero = jnp.ones((seqs, channels), jnp.float32), jnp.zeros((seqs, channels), jnp.float32)
    minus = -jnp.ones((seqs,), jnp.float32)
    suffix = carried_in(
        (decay[:, 0] * tail[:, 0], forget_seq[:, 0] * local[:, 0], first, last),
        "ctx", backward_join, (ones, zero, minus, minus), True,
    )
    end = joined_ids(last, suffix[2])[:, None] * suffix[1]
    g = (local + tail * end[:, None, :]).reshape(seqs * length, channels)
    states = h.reshape(seqs, length, channels)
    previous = jnp.concatenate(
        [start[:, None, :], inner_link[:, 1:, None] * states[:, :-1]], axis=1
    ).reshape(seqs * length, channels)
    dforget = g * (previous - jax.nn.silu(pi))
    dpi = (g * (1.0 - forget) * silu_slope(pi)).astype(jnp.bfloat16)
    dpf = (dforget * (1.0 - lower) * s * (1.0 - s)).astype(jnp.bfloat16)
    return dpi, dpf, dpg, gain_grad, jnp.sum(dforget * (1.0 - s), axis=0)


def on_device(
    block_input,
    segment_ids,
    norm_gain,
    lower,
    w_input,
    w_forget,
    w_gate,
    hidden_gain,
    w_out,
    mlp_gain,
    w_mlp_gate,
    w_mlp_up,
    w_down,
    cotangent,
):
    bfloat, f32 = jnp.bfloat16, jnp.float32
    seqs, length, width = block_input.shape
    rows_all = seqs * length
    small = lax.axis_size("shard") == 4
    Z = lax.axis_size("ctx")
    shards = [w_input, w_forget, w_gate, w_out, w_mlp_gate, w_mlp_up, w_down]
    segs = segment_ids.astype(f32)
    residual_in = block_input.reshape(rows_all, width)
    upstream = cotangent.reshape(rows_all, width)
    channels = lower.shape[0]
    if small:
        link = jnp.concatenate(
            [jnp.ones((seqs, 1), f32), jnp.where(segs[:, 1:] == segs[:, :-1], 1.0, 0.0)], axis=1
        ).reshape(rows_all, 1)
        ids = jnp.broadcast_to(
            jnp.concatenate([segs[:, 0], segs[:, -1]])[:, None], (2 * seqs, channels)
        )
        low_row, gain_row = lower[None, :], hidden_gain[None, :]
        gain_one, gain_two = norm_gain[None, :], mlp_gain[None, :]
        wide, kept = front_all(
            Z, seqs, length, shards, residual_in, upstream, gain_one, gain_two, low_row, gain_row, link, ids
        )
        (normed_one, pi, pf, pg, h, mixed_in, middle, normed_two, gate_pre, up_pre, activated, upstream_low,
         grad_down, rh, start) = kept
        wide_input, wide_forget, wide_gate, wide_out, wide_mgate, wide_mup, wide_down = wide
        grad_resid, vectors, sums, down_mine, down_other = back_all(
            Z, seqs, length, grad_down, upstream_low, normed_two, activated, gate_pre, up_pre, wide_down, wide_mgate,
            wide_mup, residual_in, middle, upstream, normed_one, mixed_in, wide_out, wide_input, wide_forget, wide_gate,
            pi, pf, pg, h, rh, start, ids, link, gain_one, gain_two, low_row, gain_row
        )
        output = middle + (down_mine.astype(f32) + down_other.astype(f32))
        grad_norm_gain, grad_mlp_gain = vectors[0], vectors[1]
        grad_hidden_gain, grad_lower = vectors[2, :channels], vectors[3, :channels]
    else:
        wide = [lax.all_gather(w.astype(bfloat), ("shard", "ctx"), axis=0, tiled=True) for w in shards]
        wide_input, wide_forget, wide_gate, wide_out, wide_mgate, wide_mup, wide_down = wide
        scale_one = inverse_rms(residual_in)
        normed_one = (residual_in * scale_one * norm_gain).astype(bfloat)
        pi = jnp.dot(normed_one, wide_input, preferred_element_type=f32)
        pf = jnp.dot(normed_one, wide_forget, preferred_element_type=f32)
        pg = jnp.dot(normed_one, wide_gate, preferred_element_type=f32)
        h, mixed_in, rh, start = mixer_forward_plain(
            seqs, length, width, pi, pf, pg, lower, hidden_gain, segs
        )
        mixer_out = lax.psum(times_back(mixed_in, wide_out).astype(bfloat), "tp").astype(f32)
        middle = residual_in + mixer_out
        scale_two = inverse_rms(middle)
        normed_two = (middle * scale_two * mlp_gain).astype(bfloat)
        gate_pre = jnp.dot(normed_two, wide_mgate, preferred_element_type=f32)
        up_pre = jnp.dot(normed_two, wide_mup, preferred_element_type=f32)
        silu_mlp = jax.nn.silu(gate_pre)
        activated = (silu_mlp * up_pre).astype(bfloat)
        upstream_low = upstream.astype(bfloat)
        grad_down = outer_sum(upstream_low, activated).astype(bfloat)
        grad_activ = jnp.dot(upstream_low, wide_down, preferred_element_type=f32)
        grad_gate_pre = (grad_activ * up_pre * silu_slope(gate_pre)).astype(bfloat)
        grad_up_pre = (grad_activ * silu_mlp).astype(bfloat)
        grad_mgate = outer_sum(normed_two, grad_gate_pre).astype(bfloat)
        grad_mup = outer_sum(normed_two, grad_up_pre).astype(bfloat)
        down_part = times_back(activated, wide_down).astype(bfloat)
        normed_part = (times_back(grad_gate_pre, wide_mgate) + times_back(grad_up_pre, wide_mup)).astype(bfloat)
        output = middle + lax.psum(down_part, "tp").astype(f32)
        grad_normed_two = lax.psum(normed_part, "tp").astype(f32)
        grad_mlp_gain = jnp.sum(grad_normed_two * middle * scale_two, axis=0)
        grad_middle = upstream + rms_backward(middle, scale_two, mlp_gain, grad_normed_two)
        middle_low = grad_middle.astype(bfloat)
        dm = jnp.dot(middle_low, wide_out, preferred_element_type=f32)
        grad_out = outer_sum(middle_low, mixed_in).astype(bfloat)
        dpi, dpf, dpg, grad_hidden_gain, grad_lower = mixer_backward_plain(
            seqs, length, width, dm, h, pi, pf, pg, lower, hidden_gain, segs, rh, start
        )
        grad_w_input = outer_sum(normed_one, dpi).astype(bfloat)
        grad_w_forget = outer_sum(normed_one, dpf).astype(bfloat)
        grad_w_gate = outer_sum(normed_one, dpg).astype(bfloat)
        grad_normed_one = lax.psum(
            (
                times_back(dpi, wide_input) + times_back(dpf, wide_forget) + times_back(dpg, wide_gate)
            ).astype(bfloat),
            "tp",
        ).astype(f32)
        grad_norm_gain = jnp.sum(grad_normed_one * residual_in * scale_one, axis=0)
        grad_resid = grad_middle + rms_backward(residual_in, scale_one, norm_gain, grad_normed_one)
        vectors = lax.psum(
            jnp.concatenate([grad_norm_gain, grad_mlp_gain, grad_lower, grad_hidden_gain]), ("shard", "ctx")
        )
        grad_norm_gain, grad_mlp_gain = vectors[:width], vectors[width : 2 * width]
        grad_lower = vectors[2 * width : 2 * width + channels]
        grad_hidden_gain = vectors[2 * width + channels :]
        sums = [
            lax.psum_scatter(p, ("shard", "ctx"), scatter_dimension=0, tiled=True).astype(f32)
            for p in (grad_down, grad_mgate, grad_mup, grad_out, grad_w_input, grad_w_forget, grad_w_gate)
        ]
    return (
        output.reshape(block_input.shape),
        grad_resid.reshape(block_input.shape),
        grad_norm_gain,
        grad_lower,
        sums[4],
        sums[5],
        sums[6],
        grad_hidden_gain,
        sums[3],
        grad_mlp_gain,
        sums[1],
        sums[2],
        sums[0],
    )


def solution(mesh):
    return jax.shard_map(
        on_device,
        mesh=mesh,
        in_specs=(
            P("shard", "ctx", None),
            P("shard", "ctx"),
            P(),
            P("tp"),
            P(("shard", "ctx"), "tp"),
            P(("shard", "ctx"), "tp"),
            P(("shard", "ctx"), "tp"),
            P("tp"),
            P(("shard", "ctx"), "tp"),
            P(),
            P(("shard", "ctx"), "tp"),
            P(("shard", "ctx"), "tp"),
            P(("shard", "ctx"), "tp"),
            P("shard", "ctx", None),
        ),
        out_specs=(
            P("shard", "ctx", None),
            P("shard", "ctx", None),
            P(),
            P("tp"),
            P(("shard", "ctx"), "tp"),
            P(("shard", "ctx"), "tp"),
            P(("shard", "ctx"), "tp"),
            P("tp"),
            P(("shard", "ctx"), "tp"),
            P(),
            P(("shard", "ctx"), "tp"),
            P(("shard", "ctx"), "tp"),
            P(("shard", "ctx"), "tp"),
        ),
        check_vma=False,
    )
```
